32 devices in a mesh: fsdp: 4 (over y, x), ctx: 4 (over z), tp: 2 (over core).
Axes of the slice: x: 2, y: 2, z: 4, core: 2. Of those that a mesh axis runs over, the one named last changes fastest.
Arguments:
- tokens: bfloat16 [8, 2048, 768], P('fsdp', 'ctx'), may hold values from -6 to 6
- doc_lengths: int32 [8, 8], P('fsdp'), may hold values from 1 to 1536, 2048 in all within a row
- keep: int32 [8, 2048], P('fsdp', 'ctx'), may hold values 0 or 1
- w_query: bfloat16 [768, 768], P('fsdp', 'tp'), may hold values from -0.21875 to 0.21875
- b_query: float32 [768], P('tp'), may hold values from -3 to 3
- w_key: bfloat16 [768, 768], P('fsdp', 'tp'), may hold values from -0.21875 to 0.21875
- w_value: bfloat16 [768, 768], P('fsdp', 'tp'), may hold values from -0.21875 to 0.21875
- b_value: float32 [768], P('tp'), may hold values from -3 to 3
- w_out: bfloat16 [768, 768], P('fsdp', 'tp'), may hold values from -0.4375 to 0.4375
- b_out: float32 [768], replicated, may hold values from -3 to 3
- gain_one: float32 [768], replicated, may hold values from 0.5 to 1.5
- shift_one: float32 [768], replicated, may hold values from -2 to 2
- w_up: bfloat16 [768, 2, 3072], P('fsdp', None, 'tp'), may hold values from -0.21875 to 0.21875
- w_down: bfloat16 [768, 3072], P('fsdp', 'tp'), may hold values from -0.15625 to 0.15625
- b_down: float32 [768], replicated, may hold values from -3 to 3
- gain_two: float32 [768], replicated, may hold values from 0.5 to 1.5
- shift_two: float32 [768], replicated, may hold values from -2 to 2
- cotangent: bfloat16 [8, 2048, 768], P('fsdp', 'ctx'), may hold values from -6 to 6
Outputs:
- out: bfloat16 [8, 2048, 768], P('fsdp', 'ctx')
- d_tokens: float32 [8, 2048, 768], P('fsdp', 'ctx')
- d_w_query: float32 [768, 768], P('fsdp', 'tp')
- d_b_query: float32 [768], P('tp')
- d_w_key: float32 [768, 768], P('fsdp', 'tp')
- d_w_value: float32 [768, 768], P('fsdp', 'tp')
- d_b_value: float32 [768], P('tp')
- d_w_out: float32 [768, 768], P('fsdp', 'tp')
- d_b_out: float32 [768], replicated
- d_gain_one: float32 [768], replicated
- d_shift_one: float32 [768], replicated
- d_w_up: float32 [768, 2, 3072], P('fsdp', None, 'tp')
- d_w_down: float32 [768, 3072], P('fsdp', 'tp')
- d_b_down: float32 [768], replicated
- d_gain_two: float32 [768], replicated
- d_shift_two: float32 [768], replicated
The draws below stay inside these ranges and needn't reach their ends.
Inputs may be any that keep to these rules, and one draw needn't show every extreme that they name: `doc_lengths`: row b lists the lengths of the 8 documents of sequence b in order; they sum to 2048. `keep`: 0 marks a padding token, which only itself attends to.
All inputs are finite; a program needn't handle non-finite values. No bound on the sum of `keep` on one device may be relied on, other than what follows from the above.
Results may differ from the reference program's by a relative error of at most 0.029.
Values may be sent and summed in bfloat16 or wider, within the bound.
A program may use at most 256 MiB of HBM per device.

```python
import math
import jax
import jax.numpy as jnp
import numpy as np
from jax import lax

D = 768
HEADS = 12
HEAD = 64
FF = 3072
DOCS = 8
SEQ = 2048
BATCH = 8
DOC_MOST = 1536


def set_ends(values, rng, smallest, top_value):
    dims = values.shape
    place = [jax.random.randint(jax.random.fold_in(rng, axis), (), 0, dims[axis]) for axis in range(len(dims))]
    values = values.at[tuple(place)].set(smallest)
    longest = dims.index(max(dims))
    place[longest] = (place[longest] + 1) % dims[longest]
    return values.at[tuple(place)].set(top_value)


def block_levels(stream_key, extent, cuts, low, largest):
    def one(axis_at, parts):
        draws = jax.random.uniform(jax.random.fold_in(jax.random.fold_in(stream_key, 6), axis_at), (parts,), jnp.float32, low / len(cuts), largest / len(cuts))
        return jnp.repeat(jnp.exp(draws), extent[axis_at] // parts).reshape((-1,) + (1,) * (len(extent) - axis_at - 1))

    loudness = one(*cuts[0])
    for cut in cuts[1:]:
        loudness = loudness * one(*cut)
    return loudness


def length_profile(number_of, total, bound, lean):
    portions = [(1 << 20) // math.isqrt(rank ** lean) + 1 for rank in range(2, number_of + 1)]
    rest, given = total - bound - (number_of - 1), [1] * (number_of - 1)
    while rest > 0:
        free = [i for i in range(number_of - 1) if given[i] < bound]
        whole, left = sum([portions[i] for i in free]), rest
        for i in free:
            extra = min(bound - given[i], max(1, left * portions[i] // whole), rest)
            given[i] = given[i] + extra
            rest = rest - extra
    return np.array([bound] + given)


def uneven(key, amount, total, limit, skew):
    if amount == 2:
        one = jax.random.randint(key, (), max(1, total - limit), min(limit, total - 1) + 1)
        return jnp.stack([one, total - one])
    sizes = jnp.asarray(length_profile(amount, total, limit, skew), jnp.int32)
    couples = (amount - 1) // 2
    giver, receiver = sizes[1:1 + 2 * couples:2], sizes[2:2 + 2 * couples:2]
    margin = jnp.minimum(giver - 1, limit - receiver)
    passed = jax.random.randint(jax.random.fold_in(key, 1), (couples,), 0, 1 << 20) % (margin + 1)
    sizes = sizes.at[1:1 + 2 * couples:2].set(giver - passed).at[2:2 + 2 * couples:2].set(receiver + passed)
    return sizes[jax.random.permutation(jax.random.fold_in(key, 2), amount)]


def noise(rng, shape, scale, most, cuts=(), kind=jnp.bfloat16):
    loudness = block_levels(rng, shape, cuts, -0.22, 0.18) if cuts else 1.0
    values = jax.random.normal(rng, shape, jnp.float32) * scale * loudness
    return jnp.minimum(jnp.maximum(values, -most), most).astype(kind)


def setup_inputs(seed: int = 0) -> dict:
    seeds = jax.random.split(jax.random.key(seed), 19)
    return {
        "tokens": noise(seeds[0], (BATCH, SEQ, D), 1.0, 6.0, ((0, 4), (1, 4))),
        "doc_lengths": jax.vmap(lambda own: uneven(own, DOCS, SEQ, DOC_MOST, 2))(jax.random.split(seeds[1], BATCH)).reshape((BATCH, DOCS)).astype(jnp.int32),
        "keep": set_ends((jax.random.randint(seeds[2], (BATCH, SEQ), 0, 16) < 15).astype(jnp.int32), jax.random.fold_in(seeds[2], 1), 0, 1),
        "w_query": noise(seeds[3], (D, D), D ** -0.5, 0.21875, ((0, 4), (1, 2))),
        "b_query": noise(seeds[4], (D,), 0.5, 3.0, ((0, 2),), jnp.float32),
        "w_key": noise(seeds[5], (D, D), D ** -0.5, 0.21875, ((0, 4), (1, 2))),
        "w_value": noise(seeds[6], (D, D), D ** -0.5, 0.21875, ((0, 4), (1, 2))),
        "b_value": noise(seeds[7], (D,), 0.5, 3.0, ((0, 2),), jnp.float32),
        "w_out": noise(seeds[8], (D, D), (D // 4) ** -0.5, 0.4375, ((0, 4), (1, 2))),
        "b_out": noise(seeds[9], (D,), 0.5, 3.0, (), jnp.float32),
        "gain_one": jnp.clip(1.0 + 0.1 * jax.random.normal(seeds[10], (D,), jnp.float32), 0.5, 1.5),
        "shift_one": noise(seeds[11], (D,), 0.3, 2.0, (), jnp.float32),
        "w_up": noise(seeds[12], (D, 2, FF), D ** -0.5, 0.21875, ((0, 4), (2, 2))),
        "w_down": noise(seeds[13], (D, FF), (FF // 2) ** -0.5, 0.15625, ((0, 4), (1, 2))),
        "b_down": noise(seeds[14], (D,), 0.5, 3.0, (), jnp.float32),
        "gain_two": jnp.clip(1.0 + 0.1 * jax.random.normal(seeds[15], (D,), jnp.float32), 0.5, 1.5),
        "shift_two": noise(seeds[16], (D,), 0.3, 2.0, (), jnp.float32),
        "cotangent": noise(seeds[17], (BATCH, SEQ, D), 1.0, 6.0, ((0, 4), (1, 4))),
    }


NORM_EPS = 1e-12
MASKED = -1e+30
HIGH = lax.Precision.HIGHEST

@jax.custom_vjp
def low(v):
    return lax.optimization_barrier(v.astype(jnp.bfloat16)).astype(jnp.float32)

@jax.custom_vjp
def low_back(v):
    return v

def low_keep(v):
    return (low(v), None)

def low_pass(kept, grad):
    return (grad,)

def back_keep(v):
    return (v, None)

def back_low(kept, grad):
    return (low(grad),)
low.defvjp(low_keep, low_pass)
low_back.defvjp(back_keep, back_low)

def layer_norm(residual, norm_gain, norm_shift):
    centered = residual - lax.optimization_barrier(jnp.mean(residual, -1, keepdims=True))
    normed = centered * lax.rsqrt(lax.optimization_barrier(jnp.mean(centered * centered, -1, keepdims=True)) + NORM_EPS)
    return normed * norm_gain + norm_shift

def head_slopes():
    head_index = jnp.arange(HEADS, dtype=jnp.int32)
    head_float = head_index.astype(jnp.float32)
    return jnp.where(head_index < 8, jnp.exp2(-(head_float + 1.0)), jnp.exp2(-(head_float - 7.5)))

def attention(queries, key_rows, value_rows, seg_ids, keep_row, slopes):
    block_len = min(512, SEQ)
    positions = jnp.arange(SEQ, dtype=jnp.int32)

    def one_block(block_index):
        first_row = block_index * block_len
        query_part = lax.dynamic_slice_in_dim(queries, first_row, block_len, 0)
        query_pos = first_row + jnp.arange(block_len, dtype=jnp.int32)
        query_seg = lax.dynamic_slice_in_dim(seg_ids, first_row, block_len, 0)
        scores = jnp.einsum('qhd,khd->hqk', query_part, key_rows, precision=HIGH) * 0.125
        distance = jnp.abs(query_pos[:, None] - positions[None, :]).astype(jnp.float32)
        scores = low_back(scores - slopes[:, None, None] * distance[None])
        allowed = (query_seg[:, None] == seg_ids[None, :]) & ((keep_row[None, :] == 1) | (query_pos[:, None] == positions[None, :]))
        scores = jnp.where(allowed[None], scores, MASKED)
        row_max = lax.optimization_barrier(jnp.max(scores, -1, keepdims=True))
        exponent = jnp.exp(scores - row_max)
        probs = low(exponent / lax.optimization_barrier(jnp.sum(exponent, -1, keepdims=True)))
        return jnp.einsum('hqk,khd->qhd', probs, value_rows, precision=HIGH).reshape(block_len, HEADS * HEAD)
    outputs = lax.map(jax.checkpoint(one_block), jnp.arange(SEQ // block_len, dtype=jnp.int32))
    return outputs.reshape(SEQ, HEADS * HEAD)

def layer(params, token_row, seg_ids, keep_row, slopes):
    w_query, b_query, w_key, w_value, b_value, w_out, b_out, gain_one, shift_one, w_up, w_down, b_down, gain_two, shift_two = params
    queries = low_back(low(jnp.dot(token_row, w_query, precision=HIGH) + b_query))
    key_rows = low_back(low(jnp.dot(token_row, w_key, precision=HIGH)))
    value_rows = low_back(low(jnp.dot(token_row, w_value, precision=HIGH) + b_value))
    attended = low_back(low(attention(queries.reshape(SEQ, HEADS, HEAD), key_rows.reshape(SEQ, HEADS, HEAD), value_rows.reshape(SEQ, HEADS, HEAD), seg_ids, keep_row, slopes)))
    branch_att = low_back(jnp.dot(attended, w_out.T, precision=HIGH) + b_out)
    first_out = layer_norm(token_row + branch_att, gain_one, shift_one)
    first_low = low(first_out)
    gate_up = low_back(jnp.einsum('ld,dcf->lcf', first_low, w_up, precision=HIGH))
    hidden = low(jax.nn.gelu(gate_up[:, 0], approximate=False) * gate_up[:, 1])
    branch_ffn = low_back(jnp.dot(hidden, w_down.T, precision=HIGH) + b_down)
    return layer_norm(first_out + branch_ffn, gain_two, shift_two)

def reference(tokens, doc_lengths, keep, w_query, b_query, w_key, w_value, b_value, w_out, b_out, gain_one, shift_one, w_up, w_down, b_down, gain_two, shift_two, cotangent):
    params = tuple((weight_arg.astype(jnp.float32) for weight_arg in (w_query, b_query, w_key, w_value, b_value, w_out, b_out, gain_one, shift_one, w_up, w_down, b_down, gain_two, shift_two)))
    positions = jnp.arange(SEQ, dtype=jnp.int32)
    bounds = jnp.cumsum(doc_lengths, -1).astype(jnp.int32)
    seg_all = lax.optimization_barrier(jnp.sum((bounds[:, None, :] <= positions[None, :, None]).astype(jnp.int32), -1)).astype(jnp.int32)
    slopes = head_slopes()

    def per_sequence(totals, items):
        token_row, grad_row, seg_ids, keep_row = items
        result, pullback = jax.vjp(lambda weights, inputs: layer(weights, inputs, seg_ids, keep_row, slopes), params, token_row.astype(jnp.float32))
        weight_grads, input_grad = pullback(grad_row.astype(jnp.float32))
        totals = jax.tree.map(lambda left, right: left + right, totals, weight_grads)
        return (totals, (result.astype(jnp.bfloat16), input_grad))
    zeros = jax.tree.map(jnp.zeros_like, params)
    totals, (outputs, input_grads) = lax.scan(per_sequence, zeros, (tokens, cotangent, seg_all, keep))
    d_w_query, d_b_query, d_w_key, d_w_value, d_b_value, d_w_out, d_b_out, d_gain_one, d_shift_one, d_w_up, d_w_down, d_b_down, d_gain_two, d_shift_two = totals
    return (outputs, input_grads, d_w_query, d_b_query, d_w_key, d_w_value, d_b_value, d_w_out, d_b_out, d_gain_one, d_shift_one, d_w_up, d_w_down, d_b_down, d_gain_two, d_shift_two)
```

```python
import functools

import jax
import jax.numpy as jnp
from jax import lax
from jax.experimental import pallas as pl
from jax.experimental.pallas import tpu as pltpu
from jax.sharding import PartitionSpec as P

HEAD = 64


NORM_EPS = 1e-12
MASKED = -1e30


def layer_norm(residual, norm_gain, norm_shift):
    centered = residual - jnp.mean(residual, -1, keepdims=True)
    inv_scale = lax.rsqrt(jnp.mean(centered * centered, -1, keepdims=True) + NORM_EPS)
    normed = centered * inv_scale
    return (normed * norm_gain + norm_shift, normed, inv_scale)


def norm_back(grad_out, normed, inv_scale, norm_gain):
    grad_norm = grad_out * norm_gain
    mean_grad = jnp.mean(grad_norm, -1, keepdims=True)
    mean_cross = jnp.mean(grad_norm * normed, -1, keepdims=True)
    grad_in = (grad_norm - mean_grad - normed * mean_cross) * inv_scale
    return (grad_in, jnp.sum(grad_out * normed, 0), jnp.sum(grad_out, 0))


def head_slopes(first_head, head_count):
    head_index = first_head + jnp.arange(head_count, dtype=jnp.int32)
    head_float = head_index.astype(jnp.float32)
    return jnp.where(head_index < 8, jnp.exp2(-(head_float + 1.0)), jnp.exp2(-(head_float - 7.5)))


def segment_ids(lengths, positions):
    bounds = jnp.cumsum(lengths, -1)
    return jnp.sum((bounds[:, None, :] <= positions[None, :, None]).astype(jnp.int32), -1)


def score_block(query_heads, query_pos, query_seg, key_heads, key_pos, key_seg, key_keep, slopes):
    scores = (
        jnp.einsum("sqhd,skhd->shqk", query_heads, key_heads, preferred_element_type=jnp.float32)
        * 0.125
    )
    distance = jnp.abs(query_pos[:, None] - key_pos[None, :]).astype(jnp.float32)
    scores = scores - slopes[None, :, None, None] * distance[None, None]
    same_doc = query_seg[:, None, :, None] == key_seg[:, None, None, :]
    visible = (key_keep[:, None, None, :] == 1) | (query_pos[:, None] == key_pos[None, :])[
        None, None
    ]
    return (scores, same_doc & visible)


def grad_block(
    query_heads,
    query_pos,
    query_seg,
    grad_heads,
    log_total,
    delta,
    key_heads,
    value_heads,
    key_pos,
    key_seg,
    key_keep,
    slopes,
):
    scores, allowed = score_block(
        query_heads, query_pos, query_seg, key_heads, key_pos, key_seg, key_keep, slopes
    )
    probs = jnp.where(allowed, jnp.exp(scores - log_total[..., None]), 0.0)
    grad_probs = jnp.einsum(
        "sqhd,skhd->shqk", grad_heads, value_heads, preferred_element_type=jnp.float32
    )
    grad_scores = (probs * (grad_probs - delta[..., None])).astype(jnp.bfloat16)
    grad_query = (
        jnp.einsum("shqk,skhd->sqhd", grad_scores, key_heads, preferred_element_type=jnp.float32)
        * 0.125
    )
    grad_key = (
        jnp.einsum("shqk,sqhd->skhd", grad_scores, query_heads, preferred_element_type=jnp.float32)
        * 0.125
    )
    grad_value = jnp.einsum(
        "shqk,sqhd->skhd",
        probs.astype(jnp.bfloat16),
        grad_heads,
        preferred_element_type=jnp.float32,
    )
    return (grad_query, grad_key, grad_value)


def intersections(query_seg, key_seg):
    return jnp.any((key_seg[:, 0] <= query_seg[:, -1]) & (key_seg[:, -1] >= query_seg[:, 0]))


def guarded(active, update, current):
    return lax.cond(active, update, lambda untouched: untouched, current)


def over_blocks(length, advance, current):
    block_len = 512
    block_count = length // block_len
    return lax.fori_loop(
        0,
        block_count,
        lambda block_index, running: advance(running, block_index * block_len, block_len),
        current,
    )


def per_device_general(
    tokens,
    doc_lengths,
    keep,
    w_query,
    b_query,
    w_key,
    w_value,
    b_value,
    w_out,
    b_out,
    gain_one,
    shift_one,
    w_up,
    w_down,
    b_down,
    gain_two,
    shift_two,
    cotangent,
):
    seq_count, block_rows, model_width = tokens.shape
    local_heads = b_query.shape[0] // HEAD
    head_width = local_heads * HEAD
    row_count = seq_count * block_rows
    slopes = head_slopes(lax.axis_index("tp") * local_heads, local_heads)
    own_pos = lax.axis_index("ctx") * block_rows + jnp.arange(block_rows, dtype=jnp.int32)
    own_seg = segment_ids(doc_lengths, own_pos)
    token_rows = tokens.reshape(row_count, model_width)
    full_query, full_key, full_value, full_out = (
        lax.all_gather(w_query, "fsdp", axis=0, tiled=True),
        lax.all_gather(w_key, "fsdp", axis=0, tiled=True),
        lax.all_gather(w_value, "fsdp", axis=0, tiled=True),
        lax.all_gather(w_out, "fsdp", axis=0, tiled=True),
    )
    queries = (
        jnp.dot(token_rows, full_query, preferred_element_type=jnp.float32) + b_query
    ).astype(jnp.bfloat16)
    key_rows = jnp.dot(token_rows, full_key, preferred_element_type=jnp.float32).astype(
        jnp.bfloat16
    )
    values = (jnp.dot(token_rows, full_value, preferred_element_type=jnp.float32) + b_value).astype(
        jnp.bfloat16
    )
    query_heads = queries.reshape(seq_count, block_rows, local_heads, HEAD)
    key_value = jnp.concatenate([key_rows, values], -1).reshape(
        seq_count, block_rows, 2 * head_width
    )

    def split_pairs(slab_pairs, block_len):
        return (
            slab_pairs[..., :head_width].reshape(seq_count, block_len, local_heads, HEAD),
            slab_pairs[..., head_width:].reshape(seq_count, block_len, local_heads, HEAD),
        )

    def key_slab(pairs, piece_keep, offset, block_len):
        slab_pairs = lax.dynamic_slice_in_dim(pairs, offset, block_len, 1)
        slab_keep = lax.dynamic_slice_in_dim(piece_keep, offset, block_len, 1)
        key_pos = offset + jnp.arange(block_len, dtype=jnp.int32)
        key_seg = segment_ids(doc_lengths, key_pos)
        slab_keys, slab_values = split_pairs(slab_pairs, block_len)
        return (slab_keys, slab_values, slab_keep, key_pos, key_seg)

    start_state = (
        jnp.full((seq_count, local_heads, block_rows), MASKED, jnp.float32),
        jnp.zeros((seq_count, local_heads, block_rows), jnp.float32),
        jnp.zeros((seq_count, local_heads, block_rows, HEAD), jnp.float32),
    )
    pairs = lax.all_gather(key_value, "ctx", axis=1, tiled=True)
    piece_keep = lax.all_gather(keep, "ctx", axis=1, tiled=True)

    def advance(partial_value, offset, block_len):
        slab_keys, slab_values, slab_keep, key_pos, key_seg = key_slab(
            pairs, piece_keep, offset, block_len
        )

        def update(current):
            row_max, row_sum, weighted = current
            scores, allowed = score_block(
                query_heads, own_pos, own_seg, slab_keys, key_pos, key_seg, slab_keep, slopes
            )
            scores = jnp.where(allowed, scores, MASKED)
            new_max = jnp.maximum(row_max, jnp.max(scores, -1))
            factor = jnp.exp(row_max - new_max)
            weights = jnp.where(allowed, jnp.exp(scores - new_max[..., None]), 0.0)
            row_sum = row_sum * factor + jnp.sum(weights, -1)
            weighted = weighted * factor[..., None] + jnp.einsum(
                "shqk,skhd->shqd",
                weights.astype(jnp.bfloat16),
                slab_values,
                preferred_element_type=jnp.float32,
            )
            return (new_max, row_sum, weighted)

        return guarded(intersections(own_seg, key_seg), update, partial_value)

    row_max, row_sum, weighted = over_blocks(pairs.shape[1], advance, start_state)
    attended = (
        (weighted / row_sum[..., None])
        .transpose(0, 2, 1, 3)
        .reshape(row_count, head_width)
        .astype(jnp.bfloat16)
    )
    log_total = row_max + jnp.log(row_sum)
    att_part = jnp.einsum("rh,dh->rd", attended, full_out, preferred_element_type=jnp.float32)
    branch_att = lax.psum(att_part.astype(jnp.bfloat16), "tp").astype(jnp.float32) + b_out
    first_out, normed_one, inv_one = layer_norm(
        token_rows.astype(jnp.float32) + branch_att, gain_one, shift_one
    )
    first_low = first_out.astype(jnp.bfloat16)
    full_up, full_down = (
        lax.all_gather(w_up, "fsdp", axis=0, tiled=True),
        lax.all_gather(w_down, "fsdp", axis=0, tiled=True),
    )
    gate_up = jnp.einsum("rd,dcf->rcf", first_low, full_up, preferred_element_type=jnp.float32)
    product, gelu_back = jax.vjp(
        lambda gate_part, up_part: jax.nn.gelu(gate_part, approximate=False) * up_part,
        gate_up[:, 0],
        gate_up[:, 1],
    )
    hidden = product.astype(jnp.bfloat16)
    ffn_part = jnp.einsum("rf,df->rd", hidden, full_down, preferred_element_type=jnp.float32)
    branch_ffn = lax.psum(ffn_part.astype(jnp.bfloat16), "tp").astype(jnp.float32) + b_down
    result, normed_two, inv_two = layer_norm(first_out + branch_ffn, gain_two, shift_two)
    grad_in = cotangent.reshape(row_count, model_width).astype(jnp.float32)
    grad_two, d_gain_two, d_shift_two = norm_back(grad_in, normed_two, inv_two, gain_two)
    grad_ffn = grad_two.astype(jnp.bfloat16)
    d_b_down = jnp.sum(grad_ffn.astype(jnp.float32), 0)
    d_w_down = jnp.einsum("rd,rf->df", grad_ffn, hidden, preferred_element_type=jnp.float32)
    grad_hidden = jnp.einsum("rd,df->rf", grad_ffn, full_down, preferred_element_type=jnp.float32)
    grad_gate, grad_up = gelu_back(grad_hidden)
    grad_gate_up = jnp.stack([grad_gate, grad_up], 1).astype(jnp.bfloat16)
    d_w_up = jnp.einsum("rd,rcf->dcf", first_low, grad_gate_up, preferred_element_type=jnp.float32)
    first_part = jnp.einsum(
        "rcf,dcf->rd", grad_gate_up, full_up, preferred_element_type=jnp.float32
    )
    grad_first = grad_two + lax.psum(first_part.astype(jnp.bfloat16), "tp").astype(jnp.float32)
    grad_one, d_gain_one, d_shift_one = norm_back(grad_first, normed_one, inv_one, gain_one)
    grad_att = grad_one.astype(jnp.bfloat16)
    d_b_out = jnp.sum(grad_att.astype(jnp.float32), 0)
    d_w_out = jnp.einsum("rd,rh->dh", grad_att, attended, preferred_element_type=jnp.float32)
    grad_attended = jnp.einsum(
        "rd,dh->rh", grad_att, full_out, preferred_element_type=jnp.float32
    ).astype(jnp.bfloat16)
    grad_heads = grad_attended.reshape(seq_count, block_rows, local_heads, HEAD)
    delta = jnp.einsum(
        "sqhd,sqhd->shq",
        grad_heads,
        attended.reshape(seq_count, block_rows, local_heads, HEAD),
        preferred_element_type=jnp.float32,
    )
    query_zero = jnp.zeros((seq_count, block_rows, local_heads, HEAD), jnp.float32)
    full_len = block_rows * lax.axis_size("ctx")
    term_zero = jnp.zeros((seq_count, full_len, 2 * head_width), jnp.float32)
    return_pairs = lax.all_gather(key_value, "ctx", axis=1, tiled=True)
    return_piece_keep = lax.all_gather(keep, "ctx", axis=1, tiled=True)

    def advance(partial_value, offset, block_len):
        slab_keys, slab_values, slab_keep, key_pos, key_seg = key_slab(
            return_pairs, return_piece_keep, offset, block_len
        )

        def update(current):
            query_grad, key_terms = current
            part_query, part_key, part_value = grad_block(
                query_heads,
                own_pos,
                own_seg,
                grad_heads,
                log_total,
                delta,
                slab_keys,
                slab_values,
                key_pos,
                key_seg,
                slab_keep,
                slopes,
            )
            slab_grads = jnp.concatenate(
                [
                    part_key.reshape(seq_count, block_len, head_width),
                    part_value.reshape(seq_count, block_len, head_width),
                ],
                -1,
            )
            return (
                query_grad + part_query,
                lax.dynamic_update_slice_in_dim(key_terms, slab_grads, offset, 1),
            )

        return guarded(intersections(own_seg, key_seg), update, partial_value)

    query_grad, key_terms = over_blocks(return_pairs.shape[1], advance, (query_zero, term_zero))
    pair_grads = lax.psum_scatter(
        key_terms.astype(jnp.bfloat16), "ctx", scatter_dimension=1, tiled=True
    ).astype(jnp.float32)
    query_low = query_grad.reshape(row_count, head_width).astype(jnp.bfloat16)
    pair_low = pair_grads.reshape(row_count, 2 * head_width).astype(jnp.bfloat16)
    grad_project = jnp.concatenate([query_low, pair_low], -1)
    joined_weights = jnp.concatenate([full_query, full_key, full_value], -1)
    joined_grads = jnp.einsum(
        "rd,rh->dh", token_rows, grad_project, preferred_element_type=jnp.float32
    )
    input_part = jnp.einsum(
        "rh,dh->rd", grad_project, joined_weights, preferred_element_type=jnp.float32
    )
    d_tokens = grad_one + lax.psum(input_part.astype(jnp.bfloat16), "tp").astype(jnp.float32)
    d_b_query = jnp.sum(query_low.astype(jnp.float32), 0)
    d_b_value = jnp.sum(pair_low[:, head_width:].astype(jnp.float32), 0)
    d_w_query = joined_grads[:, :head_width]
    d_w_key = joined_grads[:, head_width : 2 * head_width]
    d_w_value = joined_grads[:, 2 * head_width :]
    shard_grads = (
        lax.psum_scatter(
            d_w_query.astype(jnp.bfloat16), "fsdp", scatter_dimension=0, tiled=True
        ).astype(jnp.float32),
        lax.psum_scatter(
            d_w_key.astype(jnp.bfloat16), "fsdp", scatter_dimension=0, tiled=True
        ).astype(jnp.float32),
        lax.psum_scatter(
            d_w_value.astype(jnp.bfloat16), "fsdp", scatter_dimension=0, tiled=True
        ).astype(jnp.float32),
        lax.psum_scatter(
            d_w_out.astype(jnp.bfloat16), "fsdp", scatter_dimension=0, tiled=True
        ).astype(jnp.float32),
        lax.psum_scatter(
            d_w_up.astype(jnp.bfloat16), "fsdp", scatter_dimension=0, tiled=True
        ).astype(jnp.float32),
        lax.psum_scatter(
            d_w_down.astype(jnp.bfloat16), "fsdp", scatter_dimension=0, tiled=True
        ).astype(jnp.float32),
    )
    sum_query, sum_key, sum_value, sum_out, sum_up, sum_down = (
        lax.psum(shard_grads[0].astype(jnp.bfloat16), "ctx").astype(jnp.float32),
        lax.psum(shard_grads[1].astype(jnp.bfloat16), "ctx").astype(jnp.float32),
        lax.psum(shard_grads[2].astype(jnp.bfloat16), "ctx").astype(jnp.float32),
        lax.psum(shard_grads[3].astype(jnp.bfloat16), "ctx").astype(jnp.float32),
        lax.psum(shard_grads[4].astype(jnp.bfloat16), "ctx").astype(jnp.float32),
        lax.psum(shard_grads[5].astype(jnp.bfloat16), "ctx").astype(jnp.float32),
    )
    (
        total_b_query,
        total_b_value,
        total_b_out,
        total_b_down,
        total_gain_one,
        total_shift_one,
        total_gain_two,
        total_shift_two,
    ) = lax.psum(
        (d_b_query, d_b_value, d_b_out, d_b_down, d_gain_one, d_shift_one, d_gain_two, d_shift_two),
        ("fsdp", "ctx"),
    )
    return (
        result.reshape(seq_count, block_rows, model_width).astype(jnp.bfloat16),
        d_tokens.reshape(seq_count, block_rows, model_width),
        sum_query,
        total_b_query,
        sum_key,
        sum_value,
        total_b_value,
        sum_out,
        total_b_out,
        total_gain_one,
        total_shift_one,
        sum_up,
        sum_down,
        total_b_down,
        total_gain_two,
        total_shift_two,
    )


LANES = 128
TILE = 256
DOC_ROW, KEEP_ROW, POS_ROW, LINE_ROW, LOG_ROW, FEAT_END = 64, 72, 73, 79, 82, 85
TP_SWAP = [(0, 1), (1, 0)]
X_SWAP = [(0, 1), (1, 0), (2, 3), (3, 2)]
Y_SWAP = [(0, 2), (2, 0), (1, 3), (3, 1)]
D_SWAP = [(0, 3), (3, 0), (1, 2), (2, 1)]
PAIR_SWAP = [(0, 1), (1, 0), (2, 3), (3, 2)]
CROSS_SWAP = [(0, 2), (2, 0), (1, 3), (3, 1)]
MID_SWAP = [(1, 2), (2, 1)]


def dot(left, right, dims=((1,), (0,))):
    return lax.dot_general(left, right, (dims, ((), ())), preferred_element_type=jnp.float32)


def three_terms(value, low):
    high = low(value)
    middle = low(value - high)
    return high, middle, low(value - high - middle)


def narrow(value):
    return lax.reduce_precision(value, 8, 7)


def project_kernel(x_ref, w_ref, bias_ref, key_feat_ref, query_feat_ref, qt_ref, q_ref, k_ref, kt_ref, v_ref, vt_ref):
    heads = q_ref.shape[0]
    rows = x_ref.shape[0]
    y = dot(x_ref[...], w_ref[...]) + bias_ref[...]
    y = y.astype(jnp.bfloat16).astype(jnp.float32)
    lane = lax.broadcasted_iota(jnp.int32, (rows, LANES), 1)
    sub = lax.broadcasted_iota(jnp.int32, (LANES, rows), 0)

    def head_part(index):
        pair = y[:, index // 2 * LANES : (index // 2 + 1) * LANES]
        if index % 2:
            pair = pltpu.roll(pair, HEAD, 1)
        return jnp.where(lane < HEAD, pair, 0.0)

    for head in range(heads):
        query = head_part(head) * 0.125
        q_ref[head] = query[:, :HEAD].astype(jnp.bfloat16)
        qt_ref[head] = (query.T + query_feat_ref[head].astype(jnp.float32)).astype(jnp.bfloat16)
        key = head_part(heads + head)
        k_ref[head] = (key + key_feat_ref[...].astype(jnp.float32)).astype(jnp.bfloat16)
        kt_ref[head] = key.T[:HEAD].astype(jnp.bfloat16)
        value = head_part(2 * heads + head)
        ones = (lane >= HEAD) & (lane < HEAD + 3)
        v_ref[head] = jnp.where(ones, 1.0, value).astype(jnp.bfloat16)
        vt_ref[head] = jnp.where(sub == HEAD, 1.0, value.T)[:80].astype(jnp.bfloat16)


def project(x, weight, bias, key_feat, query_feat, heads):
    length, width = x.shape
    rows = 2 * TILE
    return pl.pallas_call(
        project_kernel,
        grid=(length // rows,),
        in_specs=[
            pl.BlockSpec((rows, width), lambda i: (i, 0)),
            pl.BlockSpec(weight.shape, lambda i: (0, 0)),
            pl.BlockSpec(bias.shape, lambda i: (0, 0)),
            pl.BlockSpec((rows, LANES), lambda i: (i, 0)),
            pl.BlockSpec((heads, LANES, rows), lambda i: (0, 0, i)),
        ],
        out_specs=[
            pl.BlockSpec((heads, LANES, rows), lambda i: (0, 0, i)),
            pl.BlockSpec((heads, rows, HEAD), lambda i: (0, i, 0)),
            pl.BlockSpec((heads, rows, LANES), lambda i: (0, i, 0)),
            pl.BlockSpec((heads, HEAD, rows), lambda i: (0, 0, i)),
            pl.BlockSpec((heads, rows, LANES), lambda i: (0, i, 0)),
            pl.BlockSpec((heads, 80, rows), lambda i: (0, 0, i)),
        ],
        out_shape=[
            jax.ShapeDtypeStruct((heads, LANES, length), jnp.bfloat16),
            jax.ShapeDtypeStruct((heads, length, HEAD), jnp.bfloat16),
            jax.ShapeDtypeStruct((heads, length, LANES), jnp.bfloat16),
            jax.ShapeDtypeStruct((heads, HEAD, length), jnp.bfloat16),
            jax.ShapeDtypeStruct((heads, length, LANES), jnp.bfloat16),
            jax.ShapeDtypeStruct((heads, 80, length), jnp.bfloat16),
        ],
        compiler_params=pltpu.CompilerParams(vmem_limit_bytes=40 << 20),
        cost_estimate=pl.CostEstimate(
            flops=2 * length * width * weight.shape[1], bytes_accessed=12 << 20, transcendentals=0
        ),
        name="project",
    )(x, weight, bias, key_feat, query_feat)


def side_signs(rows):
    sub = lax.broadcasted_iota(jnp.int32, (LANES, rows), 0)
    bias_rows = (sub >= POS_ROW) & (sub < LOG_ROW)
    after = jnp.where(bias_rows, -1.0, 1.0).astype(jnp.bfloat16)
    same = jnp.where(bias_rows, 0.0, 1.0).astype(jnp.bfloat16)
    bare = jnp.where(bias_rows | (sub == KEEP_ROW), 0.0, 1.0).astype(jnp.bfloat16)
    return after, same, bare


def diagonal_scores(keys, query_t, same, bare, slope):
    rows = lax.broadcasted_iota(jnp.int32, (TILE, TILE), 0)
    cols = lax.broadcasted_iota(jnp.int32, (TILE, TILE), 1)
    apart = jnp.abs(rows - cols)
    full = dot(keys, query_t * same) - slope * apart.astype(jnp.float32)
    return jnp.where(apart == 0, dot(keys, query_t * bare), full)


def attend_kernel(span_ref, slope_ref, qt_ref, k_ref, vt_ref, o_ref, ot_ref, lse_ref, max_ref, acc_ref):
    heads = qt_ref.shape[0]
    block = pl.program_id(0)
    after, same, bare = side_signs(TILE)

    def tile_rows(tile):
        return pl.ds(pl.multiple_of(tile * TILE, TILE), TILE)

    own = tile_rows(block)
    for head in range(heads):
        scores = diagonal_scores(k_ref[head, own, :], qt_ref[head], same, bare, slope_ref[head])
        top = jnp.max(scores, 0, keepdims=True)
        weights = jnp.exp(scores - top).astype(jnp.bfloat16)
        max_ref[head] = top
        acc_ref[head] = dot(vt_ref[head, :, own], weights)

    def step(tile, sign):
        for head in range(heads):
            query_t = qt_ref[head] if sign is None else qt_ref[head] * sign
            scores = dot(k_ref[head, tile_rows(tile), :], query_t)
            old = max_ref[head]
            top = jnp.maximum(old, jnp.max(scores, 0, keepdims=True))
            weights = jnp.exp(scores - top).astype(jnp.bfloat16)
            max_ref[head] = top
            acc_ref[head] = acc_ref[head] * jnp.exp(old - top) + dot(
                vt_ref[head, :, tile_rows(tile)], weights
            )

    @pl.loop(span_ref[0, block], block)
    def _(tile):
        step(tile, None)

    @pl.loop(block + 1, span_ref[1, block])
    def _(tile):
        step(tile, after)

    parts = []
    for head in range(heads):
        total = acc_ref[head, HEAD : HEAD + 1, :]
        out_t = acc_ref[head, :HEAD, :] / total
        ot_ref[head] = out_t
        parts.append(out_t)
        lse_ref[head] = max_ref[head] + jnp.log(total)
    o_ref[...] = jnp.concatenate(parts, 0).T.astype(jnp.bfloat16)


def attend(spans, slopes, query_t, keys, value_t):
    heads, _, length = query_t.shape
    blocks = length // TILE
    return pl.pallas_call(
        attend_kernel,
        grid_spec=pltpu.PrefetchScalarGridSpec(
            num_scalar_prefetch=2,
            grid=(blocks,),
            in_specs=[
                pl.BlockSpec((heads, LANES, TILE), lambda i, *_: (0, 0, i)),
                pl.BlockSpec(keys.shape, lambda i, *_: (0, 0, 0)),
                pl.BlockSpec(value_t.shape, lambda i, *_: (0, 0, 0)),
            ],
            out_specs=[
                pl.BlockSpec((TILE, heads * HEAD), lambda i, *_: (i, 0)),
                pl.BlockSpec((heads, HEAD, TILE), lambda i, *_: (0, 0, i)),
                pl.BlockSpec((heads, 1, TILE), lambda i, *_: (0, 0, i)),
            ],
            scratch_shapes=[
                pltpu.VMEM((heads, 1, TILE), jnp.float32),
                pltpu.VMEM((heads, 80, TILE), jnp.float32),
            ],
        ),
        out_shape=[
            jax.ShapeDtypeStruct((length, heads * HEAD), jnp.bfloat16),
            jax.ShapeDtypeStruct((heads, HEAD, length), jnp.float32),
            jax.ShapeDtypeStruct((heads, 1, length), jnp.float32),
        ],
        compiler_params=pltpu.CompilerParams(vmem_limit_bytes=40 << 20),
        cost_estimate=pl.CostEstimate(
            flops=heads * length * length * 256, bytes_accessed=6 << 20, transcendentals=heads * length * length
        ),
        name="attend",
    )(spans, slopes, query_t, keys, value_t)


def attend_back_kernel(
    span_ref, slope_ref, qt_ref, q_ref, k_ref, kt_ref, v_ref, g_ref, ot_ref, lse_ref,
    dq_ref, dk_ref, dv_ref, qt_log, grad_heads, grad_t, query_acc, key_acc, value_acc,
):
    heads = qt_ref.shape[0]
    blocks = pl.num_programs(0)
    block = pl.program_id(0)
    length = qt_ref.shape[2]
    after, same, bare = side_signs(TILE)

    def low(value):
        return value.astype(jnp.bfloat16).astype(jnp.float32)

    def tile_rows(tile):
        return pl.ds(pl.multiple_of(tile * TILE, TILE), TILE)

    @pl.when(block == 0)
    def _():
        query_acc[...] = jnp.zeros_like(query_acc)
        sub = lax.broadcasted_iota(jnp.int32, (LANES, TILE), 0)

        @pl.loop(0, length // TILE)
        def _(tile):
            rows = tile_rows(tile)
            grad = g_ref[rows, :].astype(jnp.float32)
            turned = grad.T
            for head in range(heads):
                own = turned[head * HEAD : (head + 1) * HEAD]
                delta = jnp.sum(own * ot_ref[head, :, rows], 0, keepdims=True)
                first, second, third = three_terms(-delta, low)
                wide = jnp.concatenate([own, jnp.zeros_like(own)], 0)
                wide = jnp.where(sub == HEAD, first, wide)
                wide = jnp.where(sub == HEAD + 1, second, wide)
                wide = jnp.where(sub == HEAD + 2, third, wide)
                grad_t[head, :, rows] = wide.astype(jnp.bfloat16)
                grad_heads[head, rows, :] = own.T.astype(jnp.bfloat16)
                first, second, third = three_terms(-lse_ref[head, :, rows], low)
                query = qt_ref[head, :, rows].astype(jnp.float32)
                query = jnp.where(sub == LOG_ROW, first, query)
                query = jnp.where(sub == LOG_ROW + 1, second, query)
                query = jnp.where(sub == LOG_ROW + 2, third, query)
                qt_log[head, :, rows] = query.astype(jnp.bfloat16)

    def accumulate(head, tile, scores, first):
        rows = tile_rows(tile)
        probs = jnp.exp(scores)
        grad_probs = dot(v_ref[head], grad_t[head, :, rows])
        grad_scores = (probs * grad_probs).astype(jnp.bfloat16)
        value_part = dot(probs.astype(jnp.bfloat16), grad_heads[head, rows, :])
        key_part = dot(grad_scores, q_ref[head, rows, :])
        query_acc[head, :, rows] += dot(kt_ref[head], grad_scores)
        if first:
            value_acc[head] = value_part
            key_acc[head] = key_part
        else:
            value_acc[head] += value_part
            key_acc[head] += key_part

    for head in range(heads):
        accumulate(
            head,
            block,
            diagonal_scores(k_ref[head], qt_log[head, :, tile_rows(block)], same, bare, slope_ref[head]),
            True,
        )

    @pl.loop(span_ref[0, block], block)
    def _(tile):
        for head in range(heads):
            accumulate(head, tile, dot(k_ref[head], qt_log[head, :, tile_rows(tile)] * after), False)

    @pl.loop(block + 1, span_ref[1, block])
    def _(tile):
        for head in range(heads):
            accumulate(head, tile, dot(k_ref[head], qt_log[head, :, tile_rows(tile)]), False)

    dk_ref[...] = jnp.concatenate([key_acc[head] for head in range(heads)], 1).astype(jnp.bfloat16)
    dv_ref[...] = jnp.concatenate([value_acc[head] for head in range(heads)], 1).astype(jnp.bfloat16)

    @pl.when(block == blocks - 1)
    def _():
        @pl.loop(0, length // TILE)
        def _(tile):
            rows = tile_rows(tile)
            turned = jnp.concatenate([query_acc[head, :, rows] for head in range(heads)], 0)
            dq_ref[rows, :] = (turned.T * 0.125).astype(jnp.bfloat16)


def attend_back(spans, slopes, query_t, queries, keys, keys_t, values, grads, out_t, lse):
    heads, _, length = query_t.shape
    blocks = length // TILE
    width = heads * HEAD

    def whole(array):
        return pl.BlockSpec(array.shape, lambda i, *_: (0,) * array.ndim)

    return pl.pallas_call(
        attend_back_kernel,
        grid_spec=pltpu.PrefetchScalarGridSpec(
            num_scalar_prefetch=2,
            grid=(blocks,),
            in_specs=[
                whole(query_t),
                whole(queries),
                pl.BlockSpec((heads, TILE, LANES), lambda i, *_: (0, i, 0)),
                pl.BlockSpec((heads, HEAD, TILE), lambda i, *_: (0, 0, i)),
                pl.BlockSpec((heads, TILE, LANES), lambda i, *_: (0, i, 0)),
                whole(grads),
                whole(out_t),
                whole(lse),
            ],
            out_specs=[
                pl.BlockSpec((length, width), lambda i, *_: (0, 0)),
                pl.BlockSpec((TILE, width), lambda i, *_: (i, 0)),
                pl.BlockSpec((TILE, width), lambda i, *_: (i, 0)),
            ],
            scratch_shapes=[
                pltpu.VMEM((heads, LANES, length), jnp.bfloat16),
                pltpu.VMEM((heads, length, HEAD), jnp.bfloat16),
                pltpu.VMEM((heads, LANES, length), jnp.bfloat16),
                pltpu.VMEM((heads, HEAD, length), jnp.float32),
                pltpu.VMEM((heads, TILE, HEAD), jnp.float32),
                pltpu.VMEM((heads, TILE, HEAD), jnp.float32),
            ],
        ),
        out_shape=[jax.ShapeDtypeStruct((length, width), jnp.bfloat16)] * 3,
        compiler_params=pltpu.CompilerParams(vmem_limit_bytes=50 << 20),
        cost_estimate=pl.CostEstimate(
            flops=heads * length * length * 640, bytes_accessed=12 << 20, transcendentals=heads * length * length
        ),
        name="attend_back",
    )(spans, slopes, query_t, queries, keys, keys_t, values, grads, out_t, lse)


def gather_rows(shard, place):
    parts = (
        shard,
        lax.ppermute(shard, "fsdp", X_SWAP),
        lax.ppermute(shard, "fsdp", Y_SWAP),
        lax.ppermute(shard, "fsdp", D_SWAP),
    )
    rows = shard.shape[0]
    full = jnp.zeros((4 * rows,) + shard.shape[1:], shard.dtype)
    for other, part in enumerate(parts):
        full = lax.dynamic_update_slice_in_dim(full, part, (place ^ other) * rows, 0)
    return full


def scatter_rows(grad, place):
    rows = grad.shape[0] // 4
    low = grad.astype(jnp.bfloat16)

    def quarter(other):
        return lax.dynamic_slice_in_dim(low, (place ^ other) * rows, rows, 0)

    return sum(
        (
            lax.ppermute(quarter(other), "fsdp", swap).astype(jnp.float32)
            for other, swap in ((1, X_SWAP), (2, Y_SWAP), (3, D_SWAP))
        ),
        quarter(0).astype(jnp.float32),
    )


def line_sum(part, stage):
    part = part.astype(jnp.bfloat16)
    inner = part + lax.ppermute(part, "ctx", [(0, 1), (3, 2)])
    both = inner + lax.ppermute(inner, "ctx", MID_SWAP)
    back = lax.ppermute(both, "ctx", [(1, 0), (2, 3)])
    return jnp.where((stage == 1) | (stage == 2), both, back).astype(jnp.float32)


def tp_sum(part):
    low = part.astype(jnp.bfloat16)
    return low.astype(jnp.float32) + lax.ppermute(low, "tp", TP_SWAP).astype(jnp.float32)


def join_cores(mine, core, axis):
    other = lax.ppermute(mine, "tp", TP_SWAP)
    return jnp.concatenate(
        [jnp.where(core == 0, mine, other), jnp.where(core == 0, other, mine)], axis
    )


def pick(pair, index):
    return lax.dynamic_index_in_dim(pair, index, 0, keepdims=False)


def home_blocks(blocks, stage):
    odd = stage % 2 == 1
    far = lax.ppermute(
        jnp.where(stage < 2, blocks[1], blocks[0]), "ctx", [(1, 3), (2, 0), (0, 1), (3, 2)]
    )
    near = jnp.where(stage < 2, blocks[0], blocks[1])
    crossed = lax.ppermute(near, "ctx", MID_SWAP)
    near = jnp.where((stage == 1) | (stage == 2), crossed, near)
    return jnp.stack([jnp.where(odd, far, near), jnp.where(odd, near, far)])


def away_blocks(pair, stage):
    odd = stage % 2 == 1
    far = lax.ppermute(
        jnp.where(odd, pair[0], pair[1]), "ctx", [(3, 1), (0, 2), (1, 0), (2, 3)]
    )
    near = jnp.where(odd, pair[1], pair[0])
    crossed = lax.ppermute(near, "ctx", MID_SWAP)
    near = jnp.where((stage == 1) | (stage == 2), crossed, near)
    return jnp.stack([jnp.where(stage < 2, near, far), jnp.where(stage < 2, far, near)])


def per_device_paired(
    tokens,
    doc_lengths,
    keep,
    w_query,
    b_query,
    w_key,
    w_value,
    b_value,
    w_out,
    b_out,
    gain_one,
    shift_one,
    w_up,
    w_down,
    b_down,
    gain_two,
    shift_two,
    cotangent,
):
    _, block_rows, model_width = tokens.shape
    length = 4 * block_rows
    half_rows = block_rows // 2
    local_heads = b_query.shape[0] // HEAD
    heads = local_heads // 2
    width = heads * HEAD
    place = lax.axis_index("fsdp")
    stage = lax.axis_index("ctx")
    core = lax.axis_index("tp")
    seq, half = stage // 2, stage % 2
    inner = (stage == 1) | (stage == 2)

    def core_half(array):
        return lax.dynamic_slice_in_dim(array, core * half_rows, half_rows, 1)

    def own_columns(array):
        return lax.dynamic_slice_in_dim(array, half * width, width, array.ndim - 1)

    token_half = core_half(tokens)
    ours, theirs = pick(token_half, seq), pick(token_half, 1 - seq)
    from_pair = lax.ppermute(ours, "ctx", PAIR_SWAP)
    crossed = lax.ppermute(theirs, "ctx", MID_SWAP)
    relayed = lax.ppermute(crossed, "ctx", [(1, 0), (2, 3)])
    far_inner = lax.ppermute(theirs, "ctx", [(3, 1), (0, 2)])
    far_outer = lax.ppermute(theirs, "ctx", [(3, 0), (0, 3)])
    arrived = jnp.stack(
        [from_pair, jnp.where(inner, crossed, relayed), jnp.where(inner, far_inner, far_outer)]
    )
    arrived_other = lax.ppermute(arrived, "tp", TP_SWAP)
    block_at = (stage ^ 1, jnp.where(seq == 0, 2, 1), jnp.where(seq == 0, 3, 0))
    sequence = jnp.zeros((4, 2, half_rows, model_width), jnp.bfloat16)
    sequence = lax.dynamic_update_slice(
        sequence,
        pick(tokens, seq).reshape(1, 2, half_rows, model_width),
        (stage, 0, 0, 0),
    )
    for slot in range(3):
        sequence = lax.dynamic_update_slice(
            sequence, arrived[slot][None, None], (block_at[slot], core, 0, 0)
        )
        sequence = lax.dynamic_update_slice(
            sequence, arrived_other[slot][None, None], (block_at[slot], 1 - core, 0, 0)
        )
    sequence = sequence.reshape(length, model_width)

    keep_all = jnp.zeros((4,) + keep.shape, jnp.int32)
    keep_all = lax.dynamic_update_slice(keep_all, keep[None], (stage, 0, 0))
    for shift in range(1, 4):
        moved = lax.ppermute(keep, "ctx", [(i, (i + shift) % 4) for i in range(4)])
        keep_all = lax.dynamic_update_slice(keep_all, moved[None], ((stage - shift) % 4, 0, 0))
    keep_row = lax.dynamic_index_in_dim(keep_all, seq, 1, keepdims=False).reshape(length)

    bounds = jnp.cumsum(pick(doc_lengths, seq))
    docs = bounds.shape[0]
    positions = jnp.arange(length, dtype=jnp.int32)
    segments = jnp.sum((bounds[None, :] <= positions[:, None]).astype(jnp.int32), -1)
    starts = jnp.concatenate([jnp.zeros((1,), jnp.int32), bounds[:-1]])
    firsts = segments[:: TILE]
    lasts = segments[TILE - 1 :: TILE]
    doc_index = jnp.arange(docs, dtype=jnp.int32)
    span_from = jnp.sum(jnp.where(firsts[:, None] == doc_index, starts, 0), -1) // TILE
    span_to = (jnp.sum(jnp.where(lasts[:, None] == doc_index, bounds, 0), -1) + TILE - 1) // TILE
    spans = jnp.stack([span_from, span_to]).astype(jnp.int32)
    slopes = head_slopes(core * local_heads + half * heads, heads)
    feature = jnp.arange(LANES, dtype=jnp.int32)
    key_doc = jnp.where(segments[:, None] == feature - DOC_ROW, 0.0, MASKED)
    pos_high = (positions // 256 * 256).astype(jnp.float32)[:, None]
    pos_low = (positions % 256).astype(jnp.float32)[:, None]
    key_feat = jnp.where(feature < DOC_ROW, 0.0, 1.0)[None, :]
    key_feat = jnp.where((feature >= DOC_ROW) & (feature < DOC_ROW + docs), key_doc, key_feat)
    key_feat = jnp.where(feature == KEEP_ROW, jnp.where(keep_row == 1, 0.0, MASKED)[:, None], key_feat)
    key_feat = jnp.where((feature >= POS_ROW) & (feature < POS_ROW + 3), pos_high, key_feat)
    key_feat = jnp.where((feature >= POS_ROW + 3) & (feature < LINE_ROW), pos_low, key_feat)
    key_feat = jnp.where(feature >= FEAT_END, 0.0, key_feat).astype(jnp.bfloat16)
    rows = feature[None, :, None]
    query_feat = jnp.where(segments[None, None, :] == rows - DOC_ROW, 1.0, 0.0)
    query_feat = jnp.where(rows == KEEP_ROW, 1.0, query_feat)
    slope_terms = three_terms(slopes[:, None, None], narrow)
    line_terms = three_terms(
        -slopes[:, None, None] * positions.astype(jnp.float32)[None, None, :], narrow
    )
    for term in range(3):
        here = (rows == POS_ROW + term) | (rows == POS_ROW + 3 + term)
        query_feat = jnp.where(here, slope_terms[term], query_feat)
        query_feat = jnp.where(rows == LINE_ROW + term, line_terms[term], query_feat)
    query_feat = query_feat.astype(jnp.bfloat16)

    w_joined = jnp.concatenate([own_columns(w_query), own_columns(w_key), own_columns(w_value)], -1)
    full_joined = gather_rows(w_joined, place)
    full_out = gather_rows(w_out, place)
    full_up = gather_rows(w_up, place)
    full_down = gather_rows(w_down, place)

    bias = jnp.concatenate([own_columns(b_query), jnp.zeros((width,), jnp.float32), own_columns(b_value)])
    pad = -3 * width % LANES
    query_t, queries, keys, keys_t, values, values_t = project(
        sequence,
        jnp.pad(full_joined, ((0, 0), (0, pad))),
        jnp.pad(bias, (0, pad))[None],
        key_feat,
        query_feat,
        heads,
    )
    attended_all, attended_t, lse = attend(spans, slopes, query_t, keys, values_t)

    row_count = length // 2

    def own_half(array):
        return lax.dynamic_slice_in_dim(array, half * row_count, row_count, 0)

    def other_half(array):
        return lax.dynamic_slice_in_dim(array, (1 - half) * row_count, row_count, 0)

    mine = own_half(attended_all)
    recv = lax.ppermute(other_half(attended_all), "ctx", PAIR_SWAP)
    attended = jnp.concatenate(
        [jnp.where(half == 0, mine, recv), jnp.where(half == 0, recv, mine)], -1
    )
    token_rows = own_half(sequence)
    cotangent_half = away_blocks(core_half(cotangent), stage)
    grad_in = join_cores(cotangent_half, core, 1).reshape(row_count, model_width).astype(jnp.float32)

    branch_att = tp_sum(dot(attended, full_out, ((1,), (1,)))) + b_out
    first_out, normed_one, inv_one = layer_norm(
        token_rows.astype(jnp.float32) + branch_att, gain_one, shift_one
    )
    first_low = first_out.astype(jnp.bfloat16)
    gate_up = jnp.einsum("rd,dcf->rcf", first_low, full_up, preferred_element_type=jnp.float32)
    product, gelu_back = jax.vjp(
        lambda gate_part, up_part: jax.nn.gelu(gate_part, approximate=False) * up_part,
        gate_up[:, 0],
        gate_up[:, 1],
    )
    hidden = product.astype(jnp.bfloat16)
    branch_ffn = tp_sum(dot(hidden, full_down, ((1,), (1,)))) + b_down
    result, normed_two, inv_two = layer_norm(first_out + branch_ffn, gain_two, shift_two)
    grad_two, d_gain_two, d_shift_two = norm_back(grad_in, normed_two, inv_two, gain_two)
    grad_ffn = grad_two.astype(jnp.bfloat16)
    d_b_down = jnp.sum(grad_ffn.astype(jnp.float32), 0)
    d_w_down = dot(grad_ffn, hidden, ((0,), (0,)))
    grad_hidden = dot(grad_ffn, full_down)
    grad_gate, grad_up = gelu_back(grad_hidden)
    grad_gate_up = jnp.stack([grad_gate, grad_up], 1).astype(jnp.bfloat16)
    d_w_up = jnp.einsum("rd,rcf->dcf", first_low, grad_gate_up, preferred_element_type=jnp.float32)
    first_part = jnp.einsum(
        "rcf,dcf->rd", grad_gate_up, full_up, preferred_element_type=jnp.float32
    )
    grad_first = grad_two + tp_sum(first_part)
    grad_one, d_gain_one, d_shift_one = norm_back(grad_first, normed_one, inv_one, gain_one)
    grad_att = grad_one.astype(jnp.bfloat16)
    d_b_out = jnp.sum(grad_att.astype(jnp.float32), 0)
    d_w_out = dot(grad_att, attended, ((0,), (0,)))
    grad_attended = dot(grad_att, full_out).astype(jnp.bfloat16)

    mine = own_columns(grad_attended)
    away = lax.dynamic_slice_in_dim(grad_attended, (1 - half) * width, width, 1)
    recv = lax.ppermute(away, "ctx", PAIR_SWAP)
    grad_heads = jnp.concatenate(
        [jnp.where(half == 0, mine, recv), jnp.where(half == 0, recv, mine)], 0
    )
    d_query, d_key, d_value = attend_back(
        spans, slopes, query_t, queries, keys, keys_t, values, grad_heads, attended_t, lse
    )
    grad_project = jnp.concatenate([d_query, d_key, d_value], -1)
    d_joined = dot(sequence, grad_project, ((0,), (0,)))
    input_part = dot(grad_project, full_joined, ((1,), (1,))).astype(jnp.bfloat16)
    input_part = input_part.reshape(4, 2, half_rows, model_width)
    over_tp = lax.ppermute(
        lax.dynamic_index_in_dim(input_part, 1 - core, 1, keepdims=False), "tp", TP_SWAP
    )
    input_half = lax.dynamic_index_in_dim(input_part, core, 1, keepdims=False).astype(
        jnp.float32
    ) + over_tp.astype(jnp.float32)
    away = lax.dynamic_slice_in_dim(input_half, 2 * (1 - half), 2, 0).astype(jnp.bfloat16)
    d_rows = (
        lax.dynamic_slice_in_dim(input_half, 2 * half, 2, 0)
        + lax.ppermute(away, "ctx", PAIR_SWAP).astype(jnp.float32)
        + core_half(grad_one.reshape(2, block_rows, model_width))
    )
    d_tokens = join_cores(home_blocks(d_rows.astype(jnp.bfloat16), stage), core, 1).astype(jnp.float32)
    out = join_cores(
        home_blocks(
            core_half(result.reshape(2, block_rows, model_width)).astype(jnp.bfloat16), stage
        ),
        core,
        1,
    )

    sum_out = line_sum(scatter_rows(d_w_out, place), stage)
    sum_up = line_sum(scatter_rows(d_w_up, place), stage)
    sum_down = line_sum(scatter_rows(d_w_down, place), stage)
    joined = scatter_rows(d_joined, place).astype(jnp.bfloat16)
    joined = joined + lax.ppermute(joined, "ctx", CROSS_SWAP)
    joined_other = lax.ppermute(joined, "ctx", PAIR_SWAP)
    low_half = jnp.where(half == 0, joined, joined_other).astype(jnp.float32)
    high_half = jnp.where(half == 0, joined_other, joined).astype(jnp.float32)

    def both_halves(first):
        return jnp.concatenate(
            [low_half[..., first : first + width], high_half[..., first : first + width]], -1
        )

    d_bias = jnp.concatenate([d_query, d_value], -1).astype(jnp.float32).sum(0).reshape(2, 1, width)
    d_bias = lax.dynamic_update_slice(
        jnp.zeros((2, 2, width), jnp.float32), d_bias, (0, half, 0)
    ).reshape(2, 2 * width)
    (
        total_bias,
        total_b_out,
        total_b_down,
        total_gain_one,
        total_shift_one,
        total_gain_two,
        total_shift_two,
    ) = lax.psum(
        (d_bias, d_b_out, d_b_down, d_gain_one, d_shift_one, d_gain_two, d_shift_two),
        ("fsdp", "ctx"),
    )
    return (
        out,
        d_tokens,
        both_halves(0),
        total_bias[0],
        both_halves(width),
        both_halves(2 * width),
        total_bias[1],
        sum_out,
        total_b_out,
        total_gain_one,
        total_shift_one,
        sum_up,
        sum_down,
        total_b_down,
        total_gain_two,
        total_shift_two,
    )


def paired(mesh, tokens, doc_lengths, b_query):
    sizes = dict(mesh.shape)
    return (
        sizes == {"fsdp": 4, "ctx": 4, "tp": 2}
        and tokens.shape[0] == 8
        and tokens.shape[1] % (8 * TILE) == 0
        and doc_lengths.shape[1] <= KEEP_ROW - DOC_ROW
        and b_query.shape[0] % (4 * HEAD) == 0
    )


def solution(mesh):
    in_specs = (
        P("fsdp", "ctx", None),
        P("fsdp", None),
        P("fsdp", "ctx"),
        P("fsdp", "tp"),
        P("tp"),
        P("fsdp", "tp"),
        P("fsdp", "tp"),
        P("tp"),
        P("fsdp", "tp"),
        P(),
        P(),
        P(),
        P("fsdp", None, "tp"),
        P("fsdp", "tp"),
        P(),
        P(),
        P(),
        P("fsdp", "ctx", None),
    )
    out_specs = (
        P("fsdp", "ctx", None),
        P("fsdp", "ctx", None),
        P("fsdp", "tp"),
        P("tp"),
        P("fsdp", "tp"),
        P("fsdp", "tp"),
        P("tp"),
        P("fsdp", "tp"),
        P(),
        P(),
        P(),
        P("fsdp", None, "tp"),
        P("fsdp", "tp"),
        P(),
        P(),
        P(),
    )

    def whole(*args):
        body = per_device_paired if paired(mesh, args[0], args[1], args[4]) else per_device_general
        return jax.shard_map(
            body, mesh=mesh, in_specs=in_specs, out_specs=out_specs, check_vma=False
        )(*args)

    return whole
```

```python
import functools

import jax
import jax.numpy as jnp
from jax import lax
from jax.experimental import pallas as pl
from jax.experimental.pallas import tpu as pltpu
from jax.sharding import PartitionSpec as P

HEAD = 64


NORM_EPS = 1e-12
MASKED = -1e30


def layer_norm(residual, norm_gain, norm_shift):
    centered = residual - jnp.mean(residual, -1, keepdims=True)
    inv_scale = lax.rsqrt(jnp.mean(centered * centered, -1, keepdims=True) + NORM_EPS)
    normed = centered * inv_scale
    return (normed * norm_gain + norm_shift, normed, inv_scale)


def norm_back(grad_out, normed, inv_scale, norm_gain):
    grad_norm = grad_out * norm_gain
    mean_grad = jnp.mean(grad_norm, -1, keepdims=True)
    mean_cross = jnp.mean(grad_norm * normed, -1, keepdims=True)
    grad_in = (grad_norm - mean_grad - normed * mean_cross) * inv_scale
    return (grad_in, jnp.sum(grad_out * normed, 0), jnp.sum(grad_out, 0))


def head_slopes(first_head, head_count):
    head_index = first_head + jnp.arange(head_count, dtype=jnp.int32)
    head_float = head_index.astype(jnp.float32)
    return jnp.where(head_index < 8, jnp.exp2(-(head_float + 1.0)), jnp.exp2(-(head_float - 7.5)))


def segment_ids(lengths, positions):
    bounds = jnp.cumsum(lengths, -1)
    return jnp.sum((bounds[:, None, :] <= positions[None, :, None]).astype(jnp.int32), -1)


def score_block(query_heads, query_pos, query_seg, key_heads, key_pos, key_seg, key_keep, slopes):
    scores = (
        jnp.einsum("sqhd,skhd->shqk", query_heads, key_heads, preferred_element_type=jnp.float32)
        * 0.125
    )
    distance = jnp.abs(query_pos[:, None] - key_pos[None, :]).astype(jnp.float32)
    scores = scores - slopes[None, :, None, None] * distance[None, None]
    same_doc = query_seg[:, None, :, None] == key_seg[:, None, None, :]
    visible = (key_keep[:, None, None, :] == 1) | (query_pos[:, None] == key_pos[None, :])[
        None, None
    ]
    return (scores, same_doc & visible)


def grad_block(
    query_heads,
    query_pos,
    query_seg,
    grad_heads,
    log_total,
    delta,
    key_heads,
    value_heads,
    key_pos,
    key_seg,
    key_keep,
    slopes,
):
    scores, allowed = score_block(
        query_heads, query_pos, query_seg, key_heads, key_pos, key_seg, key_keep, slopes
    )
    probs = jnp.where(allowed, jnp.exp(scores - log_total[..., None]), 0.0)
    grad_probs = jnp.einsum(
        "sqhd,skhd->shqk", grad_heads, value_heads, preferred_element_type=jnp.float32
    )
    grad_scores = (probs * (grad_probs - delta[..., None])).astype(jnp.bfloat16)
    grad_query = (
        jnp.einsum("shqk,skhd->sqhd", grad_scores, key_heads, preferred_element_type=jnp.float32)
        * 0.125
    )
    grad_key = (
        jnp.einsum("shqk,sqhd->skhd", grad_scores, query_heads, preferred_element_type=jnp.float32)
        * 0.125
    )
    grad_value = jnp.einsum(
        "shqk,sqhd->skhd",
        probs.astype(jnp.bfloat16),
        grad_heads,
        preferred_element_type=jnp.float32,
    )
    return (grad_query, grad_key, grad_value)


def intersections(query_seg, key_seg):
    return jnp.any((key_seg[:, 0] <= query_seg[:, -1]) & (key_seg[:, -1] >= query_seg[:, 0]))


def guarded(active, update, current):
    return lax.cond(active, update, lambda untouched: untouched, current)


def over_blocks(length, advance, current):
    block_len = 512
    block_count = length // block_len
    return lax.fori_loop(
        0,
        block_count,
        lambda block_index, running: advance(running, block_index * block_len, block_len),
        current,
    )


def per_device_general(
    tokens,
    doc_lengths,
    keep,
    w_query,
    b_query,
    w_key,
    w_value,
    b_value,
    w_out,
    b_out,
    gain_one,
    shift_one,
    w_up,
    w_down,
    b_down,
    gain_two,
    shift_two,
    cotangent,
):
    seq_count, block_rows, model_width = tokens.shape
    local_heads = b_query.shape[0] // HEAD
    head_width = local_heads * HEAD
    row_count = seq_count * block_rows
    slopes = head_slopes(lax.axis_index("tp") * local_heads, local_heads)
    own_pos = lax.axis_index("ctx") * block_rows + jnp.arange(block_rows, dtype=jnp.int32)
    own_seg = segment_ids(doc_lengths, own_pos)
    token_rows = tokens.reshape(row_count, model_width)
    full_query, full_key, full_value, full_out = (
        lax.all_gather(w_query, "fsdp", axis=0, tiled=True),
        lax.all_gather(w_key, "fsdp", axis=0, tiled=True),
        lax.all_gather(w_value, "fsdp", axis=0, tiled=True),
        lax.all_gather(w_out, "fsdp", axis=0, tiled=True),
    )
    queries = (
        jnp.dot(token_rows, full_query, preferred_element_type=jnp.float32) + b_query
    ).astype(jnp.bfloat16)
    key_rows = jnp.dot(token_rows, full_key, preferred_element_type=jnp.float32).astype(
        jnp.bfloat16
    )
    values = (jnp.dot(token_rows, full_value, preferred_element_type=jnp.float32) + b_value).astype(
        jnp.bfloat16
    )
    query_heads = queries.reshape(seq_count, block_rows, local_heads, HEAD)
    key_value = jnp.concatenate([key_rows, values], -1).reshape(
        seq_count, block_rows, 2 * head_width
    )

    def split_pairs(slab_pairs, block_len):
        return (
            slab_pairs[..., :head_width].reshape(seq_count, block_len, local_heads, HEAD),
            slab_pairs[..., head_width:].reshape(seq_count, block_len, local_heads, HEAD),
        )

    def key_slab(pairs, piece_keep, offset, block_len):
        slab_pairs = lax.dynamic_slice_in_dim(pairs, offset, block_len, 1)
        slab_keep = lax.dynamic_slice_in_dim(piece_keep, offset, block_len, 1)
        key_pos = offset + jnp.arange(block_len, dtype=jnp.int32)
        key_seg = segment_ids(doc_lengths, key_pos)
        slab_keys, slab_values = split_pairs(slab_pairs, block_len)
        return (slab_keys, slab_values, slab_keep, key_pos, key_seg)

    start_state = (
        jnp.full((seq_count, local_heads, block_rows), MASKED, jnp.float32),
        jnp.zeros((seq_count, local_heads, block_rows), jnp.float32),
        jnp.zeros((seq_count, local_heads, block_rows, HEAD), jnp.float32),
    )
    pairs = lax.all_gather(key_value, "ctx", axis=1, tiled=True)
    piece_keep = lax.all_gather(keep, "ctx", axis=1, tiled=True)

    def advance(partial_value, offset, block_len):
        slab_keys, slab_values, slab_keep, key_pos, key_seg = key_slab(
            pairs, piece_keep, offset, block_len
        )

        def update(current):
            row_max, row_sum, weighted = current
            scores, allowed = score_block(
                query_heads, own_pos, own_seg, slab_keys, key_pos, key_seg, slab_keep, slopes
            )
            scores = jnp.where(allowed, scores, MASKED)
            new_max = jnp.maximum(row_max, jnp.max(scores, -1))
            factor = jnp.exp(row_max - new_max)
            weights = jnp.where(allowed, jnp.exp(scores - new_max[..., None]), 0.0)
            row_sum = row_sum * factor + jnp.sum(weights, -1)
            weighted = weighted * factor[..., None] + jnp.einsum(
                "shqk,skhd->shqd",
                weights.astype(jnp.bfloat16),
                slab_values,
                preferred_element_type=jnp.float32,
            )
            return (new_max, row_sum, weighted)

        return guarded(intersections(own_seg, key_seg), update, partial_value)

    row_max, row_sum, weighted = over_blocks(pairs.shape[1], advance, start_state)
    attended = (
        (weighted / row_sum[..., None])
        .transpose(0, 2, 1, 3)
        .reshape(row_count, head_width)
        .astype(jnp.bfloat16)
    )
    log_total = row_max + jnp.log(row_sum)
    att_part = jnp.einsum("rh,dh->rd", attended, full_out, preferred_element_type=jnp.float32)
    branch_att = lax.psum(att_part.astype(jnp.bfloat16), "tp").astype(jnp.float32) + b_out
    first_out, normed_one, inv_one = layer_norm(
        token_rows.astype(jnp.float32) + branch_att, gain_one, shift_one
    )
    first_low = first_out.astype(jnp.bfloat16)
    full_up, full_down = (
        lax.all_gather(w_up, "fsdp", axis=0, tiled=True),
        lax.all_gather(w_down, "fsdp", axis=0, tiled=True),
    )
    gate_up = jnp.einsum("rd,dcf->rcf", first_low, full_up, preferred_element_type=jnp.float32)
    product, gelu_back = jax.vjp(
        lambda gate_part, up_part: jax.nn.gelu(gate_part, approximate=False) * up_part,
        gate_up[:, 0],
        gate_up[:, 1],
    )
    hidden = product.astype(jnp.bfloat16)
    ffn_part = jnp.einsum("rf,df->rd", hidden, full_down, preferred_element_type=jnp.float32)
    branch_ffn = lax.psum(ffn_part.astype(jnp.bfloat16), "tp").astype(jnp.float32) + b_down
    result, normed_two, inv_two = layer_norm(first_out + branch_ffn, gain_two, shift_two)
    grad_in = cotangent.reshape(row_count, model_width).astype(jnp.float32)
    grad_two, d_gain_two, d_shift_two = norm_back(grad_in, normed_two, inv_two, gain_two)
    grad_ffn = grad_two.astype(jnp.bfloat16)
    d_b_down = jnp.sum(grad_ffn.astype(jnp.float32), 0)
    d_w_down = jnp.einsum("rd,rf->df", grad_ffn, hidden, preferred_element_type=jnp.float32)
    grad_hidden = jnp.einsum("rd,df->rf", grad_ffn, full_down, preferred_element_type=jnp.float32)
    grad_gate, grad_up = gelu_back(grad_hidden)
    grad_gate_up = jnp.stack([grad_gate, grad_up], 1).astype(jnp.bfloat16)
    d_w_up = jnp.einsum("rd,rcf->dcf", first_low, grad_gate_up, preferred_element_type=jnp.float32)
    first_part = jnp.einsum(
        "rcf,dcf->rd", grad_gate_up, full_up, preferred_element_type=jnp.float32
    )
    grad_first = grad_two + lax.psum(first_part.astype(jnp.bfloat16), "tp").astype(jnp.float32)
    grad_one, d_gain_one, d_shift_one = norm_back(grad_first, normed_one, inv_one, gain_one)
    grad_att = grad_one.astype(jnp.bfloat16)
    d_b_out = jnp.sum(grad_att.astype(jnp.float32), 0)
    d_w_out = jnp.einsum("rd,rh->dh", grad_att, attended, preferred_element_type=jnp.float32)
    grad_attended = jnp.einsum(
        "rd,dh->rh", grad_att, full_out, preferred_element_type=jnp.float32
    ).astype(jnp.bfloat16)
    grad_heads = grad_attended.reshape(seq_count, block_rows, local_heads, HEAD)
    delta = jnp.einsum(
        "sqhd,sqhd->shq",
        grad_heads,
        attended.reshape(seq_count, block_rows, local_heads, HEAD),
        preferred_element_type=jnp.float32,
    )
    query_zero = jnp.zeros((seq_count, block_rows, local_heads, HEAD), jnp.float32)
    full_len = block_rows * lax.axis_size("ctx")
    term_zero = jnp.zeros((seq_count, full_len, 2 * head_width), jnp.float32)
    return_pairs = lax.all_gather(key_value, "ctx", axis=1, tiled=True)
    return_piece_keep = lax.all_gather(keep, "ctx", axis=1, tiled=True)

    def advance(partial_value, offset, block_len):
        slab_keys, slab_values, slab_keep, key_pos, key_seg = key_slab(
            return_pairs, return_piece_keep, offset, block_len
        )

        def update(current):
            query_grad, key_terms = current
            part_query, part_key, part_value = grad_block(
                query_heads,
                own_pos,
                own_seg,
                grad_heads,
                log_total,
                delta,
                slab_keys,
                slab_values,
                key_pos,
                key_seg,
                slab_keep,
                slopes,
            )
            slab_grads = jnp.concatenate(
                [
                    part_key.reshape(seq_count, block_len, head_width),
                    part_value.reshape(seq_count, block_len, head_width),
                ],
                -1,
            )
            return (
                query_grad + part_query,
                lax.dynamic_update_slice_in_dim(key_terms, slab_grads, offset, 1),
            )

        return guarded(intersections(own_seg, key_seg), update, partial_value)

    query_grad, key_terms = over_blocks(return_pairs.shape[1], advance, (query_zero, term_zero))
    pair_grads = lax.psum_scatter(
        key_terms.astype(jnp.bfloat16), "ctx", scatter_dimension=1, tiled=True
    ).astype(jnp.float32)
    query_low = query_grad.reshape(row_count, head_width).astype(jnp.bfloat16)
    pair_low = pair_grads.reshape(row_count, 2 * head_width).astype(jnp.bfloat16)
    grad_project = jnp.concatenate([query_low, pair_low], -1)
    joined_weights = jnp.concatenate([full_query, full_key, full_value], -1)
    joined_grads = jnp.einsum(
        "rd,rh->dh", token_rows, grad_project, preferred_element_type=jnp.float32
    )
    input_part = jnp.einsum(
        "rh,dh->rd", grad_project, joined_weights, preferred_element_type=jnp.float32
    )
    d_tokens = grad_one + lax.psum(input_part.astype(jnp.bfloat16), "tp").astype(jnp.float32)
    d_b_query = jnp.sum(query_low.astype(jnp.float32), 0)
    d_b_value = jnp.sum(pair_low[:, head_width:].astype(jnp.float32), 0)
    d_w_query = joined_grads[:, :head_width]
    d_w_key = joined_grads[:, head_width : 2 * head_width]
    d_w_value = joined_grads[:, 2 * head_width :]
    shard_grads = (
        lax.psum_scatter(
            d_w_query.astype(jnp.bfloat16), "fsdp", scatter_dimension=0, tiled=True
        ).astype(jnp.float32),
        lax.psum_scatter(
            d_w_key.astype(jnp.bfloat16), "fsdp", scatter_dimension=0, tiled=True
        ).astype(jnp.float32),
        lax.psum_scatter(
            d_w_value.astype(jnp.bfloat16), "fsdp", scatter_dimension=0, tiled=True
        ).astype(jnp.float32),
        lax.psum_scatter(
            d_w_out.astype(jnp.bfloat16), "fsdp", scatter_dimension=0, tiled=True
        ).astype(jnp.float32),
        lax.psum_scatter(
            d_w_up.astype(jnp.bfloat16), "fsdp", scatter_dimension=0, tiled=True
        ).astype(jnp.float32),
        lax.psum_scatter(
            d_w_down.astype(jnp.bfloat16), "fsdp", scatter_dimension=0, tiled=True
        ).astype(jnp.float32),
    )
    sum_query, sum_key, sum_value, sum_out, sum_up, sum_down = (
        lax.psum(shard_grads[0].astype(jnp.bfloat16), "ctx").astype(jnp.float32),
        lax.psum(shard_grads[1].astype(jnp.bfloat16), "ctx").astype(jnp.float32),
        lax.psum(shard_grads[2].astype(jnp.bfloat16), "ctx").astype(jnp.float32),
        lax.psum(shard_grads[3].astype(jnp.bfloat16), "ctx").astype(jnp.float32),
        lax.psum(shard_grads[4].astype(jnp.bfloat16), "ctx").astype(jnp.float32),
        lax.psum(shard_grads[5].astype(jnp.bfloat16), "ctx").astype(jnp.float32),
    )
    (
        total_b_query,
        total_b_value,
        total_b_out,
        total_b_down,
        total_gain_one,
        total_shift_one,
        total_gain_two,
        total_shift_two,
    ) = lax.psum(
        (d_b_query, d_b_value, d_b_out, d_b_down, d_gain_one, d_shift_one, d_gain_two, d_shift_two),
        ("fsdp", "ctx"),
    )
    return (
        result.reshape(seq_count, block_rows, model_width).astype(jnp.bfloat16),
        d_tokens.reshape(seq_count, block_rows, model_width),
        sum_query,
        total_b_query,
        sum_key,
        sum_value,
        total_b_value,
        sum_out,
        total_b_out,
        total_gain_one,
        total_shift_one,
        sum_up,
        sum_down,
        total_b_down,
        total_gain_two,
        total_shift_two,
    )


LANES = 128
MESH = pl.DeviceIdType.MESH
TILE = 256
DOC_ROW, KEEP_ROW, POS_ROW, LINE_ROW, LOG_ROW, FEAT_END = 64, 72, 73, 79, 82, 85
X_SWAP = [(0, 1), (1, 0), (2, 3), (3, 2)]
Y_SWAP = [(0, 2), (2, 0), (1, 3), (3, 1)]
D_SWAP = [(0, 3), (3, 0), (1, 2), (2, 1)]


def dot(left, right, dims=((1,), (0,))):
    return lax.dot_general(left, right, (dims, ((), ())), preferred_element_type=jnp.float32)


def three_terms(value, low):
    high = low(value)
    middle = low(value - high)
    return high, middle, low(value - high - middle)


def narrow(value):
    return lax.reduce_precision(value, 8, 7)


def project_kernel(x_ref, w_ref, bias_ref, key_feat_ref, query_feat_ref, qt_ref, q_ref, k_ref, kt_ref, v_ref, vt_ref):
    heads = q_ref.shape[0]
    rows = x_ref.shape[0]
    y = dot(x_ref[...], w_ref[...]) + bias_ref[...]
    y = y.astype(jnp.bfloat16).astype(jnp.float32)
    lane = lax.broadcasted_iota(jnp.int32, (rows, LANES), 1)
    sub = lax.broadcasted_iota(jnp.int32, (LANES, rows), 0)

    def head_part(index):
        pair = y[:, index // 2 * LANES : (index // 2 + 1) * LANES]
        if index % 2:
            pair = pltpu.roll(pair, HEAD, 1)
        return jnp.where(lane < HEAD, pair, 0.0)

    for head in range(heads):
        query = head_part(head) * 0.125
        q_ref[head] = query[:, :HEAD].astype(jnp.bfloat16)
        qt_ref[head] = (query.T + query_feat_ref[head].astype(jnp.float32)).astype(jnp.bfloat16)
        key = head_part(heads + head)
        k_ref[head] = (key + key_feat_ref[...].astype(jnp.float32)).astype(jnp.bfloat16)
        kt_ref[head] = key.T[:HEAD].astype(jnp.bfloat16)
        value = head_part(2 * heads + head)
        ones = (lane >= HEAD) & (lane < HEAD + 3)
        v_ref[head] = jnp.where(ones, 1.0, value).astype(jnp.bfloat16)
        vt_ref[head] = jnp.where(sub == HEAD, 1.0, value.T)[:80].astype(jnp.bfloat16)


def project(x, weight, bias, key_feat, query_feat, heads):
    length, width = x.shape
    rows = 2 * TILE
    return pl.pallas_call(
        project_kernel,
        grid=(length // rows,),
        in_specs=[
            pl.BlockSpec((rows, width), lambda i: (i, 0)),
            pl.BlockSpec(weight.shape, lambda i: (0, 0)),
            pl.BlockSpec(bias.shape, lambda i: (0, 0)),
            pl.BlockSpec((rows, LANES), lambda i: (i, 0)),
            pl.BlockSpec((heads, LANES, rows), lambda i: (0, 0, i)),
        ],
        out_specs=[
            pl.BlockSpec((heads, LANES, rows), lambda i: (0, 0, i)),
            pl.BlockSpec((heads, rows, HEAD), lambda i: (0, i, 0)),
            pl.BlockSpec((heads, rows, LANES), lambda i: (0, i, 0)),
            pl.BlockSpec((heads, HEAD, rows), lambda i: (0, 0, i)),
            pl.BlockSpec((heads, rows, LANES), lambda i: (0, i, 0)),
            pl.BlockSpec((heads, 80, rows), lambda i: (0, 0, i)),
        ],
        out_shape=[
            jax.ShapeDtypeStruct((heads, LANES, length), jnp.bfloat16),
            jax.ShapeDtypeStruct((heads, length, HEAD), jnp.bfloat16),
            jax.ShapeDtypeStruct((heads, length, LANES), jnp.bfloat16),
            jax.ShapeDtypeStruct((heads, HEAD, length), jnp.bfloat16),
            jax.ShapeDtypeStruct((heads, length, LANES), jnp.bfloat16),
            jax.ShapeDtypeStruct((heads, 80, length), jnp.bfloat16),
        ],
        compiler_params=pltpu.CompilerParams(vmem_limit_bytes=40 << 20),
        cost_estimate=pl.CostEstimate(
            flops=2 * length * width * weight.shape[1], bytes_accessed=12 << 20, transcendentals=0
        ),
        name="project",
    )(x, weight, bias, key_feat, query_feat)


def side_signs(rows):
    sub = lax.broadcasted_iota(jnp.int32, (LANES, rows), 0)
    bias_rows = (sub >= POS_ROW) & (sub < LOG_ROW)
    after = jnp.where(bias_rows, -1.0, 1.0).astype(jnp.bfloat16)
    same = jnp.where(bias_rows, 0.0, 1.0).astype(jnp.bfloat16)
    bare = jnp.where(bias_rows | (sub == KEEP_ROW), 0.0, 1.0).astype(jnp.bfloat16)
    return after, same, bare


def diagonal_scores(keys, query_t, same, bare, slope):
    rows = lax.broadcasted_iota(jnp.int32, (TILE, TILE), 0)
    cols = lax.broadcasted_iota(jnp.int32, (TILE, TILE), 1)
    apart = jnp.abs(rows - cols)
    full = dot(keys, query_t * same) - slope * apart.astype(jnp.float32)
    return jnp.where(apart == 0, dot(keys, query_t * bare), full)


def attend_kernel(span_ref, slope_ref, qt_ref, k_ref, vt_ref, o_ref, ot_ref, lse_ref, max_ref, acc_ref):
    heads = qt_ref.shape[0]
    block = pl.program_id(0)
    after, same, bare = side_signs(TILE)

    def tile_rows(tile):
        return pl.ds(pl.multiple_of(tile * TILE, TILE), TILE)

    own = tile_rows(block)
    for head in range(heads):
        scores = diagonal_scores(k_ref[head, own, :], qt_ref[head], same, bare, slope_ref[head])
        top = jnp.max(scores, 0, keepdims=True)
        weights = jnp.exp(scores - top).astype(jnp.bfloat16)
        max_ref[head] = top
        acc_ref[head] = dot(vt_ref[head, :, own], weights)

    def step(tile, sign):
        for head in range(heads):
            query_t = qt_ref[head] if sign is None else qt_ref[head] * sign
            scores = dot(k_ref[head, tile_rows(tile), :], query_t)
            old = max_ref[head]
            top = jnp.maximum(old, jnp.max(scores, 0, keepdims=True))
            weights = jnp.exp(scores - top).astype(jnp.bfloat16)
            max_ref[head] = top
            acc_ref[head] = acc_ref[head] * jnp.exp(old - top) + dot(
                vt_ref[head, :, tile_rows(tile)], weights
            )

    @pl.loop(span_ref[0, block], block)
    def _(tile):
        step(tile, None)

    @pl.loop(block + 1, span_ref[1, block])
    def _(tile):
        step(tile, after)

    parts = []
    for head in range(heads):
        total = acc_ref[head, HEAD : HEAD + 1, :]
        out_t = acc_ref[head, :HEAD, :] / total
        ot_ref[head] = out_t
        parts.append(out_t)
        lse_ref[head] = max_ref[head] + jnp.log(total)
    o_ref[...] = jnp.concatenate(parts, 0).T.astype(jnp.bfloat16)


def attend(spans, slopes, query_t, keys, value_t):
    heads, _, length = query_t.shape
    blocks = length // TILE
    return pl.pallas_call(
        attend_kernel,
        grid_spec=pltpu.PrefetchScalarGridSpec(
            num_scalar_prefetch=2,
            grid=(blocks,),
            in_specs=[
                pl.BlockSpec((heads, LANES, TILE), lambda i, *_: (0, 0, i)),
                pl.BlockSpec(keys.shape, lambda i, *_: (0, 0, 0)),
                pl.BlockSpec(value_t.shape, lambda i, *_: (0, 0, 0)),
            ],
            out_specs=[
                pl.BlockSpec((TILE, heads * HEAD), lambda i, *_: (i, 0)),
                pl.BlockSpec((heads, HEAD, TILE), lambda i, *_: (0, 0, i)),
                pl.BlockSpec((heads, 1, TILE), lambda i, *_: (0, 0, i)),
            ],
            scratch_shapes=[
                pltpu.VMEM((heads, 1, TILE), jnp.float32),
                pltpu.VMEM((heads, 80, TILE), jnp.float32),
            ],
        ),
        out_shape=[
            jax.ShapeDtypeStruct((length, heads * HEAD), jnp.bfloat16),
            jax.ShapeDtypeStruct((heads, HEAD, length), jnp.float32),
            jax.ShapeDtypeStruct((heads, 1, length), jnp.float32),
        ],
        compiler_params=pltpu.CompilerParams(vmem_limit_bytes=40 << 20),
        cost_estimate=pl.CostEstimate(
            flops=heads * length * length * 256, bytes_accessed=6 << 20, transcendentals=heads * length * length
        ),
        name="attend",
    )(spans, slopes, query_t, keys, value_t)


def attend_back_kernel(
    span_ref, slope_ref, qt_ref, q_ref, k_ref, kt_ref, v_ref, g_ref, ot_ref, lse_ref,
    dq_ref, dk_ref, dv_ref, qt_log, grad_heads, grad_t, query_acc, key_acc, value_acc,
):
    heads = qt_ref.shape[0]
    blocks = pl.num_programs(0)
    block = pl.program_id(0)
    length = qt_ref.shape[2]
    after, same, bare = side_signs(TILE)

    def low(value):
        return value.astype(jnp.bfloat16).astype(jnp.float32)

    def tile_rows(tile):
        return pl.ds(pl.multiple_of(tile * TILE, TILE), TILE)

    @pl.when(block == 0)
    def _():
        query_acc[...] = jnp.zeros_like(query_acc)
        sub = lax.broadcasted_iota(jnp.int32, (LANES, TILE), 0)

        @pl.loop(0, length // TILE)
        def _(tile):
            rows = tile_rows(tile)
            grad = g_ref[rows, :].astype(jnp.float32)
            turned = grad.T
            for head in range(heads):
                own = turned[head * HEAD : (head + 1) * HEAD]
                delta = jnp.sum(own * ot_ref[head, :, rows], 0, keepdims=True)
                first, second, third = three_terms(-delta, low)
                wide = jnp.concatenate([own, jnp.zeros_like(own)], 0)
                wide = jnp.where(sub == HEAD, first, wide)
                wide = jnp.where(sub == HEAD + 1, second, wide)
                wide = jnp.where(sub == HEAD + 2, third, wide)
                grad_t[head, :, rows] = wide.astype(jnp.bfloat16)
                grad_heads[head, rows, :] = own.T.astype(jnp.bfloat16)
                first, second, third = three_terms(-lse_ref[head, :, rows], low)
                query = qt_ref[head, :, rows].astype(jnp.float32)
                query = jnp.where(sub == LOG_ROW, first, query)
                query = jnp.where(sub == LOG_ROW + 1, second, query)
                query = jnp.where(sub == LOG_ROW + 2, third, query)
                qt_log[head, :, rows] = query.astype(jnp.bfloat16)

    def accumulate(head, tile, scores, first):
        rows = tile_rows(tile)
        probs = jnp.exp(scores)
        grad_probs = dot(v_ref[head], grad_t[head, :, rows])
        grad_scores = (probs * grad_probs).astype(jnp.bfloat16)
        value_part = dot(probs.astype(jnp.bfloat16), grad_heads[head, rows, :])
        key_part = dot(grad_scores, q_ref[head, rows, :])
        query_acc[head, :, rows] += dot(kt_ref[head], grad_scores)
        if first:
            value_acc[head] = value_part
            key_acc[head] = key_part
        else:
            value_acc[head] += value_part
            key_acc[head] += key_part

    for head in range(heads):
        accumulate(
            head,
            block,
            diagonal_scores(k_ref[head], qt_log[head, :, tile_rows(block)], same, bare, slope_ref[head]),
            True,
        )

    @pl.loop(span_ref[0, block], block)
    def _(tile):
        for head in range(heads):
            accumulate(head, tile, dot(k_ref[head], qt_log[head, :, tile_rows(tile)] * after), False)

    @pl.loop(block + 1, span_ref[1, block])
    def _(tile):
        for head in range(heads):
            accumulate(head, tile, dot(k_ref[head], qt_log[head, :, tile_rows(tile)]), False)

    dk_ref[...] = jnp.concatenate([key_acc[head] for head in range(heads)], 1).astype(jnp.bfloat16)
    dv_ref[...] = jnp.concatenate([value_acc[head] for head in range(heads)], 1).astype(jnp.bfloat16)

    @pl.when(block == blocks - 1)
    def _():
        @pl.loop(0, length // TILE)
        def _(tile):
            rows = tile_rows(tile)
            turned = jnp.concatenate([query_acc[head, :, rows] for head in range(heads)], 0)
            dq_ref[rows, :] = (turned.T * 0.125).astype(jnp.bfloat16)


def attend_back(spans, slopes, query_t, queries, keys, keys_t, values, grads, out_t, lse):
    heads, _, length = query_t.shape
    blocks = length // TILE
    width = heads * HEAD

    def whole(array):
        return pl.BlockSpec(array.shape, lambda i, *_: (0,) * array.ndim)

    return pl.pallas_call(
        attend_back_kernel,
        grid_spec=pltpu.PrefetchScalarGridSpec(
            num_scalar_prefetch=2,
            grid=(blocks,),
            in_specs=[
                whole(query_t),
                whole(queries),
                pl.BlockSpec((heads, TILE, LANES), lambda i, *_: (0, i, 0)),
                pl.BlockSpec((heads, HEAD, TILE), lambda i, *_: (0, 0, i)),
                pl.BlockSpec((heads, TILE, LANES), lambda i, *_: (0, i, 0)),
                whole(grads),
                whole(out_t),
                whole(lse),
            ],
            out_specs=[
                pl.BlockSpec((length, width), lambda i, *_: (0, 0)),
                pl.BlockSpec((TILE, width), lambda i, *_: (i, 0)),
                pl.BlockSpec((TILE, width), lambda i, *_: (i, 0)),
            ],
            scratch_shapes=[
                pltpu.VMEM((heads, LANES, length), jnp.bfloat16),
                pltpu.VMEM((heads, length, HEAD), jnp.bfloat16),
                pltpu.VMEM((heads, LANES, length), jnp.bfloat16),
                pltpu.VMEM((heads, HEAD, length), jnp.float32),
                pltpu.VMEM((heads, TILE, HEAD), jnp.float32),
                pltpu.VMEM((heads, TILE, HEAD), jnp.float32),
            ],
        ),
        out_shape=[jax.ShapeDtypeStruct((length, width), jnp.bfloat16)] * 3,
        compiler_params=pltpu.CompilerParams(vmem_limit_bytes=50 << 20),
        cost_estimate=pl.CostEstimate(
            flops=heads * length * length * 640, bytes_accessed=12 << 20, transcendentals=heads * length * length
        ),
        name="attend_back",
    )(spans, slopes, query_t, queries, keys, keys_t, values, grads, out_t, lse)


def start_kernel(
    tokens, keep, w_joined, w_out, w_down, sequence, keep_all, full_joined, full_out, full_down,
    z_send, z_recv, tp_send, tp_recv, w_send, w_recv, keep_send, keep_recv, local_sem,
):
    place, stage, core = lax.axis_index("fsdp"), lax.axis_index("ctx"), lax.axis_index("tp")
    seq = stage // 2
    half_rows = sequence.shape[2]
    barrier = pltpu.get_barrier_semaphore()
    peers = [(place ^ other, stage, core) for other in (1, 2, 3)]
    peers += [(place, lax.rem(stage + shift, 4), core) for shift in (1, 2, 3)]
    peers += [(place, stage, 1 - core)]
    for peer in peers:
        pl.semaphore_signal(barrier, inc=1, device_id=peer, device_id_type=MESH)
    pl.semaphore_wait(barrier, len(peers))

    rows = pl.ds(pl.multiple_of(core * half_rows, half_rows), half_rows)
    ours, theirs = tokens.at[seq, rows], tokens.at[1 - seq, rows]

    def send(source, block, target, slot):
        return pltpu.make_async_remote_copy(
            source, sequence.at[block, core], z_send.at[slot], z_recv.at[block],
            device_id=(place, target, core), device_id_type=MESH,
        )

    def arrival(block):
        return pltpu.make_async_remote_copy(
            ours, sequence.at[block, core], z_send.at[0], z_recv.at[block],
            device_id=(place, stage, 1 - core), device_id_type=MESH,
        )

    def share(block):
        return pltpu.make_async_remote_copy(
            sequence.at[block, core], sequence.at[block, core], tp_send.at[block], tp_recv.at[block],
            device_id=(place, stage, 1 - core), device_id_type=MESH,
        )

    def shared(block):
        return pltpu.make_async_remote_copy(
            sequence.at[block, 1 - core], sequence.at[block, 1 - core], tp_send.at[block], tp_recv.at[block],
            device_id=(place, stage, 1 - core), device_id_type=MESH,
        )

    first = send(ours, stage, stage ^ 1, 0)
    ends = ((0, 2, 3), (3, 1, 0))
    mids = ((1, 2, 0), (2, 1, 3))
    for own, near, _ in mids:

        @pl.when(stage == own)
        def _():
            send(theirs, own, near, 1).start()

    first.start()
    for own, near, far in ends:

        @pl.when(stage == own)
        def _():
            send(theirs, own, far, 1).start()
            send(theirs, own, near, 2).start()

    weights = []
    for index, (shard, full) in enumerate(
        ((w_joined, full_joined), (w_out, full_out), (w_down, full_down))
    ):
        for other in (1, 2, 3):
            sem = 3 * index + other - 1
            weights.append(
                pltpu.make_async_remote_copy(
                    shard, full.at[place], w_send.at[sem], w_recv.at[sem],
                    device_id=(place ^ other, stage, core), device_id_type=MESH,
                )
            )
            weights[-1].start()
    flags = []
    for shift in (1, 2, 3):
        flags.append(
            pltpu.make_async_remote_copy(
                keep, keep_all.at[stage], keep_send.at[shift - 1], keep_recv.at[shift - 1],
                device_id=(place, lax.rem(stage + shift, 4), core), device_id_type=MESH,
            )
        )
        flags[-1].start()
    local = []
    for index, (source, target) in enumerate(
        (
            (tokens.at[seq, pl.ds(0, half_rows)], sequence.at[stage, 0]),
            (tokens.at[seq, pl.ds(half_rows, half_rows)], sequence.at[stage, 1]),
            (keep, keep_all.at[stage]),
            (w_joined, full_joined.at[place]),
            (w_out, full_out.at[place]),
            (w_down, full_down.at[place]),
        )
    ):
        local.append(pltpu.make_async_copy(source, target, local_sem.at[index]))
        local[-1].start()

    for own, near, end in mids:
        far = 3 - end

        @pl.when(stage == own)
        def _():
            arrival(near).wait_recv()
            send(sequence.at[near, core], near, end, 2).start()
            share(near).start()
            arrival(end).wait_recv()
            share(end).start()
            arrival(far).wait_recv()
            share(far).start()
            send(theirs, own, near, 1).wait_send()
            send(sequence.at[near, core], near, end, 2).wait_send()
            for block in (near, end, far):
                share(block).wait_send()
                shared(block).wait_recv()

    for own, near, far in ends:

        @pl.when(stage == own)
        def _():
            inner = 3 - near
            for block in (inner, far, near):
                arrival(block).wait_recv()
                share(block).start()
            send(theirs, own, near, 1).wait_send()
            send(theirs, own, near, 2).wait_send()
            for block in (inner, far, near):
                share(block).wait_send()
                shared(block).wait_recv()

    first.wait_send()
    for copy in weights + flags:
        copy.wait()
    for copy in local:
        copy.wait()


def start(tokens, keep, w_joined, w_out, w_down):
    _, block_rows, width = tokens.shape
    dma = pltpu.SemaphoreType.DMA
    return pl.pallas_call(
        start_kernel,
        in_specs=[pl.BlockSpec(memory_space=pl.ANY)] * 5,
        out_specs=[pl.BlockSpec(memory_space=pl.ANY)] * 5,
        out_shape=[
            jax.ShapeDtypeStruct((4, 2, block_rows // 2, width), tokens.dtype),
            jax.ShapeDtypeStruct((4,) + keep.shape, keep.dtype),
            jax.ShapeDtypeStruct((4,) + w_joined.shape, w_joined.dtype),
            jax.ShapeDtypeStruct((4,) + w_out.shape, w_out.dtype),
            jax.ShapeDtypeStruct((4,) + w_down.shape, w_down.dtype),
        ],
        scratch_shapes=[
            dma((3,)), dma((4,)), dma((4,)), dma((4,)), dma((9,)), dma((9,)), dma((3,)), dma((3,)), dma((6,)),
        ],
        compiler_params=pltpu.CompilerParams(collective_id=0, has_side_effects=True),
        cost_estimate=pl.CostEstimate(flops=40 << 30, bytes_accessed=16 << 20, transcendentals=0),
        name="start",
    )(tokens, keep, w_joined, w_out, w_down)


def rows_norm(residual):
    centered = residual - jnp.mean(residual, -1, keepdims=True)
    inv_scale = lax.rsqrt(jnp.mean(centered * centered, -1, keepdims=True) + NORM_EPS)
    return centered * inv_scale, inv_scale


def rows_norm_back(grad_out, normed, inv_scale, norm_gain):
    grad_norm = grad_out * norm_gain
    mean_grad = jnp.mean(grad_norm, -1, keepdims=True)
    mean_cross = jnp.mean(grad_norm * normed, -1, keepdims=True)
    return (grad_norm - mean_grad - normed * mean_cross) * inv_scale


def middle_kernel(
    attended, sequence, cotangent, w_out, w_down, up_0, up_1, up_2, up_3, vectors,
    out_home, grad_one, grad_heads, pack, sums,
    token_v, mine_v, theirs_v, both_v, cot_v, out_w, down_w, up_w,
    send_a, recv_a, send_b, recv_b, send_c, recv_c,
    normed_v, inv_v, low_v, hidden_v, gate_v, lift_v, grad_v, ffn_v, att_v, result_v, keep_v, away_v, tile_v,
    load_sem, pair_send, pair_recv, cot_send, cot_recv, cot_pass, cot_took,
    a_send, a_recv, b_send, b_recv, c_send, c_recv, out_send, out_recv, out_pass, out_took,
    one_sem, keep_sem, away_send, away_recv, tile_sem,
):
    place, stage, core = lax.axis_index("fsdp"), lax.axis_index("ctx"), lax.axis_index("tp")
    seq, half = stage // 2, stage % 2
    pair = stage ^ 1
    chunks = token_v.shape[0]
    units = hidden_v.shape[2]
    wide = 512
    quarter = up_0.shape[0]

    barrier = pltpu.get_barrier_semaphore()
    peers = [(place, lax.rem(stage + shift, 4), core) for shift in (1, 2, 3)]
    peers += [(place, stage, 1 - core)]
    for peer in peers:
        pl.semaphore_signal(barrier, inc=1, device_id=peer, device_id_type=MESH)
    pl.semaphore_wait(barrier, len(peers))

    def remote(source, target, send, recv, device):
        return pltpu.make_async_remote_copy(
            source, target, send, recv, device_id=device, device_id_type=MESH
        )

    partner = (place, pair, core)
    other_core = (place, stage, 1 - core)

    def pair_copy(c):
        return remote(
            attended.at[(1 - half) * chunks + c], theirs_v.at[c], pair_send.at[c], pair_recv.at[c], partner
        )

    for c in range(chunks):
        pair_copy(c).start()

    def cot_owner(which):
        return 2 * which + stage // 2

    def cot_copy(which):
        return remote(
            cotangent.at[which, core], cot_v.at[stage % 2, core],
            cot_send.at[which], cot_recv.at[stage % 2], (place, cot_owner(which), core),
        )

    def cot_local(which):
        return pltpu.make_async_copy(cotangent.at[which], cot_v.at[stage % 2], cot_send.at[which])

    for which in (0, 1):

        @pl.when(cot_owner(which) == stage)
        def _():
            cot_local(which).start()

        @pl.when(cot_owner(which) != stage)
        def _():
            cot_copy(which).start()

    def cot_arrival(block):
        return remote(
            cot_v.at[block, core], cot_v.at[block, core], cot_pass.at[block], cot_recv.at[block], other_core
        )

    def cot_share(block, whose):
        return remote(
            cot_v.at[block, whose], cot_v.at[block, whose], cot_pass.at[block], cot_took.at[block], other_core
        )

    loads = [
        pltpu.make_async_copy(attended.at[pl.ds(half * chunks, chunks)], mine_v, load_sem.at[0]),
        pltpu.make_async_copy(w_out, out_w, load_sem.at[1]),
        pltpu.make_async_copy(sequence.at[pl.ds(half * chunks, chunks)], token_v, load_sem.at[2]),
        pltpu.make_async_copy(w_down, down_w, load_sem.at[3]),
    ]
    for other, shard in enumerate((up_0, up_1, up_2, up_3)):
        rows = pl.ds(pl.multiple_of((place ^ other) * quarter, quarter), quarter)
        loads.append(pltpu.make_async_copy(shard, up_w.at[rows], load_sem.at[4 + other]))
    for load in loads:
        load.start()

    def vector(index):
        return vectors[index : index + 1, :]

    b_out, gain_one, shift_one, b_down, gain_two, shift_two = (vector(i) for i in range(6))
    sums[...] = jnp.zeros_like(sums)

    def add_sum(index, rows):
        sums[index : index + 1, :] += jnp.sum(rows, 0, keepdims=True)

    def exchange(c, sent, got, send, recv):
        return remote(sent.at[c], got.at[c], send.at[c], recv.at[c], other_core)

    def total(c, sent, got):
        return sent[c].astype(jnp.float32) + got[c].astype(jnp.float32)

    loads[0].wait()
    loads[1].wait()

    @pl.loop(0, chunks)
    def _(c):
        pair_copy(c).wait_recv()
        first, second = mine_v[c], theirs_v[c]
        both = jnp.where(
            half == 0, jnp.concatenate([first, second], 1), jnp.concatenate([second, first], 1)
        )
        both_v[c] = both
        send_a[c] = dot(both, out_w[...], ((1,), (1,))).astype(jnp.bfloat16)
        exchange(c, send_a, recv_a, a_send, a_recv).start()

    for load in loads[2:]:
        load.wait()

    @pl.loop(0, chunks)
    def _(c):
        exchange(c, send_a, recv_a, a_send, a_recv).wait_recv()

        @pl.when(c == chunks - 1)
        def _():
            for block in (0, 1):

                @pl.when(2 * half + block != stage)
                def _():
                    cot_arrival(block).wait_recv()
                    cot_share(block, core).start()

        residual = token_v[c].astype(jnp.float32) + (total(c, send_a, recv_a) + b_out)
        normed, inv_scale = rows_norm(residual)
        normed_v[c] = normed
        inv_v[c] = inv_scale
        low_v[c] = (normed * gain_one + shift_one).astype(jnp.bfloat16)
        for n in range(0, units, wide):
            gate = dot(low_v[c], up_w[:, n : n + wide])
            lift = dot(low_v[c], up_w[:, units + n : units + n + wide])
            chance = 0.5 + 0.5 * lax.erf(gate * 0.7071067811865476)
            density = jnp.exp(gate * gate * -0.5) * 0.3989422804014327
            gelu = gate * chance
            hidden_v[c, :, n : n + wide] = (gelu * lift).astype(jnp.bfloat16)
            gate_v[c, :, n : n + wide] = (lift * (chance + gate * density)).astype(jnp.bfloat16)
            lift_v[c, :, n : n + wide] = gelu.astype(jnp.bfloat16)
        send_b[c] = dot(hidden_v[c], down_w[...], ((1,), (1,))).astype(jnp.bfloat16)
        exchange(c, send_b, recv_b, b_send, b_recv).start()

    for block in (0, 1):

        @pl.when(2 * half + block != stage)
        def _():
            cot_share(block, core).wait_send()
            cot_share(block, 1 - core).wait_recv()

    for which in (0, 1):

        @pl.when(cot_owner(which) == stage)
        def _():
            cot_local(which).wait()

        @pl.when(cot_owner(which) != stage)
        def _():
            cot_copy(which).wait_send()

    def home(c):
        return 2 * half + c // 2

    def out_copy(c):
        return remote(
            result_v.at[c], out_home.at[seq, core], out_send.at[c], out_recv.at[seq], (place, home(c), core)
        )

    def out_local(c):
        return pltpu.make_async_copy(result_v.at[c], out_home.at[seq, c % 2], out_send.at[c])

    @pl.loop(0, chunks)
    def _(c):
        exchange(c, send_b, recv_b, b_send, b_recv).wait_recv()
        normed_one = normed_v[c]
        residual = normed_one * gain_one + shift_one + (total(c, send_b, recv_b) + b_down)
        normed, inv_scale = rows_norm(residual)
        result_v[c] = (normed * gain_two + shift_two).astype(jnp.bfloat16)

        @pl.when(home(c) == stage)
        def _():
            out_local(c).start()

        @pl.when((home(c) != stage) & (c % 2 == core))
        def _():
            out_copy(c).start()

        grad_in = cot_v[c // 2, c % 2].astype(jnp.float32)
        add_sum(0, grad_in * normed)
        add_sum(1, grad_in)
        grad_two = rows_norm_back(grad_in, normed, inv_scale, gain_two)
        grad_v[c] = grad_two
        grad_ffn = grad_two.astype(jnp.bfloat16)
        ffn_v[c] = grad_ffn
        add_sum(2, grad_ffn.astype(jnp.float32))
        for n in range(0, units, wide):
            grad_hidden = dot(ffn_v[c], down_w[:, n : n + wide])
            gate_v[c, :, n : n + wide] = (grad_hidden * gate_v[c, :, n : n + wide]).astype(jnp.bfloat16)
            lift_v[c, :, n : n + wide] = (grad_hidden * lift_v[c, :, n : n + wide]).astype(jnp.bfloat16)
        send_c[c] = (
            dot(gate_v[c], up_w[:, :units], ((1,), (1,))) + dot(lift_v[c], up_w[:, units:], ((1,), (1,)))
        ).astype(jnp.bfloat16)
        exchange(c, send_c, recv_c, c_send, c_recv).start()

    def one_copy(c):
        return pltpu.make_async_copy(grad_v.at[c], grad_one.at[c], one_sem.at[c])

    def keep_copy(c):
        return pltpu.make_async_copy(keep_v.at[c], grad_heads.at[half * chunks + c], keep_sem.at[c])

    def away_copy(c, whose):
        return remote(
            away_v.at[c], grad_heads.at[whose * chunks + c], away_send.at[c], away_recv.at[c], partner
        )

    @pl.loop(0, chunks)
    def _(c):
        exchange(c, send_c, recv_c, c_send, c_recv).wait_recv()
        grad_first = grad_v[c] + total(c, send_c, recv_c)
        normed = normed_v[c]
        add_sum(3, grad_first * normed)
        add_sum(4, grad_first)
        grad_res = rows_norm_back(grad_first, normed, inv_v[c], gain_one)
        grad_v[c] = grad_res
        one_copy(c).start()
        grad_att = grad_res.astype(jnp.bfloat16)
        att_v[c] = grad_att
        add_sum(5, grad_att.astype(jnp.float32))
        heads = dot(att_v[c], out_w[...]).astype(jnp.bfloat16)
        first, second = heads[:, : heads.shape[1] // 2], heads[:, heads.shape[1] // 2 :]
        keep_v[c] = jnp.where(half == 0, first, second)
        away_v[c] = jnp.where(half == 0, second, first)
        away_copy(c, half).start()
        keep_copy(c).start()

    tile = tile_v.shape[2]

    def tile_copy(slot, row, column):
        return pltpu.make_async_copy(
            tile_v.at[slot, pl.ds(row * quarter, quarter)],
            pack.at[place ^ row, :, pl.ds(pl.multiple_of(column * tile, tile), tile)],
            tile_sem.at[slot, row],
        )

    def weight_tile(column, left, right):
        slot = lax.rem(column, 2)

        @pl.when(column >= 2)
        def _():
            for row in range(4):
                tile_copy(slot, row, column - 2).wait()

        rows = left.shape[0] * left.shape[1]
        tile_v[slot] = dot(
            left[...].reshape(rows, left.shape[2]), right.reshape(rows, tile), ((0,), (0,))
        ).astype(jnp.bfloat16)
        for row in range(4):
            tile_copy(slot, row, column).start()

    out_tiles = both_v.shape[2] // tile
    unit_tiles = units // tile

    def columns(index):
        return pl.ds(pl.multiple_of(index * tile, tile), tile)

    @pl.loop(0, out_tiles)
    def _(i):
        weight_tile(i, att_v, both_v[:, :, columns(i)])

    @pl.loop(0, unit_tiles)
    def _(i):
        weight_tile(out_tiles + i, ffn_v, hidden_v[:, :, columns(i)])

    @pl.loop(0, unit_tiles)
    def _(i):
        weight_tile(out_tiles + unit_tiles + i, low_v, gate_v[:, :, columns(i)])

    @pl.loop(0, unit_tiles)
    def _(i):
        weight_tile(out_tiles + 2 * unit_tiles + i, low_v, lift_v[:, :, columns(i)])

    last = out_tiles + 3 * unit_tiles
    for column in (last - 2, last - 1):
        for row in range(4):
            tile_copy(column % 2, row, column).wait()

    def out_arrival(which):
        return remote(
            out_home.at[which, core], out_home.at[which, core], out_pass.at[which], out_recv.at[which], other_core
        )

    def out_share(which, whose):
        return remote(
            out_home.at[which, whose], out_home.at[which, whose], out_pass.at[which], out_took.at[which], other_core
        )

    for which in (0, 1):

        @pl.when(cot_owner(which) != stage)
        def _():
            out_arrival(which).wait_recv()
            out_share(which, core).start()

    @pl.loop(0, chunks)
    def _(c):
        pair_copy(c).wait_send()
        exchange(c, send_a, recv_a, a_send, a_recv).wait_send()
        exchange(c, send_b, recv_b, b_send, b_recv).wait_send()
        exchange(c, send_c, recv_c, c_send, c_recv).wait_send()
        one_copy(c).wait()
        keep_copy(c).wait()
        away_copy(c, half).wait_send()
        away_copy(c, 1 - half).wait_recv()

        @pl.when(home(c) == stage)
        def _():
            out_local(c).wait()

        @pl.when((home(c) != stage) & (c % 2 == core))
        def _():
            out_copy(c).wait_send()

    for which in (0, 1):

        @pl.when(cot_owner(which) != stage)
        def _():
            out_share(which, core).wait_send()
            out_share(which, 1 - core).wait_recv()


def middle(attended, sequence, cotangent, w_out, w_down, up_shards, vectors):
    chunks, rows, width = 4, sequence.shape[1], sequence.shape[2]
    head_width, units = w_out.shape[1], w_down.shape[1]
    columns = head_width + 3 * units
    dma, bf16, f32 = pltpu.SemaphoreType.DMA, jnp.bfloat16, jnp.float32

    def vmem(shape, dtype=bf16):
        return pltpu.VMEM(shape, dtype)

    wide = (chunks, rows, width)
    inner = (chunks, rows, units)
    narrow_rows = (chunks, rows, head_width // 2)
    four, two = dma((chunks,)), dma((2,))
    return pl.pallas_call(
        middle_kernel,
        in_specs=[pl.BlockSpec(memory_space=pl.ANY)] * 9 + [pl.BlockSpec(memory_space=pltpu.VMEM)],
        out_specs=[pl.BlockSpec(memory_space=pl.ANY)] * 4 + [pl.BlockSpec(memory_space=pltpu.VMEM)],
        out_shape=[
            jax.ShapeDtypeStruct((2, 2, rows, width), bf16),
            jax.ShapeDtypeStruct(wide, f32),
            jax.ShapeDtypeStruct((2 * chunks, rows, head_width // 2), bf16),
            jax.ShapeDtypeStruct((4, width // 4, columns), bf16),
            jax.ShapeDtypeStruct((8, width), f32),
        ],
        scratch_shapes=[
            vmem(wide), vmem(narrow_rows), vmem(narrow_rows), vmem((chunks, rows, head_width)),
            vmem((2, 2, rows, width)), vmem((width, head_width)), vmem((width, units)), vmem((width, 2 * units)),
            vmem(wide), vmem(wide), vmem(wide), vmem(wide), vmem(wide), vmem(wide),
            vmem(wide, f32), vmem((chunks, rows, 1), f32), vmem(wide),
            vmem(inner), vmem(inner), vmem(inner),
            vmem(wide, f32), vmem(wide), vmem(wide), vmem(wide), vmem(narrow_rows), vmem(narrow_rows),
            vmem((2, width, 384)),
            dma((8,)), four, four, two, two, two, two,
            four, four, four, four, four, four, four, two, two, two,
            four, four, four, four, dma((2, 4)),
        ],
        compiler_params=pltpu.CompilerParams(
            collective_id=1, has_side_effects=True, vmem_limit_bytes=60 << 20
        ),
        cost_estimate=pl.CostEstimate(flops=50 << 30, bytes_accessed=32 << 20, transcendentals=0),
        name="middle",
    )(attended, sequence, cotangent, w_out, w_down, *up_shards, vectors)


def tail_kernel(
    d_query, d_key, d_value, w_joined, sums_in, sequence, grad_one, pack, moved_1, moved_2, moved_3,
    home, shard, joined, sums,
    token_v, one_v, part_v, project_v, own_v, tp_sent, tp_got, pair_sent, pair_got, final_v,
    summed_v, end_got, inner_v, mid_got, total_v, joined_v, quarter_got, cross_sent, cross_got, full_v,
    step_v, step_got,
    load_sem, tp_send, tp_recv, pair_send, pair_recv, home_send, home_recv, home_pass, home_took, home_local,
    end_send, end_recv, mid_send, mid_recv, back_send, back_recv, shard_sem,
    quarter_send, quarter_recv, cross_send, cross_recv, half_send, half_recv, half_local, step_send, step_recv,
):
    place, stage, core = lax.axis_index("fsdp"), lax.axis_index("ctx"), lax.axis_index("tp")
    seq, half = stage // 2, stage % 2
    bf16, f32 = jnp.bfloat16, jnp.float32
    pieces = summed_v.shape[0]
    piece = summed_v.shape[2]
    quarter = joined_v.shape[0] // 4
    width = d_query.shape[2]

    barrier = pltpu.get_barrier_semaphore()
    peers = [(place ^ other, stage, core) for other in (1, 2, 3)]
    peers += [(place, lax.rem(stage + shift, 4), core) for shift in (1, 2, 3)]
    peers += [(place, stage, 1 - core)]
    for peer in peers:
        pl.semaphore_signal(barrier, inc=1, device_id=peer, device_id_type=MESH)
    pl.semaphore_wait(barrier, len(peers))

    def remote(source, target, send, recv, device):
        return pltpu.make_async_remote_copy(
            source, target, send, recv, device_id=device, device_id_type=MESH
        )

    other_core = (place, stage, 1 - core)
    partner = (place, stage ^ 1, core)
    at_end = (stage == 0) | (stage == 3)
    across = (place, jnp.where(at_end, stage, 3 - stage), core)
    inward = (place, jnp.where(stage < 2, 1, 2), core)
    outward = (place, jnp.where(stage < 2, 0, 3), core)

    loads = [
        pltpu.make_async_copy(source, part_v.at[index], load_sem.at[index])
        for index, source in enumerate((pack.at[0], moved_1, moved_2, moved_3))
    ]
    loads.append(pltpu.make_async_copy(sequence, token_v, load_sem.at[4]))
    loads.append(pltpu.make_async_copy(grad_one, one_v, load_sem.at[5]))
    for load in loads:
        load.start()

    def input_share(chunk):
        rows = jnp.concatenate([d_query[chunk], d_key[chunk], d_value[chunk]], 1)
        project_v[chunk] = rows
        return dot(rows, w_joined[...], ((1,), (1,)))

    def block_of(i):
        return jnp.where(i < 2, 2 * (1 - half) + i, 2 * half + i - 2)

    def tp_copy(i):
        return remote(tp_sent.at[i], tp_got.at[i], tp_send.at[i], tp_recv.at[i], other_core)

    @pl.loop(0, 4)
    def _(i):
        block = block_of(i)
        tp_sent[i] = input_share(2 * block + 1 - core).astype(bf16)
        tp_copy(i).start()
        own_v[i] = input_share(2 * block + core)

    def pair_copy(i):
        return remote(pair_sent.at[i], pair_got.at[i], pair_send.at[i], pair_recv.at[i], partner)

    @pl.loop(0, 2)
    def _(i):
        tp_copy(i).wait_recv()
        pair_sent[i] = (own_v[i] + tp_got[i].astype(f32)).astype(bf16)
        pair_copy(i).start()

    def end_copy(j):
        return remote(summed_v.at[j], end_got.at[j], end_send.at[j], end_recv.at[j], inward)

    def mid_copy(j):
        return remote(inner_v.at[j], mid_got.at[j], mid_send.at[j], mid_recv.at[j], across)

    def columns(j):
        return pl.ds(j * piece, piece)

    def back_copy(j):
        return remote(total_v.at[j], shard.at[:, columns(j)], back_send.at[j], back_recv.at[j], outward)

    def shard_copy(j):
        return pltpu.make_async_copy(total_v.at[j], shard.at[:, columns(j)], shard_sem.at[j])

    for load in loads[:4]:
        load.wait()
    for j in range(pieces):
        terms = [part_v[index, :, j * piece : (j + 1) * piece].astype(f32) for index in range(4)]
        summed_v[j] = (terms[0] + terms[1] + (terms[2] + terms[3])).astype(bf16)

        @pl.when(at_end)
        def _():
            end_copy(j).start()

    loads[4].wait()
    tokens = token_v[...].reshape(-1, token_v.shape[2])
    project = project_v[...].reshape(-1, project_v.shape[2])
    strip = 256
    for row in range(0, joined_v.shape[0], strip):
        joined_v[row : row + strip, :] = dot(
            tokens[:, row : row + strip], project, ((0,), (0,))
        ).astype(bf16)

    def quarter_copy(other):
        rows = pl.ds(pl.multiple_of((place ^ other) * quarter, quarter), quarter)
        return remote(
            joined_v.at[rows], quarter_got.at[other - 1], quarter_send.at[other - 1], quarter_recv.at[other - 1],
            (place ^ other, stage, core),
        )

    for other in (1, 2, 3):
        quarter_copy(other).start()

    def column_sum(grads):
        return jnp.sum(grads[...].reshape(-1, width).astype(f32), 0, keepdims=True)

    bias_parts = []
    for total in (column_sum(d_query), column_sum(d_value)):
        for which in (0, 1):
            bias_parts.append(jnp.where(half == which, total, 0.0))
    bias = jnp.concatenate(bias_parts, 1)
    step_v[0] = sums_in[...]
    step_v[0, 6:7, :] = bias
    steps = [(place ^ 1, stage, core), (place ^ 2, stage, core), partner, (place, stage ^ 2, core)]

    def step_copy(index):
        return remote(
            step_v.at[index], step_got.at[index], step_send.at[index], step_recv.at[index], steps[index]
        )

    def step_on(index):
        step_copy(index).wait_recv()
        step_v[index + 1] = step_v[index] + step_got[index]
        if index < 3:
            step_copy(index + 1).start()

    step_copy(0).start()

    loads[5].wait()

    def home_copy(i):
        return remote(
            final_v.at[i], home.at[seq, core], home_send.at[i], home_recv.at[seq], (place, 2 * half + i, core)
        )

    def home_direct(i):
        return remote(final_v.at[i], home.at[seq, core], home_send.at[i], home_took.at[seq], other_core)

    def home_here(i):
        return pltpu.make_async_copy(final_v.at[i], home.at[seq, core], home_local)

    for i in range(2):
        tp_copy(i + 2).wait_recv()
        pair_copy(i).wait_recv()
        final_v[i] = (
            own_v[i + 2] + tp_got[i + 2].astype(f32) + pair_got[i].astype(f32) + one_v[2 * i + core]
        ).astype(bf16)

        @pl.when(2 * half + i == stage)
        def _():
            home_direct(i).start()
            home_here(i).start()

        @pl.when(2 * half + i != stage)
        def _():
            home_copy(i).start()

    step_on(0)
    for other in (1, 2, 3):
        quarter_copy(other).wait_recv()
    own_rows = pl.ds(pl.multiple_of(place * quarter, quarter), quarter)
    cross_sent[...] = (
        joined_v[own_rows, :].astype(f32)
        + quarter_got[0].astype(f32)
        + (quarter_got[1].astype(f32) + quarter_got[2].astype(f32))
    ).astype(bf16)
    cross_copy = remote(cross_sent, cross_got, cross_send, cross_recv, (place, stage ^ 2, core))
    cross_copy.start()
    step_on(1)

    def from_end(j):
        end_copy(j).wait_recv()
        inner_v[j] = (summed_v[j].astype(f32) + end_got[j].astype(f32)).astype(bf16)
        mid_copy(j).start()

    def from_mid(j):
        mid_copy(j).wait_recv()
        total_v[j] = (inner_v[j].astype(f32) + mid_got[j].astype(f32)).astype(bf16)
        back_copy(j).start()
        shard_copy(j).start()

    @pl.when(~at_end)
    def _():
        from_end(0)
        for j in range(1, pieces):
            from_end(j)
            from_mid(j - 1)

    step_on(2)
    cross_copy.wait_recv()
    full_v[...] = (cross_sent[...].astype(f32) + cross_got[...].astype(f32)).astype(bf16)
    half_copy = remote(full_v, joined.at[half], half_send, half_recv, partner)
    half_copy.start()
    half_here = pltpu.make_async_copy(full_v, joined.at[half], half_local)
    half_here.start()
    step_on(3)
    sums[...] = step_v[4]

    def home_arrival(which):
        return remote(
            home.at[which, core], home.at[which, core], home_pass.at[which], home_recv.at[which], other_core
        )

    def home_share(which, whose):
        return remote(
            home.at[which, whose], home.at[which, whose], home_pass.at[which], home_took.at[which], other_core
        )

    for which in (0, 1):

        @pl.when(2 * which + stage // 2 != stage)
        def _():
            home_arrival(which).wait_recv()
            home_share(which, core).start()

    @pl.when(~at_end)
    def _():
        from_mid(pieces - 1)
        for j in range(pieces):
            mid_copy(j).wait_send()
            back_copy(j).wait_send()
            shard_copy(j).wait()

    @pl.when(at_end)
    def _():
        for j in range(pieces):
            end_copy(j).wait_send()
            back_copy(j).wait_recv()

    for i in range(4):
        tp_copy(i).wait_send()
        step_copy(i).wait_send()
    for i in range(2):
        pair_copy(i).wait_send()

        @pl.when(2 * half + i == stage)
        def _():
            home_direct(i).wait_send()
            home_here(i).wait()

        @pl.when(2 * half + i != stage)
        def _():
            home_copy(i).wait_send()

    for which in (0, 1):

        @pl.when(2 * which + stage // 2 != stage)
        def _():
            home_share(which, core).wait_send()

        home_share(which, 1 - core).wait_recv()
    for other in (1, 2, 3):
        quarter_copy(other).wait_send()
    cross_copy.wait_send()
    half_here.wait()
    half_copy.wait_send()
    remote(full_v, joined.at[1 - half], half_send, half_recv, partner).wait_recv()


def tail(d_query, d_key, d_value, w_joined, sums, sequence, grad_one, pack, moved):
    rows, width = sequence.shape[1:]
    columns, quarter = pack.shape[2], pack.shape[1]
    joined = w_joined.shape[1]
    pieces = 3
    dma, bf16, f32 = pltpu.SemaphoreType.DMA, jnp.bfloat16, jnp.float32

    def vmem(shape, dtype=bf16):
        return pltpu.VMEM(shape, dtype)

    any_spec, vmem_spec = pl.BlockSpec(memory_space=pl.ANY), pl.BlockSpec(memory_space=pltpu.VMEM)
    cut = (pieces, quarter, columns // pieces)
    one, two, three, four = dma, dma((2,)), dma((3,)), dma((4,))
    return pl.pallas_call(
        tail_kernel,
        in_specs=[vmem_spec] * 5 + [any_spec] * 6,
        out_specs=[any_spec] * 3 + [vmem_spec],
        out_shape=[
            jax.ShapeDtypeStruct((2, 2, rows, width), bf16),
            jax.ShapeDtypeStruct((quarter, columns), bf16),
            jax.ShapeDtypeStruct((2, quarter, joined), bf16),
            jax.ShapeDtypeStruct(sums.shape, f32),
        ],
        scratch_shapes=[
            vmem(sequence.shape), vmem(grad_one.shape, f32), vmem((4, quarter, columns)),
            vmem((8, rows, joined)), vmem((4, rows, width), f32),
            vmem((4, rows, width)), vmem((4, rows, width)), vmem((2, rows, width)), vmem((2, rows, width)),
            vmem((2, rows, width)),
            vmem(cut), vmem(cut), vmem(cut), vmem(cut), vmem(cut),
            vmem((width, joined)), vmem((3, quarter, joined)), vmem((quarter, joined)), vmem((quarter, joined)),
            vmem((quarter, joined)),
            vmem((5,) + sums.shape, f32), vmem((4,) + sums.shape, f32),
            dma((6,)), four, four, two, two, two, two, two, two, one,
            three, three, three, three, three, three, three,
            three, three, one, one, one, one, one, four, four,
        ],
        compiler_params=pltpu.CompilerParams(
            collective_id=2, has_side_effects=True, vmem_limit_bytes=60 << 20
        ),
        cost_estimate=pl.CostEstimate(flops=80 << 30, bytes_accessed=32 << 20, transcendentals=0),
        name="tail",
    )(d_query, d_key, d_value, w_joined, sums, sequence, grad_one, pack, *moved)


def pick(pair, index):
    return lax.dynamic_index_in_dim(pair, index, 0, keepdims=False)


def per_device_paired(
    tokens,
    doc_lengths,
    keep,
    w_query,
    b_query,
    w_key,
    w_value,
    b_value,
    w_out,
    b_out,
    gain_one,
    shift_one,
    w_up,
    w_down,
    b_down,
    gain_two,
    shift_two,
    cotangent,
):
    _, block_rows, model_width = tokens.shape
    length = 4 * block_rows
    half_rows = block_rows // 2
    local_heads = b_query.shape[0] // HEAD
    heads = local_heads // 2
    width = heads * HEAD
    place = lax.axis_index("fsdp")
    stage = lax.axis_index("ctx")
    core = lax.axis_index("tp")
    seq, half = stage // 2, stage % 2

    def core_half(array):
        return lax.dynamic_slice_in_dim(array, core * half_rows, half_rows, 1)

    def own_columns(array):
        return lax.dynamic_slice_in_dim(array, half * width, width, array.ndim - 1)

    w_joined = jnp.concatenate([own_columns(w_query), own_columns(w_key), own_columns(w_value)], -1)
    sequence, keep_all, full_joined, full_out, full_down = start(tokens, keep, w_joined, w_out, w_down)
    sequence = sequence.reshape(length, model_width)
    full_joined = full_joined.reshape(model_width, 3 * width)
    full_out = full_out.reshape(model_width, 2 * width)
    full_down = full_down.reshape(model_width, -1)
    keep_row = lax.dynamic_index_in_dim(keep_all, seq, 1, keepdims=False).reshape(length)

    bounds = jnp.cumsum(pick(doc_lengths, seq))
    docs = bounds.shape[0]
    positions = jnp.arange(length, dtype=jnp.int32)
    segments = jnp.sum((bounds[None, :] <= positions[:, None]).astype(jnp.int32), -1)
    starts = jnp.concatenate([jnp.zeros((1,), jnp.int32), bounds[:-1]])
    firsts = segments[:: TILE]
    lasts = segments[TILE - 1 :: TILE]
    doc_index = jnp.arange(docs, dtype=jnp.int32)
    span_from = jnp.sum(jnp.where(firsts[:, None] == doc_index, starts, 0), -1) // TILE
    span_to = (jnp.sum(jnp.where(lasts[:, None] == doc_index, bounds, 0), -1) + TILE - 1) // TILE
    spans = jnp.stack([span_from, span_to]).astype(jnp.int32)
    slopes = head_slopes(core * local_heads + half * heads, heads)
    feature = jnp.arange(LANES, dtype=jnp.int32)
    key_doc = jnp.where(segments[:, None] == feature - DOC_ROW, 0.0, MASKED)
    pos_high = (positions // 256 * 256).astype(jnp.float32)[:, None]
    pos_low = (positions % 256).astype(jnp.float32)[:, None]
    key_feat = jnp.where(feature < DOC_ROW, 0.0, 1.0)[None, :]
    key_feat = jnp.where((feature >= DOC_ROW) & (feature < DOC_ROW + docs), key_doc, key_feat)
    key_feat = jnp.where(feature == KEEP_ROW, jnp.where(keep_row == 1, 0.0, MASKED)[:, None], key_feat)
    key_feat = jnp.where((feature >= POS_ROW) & (feature < POS_ROW + 3), pos_high, key_feat)
    key_feat = jnp.where((feature >= POS_ROW + 3) & (feature < LINE_ROW), pos_low, key_feat)
    key_feat = jnp.where(feature >= FEAT_END, 0.0, key_feat).astype(jnp.bfloat16)
    rows = feature[None, :, None]
    query_feat = jnp.where(segments[None, None, :] == rows - DOC_ROW, 1.0, 0.0)
    query_feat = jnp.where(rows == KEEP_ROW, 1.0, query_feat)
    slope_terms = three_terms(slopes[:, None, None], narrow)
    line_terms = three_terms(
        -slopes[:, None, None] * positions.astype(jnp.float32)[None, None, :], narrow
    )
    for term in range(3):
        here = (rows == POS_ROW + term) | (rows == POS_ROW + 3 + term)
        query_feat = jnp.where(here, slope_terms[term], query_feat)
        query_feat = jnp.where(rows == LINE_ROW + term, line_terms[term], query_feat)
    query_feat = query_feat.astype(jnp.bfloat16)

    up_own, full_joined = lax.optimization_barrier((w_up.reshape(w_up.shape[0], -1), full_joined))
    up_shards = [up_own] + [lax.ppermute(up_own, "fsdp", swap) for swap in (X_SWAP, Y_SWAP, D_SWAP)]

    bias = jnp.concatenate([own_columns(b_query), jnp.zeros((width,), jnp.float32), own_columns(b_value)])
    pad = -3 * width % LANES
    query_t, queries, keys, keys_t, values, values_t = project(
        sequence,
        jnp.pad(full_joined, ((0, 0), (0, pad))),
        jnp.pad(bias, (0, pad))[None],
        key_feat,
        query_feat,
        heads,
    )
    attended_all, attended_t, lse = attend(spans, slopes, query_t, keys, values_t)

    row_count = length // 2
    vectors = jnp.stack([b_out, gain_one, shift_one, b_down, gain_two, shift_two, b_out, b_out])
    out, grad_one, grad_heads, pack, sums = middle(
        attended_all.reshape(8, half_rows, width),
        sequence.reshape(8, half_rows, model_width),
        cotangent.reshape(2, 2, half_rows, model_width),
        full_out,
        full_down,
        up_shards,
        vectors,
    )
    out = out.reshape(2, block_rows, model_width)
    grad_heads = grad_heads.reshape(length, width)
    moved = [
        lax.ppermute(pack[other], "fsdp", swap)
        for other, swap in ((1, X_SWAP), (2, Y_SWAP), (3, D_SWAP))
    ]
    d_query, d_key, d_value = attend_back(
        spans, slopes, query_t, queries, keys, keys_t, values, grad_heads, attended_t, lse
    )
    d_tokens, shard, joined, sums = tail(
        d_query.reshape(8, half_rows, width),
        d_key.reshape(8, half_rows, width),
        d_value.reshape(8, half_rows, width),
        full_joined,
        sums,
        sequence.reshape(8, half_rows, model_width),
        grad_one,
        pack,
        moved,
    )
    d_tokens = d_tokens.reshape(2, block_rows, model_width).astype(jnp.float32)
    shard = shard.astype(jnp.float32)
    sum_out, sum_down, sum_up = jnp.split(shard, (2 * width, 2 * width + w_down.shape[1]), 1)
    sum_up = sum_up.reshape(w_up.shape)
    joined = joined.astype(jnp.float32)

    def both_halves(first):
        return jnp.concatenate(
            [joined[0, :, first : first + width], joined[1, :, first : first + width]], -1
        )

    total_gain_two, total_shift_two, total_b_down, total_gain_one, total_shift_one, total_b_out = sums[:6]
    total_bias = sums[6].reshape(2, 2 * width)
    return (
        out,
        d_tokens,
        both_halves(0),
        total_bias[0],
        both_halves(width),
        both_halves(2 * width),
        total_bias[1],
        sum_out,
        total_b_out,
        total_gain_one,
        total_shift_one,
        sum_up,
        sum_down,
        total_b_down,
        total_gain_two,
        total_shift_two,
    )


def paired(mesh, tokens, doc_lengths, b_query):
    sizes = dict(mesh.shape)
    return (
        sizes == {"fsdp": 4, "ctx": 4, "tp": 2}
        and tokens.shape[0] == 8
        and tokens.shape[1] % (8 * TILE) == 0
        and doc_lengths.shape[1] <= KEEP_ROW - DOC_ROW
        and b_query.shape[0] % (4 * HEAD) == 0
    )


def solution(mesh):
    in_specs = (
        P("fsdp", "ctx", None),
        P("fsdp", None),
        P("fsdp", "ctx"),
        P("fsdp", "tp"),
        P("tp"),
        P("fsdp", "tp"),
        P("fsdp", "tp"),
        P("tp"),
        P("fsdp", "tp"),
        P(),
        P(),
        P(),
        P("fsdp", None, "tp"),
        P("fsdp", "tp"),
        P(),
        P(),
        P(),
        P("fsdp", "ctx", None),
    )
    out_specs = (
        P("fsdp", "ctx", None),
        P("fsdp", "ctx", None),
        P("fsdp", "tp"),
        P("tp"),
        P("fsdp", "tp"),
        P("fsdp", "tp"),
        P("tp"),
        P("fsdp", "tp"),
        P(),
        P(),
        P(),
        P("fsdp", None, "tp"),
        P("fsdp", "tp"),
        P(),
        P(),
        P(),
    )

    def whole(*args):
        body = per_device_paired if paired(mesh, args[0], args[1], args[4]) else per_device_general
        return jax.shard_map(
            body, mesh=mesh, in_specs=in_specs, out_specs=out_specs, check_vma=False
        )(*args)

    return whole
```

```python
import functools

import jax
import jax.numpy as jnp
from jax import lax
from jax.experimental import pallas as pl
from jax.experimental.pallas import tpu as pltpu
from jax.sharding import PartitionSpec as P

HEAD = 64


NORM_EPS = 1e-12
MASKED = -1e30


def layer_norm(residual, norm_gain, norm_shift):
    centered = residual - jnp.mean(residual, -1, keepdims=True)
    inv_scale = lax.rsqrt(jnp.mean(centered * centered, -1, keepdims=True) + NORM_EPS)
    normed = centered * inv_scale
    return (normed * norm_gain + norm_shift, normed, inv_scale)


def norm_back(grad_out, normed, inv_scale, norm_gain):
    grad_norm = grad_out * norm_gain
    mean_grad = jnp.mean(grad_norm, -1, keepdims=True)
    mean_cross = jnp.mean(grad_norm * normed, -1, keepdims=True)
    grad_in = (grad_norm - mean_grad - normed * mean_cross) * inv_scale
    return (grad_in, jnp.sum(grad_out * normed, 0), jnp.sum(grad_out, 0))


def head_slopes(first_head, head_count):
    head_index = first_head + jnp.arange(head_count, dtype=jnp.int32)
    head_float = head_index.astype(jnp.float32)
    return jnp.where(head_index < 8, jnp.exp2(-(head_float + 1.0)), jnp.exp2(-(head_float - 7.5)))


def segment_ids(lengths, positions):
    bounds = jnp.cumsum(lengths, -1)
    return jnp.sum((bounds[:, None, :] <= positions[None, :, None]).astype(jnp.int32), -1)


def score_block(query_heads, query_pos, query_seg, key_heads, key_pos, key_seg, key_keep, slopes):
    scores = (
        jnp.einsum("sqhd,skhd->shqk", query_heads, key_heads, preferred_element_type=jnp.float32)
        * 0.125
    )
    distance = jnp.abs(query_pos[:, None] - key_pos[None, :]).astype(jnp.float32)
    scores = scores - slopes[None, :, None, None] * distance[None, None]
    same_doc = query_seg[:, None, :, None] == key_seg[:, None, None, :]
    visible = (key_keep[:, None, None, :] == 1) | (query_pos[:, None] == key_pos[None, :])[
        None, None
    ]
    return (scores, same_doc & visible)


def grad_block(
    query_heads,
    query_pos,
    query_seg,
    grad_heads,
    log_total,
    delta,
    key_heads,
    value_heads,
    key_pos,
    key_seg,
    key_keep,
    slopes,
):
    scores, allowed = score_block(
        query_heads, query_pos, query_seg, key_heads, key_pos, key_seg, key_keep, slopes
    )
    probs = jnp.where(allowed, jnp.exp(scores - log_total[..., None]), 0.0)
    grad_probs = jnp.einsum(
        "sqhd,skhd->shqk", grad_heads, value_heads, preferred_element_type=jnp.float32
    )
    grad_scores = (probs * (grad_probs - delta[..., None])).astype(jnp.bfloat16)
    grad_query = (
        jnp.einsum("shqk,skhd->sqhd", grad_scores, key_heads, preferred_element_type=jnp.float32)
        * 0.125
    )
    grad_key = (
        jnp.einsum("shqk,sqhd->skhd", grad_scores, query_heads, preferred_element_type=jnp.float32)
        * 0.125
    )
    grad_value = jnp.einsum(
        "shqk,sqhd->skhd",
        probs.astype(jnp.bfloat16),
        grad_heads,
        preferred_element_type=jnp.float32,
    )
    return (grad_query, grad_key, grad_value)


def intersections(query_seg, key_seg):
    return jnp.any((key_seg[:, 0] <= query_seg[:, -1]) & (key_seg[:, -1] >= query_seg[:, 0]))


def guarded(active, update, current):
    return lax.cond(active, update, lambda untouched: untouched, current)


def over_blocks(length, advance, current):
    block_len = 512
    block_count = length // block_len
    return lax.fori_loop(
        0,
        block_count,
        lambda block_index, running: advance(running, block_index * block_len, block_len),
        current,
    )


def per_device_general(
    tokens,
    doc_lengths,
    keep,
    w_query,
    b_query,
    w_key,
    w_value,
    b_value,
    w_out,
    b_out,
    gain_one,
    shift_one,
    w_up,
    w_down,
    b_down,
    gain_two,
    shift_two,
    cotangent,
):
    seq_count, block_rows, model_width = tokens.shape
    local_heads = b_query.shape[0] // HEAD
    head_width = local_heads * HEAD
    row_count = seq_count * block_rows
    slopes = head_slopes(lax.axis_index("tp") * local_heads, local_heads)
    own_pos = lax.axis_index("ctx") * block_rows + jnp.arange(block_rows, dtype=jnp.int32)
    own_seg = segment_ids(doc_lengths, own_pos)
    token_rows = tokens.reshape(row_count, model_width)
    full_query, full_key, full_value, full_out = (
        lax.all_gather(w_query, "fsdp", axis=0, tiled=True),
        lax.all_gather(w_key, "fsdp", axis=0, tiled=True),
        lax.all_gather(w_value, "fsdp", axis=0, tiled=True),
        lax.all_gather(w_out, "fsdp", axis=0, tiled=True),
    )
    queries = (
        jnp.dot(token_rows, full_query, preferred_element_type=jnp.float32) + b_query
    ).astype(jnp.bfloat16)
    key_rows = jnp.dot(token_rows, full_key, preferred_element_type=jnp.float32).astype(
        jnp.bfloat16
    )
    values = (jnp.dot(token_rows, full_value, preferred_element_type=jnp.float32) + b_value).astype(
        jnp.bfloat16
    )
    query_heads = queries.reshape(seq_count, block_rows, local_heads, HEAD)
    key_value = jnp.concatenate([key_rows, values], -1).reshape(
        seq_count, block_rows, 2 * head_width
    )

    def split_pairs(slab_pairs, block_len):
        return (
            slab_pairs[..., :head_width].reshape(seq_count, block_len, local_heads, HEAD),
            slab_pairs[..., head_width:].reshape(seq_count, block_len, local_heads, HEAD),
        )

    def key_slab(pairs, piece_keep, offset, block_len):
        slab_pairs = lax.dynamic_slice_in_dim(pairs, offset, block_len, 1)
        slab_keep = lax.dynamic_slice_in_dim(piece_keep, offset, block_len, 1)
        key_pos = offset + jnp.arange(block_len, dtype=jnp.int32)
        key_seg = segment_ids(doc_lengths, key_pos)
        slab_keys, slab_values = split_pairs(slab_pairs, block_len)
        return (slab_keys, slab_values, slab_keep, key_pos, key_seg)

    start_state = (
        jnp.full((seq_count, local_heads, block_rows), MASKED, jnp.float32),
        jnp.zeros((seq_count, local_heads, block_rows), jnp.float32),
        jnp.zeros((seq_count, local_heads, block_rows, HEAD), jnp.float32),
    )
    pairs = lax.all_gather(key_value, "ctx", axis=1, tiled=True)
    piece_keep = lax.all_gather(keep, "ctx", axis=1, tiled=True)

    def advance(partial_value, offset, block_len):
        slab_keys, slab_values, slab_keep, key_pos, key_seg = key_slab(
            pairs, piece_keep, offset, block_len
        )

        def update(current):
            row_max, row_sum, weighted = current
            scores, allowed = score_block(
                query_heads, own_pos, own_seg, slab_keys, key_pos, key_seg, slab_keep, slopes
            )
            scores = jnp.where(allowed, scores, MASKED)
            new_max = jnp.maximum(row_max, jnp.max(scores, -1))
            factor = jnp.exp(row_max - new_max)
            weights = jnp.where(allowed, jnp.exp(scores - new_max[..., None]), 0.0)
            row_sum = row_sum * factor + jnp.sum(weights, -1)
            weighted = weighted * factor[..., None] + jnp.einsum(
                "shqk,skhd->shqd",
                weights.astype(jnp.bfloat16),
                slab_values,
                preferred_element_type=jnp.float32,
            )
            return (new_max, row_sum, weighted)

        return guarded(intersections(own_seg, key_seg), update, partial_value)

    row_max, row_sum, weighted = over_blocks(pairs.shape[1], advance, start_state)
    attended = (
        (weighted / row_sum[..., None])
        .transpose(0, 2, 1, 3)
        .reshape(row_count, head_width)
        .astype(jnp.bfloat16)
    )
    log_total = row_max + jnp.log(row_sum)
    att_part = jnp.einsum("rh,dh->rd", attended, full_out, preferred_element_type=jnp.float32)
    branch_att = lax.psum(att_part.astype(jnp.bfloat16), "tp").astype(jnp.float32) + b_out
    first_out, normed_one, inv_one = layer_norm(
        token_rows.astype(jnp.float32) + branch_att, gain_one, shift_one
    )
    first_low = first_out.astype(jnp.bfloat16)
    full_up, full_down = (
        lax.all_gather(w_up, "fsdp", axis=0, tiled=True),
        lax.all_gather(w_down, "fsdp", axis=0, tiled=True),
    )
    gate_up = jnp.einsum("rd,dcf->rcf", first_low, full_up, preferred_element_type=jnp.float32)
    product, gelu_back = jax.vjp(
        lambda gate_part, up_part: jax.nn.gelu(gate_part, approximate=False) * up_part,
        gate_up[:, 0],
        gate_up[:, 1],
    )
    hidden = product.astype(jnp.bfloat16)
    ffn_part = jnp.einsum("rf,df->rd", hidden, full_down, preferred_element_type=jnp.float32)
    branch_ffn = lax.psum(ffn_part.astype(jnp.bfloat16), "tp").astype(jnp.float32) + b_down
    result, normed_two, inv_two = layer_norm(first_out + branch_ffn, gain_two, shift_two)
    grad_in = cotangent.reshape(row_count, model_width).astype(jnp.float32)
    grad_two, d_gain_two, d_shift_two = norm_back(grad_in, normed_two, inv_two, gain_two)
    grad_ffn = grad_two.astype(jnp.bfloat16)
    d_b_down = jnp.sum(grad_ffn.astype(jnp.float32), 0)
    d_w_down = jnp.einsum("rd,rf->df", grad_ffn, hidden, preferred_element_type=jnp.float32)
    grad_hidden = jnp.einsum("rd,df->rf", grad_ffn, full_down, preferred_element_type=jnp.float32)
    grad_gate, grad_up = gelu_back(grad_hidden)
    grad_gate_up = jnp.stack([grad_gate, grad_up], 1).astype(jnp.bfloat16)
    d_w_up = jnp.einsum("rd,rcf->dcf", first_low, grad_gate_up, preferred_element_type=jnp.float32)
    first_part = jnp.einsum(
        "rcf,dcf->rd", grad_gate_up, full_up, preferred_element_type=jnp.float32
    )
    grad_first = grad_two + lax.psum(first_part.astype(jnp.bfloat16), "tp").astype(jnp.float32)
    grad_one, d_gain_one, d_shift_one = norm_back(grad_first, normed_one, inv_one, gain_one)
    grad_att = grad_one.astype(jnp.bfloat16)
    d_b_out = jnp.sum(grad_att.astype(jnp.float32), 0)
    d_w_out = jnp.einsum("rd,rh->dh", grad_att, attended, preferred_element_type=jnp.float32)
    grad_attended = jnp.einsum(
        "rd,dh->rh", grad_att, full_out, preferred_element_type=jnp.float32
    ).astype(jnp.bfloat16)
    grad_heads = grad_attended.reshape(seq_count, block_rows, local_heads, HEAD)
    delta = jnp.einsum(
        "sqhd,sqhd->shq",
        grad_heads,
        attended.reshape(seq_count, block_rows, local_heads, HEAD),
        preferred_element_type=jnp.float32,
    )
    query_zero = jnp.zeros((seq_count, block_rows, local_heads, HEAD), jnp.float32)
    full_len = block_rows * lax.axis_size("ctx")
    term_zero = jnp.zeros((seq_count, full_len, 2 * head_width), jnp.float32)
    return_pairs = lax.all_gather(key_value, "ctx", axis=1, tiled=True)
    return_piece_keep = lax.all_gather(keep, "ctx", axis=1, tiled=True)

    def advance(partial_value, offset, block_len):
        slab_keys, slab_values, slab_keep, key_pos, key_seg = key_slab(
            return_pairs, return_piece_keep, offset, block_len
        )

        def update(current):
            query_grad, key_terms = current
            part_query, part_key, part_value = grad_block(
                query_heads,
                own_pos,
                own_seg,
                grad_heads,
                log_total,
                delta,
                slab_keys,
                slab_values,
                key_pos,
                key_seg,
                slab_keep,
                slopes,
            )
            slab_grads = jnp.concatenate(
                [
                    part_key.reshape(seq_count, block_len, head_width),
                    part_value.reshape(seq_count, block_len, head_width),
                ],
                -1,
            )
            return (
                query_grad + part_query,
                lax.dynamic_update_slice_in_dim(key_terms, slab_grads, offset, 1),
            )

        return guarded(intersections(own_seg, key_seg), update, partial_value)

    query_grad, key_terms = over_blocks(return_pairs.shape[1], advance, (query_zero, term_zero))
    pair_grads = lax.psum_scatter(
        key_terms.astype(jnp.bfloat16), "ctx", scatter_dimension=1, tiled=True
    ).astype(jnp.float32)
    query_low = query_grad.reshape(row_count, head_width).astype(jnp.bfloat16)
    pair_low = pair_grads.reshape(row_count, 2 * head_width).astype(jnp.bfloat16)
    grad_project = jnp.concatenate([query_low, pair_low], -1)
    joined_weights = jnp.concatenate([full_query, full_key, full_value], -1)
    joined_grads = jnp.einsum(
        "rd,rh->dh", token_rows, grad_project, preferred_element_type=jnp.float32
    )
    input_part = jnp.einsum(
        "rh,dh->rd", grad_project, joined_weights, preferred_element_type=jnp.float32
    )
    d_tokens = grad_one + lax.psum(input_part.astype(jnp.bfloat16), "tp").astype(jnp.float32)
    d_b_query = jnp.sum(query_low.astype(jnp.float32), 0)
    d_b_value = jnp.sum(pair_low[:, head_width:].astype(jnp.float32), 0)
    d_w_query = joined_grads[:, :head_width]
    d_w_key = joined_grads[:, head_width : 2 * head_width]
    d_w_value = joined_grads[:, 2 * head_width :]
    shard_grads = (
        lax.psum_scatter(
            d_w_query.astype(jnp.bfloat16), "fsdp", scatter_dimension=0, tiled=True
        ).astype(jnp.float32),
        lax.psum_scatter(
            d_w_key.astype(jnp.bfloat16), "fsdp", scatter_dimension=0, tiled=True
        ).astype(jnp.float32),
        lax.psum_scatter(
            d_w_value.astype(jnp.bfloat16), "fsdp", scatter_dimension=0, tiled=True
        ).astype(jnp.float32),
        lax.psum_scatter(
            d_w_out.astype(jnp.bfloat16), "fsdp", scatter_dimension=0, tiled=True
        ).astype(jnp.float32),
        lax.psum_scatter(
            d_w_up.astype(jnp.bfloat16), "fsdp", scatter_dimension=0, tiled=True
        ).astype(jnp.float32),
        lax.psum_scatter(
            d_w_down.astype(jnp.bfloat16), "fsdp", scatter_dimension=0, tiled=True
        ).astype(jnp.float32),
    )
    sum_query, sum_key, sum_value, sum_out, sum_up, sum_down = (
        lax.psum(shard_grads[0].astype(jnp.bfloat16), "ctx").astype(jnp.float32),
        lax.psum(shard_grads[1].astype(jnp.bfloat16), "ctx").astype(jnp.float32),
        lax.psum(shard_grads[2].astype(jnp.bfloat16), "ctx").astype(jnp.float32),
        lax.psum(shard_grads[3].astype(jnp.bfloat16), "ctx").astype(jnp.float32),
        lax.psum(shard_grads[4].astype(jnp.bfloat16), "ctx").astype(jnp.float32),
        lax.psum(shard_grads[5].astype(jnp.bfloat16), "ctx").astype(jnp.float32),
    )
    (
        total_b_query,
        total_b_value,
        total_b_out,
        total_b_down,
        total_gain_one,
        total_shift_one,
        total_gain_two,
        total_shift_two,
    ) = lax.psum(
        (d_b_query, d_b_value, d_b_out, d_b_down, d_gain_one, d_shift_one, d_gain_two, d_shift_two),
        ("fsdp", "ctx"),
    )
    return (
        result.reshape(seq_count, block_rows, model_width).astype(jnp.bfloat16),
        d_tokens.reshape(seq_count, block_rows, model_width),
        sum_query,
        total_b_query,
        sum_key,
        sum_value,
        total_b_value,
        sum_out,
        total_b_out,
        total_gain_one,
        total_shift_one,
        sum_up,
        sum_down,
        total_b_down,
        total_gain_two,
        total_shift_two,
    )


LANES = 128
MESH = pl.DeviceIdType.MESH
TILE = 256
DOC_ROW, KEEP_ROW, POS_ROW, LINE_ROW, LOG_ROW, FEAT_END = 64, 72, 73, 79, 82, 85
X_SWAP = [(0, 1), (1, 0), (2, 3), (3, 2)]
Y_SWAP = [(0, 2), (2, 0), (1, 3), (3, 1)]
D_SWAP = [(0, 3), (3, 0), (1, 2), (2, 1)]


def dot(left, right, dims=((1,), (0,))):
    return lax.dot_general(left, right, (dims, ((), ())), preferred_element_type=jnp.float32)


def three_terms(value, low):
    high = low(value)
    middle = low(value - high)
    return high, middle, low(value - high - middle)


def narrow(value):
    return lax.reduce_precision(value, 8, 7)


def project_kernel(x_ref, w_ref, bias_ref, key_feat_ref, query_feat_ref, qt_ref, q_ref, k_ref, kt_ref, v_ref, vt_ref):
    heads = q_ref.shape[0]
    rows = x_ref.shape[0]
    y = dot(x_ref[...], w_ref[...]) + bias_ref[...]
    y = y.astype(jnp.bfloat16).astype(jnp.float32)
    lane = lax.broadcasted_iota(jnp.int32, (rows, LANES), 1)
    sub = lax.broadcasted_iota(jnp.int32, (LANES, rows), 0)

    def head_part(index):
        pair = y[:, index // 2 * LANES : (index // 2 + 1) * LANES]
        if index % 2:
            pair = pltpu.roll(pair, HEAD, 1)
        return jnp.where(lane < HEAD, pair, 0.0)

    for head in range(heads):
        query = head_part(head) * 0.125
        q_ref[head] = query[:, :HEAD].astype(jnp.bfloat16)
        qt_ref[head] = (query.T + query_feat_ref[head].astype(jnp.float32)).astype(jnp.bfloat16)
        key = head_part(heads + head)
        k_ref[head] = (key + key_feat_ref[...].astype(jnp.float32)).astype(jnp.bfloat16)
        kt_ref[head] = key.T[:HEAD].astype(jnp.bfloat16)
        value = head_part(2 * heads + head)
        ones = (lane >= HEAD) & (lane < HEAD + 3)
        v_ref[head] = jnp.where(ones, 1.0, value).astype(jnp.bfloat16)
        vt_ref[head] = jnp.where(sub == HEAD, 1.0, value.T)[:80].astype(jnp.bfloat16)


def project(x, weight, bias, key_feat, query_feat, heads):
    length, width = x.shape
    rows = 2 * TILE
    return pl.pallas_call(
        project_kernel,
        grid=(length // rows,),
        in_specs=[
            pl.BlockSpec((rows, width), lambda i: (i, 0)),
            pl.BlockSpec(weight.shape, lambda i: (0, 0)),
            pl.BlockSpec(bias.shape, lambda i: (0, 0)),
            pl.BlockSpec((rows, LANES), lambda i: (i, 0)),
            pl.BlockSpec((heads, LANES, rows), lambda i: (0, 0, i)),
        ],
        out_specs=[
            pl.BlockSpec((heads, LANES, rows), lambda i: (0, 0, i)),
            pl.BlockSpec((heads, rows, HEAD), lambda i: (0, i, 0)),
            pl.BlockSpec((heads, rows, LANES), lambda i: (0, i, 0)),
            pl.BlockSpec((heads, HEAD, rows), lambda i: (0, 0, i)),
            pl.BlockSpec((heads, rows, LANES), lambda i: (0, i, 0)),
            pl.BlockSpec((heads, 80, rows), lambda i: (0, 0, i)),
        ],
        out_shape=[
            jax.ShapeDtypeStruct((heads, LANES, length), jnp.bfloat16),
            jax.ShapeDtypeStruct((heads, length, HEAD), jnp.bfloat16),
            jax.ShapeDtypeStruct((heads, length, LANES), jnp.bfloat16),
            jax.ShapeDtypeStruct((heads, HEAD, length), jnp.bfloat16),
            jax.ShapeDtypeStruct((heads, length, LANES), jnp.bfloat16),
            jax.ShapeDtypeStruct((heads, 80, length), jnp.bfloat16),
        ],
        compiler_params=pltpu.CompilerParams(vmem_limit_bytes=40 << 20),
        cost_estimate=pl.CostEstimate(
            flops=2 * length * width * weight.shape[1], bytes_accessed=12 << 20, transcendentals=0
        ),
        name="project",
    )(x, weight, bias, key_feat, query_feat)


def side_signs(rows):
    sub = lax.broadcasted_iota(jnp.int32, (LANES, rows), 0)
    bias_rows = (sub >= POS_ROW) & (sub < LOG_ROW)
    after = jnp.where(bias_rows, -1.0, 1.0).astype(jnp.bfloat16)
    same = jnp.where(bias_rows, 0.0, 1.0).astype(jnp.bfloat16)
    bare = jnp.where(bias_rows | (sub == KEEP_ROW), 0.0, 1.0).astype(jnp.bfloat16)
    return after, same, bare


def diagonal_scores(keys, query_t, same, bare, slope):
    rows = lax.broadcasted_iota(jnp.int32, (TILE, TILE), 0)
    cols = lax.broadcasted_iota(jnp.int32, (TILE, TILE), 1)
    apart = jnp.abs(rows - cols)
    full = dot(keys, query_t * same) - slope * apart.astype(jnp.float32)
    return jnp.where(apart == 0, dot(keys, query_t * bare), full)


def sweep(first, last, step, most=2):
    many = (last - first) // most

    @pl.loop(0, many)
    def _(i):
        step(first + i * most, most)

    @pl.loop(first + many * most, last)
    def _(tile):
        step(tile, 1)


def attend_kernel(span_ref, slope_ref, qt_ref, k_ref, vt_ref, o_ref, ot_ref, lse_ref, max_ref, acc_ref):
    heads = qt_ref.shape[0]
    block = pl.program_id(0)
    after, same, bare = side_signs(TILE)

    def tile_rows(tile, count=1):
        return pl.ds(pl.multiple_of(tile * TILE, TILE), count * TILE)

    own = tile_rows(block)
    for head in range(heads):
        scores = diagonal_scores(k_ref[head, own, :], qt_ref[head], same, bare, slope_ref[head])
        top = jnp.max(scores, 0, keepdims=True)
        weights = jnp.exp(scores - top).astype(jnp.bfloat16)
        max_ref[head] = top
        acc_ref[head] = dot(vt_ref[head, :, own], weights)

    def step(tile, count, sign):
        each = range(heads)
        keys = [k_ref[head, tile_rows(tile, count), :] for head in each]
        values = [vt_ref[head, :, tile_rows(tile, count)] for head in each]
        queries = [qt_ref[head] if sign is None else qt_ref[head] * sign for head in each]
        old = [max_ref[head] for head in each]
        acc = [acc_ref[head] for head in each]
        scores = [dot(keys[head], queries[head]) for head in each]
        top = [jnp.maximum(old[head], jnp.max(scores[head], 0, keepdims=True)) for head in each]
        weights = [jnp.exp(scores[head] - top[head]).astype(jnp.bfloat16) for head in each]
        parts = [dot(values[head], weights[head]) for head in each]
        for head in each:
            max_ref[head] = top[head]
            acc_ref[head] = acc[head] * jnp.exp(old[head] - top[head]) + parts[head]

    sweep(span_ref[0, block], block, lambda tile, count: step(tile, count, None))
    sweep(block + 1, span_ref[1, block], lambda tile, count: step(tile, count, after))

    parts = []
    for head in range(heads):
        total = acc_ref[head, HEAD : HEAD + 1, :]
        out_t = acc_ref[head, :HEAD, :] / total
        ot_ref[head] = out_t
        parts.append(out_t)
        lse_ref[head] = max_ref[head] + jnp.log(total)
    o_ref[...] = jnp.concatenate(parts, 0).T.astype(jnp.bfloat16)


def attend(spans, slopes, query_t, keys, value_t):
    heads, _, length = query_t.shape
    blocks = length // TILE
    return pl.pallas_call(
        attend_kernel,
        grid_spec=pltpu.PrefetchScalarGridSpec(
            num_scalar_prefetch=2,
            grid=(blocks,),
            in_specs=[
                pl.BlockSpec((heads, LANES, TILE), lambda i, *_: (0, 0, i)),
                pl.BlockSpec(keys.shape, lambda i, *_: (0, 0, 0)),
                pl.BlockSpec(value_t.shape, lambda i, *_: (0, 0, 0)),
            ],
            out_specs=[
                pl.BlockSpec((TILE, heads * HEAD), lambda i, *_: (i, 0)),
                pl.BlockSpec((heads, HEAD, TILE), lambda i, *_: (0, 0, i)),
                pl.BlockSpec((heads, 1, TILE), lambda i, *_: (0, 0, i)),
            ],
            scratch_shapes=[
                pltpu.VMEM((heads, 1, TILE), jnp.float32),
                pltpu.VMEM((heads, 80, TILE), jnp.float32),
            ],
        ),
        out_shape=[
            jax.ShapeDtypeStruct((length, heads * HEAD), jnp.bfloat16),
            jax.ShapeDtypeStruct((heads, HEAD, length), jnp.float32),
            jax.ShapeDtypeStruct((heads, 1, length), jnp.float32),
        ],
        compiler_params=pltpu.CompilerParams(vmem_limit_bytes=40 << 20),
        cost_estimate=pl.CostEstimate(
            flops=heads * length * length * 256, bytes_accessed=6 << 20, transcendentals=heads * length * length
        ),
        name="attend",
    )(spans, slopes, query_t, keys, value_t)


def attend_back_kernel(
    span_ref, slope_ref, qt_ref, q_ref, k_ref, kt_ref, v_ref, g_ref, ot_ref, lse_ref,
    dq_ref, dk_ref, dv_ref, qt_log, grad_heads, grad_t, query_acc, key_acc, value_acc,
):
    heads = qt_ref.shape[0]
    blocks = pl.num_programs(0)
    block = pl.program_id(0)
    length = qt_ref.shape[2]
    after, same, bare = side_signs(TILE)

    def low(value):
        return value.astype(jnp.bfloat16).astype(jnp.float32)

    def tile_rows(tile, count=1):
        return pl.ds(pl.multiple_of(tile * TILE, TILE), count * TILE)

    @pl.when(block == 0)
    def _():
        query_acc[...] = jnp.zeros_like(query_acc)
        sub = lax.broadcasted_iota(jnp.int32, (LANES, TILE), 0)

        @pl.loop(0, length // TILE)
        def _(tile):
            rows = tile_rows(tile)
            grad = g_ref[rows, :].astype(jnp.float32)
            turned = grad.T
            for head in range(heads):
                own = turned[head * HEAD : (head + 1) * HEAD]
                delta = jnp.sum(own * ot_ref[head, :, rows], 0, keepdims=True)
                first, second, third = three_terms(-delta, low)
                wide = jnp.concatenate([own, jnp.zeros_like(own)], 0)
                wide = jnp.where(sub == HEAD, first, wide)
                wide = jnp.where(sub == HEAD + 1, second, wide)
                wide = jnp.where(sub == HEAD + 2, third, wide)
                grad_t[head, :, rows] = wide.astype(jnp.bfloat16)
                grad_heads[head, rows, :] = own.T.astype(jnp.bfloat16)
                first, second, third = three_terms(-lse_ref[head, :, rows], low)
                query = qt_ref[head, :, rows].astype(jnp.float32)
                query = jnp.where(sub == LOG_ROW, first, query)
                query = jnp.where(sub == LOG_ROW + 1, second, query)
                query = jnp.where(sub == LOG_ROW + 2, third, query)
                qt_log[head, :, rows] = query.astype(jnp.bfloat16)

    def accumulate(tile, scores, first, count=1):
        each = range(heads)
        rows = tile_rows(tile, count)
        values = [v_ref[head] for head in each]
        turned = [grad_t[head, :, rows] for head in each]
        grads = [grad_heads[head, rows, :] for head in each]
        queries = [q_ref[head, rows, :] for head in each]
        keys_t = [kt_ref[head] for head in each]
        probs = [jnp.exp(scores[head]) for head in each]
        grad_probs = [dot(values[head], turned[head]) for head in each]
        grad_scores = [(probs[head] * grad_probs[head]).astype(jnp.bfloat16) for head in each]
        value_part = [dot(probs[head].astype(jnp.bfloat16), grads[head]) for head in each]
        key_part = [dot(grad_scores[head], queries[head]) for head in each]
        query_part = [dot(keys_t[head], grad_scores[head]) for head in each]
        for head in each:
            if first:
                value_acc[head] = value_part[head]
                key_acc[head] = key_part[head]
            else:
                value_acc[head] += value_part[head]
                key_acc[head] += key_part[head]
            query_acc[head, :, rows] += query_part[head]

    own = [qt_log[head, :, tile_rows(block)] for head in range(heads)]
    accumulate(
        block,
        [
            diagonal_scores(k_ref[head], own[head], same, bare, slope_ref[head])
            for head in range(heads)
        ],
        True,
    )
    after_wide = side_signs(2 * TILE)[0]

    def step(tile, count, sign):
        queries = [qt_log[head, :, tile_rows(tile, count)] for head in range(heads)]
        if sign is not None:
            queries = [query * sign[:, : count * TILE] for query in queries]
        accumulate(tile, [dot(k_ref[head], queries[head]) for head in range(heads)], False, count)

    sweep(span_ref[0, block], block, lambda tile, count: step(tile, count, after_wide))
    sweep(block + 1, span_ref[1, block], lambda tile, count: step(tile, count, None))

    dk_ref[...] = jnp.concatenate([key_acc[head] for head in range(heads)], 1).astype(jnp.bfloat16)
    dv_ref[...] = jnp.concatenate([value_acc[head] for head in range(heads)], 1).astype(jnp.bfloat16)

    @pl.when(block == blocks - 1)
    def _():
        @pl.loop(0, length // TILE)
        def _(tile):
            rows = tile_rows(tile)
            turned = jnp.concatenate([query_acc[head, :, rows] for head in range(heads)], 0)
            dq_ref[rows, :] = (turned.T * 0.125).astype(jnp.bfloat16)


def attend_back(spans, slopes, query_t, queries, keys, keys_t, values, grads, out_t, lse):
    heads, _, length = query_t.shape
    blocks = length // TILE
    width = heads * HEAD

    def whole(array):
        return pl.BlockSpec(array.shape, lambda i, *_: (0,) * array.ndim)

    return pl.pallas_call(
        attend_back_kernel,
        grid_spec=pltpu.PrefetchScalarGridSpec(
            num_scalar_prefetch=2,
            grid=(blocks,),
            in_specs=[
                whole(query_t),
                whole(queries),
                pl.BlockSpec((heads, TILE, LANES), lambda i, *_: (0, i, 0)),
                pl.BlockSpec((heads, HEAD, TILE), lambda i, *_: (0, 0, i)),
                pl.BlockSpec((heads, TILE, LANES), lambda i, *_: (0, i, 0)),
                whole(grads),
                whole(out_t),
                whole(lse),
            ],
            out_specs=[
                pl.BlockSpec((length, width), lambda i, *_: (0, 0)),
                pl.BlockSpec((TILE, width), lambda i, *_: (i, 0)),
                pl.BlockSpec((TILE, width), lambda i, *_: (i, 0)),
            ],
            scratch_shapes=[
                pltpu.VMEM((heads, LANES, length), jnp.bfloat16),
                pltpu.VMEM((heads, length, HEAD), jnp.bfloat16),
                pltpu.VMEM((heads, LANES, length), jnp.bfloat16),
                pltpu.VMEM((heads, HEAD, length), jnp.float32),
                pltpu.VMEM((heads, TILE, HEAD), jnp.float32),
                pltpu.VMEM((heads, TILE, HEAD), jnp.float32),
            ],
        ),
        out_shape=[jax.ShapeDtypeStruct((length, width), jnp.bfloat16)] * 3,
        compiler_params=pltpu.CompilerParams(vmem_limit_bytes=50 << 20),
        cost_estimate=pl.CostEstimate(
            flops=heads * length * length * 640, bytes_accessed=12 << 20, transcendentals=heads * length * length
        ),
        name="attend_back",
    )(spans, slopes, query_t, queries, keys, keys_t, values, grads, out_t, lse)


def start_kernel(
    tokens, keep, w_joined, w_out, w_down, sequence, keep_all, full_joined, full_out, full_down,
    z_send, z_recv, tp_send, tp_recv, w_send, w_recv, keep_send, keep_recv, local_sem,
):
    place, stage, core = lax.axis_index("fsdp"), lax.axis_index("ctx"), lax.axis_index("tp")
    seq = stage // 2
    half_rows = sequence.shape[2]
    barrier = pltpu.get_barrier_semaphore()
    peers = [(place ^ other, stage, core) for other in (1, 2, 3)]
    peers += [(place, lax.rem(stage + shift, 4), core) for shift in (1, 2, 3)]
    peers += [(place, stage, 1 - core)]
    for peer in peers:
        pl.semaphore_signal(barrier, inc=1, device_id=peer, device_id_type=MESH)
    pl.semaphore_wait(barrier, len(peers))

    rows = pl.ds(pl.multiple_of(core * half_rows, half_rows), half_rows)
    ours, theirs = tokens.at[seq, rows], tokens.at[1 - seq, rows]

    def send(source, block, target, slot):
        return pltpu.make_async_remote_copy(
            source, sequence.at[block, core], z_send.at[slot], z_recv.at[block],
            device_id=(place, target, core), device_id_type=MESH,
        )

    def arrival(block):
        return pltpu.make_async_remote_copy(
            ours, sequence.at[block, core], z_send.at[0], z_recv.at[block],
            device_id=(place, stage, 1 - core), device_id_type=MESH,
        )

    def share(block):
        return pltpu.make_async_remote_copy(
            sequence.at[block, core], sequence.at[block, core], tp_send.at[block], tp_recv.at[block],
            device_id=(place, stage, 1 - core), device_id_type=MESH,
        )

    def shared(block):
        return pltpu.make_async_remote_copy(
            sequence.at[block, 1 - core], sequence.at[block, 1 - core], tp_send.at[block], tp_recv.at[block],
            device_id=(place, stage, 1 - core), device_id_type=MESH,
        )

    first = send(ours, stage, stage ^ 1, 0)
    ends = ((0, 2, 3), (3, 1, 0))
    mids = ((1, 2, 0), (2, 1, 3))
    for own, near, _ in mids:

        @pl.when(stage == own)
        def _():
            send(theirs, own, near, 1).start()

    first.start()
    for own, near, far in ends:

        @pl.when(stage == own)
        def _():
            send(theirs, own, far, 1).start()
            send(theirs, own, near, 2).start()

    weights = []
    for index, (shard, full) in enumerate(
        ((w_joined, full_joined), (w_out, full_out), (w_down, full_down))
    ):
        for other in (1, 2, 3):
            sem = 3 * index + other - 1
            weights.append(
                pltpu.make_async_remote_copy(
                    shard, full.at[place], w_send.at[sem], w_recv.at[sem],
                    device_id=(place ^ other, stage, core), device_id_type=MESH,
                )
            )
            weights[-1].start()
    flags = []
    for shift in (1, 2, 3):
        flags.append(
            pltpu.make_async_remote_copy(
                keep, keep_all.at[stage], keep_send.at[shift - 1], keep_recv.at[shift - 1],
                device_id=(place, lax.rem(stage + shift, 4), core), device_id_type=MESH,
            )
        )
        flags[-1].start()
    local = []
    for index, (source, target) in enumerate(
        (
            (tokens.at[seq, pl.ds(0, half_rows)], sequence.at[stage, 0]),
            (tokens.at[seq, pl.ds(half_rows, half_rows)], sequence.at[stage, 1]),
            (keep, keep_all.at[stage]),
            (w_joined, full_joined.at[place]),
            (w_out, full_out.at[place]),
            (w_down, full_down.at[place]),
        )
    ):
        local.append(pltpu.make_async_copy(source, target, local_sem.at[index]))
        local[-1].start()

    for own, near, end in mids:
        far = 3 - end

        @pl.when(stage == own)
        def _():
            arrival(near).wait_recv()
            send(sequence.at[near, core], near, end, 2).start()
            share(near).start()
            arrival(end).wait_recv()
            share(end).start()
            arrival(far).wait_recv()
            share(far).start()
            send(theirs, own, near, 1).wait_send()
            send(sequence.at[near, core], near, end, 2).wait_send()
            for block in (near, end, far):
                share(block).wait_send()
                shared(block).wait_recv()

    for own, near, far in ends:

        @pl.when(stage == own)
        def _():
            inner = 3 - near
            for block in (inner, far, near):
                arrival(block).wait_recv()
                share(block).start()
            send(theirs, own, near, 1).wait_send()
            send(theirs, own, near, 2).wait_send()
            for block in (inner, far, near):
                share(block).wait_send()
                shared(block).wait_recv()

    first.wait_send()
    for copy in weights + flags:
        copy.wait()
    for copy in local:
        copy.wait()


def start(tokens, keep, w_joined, w_out, w_down):
    _, block_rows, width = tokens.shape
    dma = pltpu.SemaphoreType.DMA
    return pl.pallas_call(
        start_kernel,
        in_specs=[pl.BlockSpec(memory_space=pl.ANY)] * 5,
        out_specs=[pl.BlockSpec(memory_space=pl.ANY)] * 5,
        out_shape=[
            jax.ShapeDtypeStruct((4, 2, block_rows // 2, width), tokens.dtype),
            jax.ShapeDtypeStruct((4,) + keep.shape, keep.dtype),
            jax.ShapeDtypeStruct((4,) + w_joined.shape, w_joined.dtype),
            jax.ShapeDtypeStruct((4,) + w_out.shape, w_out.dtype),
            jax.ShapeDtypeStruct((4,) + w_down.shape, w_down.dtype),
        ],
        scratch_shapes=[
            dma((3,)), dma((4,)), dma((4,)), dma((4,)), dma((9,)), dma((9,)), dma((3,)), dma((3,)), dma((6,)),
        ],
        compiler_params=pltpu.CompilerParams(collective_id=0, has_side_effects=True),
        cost_estimate=pl.CostEstimate(flops=40 << 30, bytes_accessed=16 << 20, transcendentals=0),
        name="start",
    )(tokens, keep, w_joined, w_out, w_down)


def rows_norm(residual):
    centered = residual - jnp.mean(residual, -1, keepdims=True)
    inv_scale = lax.rsqrt(jnp.mean(centered * centered, -1, keepdims=True) + NORM_EPS)
    return centered * inv_scale, inv_scale


def rows_norm_back(grad_out, normed, inv_scale, norm_gain):
    grad_norm = grad_out * norm_gain
    mean_grad = jnp.mean(grad_norm, -1, keepdims=True)
    mean_cross = jnp.mean(grad_norm * normed, -1, keepdims=True)
    return (grad_norm - mean_grad - normed * mean_cross) * inv_scale


def middle_kernel(
    attended, sequence, cotangent, w_out, w_down, up_0, up_1, up_2, up_3, vectors,
    out_home, grad_one, grad_heads, early, late, down_sum, sums,
    token_v, mine_v, theirs_v, both_v, cot_v, out_w, down_w, up_w,
    send_a, recv_a, send_b, recv_b, send_c, recv_c,
    normed_v, inv_v, low_v, hidden_v, gate_v, lift_v, grad_v, ffn_v, att_v, result_v, keep_v, away_v, tile_v,
    down_v, down_got, load_sem, pair_send, pair_recv, cot_send, cot_recv, cot_pass, cot_took,
    a_send, a_recv, b_send, b_recv, c_send, c_recv, out_send, out_recv, out_pass, out_took,
    one_sem, keep_sem, away_send, away_recv, tile_sem, down_send, down_recv, down_sem,
):
    place, stage, core = lax.axis_index("fsdp"), lax.axis_index("ctx"), lax.axis_index("tp")
    seq, half = stage // 2, stage % 2
    pair = stage ^ 1
    chunks = token_v.shape[0]
    units = hidden_v.shape[2]
    wide = 512
    quarter = up_0.shape[0]

    barrier = pltpu.get_barrier_semaphore()
    peers = [(place ^ other, stage, core) for other in (1, 2, 3)]
    peers += [(place, lax.rem(stage + shift, 4), core) for shift in (1, 2, 3)]
    peers += [(place, stage, 1 - core)]
    for peer in peers:
        pl.semaphore_signal(barrier, inc=1, device_id=peer, device_id_type=MESH)
    pl.semaphore_wait(barrier, len(peers))

    def remote(source, target, send, recv, device):
        return pltpu.make_async_remote_copy(
            source, target, send, recv, device_id=device, device_id_type=MESH
        )

    partner = (place, pair, core)
    other_core = (place, stage, 1 - core)

    def pair_copy(c):
        return remote(
            attended.at[(1 - half) * chunks + c], theirs_v.at[c], pair_send.at[c], pair_recv.at[c], partner
        )

    for c in range(chunks):
        pair_copy(c).start()

    def cot_owner(which):
        return 2 * which + stage // 2

    def cot_copy(which):
        return remote(
            cotangent.at[which, core], cot_v.at[stage % 2, core],
            cot_send.at[which], cot_recv.at[stage % 2], (place, cot_owner(which), core),
        )

    def cot_local(which):
        return pltpu.make_async_copy(cotangent.at[which], cot_v.at[stage % 2], cot_send.at[which])

    for which in (0, 1):

        @pl.when(cot_owner(which) == stage)
        def _():
            cot_local(which).start()

        @pl.when(cot_owner(which) != stage)
        def _():
            cot_copy(which).start()

    def cot_arrival(block):
        return remote(
            cot_v.at[block, core], cot_v.at[block, core], cot_pass.at[block], cot_recv.at[block], other_core
        )

    def cot_share(block, whose):
        return remote(
            cot_v.at[block, whose], cot_v.at[block, whose], cot_pass.at[block], cot_took.at[block], other_core
        )

    loads = [
        pltpu.make_async_copy(attended.at[pl.ds(half * chunks, chunks)], mine_v, load_sem.at[0]),
        pltpu.make_async_copy(w_out, out_w, load_sem.at[1]),
        pltpu.make_async_copy(sequence.at[pl.ds(half * chunks, chunks)], token_v, load_sem.at[2]),
        pltpu.make_async_copy(w_down, down_w, load_sem.at[3]),
    ]
    for other, shard in enumerate((up_0, up_1, up_2, up_3)):
        rows = pl.ds(pl.multiple_of((place ^ other) * quarter, quarter), quarter)
        loads.append(pltpu.make_async_copy(shard, up_w.at[rows], load_sem.at[4 + other]))
    for load in loads:
        load.start()

    def vector(index):
        return vectors[index : index + 1, :]

    b_out, gain_one, shift_one, b_down, gain_two, shift_two = (vector(i) for i in range(6))
    sums[...] = jnp.zeros_like(sums)

    def add_sum(index, rows):
        sums[index : index + 1, :] += jnp.sum(rows, 0, keepdims=True)

    def exchange(c, sent, got, send, recv):
        return remote(sent.at[c], got.at[c], send.at[c], recv.at[c], other_core)

    def total(c, sent, got):
        return sent[c].astype(jnp.float32) + got[c].astype(jnp.float32)

    loads[0].wait()
    loads[1].wait()

    @pl.loop(0, chunks)
    def _(c):
        pair_copy(c).wait_recv()
        first, second = mine_v[c], theirs_v[c]
        both = jnp.where(
            half == 0, jnp.concatenate([first, second], 1), jnp.concatenate([second, first], 1)
        )
        both_v[c] = both
        send_a[c] = dot(both, out_w[...], ((1,), (1,))).astype(jnp.bfloat16)
        exchange(c, send_a, recv_a, a_send, a_recv).start()

    for load in loads[2:]:
        load.wait()

    @pl.loop(0, chunks)
    def _(c):
        exchange(c, send_a, recv_a, a_send, a_recv).wait_recv()

        @pl.when(c == chunks - 1)
        def _():
            for block in (0, 1):

                @pl.when(2 * half + block != stage)
                def _():
                    cot_arrival(block).wait_recv()
                    cot_share(block, core).start()

        residual = token_v[c].astype(jnp.float32) + (total(c, send_a, recv_a) + b_out)
        normed, inv_scale = rows_norm(residual)
        normed_v[c] = normed
        inv_v[c] = inv_scale
        low_v[c] = (normed * gain_one + shift_one).astype(jnp.bfloat16)
        for n in range(0, units, wide):
            gate = dot(low_v[c], up_w[:, n : n + wide])
            lift = dot(low_v[c], up_w[:, units + n : units + n + wide])
            chance = 0.5 + 0.5 * lax.erf(gate * 0.7071067811865476)
            density = jnp.exp(gate * gate * -0.5) * 0.3989422804014327
            gelu = gate * chance
            hidden_v[c, :, n : n + wide] = (gelu * lift).astype(jnp.bfloat16)
            gate_v[c, :, n : n + wide] = (lift * (chance + gate * density)).astype(jnp.bfloat16)
            lift_v[c, :, n : n + wide] = gelu.astype(jnp.bfloat16)
        send_b[c] = dot(hidden_v[c], down_w[...], ((1,), (1,))).astype(jnp.bfloat16)
        exchange(c, send_b, recv_b, b_send, b_recv).start()

    for block in (0, 1):

        @pl.when(2 * half + block != stage)
        def _():
            cot_share(block, core).wait_send()
            cot_share(block, 1 - core).wait_recv()

    for which in (0, 1):

        @pl.when(cot_owner(which) == stage)
        def _():
            cot_local(which).wait()

        @pl.when(cot_owner(which) != stage)
        def _():
            cot_copy(which).wait_send()

    def home(c):
        return 2 * half + c // 2

    def out_copy(c):
        return remote(
            result_v.at[c], out_home.at[seq, core], out_send.at[c], out_recv.at[seq], (place, home(c), core)
        )

    def out_local(c):
        return pltpu.make_async_copy(result_v.at[c], out_home.at[seq, c % 2], out_send.at[c])

    @pl.loop(0, chunks)
    def _(c):
        exchange(c, send_b, recv_b, b_send, b_recv).wait_recv()
        normed_one = normed_v[c]
        residual = normed_one * gain_one + shift_one + (total(c, send_b, recv_b) + b_down)
        normed, inv_scale = rows_norm(residual)
        result_v[c] = (normed * gain_two + shift_two).astype(jnp.bfloat16)

        @pl.when(home(c) == stage)
        def _():
            out_local(c).start()

        @pl.when((home(c) != stage) & (c % 2 == core))
        def _():
            out_copy(c).start()

        grad_in = cot_v[c // 2, c % 2].astype(jnp.float32)
        add_sum(0, grad_in * normed)
        add_sum(1, grad_in)
        grad_two = rows_norm_back(grad_in, normed, inv_scale, gain_two)
        grad_v[c] = grad_two
        grad_ffn = grad_two.astype(jnp.bfloat16)
        ffn_v[c] = grad_ffn
        add_sum(2, grad_ffn.astype(jnp.float32))
        for n in range(0, units, wide):
            grad_hidden = dot(ffn_v[c], down_w[:, n : n + wide])
            gate_v[c, :, n : n + wide] = (grad_hidden * gate_v[c, :, n : n + wide]).astype(jnp.bfloat16)
            lift_v[c, :, n : n + wide] = (grad_hidden * lift_v[c, :, n : n + wide]).astype(jnp.bfloat16)
        send_c[c] = (
            dot(gate_v[c], up_w[:, :units], ((1,), (1,))) + dot(lift_v[c], up_w[:, units:], ((1,), (1,)))
        ).astype(jnp.bfloat16)
        exchange(c, send_c, recv_c, c_send, c_recv).start()

    tile = tile_v.shape[2]

    def columns(index):
        return pl.ds(pl.multiple_of(index * tile, tile), tile)

    def weight_part(left, right):
        rows = left.shape[0] * left.shape[1]
        return dot(
            left[...].reshape(rows, left.shape[2]), right.reshape(rows, tile), ((0,), (0,))
        ).astype(jnp.bfloat16)

    unit_tiles = units // tile

    def down_copy(i, other):
        rows = pl.ds(pl.multiple_of((place ^ other) * quarter, quarter), quarter)
        return remote(
            down_v.at[rows, columns(i)], down_got.at[other - 1, :, columns(i)],
            down_send.at[i, other - 1], down_recv.at[i, other - 1], (place ^ other, stage, core),
        )

    @pl.loop(0, unit_tiles)
    def _(i):
        down_v[:, columns(i)] = weight_part(ffn_v, hidden_v[:, :, columns(i)])
        for other in (1, 2, 3):
            down_copy(i, other).start()

    def one_copy(c):
        return pltpu.make_async_copy(grad_v.at[c], grad_one.at[c], one_sem.at[c])

    def keep_copy(c):
        return pltpu.make_async_copy(keep_v.at[c], grad_heads.at[half * chunks + c], keep_sem.at[c])

    def away_copy(c, whose):
        return remote(
            away_v.at[c], grad_heads.at[whose * chunks + c], away_send.at[c], away_recv.at[c], partner
        )

    @pl.loop(0, chunks)
    def _(c):
        exchange(c, send_c, recv_c, c_send, c_recv).wait_recv()
        grad_first = grad_v[c] + total(c, send_c, recv_c)
        normed = normed_v[c]
        add_sum(3, grad_first * normed)
        add_sum(4, grad_first)
        grad_res = rows_norm_back(grad_first, normed, inv_v[c], gain_one)
        grad_v[c] = grad_res
        one_copy(c).start()
        grad_att = grad_res.astype(jnp.bfloat16)
        att_v[c] = grad_att
        add_sum(5, grad_att.astype(jnp.float32))
        heads = dot(att_v[c], out_w[...]).astype(jnp.bfloat16)
        first, second = heads[:, : heads.shape[1] // 2], heads[:, heads.shape[1] // 2 :]
        keep_v[c] = jnp.where(half == 0, first, second)
        away_v[c] = jnp.where(half == 0, second, first)
        away_copy(c, half).start()
        keep_copy(c).start()

    early_tiles = early.shape[2] // tile

    def tile_copy(slot, row, index):
        target, column = index
        return pltpu.make_async_copy(
            tile_v.at[slot, pl.ds(row * quarter, quarter)],
            target.at[place ^ row, :, columns(column)],
            tile_sem.at[slot, row],
        )

    def weight_tile(count, target, column, left, right):
        slot = lax.rem(count, 2)

        @pl.when(count >= 2)
        def _():
            for row in range(4):
                tile_copy(slot, row, (target, column)).wait()

        tile_v[slot] = weight_part(left, right)
        for row in range(4):
            tile_copy(slot, row, (target, column)).start()

    @pl.loop(0, unit_tiles)
    def _(i):
        weight_tile(i, early, i, low_v, gate_v[:, :, columns(i)])

    @pl.loop(unit_tiles, early_tiles)
    def _(i):
        weight_tile(i, early, i, low_v, lift_v[:, :, columns(i - unit_tiles)])

    late_units = 2 * unit_tiles - early_tiles

    @pl.loop(0, late_units)
    def _(i):
        weight_tile(early_tiles + i, late, i, low_v, lift_v[:, :, columns(early_tiles - unit_tiles + i)])

    weight_tile(2 * unit_tiles, late, late_units, att_v, both_v[...])
    for slot in (0, 1):
        for row in range(4):
            tile_copy(slot, row, (late, 0)).wait()

    for i in range(unit_tiles):
        for other in (1, 2, 3):
            down_copy(i, other).wait_recv()
    own_rows = pl.ds(pl.multiple_of(place * quarter, quarter), quarter)
    down_got[0] = (
        down_v[own_rows, :].astype(jnp.float32)
        + down_got[0].astype(jnp.float32)
        + (down_got[1].astype(jnp.float32) + down_got[2].astype(jnp.float32))
    ).astype(jnp.bfloat16)
    down_out = pltpu.make_async_copy(down_got.at[0], down_sum, down_sem)
    down_out.start()

    def out_arrival(which):
        return remote(
            out_home.at[which, core], out_home.at[which, core], out_pass.at[which], out_recv.at[which], other_core
        )

    def out_share(which, whose):
        return remote(
            out_home.at[which, whose], out_home.at[which, whose], out_pass.at[which], out_took.at[which], other_core
        )

    for which in (0, 1):

        @pl.when(cot_owner(which) != stage)
        def _():
            out_arrival(which).wait_recv()
            out_share(which, core).start()

    down_out.wait()
    for i in range(unit_tiles):
        for other in (1, 2, 3):
            down_copy(i, other).wait_send()

    @pl.loop(0, chunks)
    def _(c):
        pair_copy(c).wait_send()
        exchange(c, send_a, recv_a, a_send, a_recv).wait_send()
        exchange(c, send_b, recv_b, b_send, b_recv).wait_send()
        exchange(c, send_c, recv_c, c_send, c_recv).wait_send()
        one_copy(c).wait()
        keep_copy(c).wait()
        away_copy(c, half).wait_send()
        away_copy(c, 1 - half).wait_recv()

        @pl.when(home(c) == stage)
        def _():
            out_local(c).wait()

        @pl.when((home(c) != stage) & (c % 2 == core))
        def _():
            out_copy(c).wait_send()

    for which in (0, 1):

        @pl.when(cot_owner(which) != stage)
        def _():
            out_share(which, core).wait_send()
            out_share(which, 1 - core).wait_recv()


def middle(attended, sequence, cotangent, w_out, w_down, up_shards, vectors):
    chunks, rows, width = 4, sequence.shape[1], sequence.shape[2]
    head_width, units = w_out.shape[1], w_down.shape[1]
    tile = head_width
    early, late = 6 * tile, 2 * units + head_width - 6 * tile
    dma, bf16, f32 = pltpu.SemaphoreType.DMA, jnp.bfloat16, jnp.float32

    def vmem(shape, dtype=bf16):
        return pltpu.VMEM(shape, dtype)

    wide = (chunks, rows, width)
    inner = (chunks, rows, units)
    narrow_rows = (chunks, rows, head_width // 2)
    four, two = dma((chunks,)), dma((2,))
    return pl.pallas_call(
        middle_kernel,
        in_specs=[pl.BlockSpec(memory_space=pl.ANY)] * 9 + [pl.BlockSpec(memory_space=pltpu.VMEM)],
        out_specs=[pl.BlockSpec(memory_space=pl.ANY)] * 6 + [pl.BlockSpec(memory_space=pltpu.VMEM)],
        out_shape=[
            jax.ShapeDtypeStruct((2, 2, rows, width), bf16),
            jax.ShapeDtypeStruct(wide, f32),
            jax.ShapeDtypeStruct((2 * chunks, rows, head_width // 2), bf16),
            jax.ShapeDtypeStruct((4, width // 4, early), bf16),
            jax.ShapeDtypeStruct((4, width // 4, late), bf16),
            jax.ShapeDtypeStruct((width // 4, units), bf16),
            jax.ShapeDtypeStruct((8, width), f32),
        ],
        scratch_shapes=[
            vmem(wide), vmem(narrow_rows), vmem(narrow_rows), vmem((chunks, rows, head_width)),
            vmem((2, 2, rows, width)), vmem((width, head_width)), vmem((width, units)), vmem((width, 2 * units)),
            vmem(wide), vmem(wide), vmem(wide), vmem(wide), vmem(wide), vmem(wide),
            vmem(wide, f32), vmem((chunks, rows, 1), f32), vmem(wide),
            vmem(inner), vmem(inner), vmem(inner),
            vmem(wide, f32), vmem(wide), vmem(wide), vmem(wide), vmem(narrow_rows), vmem(narrow_rows),
            vmem((2, width, tile)), vmem((width, units)), vmem((3, width // 4, units)),
            dma((8,)), four, four, two, two, two, two,
            four, four, four, four, four, four, four, two, two, two,
            four, four, four, four, dma((2, 4)), dma((units // tile, 3)), dma((units // tile, 3)), dma,
        ],
        compiler_params=pltpu.CompilerParams(
            collective_id=1, has_side_effects=True, vmem_limit_bytes=60 << 20
        ),
        cost_estimate=pl.CostEstimate(flops=50 << 30, bytes_accessed=32 << 20, transcendentals=0),
        name="middle",
    )(attended, sequence, cotangent, w_out, w_down, *up_shards, vectors)


def tail_kernel(
    d_query, d_key, d_value, w_joined, sums_in, sequence, grad_one, early, late, moved_1, moved_2, moved_3,
    home, shard, joined, sums,
    token_v, one_v, part_v, late_v, project_v, own_v, tp_sent, tp_got, pair_sent, pair_got, final_v,
    summed_v, end_got, inner_v, mid_got, total_v, joined_v, quarter_got, cross_sent, cross_got, full_v,
    step_v, step_got,
    load_sem, late_send, late_recv, tp_send, tp_recv, pair_send, pair_recv, home_send, home_recv, home_pass, home_took, home_local,
    end_send, end_recv, mid_send, mid_recv, back_send, back_recv, shard_sem,
    quarter_send, quarter_recv, cross_send, cross_recv, half_send, half_recv, half_local, step_send, step_recv,
):
    place, stage, core = lax.axis_index("fsdp"), lax.axis_index("ctx"), lax.axis_index("tp")
    seq, half = stage // 2, stage % 2
    bf16, f32 = jnp.bfloat16, jnp.float32
    pieces = summed_v.shape[0]
    piece = summed_v.shape[2]
    quarter = joined_v.shape[0] // 4
    width = d_query.shape[2]

    barrier = pltpu.get_barrier_semaphore()
    peers = [(place ^ other, stage, core) for other in (1, 2, 3)]
    peers += [(place, lax.rem(stage + shift, 4), core) for shift in (1, 2, 3)]
    peers += [(place, stage, 1 - core)]
    for peer in peers:
        pl.semaphore_signal(barrier, inc=1, device_id=peer, device_id_type=MESH)
    pl.semaphore_wait(barrier, len(peers))

    def remote(source, target, send, recv, device):
        return pltpu.make_async_remote_copy(
            source, target, send, recv, device_id=device, device_id_type=MESH
        )

    other_core = (place, stage, 1 - core)
    partner = (place, stage ^ 1, core)
    at_end = (stage == 0) | (stage == 3)
    across = (place, jnp.where(at_end, stage, 3 - stage), core)
    inward = (place, jnp.where(stage < 2, 1, 2), core)
    outward = (place, jnp.where(stage < 2, 0, 3), core)

    loads = [
        pltpu.make_async_copy(source, part_v.at[index], load_sem.at[index])
        for index, source in enumerate((early.at[0], moved_1, moved_2, moved_3))
    ]
    loads.append(pltpu.make_async_copy(sequence, token_v, load_sem.at[4]))
    loads.append(pltpu.make_async_copy(grad_one, one_v, load_sem.at[5]))
    loads.append(pltpu.make_async_copy(late.at[0], late_v.at[0], load_sem.at[6]))

    def late_copy(other):
        return remote(
            late.at[other], late_v.at[other], late_send.at[other - 1], late_recv.at[other - 1],
            (place ^ other, stage, core),
        )

    for other in (1, 2, 3):
        late_copy(other).start()
    for load in loads:
        load.start()

    def input_share(chunk):
        rows = jnp.concatenate([d_query[chunk], d_key[chunk], d_value[chunk]], 1)
        project_v[chunk] = rows
        return dot(rows, w_joined[...], ((1,), (1,)))

    def block_of(i):
        return jnp.where(i < 2, 2 * (1 - half) + i, 2 * half + i - 2)

    def tp_copy(i):
        return remote(tp_sent.at[i], tp_got.at[i], tp_send.at[i], tp_recv.at[i], other_core)

    @pl.loop(0, 4)
    def _(i):
        block = block_of(i)
        tp_sent[i] = input_share(2 * block + 1 - core).astype(bf16)
        tp_copy(i).start()
        own_v[i] = input_share(2 * block + core)

    def pair_copy(i):
        return remote(pair_sent.at[i], pair_got.at[i], pair_send.at[i], pair_recv.at[i], partner)

    @pl.loop(0, 2)
    def _(i):
        tp_copy(i).wait_recv()
        pair_sent[i] = (own_v[i] + tp_got[i].astype(f32)).astype(bf16)
        pair_copy(i).start()

    def end_copy(j):
        return remote(summed_v.at[j], end_got.at[j], end_send.at[j], end_recv.at[j], inward)

    def mid_copy(j):
        return remote(inner_v.at[j], mid_got.at[j], mid_send.at[j], mid_recv.at[j], across)

    def columns(j):
        return pl.ds(j * piece, piece)

    def back_copy(j):
        return remote(total_v.at[j], shard.at[:, columns(j)], back_send.at[j], back_recv.at[j], outward)

    def shard_copy(j):
        return pltpu.make_async_copy(total_v.at[j], shard.at[:, columns(j)], shard_sem.at[j])

    def sum_piece(j, parts, first):
        terms = [parts[index, :, first : first + piece].astype(f32) for index in range(4)]
        summed_v[j] = (terms[0] + terms[1] + (terms[2] + terms[3])).astype(bf16)

        @pl.when(at_end)
        def _():
            end_copy(j).start()

    for load in loads[:4]:
        load.wait()
    for j in range(pieces - 1):
        sum_piece(j, part_v, j * piece)

    loads[4].wait()
    tokens = token_v[...].reshape(-1, token_v.shape[2])
    project = project_v[...].reshape(-1, project_v.shape[2])
    strip = 256
    for row in range(0, joined_v.shape[0], strip):
        joined_v[row : row + strip, :] = dot(
            tokens[:, row : row + strip], project, ((0,), (0,))
        ).astype(bf16)

    def quarter_copy(other):
        rows = pl.ds(pl.multiple_of((place ^ other) * quarter, quarter), quarter)
        return remote(
            joined_v.at[rows], quarter_got.at[other - 1], quarter_send.at[other - 1], quarter_recv.at[other - 1],
            (place ^ other, stage, core),
        )

    for other in (1, 2, 3):
        quarter_copy(other).start()

    def column_sum(grads):
        return jnp.sum(grads[...].reshape(-1, width).astype(f32), 0, keepdims=True)

    bias_parts = []
    for total in (column_sum(d_query), column_sum(d_value)):
        for which in (0, 1):
            bias_parts.append(jnp.where(half == which, total, 0.0))
    bias = jnp.concatenate(bias_parts, 1)
    step_v[0] = sums_in[...]
    step_v[0, 6:7, :] = bias
    steps = [(place ^ 1, stage, core), (place ^ 2, stage, core), partner, (place, stage ^ 2, core)]

    def step_copy(index):
        return remote(
            step_v.at[index], step_got.at[index], step_send.at[index], step_recv.at[index], steps[index]
        )

    def step_on(index):
        step_copy(index).wait_recv()
        step_v[index + 1] = step_v[index] + step_got[index]
        if index < 3:
            step_copy(index + 1).start()

    step_copy(0).start()
    loads[6].wait()
    for other in (1, 2, 3):
        late_copy(other).wait_recv()
    sum_piece(pieces - 1, late_v, 0)

    loads[5].wait()

    def home_copy(i):
        return remote(
            final_v.at[i], home.at[seq, core], home_send.at[i], home_recv.at[seq], (place, 2 * half + i, core)
        )

    def home_direct(i):
        return remote(final_v.at[i], home.at[seq, core], home_send.at[i], home_took.at[seq], other_core)

    def home_here(i):
        return pltpu.make_async_copy(final_v.at[i], home.at[seq, core], home_local)

    for i in range(2):
        tp_copy(i + 2).wait_recv()
        pair_copy(i).wait_recv()
        final_v[i] = (
            own_v[i + 2] + tp_got[i + 2].astype(f32) + pair_got[i].astype(f32) + one_v[2 * i + core]
        ).astype(bf16)

        @pl.when(2 * half + i == stage)
        def _():
            home_direct(i).start()
            home_here(i).start()

        @pl.when(2 * half + i != stage)
        def _():
            home_copy(i).start()

    step_on(0)
    for other in (1, 2, 3):
        quarter_copy(other).wait_recv()
    own_rows = pl.ds(pl.multiple_of(place * quarter, quarter), quarter)
    cross_sent[...] = (
        joined_v[own_rows, :].astype(f32)
        + quarter_got[0].astype(f32)
        + (quarter_got[1].astype(f32) + quarter_got[2].astype(f32))
    ).astype(bf16)
    cross_copy = remote(cross_sent, cross_got, cross_send, cross_recv, (place, stage ^ 2, core))
    cross_copy.start()
    step_on(1)

    def from_end(j):
        end_copy(j).wait_recv()
        inner_v[j] = (summed_v[j].astype(f32) + end_got[j].astype(f32)).astype(bf16)
        mid_copy(j).start()

    def from_mid(j):
        mid_copy(j).wait_recv()
        total_v[j] = (inner_v[j].astype(f32) + mid_got[j].astype(f32)).astype(bf16)
        back_copy(j).start()
        shard_copy(j).start()

    @pl.when(~at_end)
    def _():
        from_end(0)
        for j in range(1, pieces):
            from_end(j)
            from_mid(j - 1)

    step_on(2)
    cross_copy.wait_recv()
    full_v[...] = (cross_sent[...].astype(f32) + cross_got[...].astype(f32)).astype(bf16)
    half_copy = remote(full_v, joined.at[half], half_send, half_recv, partner)
    half_copy.start()
    half_here = pltpu.make_async_copy(full_v, joined.at[half], half_local)
    half_here.start()
    step_on(3)
    sums[...] = step_v[4]

    def home_arrival(which):
        return remote(
            home.at[which, core], home.at[which, core], home_pass.at[which], home_recv.at[which], other_core
        )

    def home_share(which, whose):
        return remote(
            home.at[which, whose], home.at[which, whose], home_pass.at[which], home_took.at[which], other_core
        )

    for which in (0, 1):

        @pl.when(2 * which + stage // 2 != stage)
        def _():
            home_arrival(which).wait_recv()
            home_share(which, core).start()

    @pl.when(~at_end)
    def _():
        from_mid(pieces - 1)
        for j in range(pieces):
            mid_copy(j).wait_send()
            back_copy(j).wait_send()
            shard_copy(j).wait()

    @pl.when(at_end)
    def _():
        for j in range(pieces):
            end_copy(j).wait_send()
            back_copy(j).wait_recv()

    for i in range(4):
        tp_copy(i).wait_send()
        step_copy(i).wait_send()
    for i in range(2):
        pair_copy(i).wait_send()

        @pl.when(2 * half + i == stage)
        def _():
            home_direct(i).wait_send()
            home_here(i).wait()

        @pl.when(2 * half + i != stage)
        def _():
            home_copy(i).wait_send()

    for which in (0, 1):

        @pl.when(2 * which + stage // 2 != stage)
        def _():
            home_share(which, core).wait_send()

        home_share(which, 1 - core).wait_recv()
    for other in (1, 2, 3):
        quarter_copy(other).wait_send()
        late_copy(other).wait_send()
    cross_copy.wait_send()
    half_here.wait()
    half_copy.wait_send()
    remote(full_v, joined.at[1 - half], half_send, half_recv, partner).wait_recv()


def tail(d_query, d_key, d_value, w_joined, sums, sequence, grad_one, early, late, moved):
    rows, width = sequence.shape[1:]
    quarter, piece = late.shape[1:]
    columns = early.shape[2] + piece
    joined = w_joined.shape[1]
    pieces = columns // piece
    dma, bf16, f32 = pltpu.SemaphoreType.DMA, jnp.bfloat16, jnp.float32

    def vmem(shape, dtype=bf16):
        return pltpu.VMEM(shape, dtype)

    any_spec, vmem_spec = pl.BlockSpec(memory_space=pl.ANY), pl.BlockSpec(memory_space=pltpu.VMEM)
    cut = (pieces, quarter, piece)
    one, two, three, four = dma, dma((2,)), dma((3,)), dma((4,))
    return pl.pallas_call(
        tail_kernel,
        in_specs=[vmem_spec] * 5 + [any_spec] * 7,
        out_specs=[any_spec] * 3 + [vmem_spec],
        out_shape=[
            jax.ShapeDtypeStruct((2, 2, rows, width), bf16),
            jax.ShapeDtypeStruct((quarter, columns), bf16),
            jax.ShapeDtypeStruct((2, quarter, joined), bf16),
            jax.ShapeDtypeStruct(sums.shape, f32),
        ],
        scratch_shapes=[
            vmem(sequence.shape), vmem(grad_one.shape, f32), vmem(early.shape), vmem(late.shape),
            vmem((8, rows, joined)), vmem((4, rows, width), f32),
            vmem((4, rows, width)), vmem((4, rows, width)), vmem((2, rows, width)), vmem((2, rows, width)),
            vmem((2, rows, width)),
            vmem(cut), vmem(cut), vmem(cut), vmem(cut), vmem(cut),
            vmem((width, joined)), vmem((3, quarter, joined)), vmem((quarter, joined)), vmem((quarter, joined)),
            vmem((quarter, joined)),
            vmem((5,) + sums.shape, f32), vmem((4,) + sums.shape, f32),
            dma((7,)), three, three, four, four, two, two, two, two, two, two, one,
            three, three, three, three, three, three, three,
            three, three, one, one, one, one, one, four, four,
        ],
        compiler_params=pltpu.CompilerParams(
            collective_id=2, has_side_effects=True, vmem_limit_bytes=60 << 20
        ),
        cost_estimate=pl.CostEstimate(flops=80 << 30, bytes_accessed=32 << 20, transcendentals=0),
        name="tail",
    )(d_query, d_key, d_value, w_joined, sums, sequence, grad_one, early, late, *moved)


def pick(pair, index):
    return lax.dynamic_index_in_dim(pair, index, 0, keepdims=False)


def per_device_paired(
    tokens,
    doc_lengths,
    keep,
    w_query,
    b_query,
    w_key,
    w_value,
    b_value,
    w_out,
    b_out,
    gain_one,
    shift_one,
    w_up,
    w_down,
    b_down,
    gain_two,
    shift_two,
    cotangent,
):
    _, block_rows, model_width = tokens.shape
    length = 4 * block_rows
    half_rows = block_rows // 2
    local_heads = b_query.shape[0] // HEAD
    heads = local_heads // 2
    width = heads * HEAD
    place = lax.axis_index("fsdp")
    stage = lax.axis_index("ctx")
    core = lax.axis_index("tp")
    seq, half = stage // 2, stage % 2

    def core_half(array):
        return lax.dynamic_slice_in_dim(array, core * half_rows, half_rows, 1)

    def own_columns(array):
        return lax.dynamic_slice_in_dim(array, half * width, width, array.ndim - 1)

    w_joined = jnp.concatenate([own_columns(w_query), own_columns(w_key), own_columns(w_value)], -1)
    sequence, keep_all, full_joined, full_out, full_down = start(tokens, keep, w_joined, w_out, w_down)
    sequence = sequence.reshape(length, model_width)
    full_joined = full_joined.reshape(model_width, 3 * width)
    full_out = full_out.reshape(model_width, 2 * width)
    full_down = full_down.reshape(model_width, -1)
    keep_row = lax.dynamic_index_in_dim(keep_all, seq, 1, keepdims=False).reshape(length)

    bounds = jnp.cumsum(pick(doc_lengths, seq))
    docs = bounds.shape[0]
    positions = jnp.arange(length, dtype=jnp.int32)
    segments = jnp.sum((bounds[None, :] <= positions[:, None]).astype(jnp.int32), -1)
    starts = jnp.concatenate([jnp.zeros((1,), jnp.int32), bounds[:-1]])
    firsts = segments[:: TILE]
    lasts = segments[TILE - 1 :: TILE]
    doc_index = jnp.arange(docs, dtype=jnp.int32)
    span_from = jnp.sum(jnp.where(firsts[:, None] == doc_index, starts, 0), -1) // TILE
    span_to = (jnp.sum(jnp.where(lasts[:, None] == doc_index, bounds, 0), -1) + TILE - 1) // TILE
    spans = jnp.stack([span_from, span_to]).astype(jnp.int32)
    slopes = head_slopes(core * local_heads + half * heads, heads)
    feature = jnp.arange(LANES, dtype=jnp.int32)
    key_doc = jnp.where(segments[:, None] == feature - DOC_ROW, 0.0, MASKED)
    pos_high = (positions // 256 * 256).astype(jnp.float32)[:, None]
    pos_low = (positions % 256).astype(jnp.float32)[:, None]
    key_feat = jnp.where(feature < DOC_ROW, 0.0, 1.0)[None, :]
    key_feat = jnp.where((feature >= DOC_ROW) & (feature < DOC_ROW + docs), key_doc, key_feat)
    key_feat = jnp.where(feature == KEEP_ROW, jnp.where(keep_row == 1, 0.0, MASKED)[:, None], key_feat)
    key_feat = jnp.where((feature >= POS_ROW) & (feature < POS_ROW + 3), pos_high, key_feat)
    key_feat = jnp.where((feature >= POS_ROW + 3) & (feature < LINE_ROW), pos_low, key_feat)
    key_feat = jnp.where(feature >= FEAT_END, 0.0, key_feat).astype(jnp.bfloat16)
    rows = feature[None, :, None]
    query_feat = jnp.where(segments[None, None, :] == rows - DOC_ROW, 1.0, 0.0)
    query_feat = jnp.where(rows == KEEP_ROW, 1.0, query_feat)
    slope_terms = three_terms(slopes[:, None, None], narrow)
    line_terms = three_terms(
        -slopes[:, None, None] * positions.astype(jnp.float32)[None, None, :], narrow
    )
    for term in range(3):
        here = (rows == POS_ROW + term) | (rows == POS_ROW + 3 + term)
        query_feat = jnp.where(here, slope_terms[term], query_feat)
        query_feat = jnp.where(rows == LINE_ROW + term, line_terms[term], query_feat)
    query_feat = query_feat.astype(jnp.bfloat16)

    up_own, full_joined = lax.optimization_barrier((w_up.reshape(w_up.shape[0], -1), full_joined))
    up_shards = [up_own] + [lax.ppermute(up_own, "fsdp", swap) for swap in (X_SWAP, Y_SWAP, D_SWAP)]

    bias = jnp.concatenate([own_columns(b_query), jnp.zeros((width,), jnp.float32), own_columns(b_value)])
    pad = -3 * width % LANES
    query_t, queries, keys, keys_t, values, values_t = project(
        sequence,
        jnp.pad(full_joined, ((0, 0), (0, pad))),
        jnp.pad(bias, (0, pad))[None],
        key_feat,
        query_feat,
        heads,
    )
    attended_all, attended_t, lse = attend(spans, slopes, query_t, keys, values_t)

    row_count = length // 2
    vectors = jnp.stack([b_out, gain_one, shift_one, b_down, gain_two, shift_two, b_out, b_out])
    out, grad_one, grad_heads, early, late, down_sum, sums = middle(
        attended_all.reshape(8, half_rows, width),
        sequence.reshape(8, half_rows, model_width),
        cotangent.reshape(2, 2, half_rows, model_width),
        full_out,
        full_down,
        up_shards,
        vectors,
    )
    out = out.reshape(2, block_rows, model_width)
    grad_heads = grad_heads.reshape(length, width)
    moved = [
        lax.ppermute(early[other], "fsdp", swap)
        for other, swap in ((1, X_SWAP), (2, Y_SWAP), (3, D_SWAP))
    ]
    d_query, d_key, d_value = attend_back(
        spans, slopes, query_t, queries, keys, keys_t, values, grad_heads, attended_t, lse
    )
    d_tokens, shard, joined, sums = tail(
        d_query.reshape(8, half_rows, width),
        d_key.reshape(8, half_rows, width),
        d_value.reshape(8, half_rows, width),
        full_joined,
        sums,
        sequence.reshape(8, half_rows, model_width),
        grad_one,
        early,
        late,
        moved,
    )
    d_tokens = d_tokens.reshape(2, block_rows, model_width).astype(jnp.float32)
    sum_up, sum_out = jnp.split(shard.astype(jnp.float32), (2 * w_up.shape[2],), 1)
    sum_up = sum_up.reshape(w_up.shape)
    sum_down = lax.psum(down_sum, "ctx").astype(jnp.float32)
    joined = joined.astype(jnp.float32)

    def both_halves(first):
        return jnp.concatenate(
            [joined[0, :, first : first + width], joined[1, :, first : first + width]], -1
        )

    total_gain_two, total_shift_two, total_b_down, total_gain_one, total_shift_one, total_b_out = sums[:6]
    total_bias = sums[6].reshape(2, 2 * width)
    return (
        out,
        d_tokens,
        both_halves(0),
        total_bias[0],
        both_halves(width),
        both_halves(2 * width),
        total_bias[1],
        sum_out,
        total_b_out,
        total_gain_one,
        total_shift_one,
        sum_up,
        sum_down,
        total_b_down,
        total_gain_two,
        total_shift_two,
    )


def paired(mesh, tokens, doc_lengths, b_query):
    sizes = dict(mesh.shape)
    return (
        sizes == {"fsdp": 4, "ctx": 4, "tp": 2}
        and tokens.shape[0] == 8
        and tokens.shape[1] % (8 * TILE) == 0
        and doc_lengths.shape[1] <= KEEP_ROW - DOC_ROW
        and b_query.shape[0] % (4 * HEAD) == 0
    )


def solution(mesh):
    in_specs = (
        P("fsdp", "ctx", None),
        P("fsdp", None),
        P("fsdp", "ctx"),
        P("fsdp", "tp"),
        P("tp"),
        P("fsdp", "tp"),
        P("fsdp", "tp"),
        P("tp"),
        P("fsdp", "tp"),
        P(),
        P(),
        P(),
        P("fsdp", None, "tp"),
        P("fsdp", "tp"),
        P(),
        P(),
        P(),
        P("fsdp", "ctx", None),
    )
    out_specs = (
        P("fsdp", "ctx", None),
        P("fsdp", "ctx", None),
        P("fsdp", "tp"),
        P("tp"),
        P("fsdp", "tp"),
        P("fsdp", "tp"),
        P("tp"),
        P("fsdp", "tp"),
        P(),
        P(),
        P(),
        P("fsdp", None, "tp"),
        P("fsdp", "tp"),
        P(),
        P(),
        P(),
    )

    def whole(*args):
        body = per_device_paired if paired(mesh, args[0], args[1], args[4]) else per_device_general
        return jax.shard_map(
            body, mesh=mesh, in_specs=in_specs, out_specs=out_specs, check_vma=False
        )(*args)

    return whole
```

```python
import functools

import jax
import jax.numpy as jnp
from jax import lax
from jax.experimental import pallas as pl
from jax.experimental.pallas import tpu as pltpu
from jax.sharding import PartitionSpec as P

HEAD = 64


NORM_EPS = 1e-12
MASKED = -1e30


def layer_norm(residual, norm_gain, norm_shift):
    centered = residual - jnp.mean(residual, -1, keepdims=True)
    inv_scale = lax.rsqrt(jnp.mean(centered * centered, -1, keepdims=True) + NORM_EPS)
    normed = centered * inv_scale
    return (normed * norm_gain + norm_shift, normed, inv_scale)


def norm_back(grad_out, normed, inv_scale, norm_gain):
    grad_norm = grad_out * norm_gain
    mean_grad = jnp.mean(grad_norm, -1, keepdims=True)
    mean_cross = jnp.mean(grad_norm * normed, -1, keepdims=True)
    grad_in = (grad_norm - mean_grad - normed * mean_cross) * inv_scale
    return (grad_in, jnp.sum(grad_out * normed, 0), jnp.sum(grad_out, 0))


def head_slopes(first_head, head_count):
    head_index = first_head + jnp.arange(head_count, dtype=jnp.int32)
    head_float = head_index.astype(jnp.float32)
    return jnp.where(head_index < 8, jnp.exp2(-(head_float + 1.0)), jnp.exp2(-(head_float - 7.5)))


def segment_ids(lengths, positions):
    bounds = jnp.cumsum(lengths, -1)
    return jnp.sum((bounds[:, None, :] <= positions[None, :, None]).astype(jnp.int32), -1)


def score_block(query_heads, query_pos, query_seg, key_heads, key_pos, key_seg, key_keep, slopes):
    scores = (
        jnp.einsum("sqhd,skhd->shqk", query_heads, key_heads, preferred_element_type=jnp.float32)
        * 0.125
    )
    distance = jnp.abs(query_pos[:, None] - key_pos[None, :]).astype(jnp.float32)
    scores = scores - slopes[None, :, None, None] * distance[None, None]
    same_doc = query_seg[:, None, :, None] == key_seg[:, None, None, :]
    visible = (key_keep[:, None, None, :] == 1) | (query_pos[:, None] == key_pos[None, :])[
        None, None
    ]
    return (scores, same_doc & visible)


def grad_block(
    query_heads,
    query_pos,
    query_seg,
    grad_heads,
    log_total,
    delta,
    key_heads,
    value_heads,
    key_pos,
    key_seg,
    key_keep,
    slopes,
):
    scores, allowed = score_block(
        query_heads, query_pos, query_seg, key_heads, key_pos, key_seg, key_keep, slopes
    )
    probs = jnp.where(allowed, jnp.exp(scores - log_total[..., None]), 0.0)
    grad_probs = jnp.einsum(
        "sqhd,skhd->shqk", grad_heads, value_heads, preferred_element_type=jnp.float32
    )
    grad_scores = (probs * (grad_probs - delta[..., None])).astype(jnp.bfloat16)
    grad_query = (
        jnp.einsum("shqk,skhd->sqhd", grad_scores, key_heads, preferred_element_type=jnp.float32)
        * 0.125
    )
    grad_key = (
        jnp.einsum("shqk,sqhd->skhd", grad_scores, query_heads, preferred_element_type=jnp.float32)
        * 0.125
    )
    grad_value = jnp.einsum(
        "shqk,sqhd->skhd",
        probs.astype(jnp.bfloat16),
        grad_heads,
        preferred_element_type=jnp.float32,
    )
    return (grad_query, grad_key, grad_value)


def intersections(query_seg, key_seg):
    return jnp.any((key_seg[:, 0] <= query_seg[:, -1]) & (key_seg[:, -1] >= query_seg[:, 0]))


def guarded(active, update, current):
    return lax.cond(active, update, lambda untouched: untouched, current)


def over_blocks(length, advance, current):
    block_len = 512
    block_count = length // block_len
    return lax.fori_loop(
        0,
        block_count,
        lambda block_index, running: advance(running, block_index * block_len, block_len),
        current,
    )


def per_device_general(
    tokens,
    doc_lengths,
    keep,
    w_query,
    b_query,
    w_key,
    w_value,
    b_value,
    w_out,
    b_out,
    gain_one,
    shift_one,
    w_up,
    w_down,
    b_down,
    gain_two,
    shift_two,
    cotangent,
):
    seq_count, block_rows, model_width = tokens.shape
    local_heads = b_query.shape[0] // HEAD
    head_width = local_heads * HEAD
    row_count = seq_count * block_rows
    slopes = head_slopes(lax.axis_index("tp") * local_heads, local_heads)
    own_pos = lax.axis_index("ctx") * block_rows + jnp.arange(block_rows, dtype=jnp.int32)
    own_seg = segment_ids(doc_lengths, own_pos)
    token_rows = tokens.reshape(row_count, model_width)
    full_query, full_key, full_value, full_out = (
        lax.all_gather(w_query, "fsdp", axis=0, tiled=True),
        lax.all_gather(w_key, "fsdp", axis=0, tiled=True),
        lax.all_gather(w_value, "fsdp", axis=0, tiled=True),
        lax.all_gather(w_out, "fsdp", axis=0, tiled=True),
    )
    queries = (
        jnp.dot(token_rows, full_query, preferred_element_type=jnp.float32) + b_query
    ).astype(jnp.bfloat16)
    key_rows = jnp.dot(token_rows, full_key, preferred_element_type=jnp.float32).astype(
        jnp.bfloat16
    )
    values = (jnp.dot(token_rows, full_value, preferred_element_type=jnp.float32) + b_value).astype(
        jnp.bfloat16
    )
    query_heads = queries.reshape(seq_count, block_rows, local_heads, HEAD)
    key_value = jnp.concatenate([key_rows, values], -1).reshape(
        seq_count, block_rows, 2 * head_width
    )

    def split_pairs(slab_pairs, block_len):
        return (
            slab_pairs[..., :head_width].reshape(seq_count, block_len, local_heads, HEAD),
            slab_pairs[..., head_width:].reshape(seq_count, block_len, local_heads, HEAD),
        )

    def key_slab(pairs, piece_keep, offset, block_len):
        slab_pairs = lax.dynamic_slice_in_dim(pairs, offset, block_len, 1)
        slab_keep = lax.dynamic_slice_in_dim(piece_keep, offset, block_len, 1)
        key_pos = offset + jnp.arange(block_len, dtype=jnp.int32)
        key_seg = segment_ids(doc_lengths, key_pos)
        slab_keys, slab_values = split_pairs(slab_pairs, block_len)
        return (slab_keys, slab_values, slab_keep, key_pos, key_seg)

    start_state = (
        jnp.full((seq_count, local_heads, block_rows), MASKED, jnp.float32),
        jnp.zeros((seq_count, local_heads, block_rows), jnp.float32),
        jnp.zeros((seq_count, local_heads, block_rows, HEAD), jnp.float32),
    )
    pairs = lax.all_gather(key_value, "ctx", axis=1, tiled=True)
    piece_keep = lax.all_gather(keep, "ctx", axis=1, tiled=True)

    def advance(partial_value, offset, block_len):
        slab_keys, slab_values, slab_keep, key_pos, key_seg = key_slab(
            pairs, piece_keep, offset, block_len
        )

        def update(current):
            row_max, row_sum, weighted = current
            scores, allowed = score_block(
                query_heads, own_pos, own_seg, slab_keys, key_pos, key_seg, slab_keep, slopes
            )
            scores = jnp.where(allowed, scores, MASKED)
            new_max = jnp.maximum(row_max, jnp.max(scores, -1))
            factor = jnp.exp(row_max - new_max)
            weights = jnp.where(allowed, jnp.exp(scores - new_max[..., None]), 0.0)
            row_sum = row_sum * factor + jnp.sum(weights, -1)
            weighted = weighted * factor[..., None] + jnp.einsum(
                "shqk,skhd->shqd",
                weights.astype(jnp.bfloat16),
                slab_values,
                preferred_element_type=jnp.float32,
            )
            return (new_max, row_sum, weighted)

        return guarded(intersections(own_seg, key_seg), update, partial_value)

    row_max, row_sum, weighted = over_blocks(pairs.shape[1], advance, start_state)
    attended = (
        (weighted / row_sum[..., None])
        .transpose(0, 2, 1, 3)
        .reshape(row_count, head_width)
        .astype(jnp.bfloat16)
    )
    log_total = row_max + jnp.log(row_sum)
    att_part = jnp.einsum("rh,dh->rd", attended, full_out, preferred_element_type=jnp.float32)
    branch_att = lax.psum(att_part.astype(jnp.bfloat16), "tp").astype(jnp.float32) + b_out
    first_out, normed_one, inv_one = layer_norm(
        token_rows.astype(jnp.float32) + branch_att, gain_one, shift_one
    )
    first_low = first_out.astype(jnp.bfloat16)
    full_up, full_down = (
        lax.all_gather(w_up, "fsdp", axis=0, tiled=True),
        lax.all_gather(w_down, "fsdp", axis=0, tiled=True),
    )
    gate_up = jnp.einsum("rd,dcf->rcf", first_low, full_up, preferred_element_type=jnp.float32)
    product, gelu_back = jax.vjp(
        lambda gate_part, up_part: jax.nn.gelu(gate_part, approximate=False) * up_part,
        gate_up[:, 0],
        gate_up[:, 1],
    )
    hidden = product.astype(jnp.bfloat16)
    ffn_part = jnp.einsum("rf,df->rd", hidden, full_down, preferred_element_type=jnp.float32)
    branch_ffn = lax.psum(ffn_part.astype(jnp.bfloat16), "tp").astype(jnp.float32) + b_down
    result, normed_two, inv_two = layer_norm(first_out + branch_ffn, gain_two, shift_two)
    grad_in = cotangent.reshape(row_count, model_width).astype(jnp.float32)
    grad_two, d_gain_two, d_shift_two = norm_back(grad_in, normed_two, inv_two, gain_two)
    grad_ffn = grad_two.astype(jnp.bfloat16)
    d_b_down = jnp.sum(grad_ffn.astype(jnp.float32), 0)
    d_w_down = jnp.einsum("rd,rf->df", grad_ffn, hidden, preferred_element_type=jnp.float32)
    grad_hidden = jnp.einsum("rd,df->rf", grad_ffn, full_down, preferred_element_type=jnp.float32)
    grad_gate, grad_up = gelu_back(grad_hidden)
    grad_gate_up = jnp.stack([grad_gate, grad_up], 1).astype(jnp.bfloat16)
    d_w_up = jnp.einsum("rd,rcf->dcf", first_low, grad_gate_up, preferred_element_type=jnp.float32)
    first_part = jnp.einsum(
        "rcf,dcf->rd", grad_gate_up, full_up, preferred_element_type=jnp.float32
    )
    grad_first = grad_two + lax.psum(first_part.astype(jnp.bfloat16), "tp").astype(jnp.float32)
    grad_one, d_gain_one, d_shift_one = norm_back(grad_first, normed_one, inv_one, gain_one)
    grad_att = grad_one.astype(jnp.bfloat16)
    d_b_out = jnp.sum(grad_att.astype(jnp.float32), 0)
    d_w_out = jnp.einsum("rd,rh->dh", grad_att, attended, preferred_element_type=jnp.float32)
    grad_attended = jnp.einsum(
        "rd,dh->rh", grad_att, full_out, preferred_element_type=jnp.float32
    ).astype(jnp.bfloat16)
    grad_heads = grad_attended.reshape(seq_count, block_rows, local_heads, HEAD)
    delta = jnp.einsum(
        "sqhd,sqhd->shq",
        grad_heads,
        attended.reshape(seq_count, block_rows, local_heads, HEAD),
        preferred_element_type=jnp.float32,
    )
    query_zero = jnp.zeros((seq_count, block_rows, local_heads, HEAD), jnp.float32)
    full_len = block_rows * lax.axis_size("ctx")
    term_zero = jnp.zeros((seq_count, full_len, 2 * head_width), jnp.float32)
    return_pairs = lax.all_gather(key_value, "ctx", axis=1, tiled=True)
    return_piece_keep = lax.all_gather(keep, "ctx", axis=1, tiled=True)

    def advance(partial_value, offset, block_len):
        slab_keys, slab_values, slab_keep, key_pos, key_seg = key_slab(
            return_pairs, return_piece_keep, offset, block_len
        )

        def update(current):
            query_grad, key_terms = current
            part_query, part_key, part_value = grad_block(
                query_heads,
                own_pos,
                own_seg,
                grad_heads,
                log_total,
                delta,
                slab_keys,
                slab_values,
                key_pos,
                key_seg,
                slab_keep,
                slopes,
            )
            slab_grads = jnp.concatenate(
                [
                    part_key.reshape(seq_count, block_len, head_width),
                    part_value.reshape(seq_count, block_len, head_width),
                ],
                -1,
            )
            return (
                query_grad + part_query,
                lax.dynamic_update_slice_in_dim(key_terms, slab_grads, offset, 1),
            )

        return guarded(intersections(own_seg, key_seg), update, partial_value)

    query_grad, key_terms = over_blocks(return_pairs.shape[1], advance, (query_zero, term_zero))
    pair_grads = lax.psum_scatter(
        key_terms.astype(jnp.bfloat16), "ctx", scatter_dimension=1, tiled=True
    ).astype(jnp.float32)
    query_low = query_grad.reshape(row_count, head_width).astype(jnp.bfloat16)
    pair_low = pair_grads.reshape(row_count, 2 * head_width).astype(jnp.bfloat16)
    grad_project = jnp.concatenate([query_low, pair_low], -1)
    joined_weights = jnp.concatenate([full_query, full_key, full_value], -1)
    joined_grads = jnp.einsum(
        "rd,rh->dh", token_rows, grad_project, preferred_element_type=jnp.float32
    )
    input_part = jnp.einsum(
        "rh,dh->rd", grad_project, joined_weights, preferred_element_type=jnp.float32
    )
    d_tokens = grad_one + lax.psum(input_part.astype(jnp.bfloat16), "tp").astype(jnp.float32)
    d_b_query = jnp.sum(query_low.astype(jnp.float32), 0)
    d_b_value = jnp.sum(pair_low[:, head_width:].astype(jnp.float32), 0)
    d_w_query = joined_grads[:, :head_width]
    d_w_key = joined_grads[:, head_width : 2 * head_width]
    d_w_value = joined_grads[:, 2 * head_width :]
    shard_grads = (
        lax.psum_scatter(
            d_w_query.astype(jnp.bfloat16), "fsdp", scatter_dimension=0, tiled=True
        ).astype(jnp.float32),
        lax.psum_scatter(
            d_w_key.astype(jnp.bfloat16), "fsdp", scatter_dimension=0, tiled=True
        ).astype(jnp.float32),
        lax.psum_scatter(
            d_w_value.astype(jnp.bfloat16), "fsdp", scatter_dimension=0, tiled=True
        ).astype(jnp.float32),
        lax.psum_scatter(
            d_w_out.astype(jnp.bfloat16), "fsdp", scatter_dimension=0, tiled=True
        ).astype(jnp.float32),
        lax.psum_scatter(
            d_w_up.astype(jnp.bfloat16), "fsdp", scatter_dimension=0, tiled=True
        ).astype(jnp.float32),
        lax.psum_scatter(
            d_w_down.astype(jnp.bfloat16), "fsdp", scatter_dimension=0, tiled=True
        ).astype(jnp.float32),
    )
    sum_query, sum_key, sum_value, sum_out, sum_up, sum_down = (
        lax.psum(shard_grads[0].astype(jnp.bfloat16), "ctx").astype(jnp.float32),
        lax.psum(shard_grads[1].astype(jnp.bfloat16), "ctx").astype(jnp.float32),
        lax.psum(shard_grads[2].astype(jnp.bfloat16), "ctx").astype(jnp.float32),
        lax.psum(shard_grads[3].astype(jnp.bfloat16), "ctx").astype(jnp.float32),
        lax.psum(shard_grads[4].astype(jnp.bfloat16), "ctx").astype(jnp.float32),
        lax.psum(shard_grads[5].astype(jnp.bfloat16), "ctx").astype(jnp.float32),
    )
    (
        total_b_query,
        total_b_value,
        total_b_out,
        total_b_down,
        total_gain_one,
        total_shift_one,
        total_gain_two,
        total_shift_two,
    ) = lax.psum(
        (d_b_query, d_b_value, d_b_out, d_b_down, d_gain_one, d_shift_one, d_gain_two, d_shift_two),
        ("fsdp", "ctx"),
    )
    return (
        result.reshape(seq_count, block_rows, model_width).astype(jnp.bfloat16),
        d_tokens.reshape(seq_count, block_rows, model_width),
        sum_query,
        total_b_query,
        sum_key,
        sum_value,
        total_b_value,
        sum_out,
        total_b_out,
        total_gain_one,
        total_shift_one,
        sum_up,
        sum_down,
        total_b_down,
        total_gain_two,
        total_shift_two,
    )


LANES = 128
MESH = pl.DeviceIdType.MESH
TILE = 256
DOC_ROW, KEEP_ROW, POS_ROW, LINE_ROW, LOG_ROW, FEAT_END = 64, 72, 73, 79, 82, 85
X_SWAP = [(0, 1), (1, 0), (2, 3), (3, 2)]
Y_SWAP = [(0, 2), (2, 0), (1, 3), (3, 1)]
D_SWAP = [(0, 3), (3, 0), (1, 2), (2, 1)]


def dot(left, right, dims=((1,), (0,))):
    return lax.dot_general(left, right, (dims, ((), ())), preferred_element_type=jnp.float32)


def three_terms(value, low):
    high = low(value)
    middle = low(value - high)
    return high, middle, low(value - high - middle)


def narrow(value):
    return lax.reduce_precision(value, 8, 7)


def project_kernel(x_ref, w_ref, bias_ref, key_feat_ref, query_feat_ref, qt_ref, q_ref, k_ref, kt_ref, v_ref, vt_ref):
    heads = q_ref.shape[0]
    rows = x_ref.shape[0]
    y = dot(x_ref[...], w_ref[...]) + bias_ref[...]
    y = y.astype(jnp.bfloat16).astype(jnp.float32)
    lane = lax.broadcasted_iota(jnp.int32, (rows, LANES), 1)
    sub = lax.broadcasted_iota(jnp.int32, (LANES, rows), 0)

    def head_part(index):
        pair = y[:, index // 2 * LANES : (index // 2 + 1) * LANES]
        if index % 2:
            pair = pltpu.roll(pair, HEAD, 1)
        return jnp.where(lane < HEAD, pair, 0.0)

    for head in range(heads):
        query = head_part(head) * 0.125
        q_ref[head] = query[:, :HEAD].astype(jnp.bfloat16)
        qt_ref[head] = (query.T + query_feat_ref[head].astype(jnp.float32)).astype(jnp.bfloat16)
        key = head_part(heads + head)
        k_ref[head] = (key + key_feat_ref[...].astype(jnp.float32)).astype(jnp.bfloat16)
        kt_ref[head] = key.T[:HEAD].astype(jnp.bfloat16)
        value = head_part(2 * heads + head)
        ones = (lane >= HEAD) & (lane < HEAD + 3)
        v_ref[head] = jnp.where(ones, 1.0, value).astype(jnp.bfloat16)
        vt_ref[head] = jnp.where(sub == HEAD, 1.0, value.T)[:80].astype(jnp.bfloat16)


def project(x, weight, bias, key_feat, query_feat, heads):
    length, width = x.shape
    rows = 2 * TILE
    return pl.pallas_call(
        project_kernel,
        grid=(length // rows,),
        in_specs=[
            pl.BlockSpec((rows, width), lambda i: (i, 0)),
            pl.BlockSpec(weight.shape, lambda i: (0, 0)),
            pl.BlockSpec(bias.shape, lambda i: (0, 0)),
            pl.BlockSpec((rows, LANES), lambda i: (i, 0)),
            pl.BlockSpec((heads, LANES, rows), lambda i: (0, 0, i)),
        ],
        out_specs=[
            pl.BlockSpec((heads, LANES, rows), lambda i: (0, 0, i)),
            pl.BlockSpec((heads, rows, HEAD), lambda i: (0, i, 0)),
            pl.BlockSpec((heads, rows, LANES), lambda i: (0, i, 0)),
            pl.BlockSpec((heads, HEAD, rows), lambda i: (0, 0, i)),
            pl.BlockSpec((heads, rows, LANES), lambda i: (0, i, 0)),
            pl.BlockSpec((heads, 80, rows), lambda i: (0, 0, i)),
        ],
        out_shape=[
            jax.ShapeDtypeStruct((heads, LANES, length), jnp.bfloat16),
            jax.ShapeDtypeStruct((heads, length, HEAD), jnp.bfloat16),
            jax.ShapeDtypeStruct((heads, length, LANES), jnp.bfloat16),
            jax.ShapeDtypeStruct((heads, HEAD, length), jnp.bfloat16),
            jax.ShapeDtypeStruct((heads, length, LANES), jnp.bfloat16),
            jax.ShapeDtypeStruct((heads, 80, length), jnp.bfloat16),
        ],
        compiler_params=pltpu.CompilerParams(vmem_limit_bytes=40 << 20),
        cost_estimate=pl.CostEstimate(
            flops=2 * length * width * weight.shape[1], bytes_accessed=12 << 20, transcendentals=0
        ),
        name="project",
    )(x, weight, bias, key_feat, query_feat)


def side_signs(rows):
    sub = lax.broadcasted_iota(jnp.int32, (LANES, rows), 0)
    bias_rows = (sub >= POS_ROW) & (sub < LOG_ROW)
    after = jnp.where(bias_rows, -1.0, 1.0).astype(jnp.bfloat16)
    same = jnp.where(bias_rows, 0.0, 1.0).astype(jnp.bfloat16)
    bare = jnp.where(bias_rows | (sub == KEEP_ROW), 0.0, 1.0).astype(jnp.bfloat16)
    return after, same, bare


def diagonal_scores(keys, query_t, same, bare, slope):
    rows = lax.broadcasted_iota(jnp.int32, (TILE, TILE), 0)
    cols = lax.broadcasted_iota(jnp.int32, (TILE, TILE), 1)
    apart = jnp.abs(rows - cols)
    full = dot(keys, query_t * same) - slope * apart.astype(jnp.float32)
    return jnp.where(apart == 0, dot(keys, query_t * bare), full)


def sweep(first, last, step, most=2):
    many = (last - first) // most

    @pl.loop(0, many)
    def _(i):
        step(first + i * most, most)

    @pl.loop(first + many * most, last)
    def _(tile):
        step(tile, 1)


def attend_kernel(span_ref, slope_ref, qt_ref, k_ref, vt_ref, o_ref, ot_ref, lse_ref, max_ref, acc_ref):
    heads = qt_ref.shape[0]
    block = pl.program_id(0)
    after, same, bare = side_signs(TILE)

    def tile_rows(tile, count=1):
        return pl.ds(pl.multiple_of(tile * TILE, TILE), count * TILE)

    own = tile_rows(block)
    for head in range(heads):
        scores = diagonal_scores(k_ref[head, own, :], qt_ref[head], same, bare, slope_ref[head])
        top = jnp.max(scores, 0, keepdims=True)
        weights = jnp.exp(scores - top).astype(jnp.bfloat16)
        max_ref[head] = top
        acc_ref[head] = dot(vt_ref[head, :, own], weights)

    def step(tile, count, sign):
        each = range(heads)
        keys = [k_ref[head, tile_rows(tile, count), :] for head in each]
        values = [vt_ref[head, :, tile_rows(tile, count)] for head in each]
        queries = [qt_ref[head] if sign is None else qt_ref[head] * sign for head in each]
        old = [max_ref[head] for head in each]
        acc = [acc_ref[head] for head in each]
        scores = [dot(keys[head], queries[head]) for head in each]
        top = [jnp.maximum(old[head], jnp.max(scores[head], 0, keepdims=True)) for head in each]
        weights = [jnp.exp(scores[head] - top[head]).astype(jnp.bfloat16) for head in each]
        parts = [dot(values[head], weights[head]) for head in each]
        for head in each:
            max_ref[head] = top[head]
            acc_ref[head] = acc[head] * jnp.exp(old[head] - top[head]) + parts[head]

    sweep(span_ref[0, block], block, lambda tile, count: step(tile, count, None))
    sweep(block + 1, span_ref[1, block], lambda tile, count: step(tile, count, after))

    parts = []
    for head in range(heads):
        total = acc_ref[head, HEAD : HEAD + 1, :]
        out_t = acc_ref[head, :HEAD, :] / total
        ot_ref[head] = out_t
        parts.append(out_t)
        lse_ref[head] = max_ref[head] + jnp.log(total)
    o_ref[...] = jnp.concatenate(parts, 0).T.astype(jnp.bfloat16)


def attend(spans, slopes, query_t, keys, value_t):
    heads, _, length = query_t.shape
    blocks = length // TILE
    return pl.pallas_call(
        attend_kernel,
        grid_spec=pltpu.PrefetchScalarGridSpec(
            num_scalar_prefetch=2,
            grid=(blocks,),
            in_specs=[
                pl.BlockSpec((heads, LANES, TILE), lambda i, *_: (0, 0, i)),
                pl.BlockSpec(keys.shape, lambda i, *_: (0, 0, 0)),
                pl.BlockSpec(value_t.shape, lambda i, *_: (0, 0, 0)),
            ],
            out_specs=[
                pl.BlockSpec((TILE, heads * HEAD), lambda i, *_: (i, 0)),
                pl.BlockSpec((heads, HEAD, TILE), lambda i, *_: (0, 0, i)),
                pl.BlockSpec((heads, 1, TILE), lambda i, *_: (0, 0, i)),
            ],
            scratch_shapes=[
                pltpu.VMEM((heads, 1, TILE), jnp.float32),
                pltpu.VMEM((heads, 80, TILE), jnp.float32),
            ],
        ),
        out_shape=[
            jax.ShapeDtypeStruct((length, heads * HEAD), jnp.bfloat16),
            jax.ShapeDtypeStruct((heads, HEAD, length), jnp.float32),
            jax.ShapeDtypeStruct((heads, 1, length), jnp.float32),
        ],
        compiler_params=pltpu.CompilerParams(vmem_limit_bytes=40 << 20),
        cost_estimate=pl.CostEstimate(
            flops=heads * length * length * 256, bytes_accessed=6 << 20, transcendentals=heads * length * length
        ),
        name="attend",
    )(spans, slopes, query_t, keys, value_t)


def attend_back_kernel(
    span_ref, slope_ref, qt_ref, q_ref, k_ref, kt_ref, v_ref, g_ref, ot_ref, lse_ref,
    dq_ref, dk_ref, dv_ref, qt_log, grad_heads, grad_t, query_acc, key_acc, value_acc,
):
    heads = qt_ref.shape[0]
    blocks = pl.num_programs(0)
    block = pl.program_id(0)
    length = qt_ref.shape[2]
    after, same, bare = side_signs(TILE)

    def low(value):
        return value.astype(jnp.bfloat16).astype(jnp.float32)

    def tile_rows(tile, count=1):
        return pl.ds(pl.multiple_of(tile * TILE, TILE), count * TILE)

    @pl.when(block == 0)
    def _():
        query_acc[...] = jnp.zeros_like(query_acc)
        sub = lax.broadcasted_iota(jnp.int32, (LANES, TILE), 0)

        @pl.loop(0, length // TILE)
        def _(tile):
            rows = tile_rows(tile)
            grad = g_ref[rows, :].astype(jnp.float32)
            turned = grad.T
            for head in range(heads):
                own = turned[head * HEAD : (head + 1) * HEAD]
                delta = jnp.sum(own * ot_ref[head, :, rows], 0, keepdims=True)
                first, second, third = three_terms(-delta, low)
                wide = jnp.concatenate([own, jnp.zeros_like(own)], 0)
                wide = jnp.where(sub == HEAD, first, wide)
                wide = jnp.where(sub == HEAD + 1, second, wide)
                wide = jnp.where(sub == HEAD + 2, third, wide)
                grad_t[head, :, rows] = wide.astype(jnp.bfloat16)
                grad_heads[head, rows, :] = own.T.astype(jnp.bfloat16)
                first, second, third = three_terms(-lse_ref[head, :, rows], low)
                query = qt_ref[head, :, rows].astype(jnp.float32)
                query = jnp.where(sub == LOG_ROW, first, query)
                query = jnp.where(sub == LOG_ROW + 1, second, query)
                query = jnp.where(sub == LOG_ROW + 2, third, query)
                qt_log[head, :, rows] = query.astype(jnp.bfloat16)

    def accumulate(tile, scores, first, count=1):
        each = range(heads)
        rows = tile_rows(tile, count)
        values = [v_ref[head] for head in each]
        turned = [grad_t[head, :, rows] for head in each]
        grads = [grad_heads[head, rows, :] for head in each]
        queries = [q_ref[head, rows, :] for head in each]
        keys_t = [kt_ref[head] for head in each]
        probs = [jnp.exp(scores[head]) for head in each]
        grad_probs = [dot(values[head], turned[head]) for head in each]
        grad_scores = [(probs[head] * grad_probs[head]).astype(jnp.bfloat16) for head in each]
        value_part = [dot(probs[head].astype(jnp.bfloat16), grads[head]) for head in each]
        key_part = [dot(grad_scores[head], queries[head]) for head in each]
        query_part = [dot(keys_t[head], grad_scores[head]) for head in each]
        for head in each:
            if first:
                value_acc[head] = value_part[head]
                key_acc[head] = key_part[head]
            else:
                value_acc[head] += value_part[head]
                key_acc[head] += key_part[head]
            query_acc[head, :, rows] += query_part[head]

    own = [qt_log[head, :, tile_rows(block)] for head in range(heads)]
    accumulate(
        block,
        [
            diagonal_scores(k_ref[head], own[head], same, bare, slope_ref[head])
            for head in range(heads)
        ],
        True,
    )
    after_wide = side_signs(2 * TILE)[0]

    def step(tile, count, sign):
        queries = [qt_log[head, :, tile_rows(tile, count)] for head in range(heads)]
        if sign is not None:
            queries = [query * sign[:, : count * TILE] for query in queries]
        accumulate(tile, [dot(k_ref[head], queries[head]) for head in range(heads)], False, count)

    sweep(span_ref[0, block], block, lambda tile, count: step(tile, count, after_wide))
    sweep(block + 1, span_ref[1, block], lambda tile, count: step(tile, count, None))

    dk_ref[...] = jnp.concatenate([key_acc[head] for head in range(heads)], 1).astype(jnp.bfloat16)
    dv_ref[...] = jnp.concatenate([value_acc[head] for head in range(heads)], 1).astype(jnp.bfloat16)

    @pl.when(block == blocks - 1)
    def _():
        @pl.loop(0, length // TILE)
        def _(tile):
            rows = tile_rows(tile)
            turned = jnp.concatenate([query_acc[head, :, rows] for head in range(heads)], 0)
            dq_ref[rows, :] = (turned.T * 0.125).astype(jnp.bfloat16)


def attend_back(spans, slopes, query_t, queries, keys, keys_t, values, grads, out_t, lse):
    heads, _, length = query_t.shape
    blocks = length // TILE
    width = heads * HEAD

    def whole(array):
        return pl.BlockSpec(array.shape, lambda i, *_: (0,) * array.ndim)

    return pl.pallas_call(
        attend_back_kernel,
        grid_spec=pltpu.PrefetchScalarGridSpec(
            num_scalar_prefetch=2,
            grid=(blocks,),
            in_specs=[
                whole(query_t),
                whole(queries),
                pl.BlockSpec((heads, TILE, LANES), lambda i, *_: (0, i, 0)),
                pl.BlockSpec((heads, HEAD, TILE), lambda i, *_: (0, 0, i)),
                pl.BlockSpec((heads, TILE, LANES), lambda i, *_: (0, i, 0)),
                whole(grads),
                whole(out_t),
                whole(lse),
            ],
            out_specs=[
                pl.BlockSpec((length, width), lambda i, *_: (0, 0)),
                pl.BlockSpec((TILE, width), lambda i, *_: (i, 0)),
                pl.BlockSpec((TILE, width), lambda i, *_: (i, 0)),
            ],
            scratch_shapes=[
                pltpu.VMEM((heads, LANES, length), jnp.bfloat16),
                pltpu.VMEM((heads, length, HEAD), jnp.bfloat16),
                pltpu.VMEM((heads, LANES, length), jnp.bfloat16),
                pltpu.VMEM((heads, HEAD, length), jnp.float32),
                pltpu.VMEM((heads, TILE, HEAD), jnp.float32),
                pltpu.VMEM((heads, TILE, HEAD), jnp.float32),
            ],
        ),
        out_shape=[jax.ShapeDtypeStruct((length, width), jnp.bfloat16)] * 3,
        compiler_params=pltpu.CompilerParams(vmem_limit_bytes=50 << 20),
        cost_estimate=pl.CostEstimate(
            flops=heads * length * length * 640, bytes_accessed=12 << 20, transcendentals=heads * length * length
        ),
        name="attend_back",
    )(spans, slopes, query_t, queries, keys, keys_t, values, grads, out_t, lse)


def start_kernel(
    tokens, keep, w_joined, w_out, w_down, sequence, keep_all, full_joined, full_out, full_down,
    z_send, z_recv, tp_send, tp_recv, w_send, w_recv, down_send, down_recv, keep_send, keep_recv, local_sem,
):
    place, stage, core = lax.axis_index("fsdp"), lax.axis_index("ctx"), lax.axis_index("tp")
    seq = stage // 2
    half_rows = sequence.shape[2]
    barrier = pltpu.get_barrier_semaphore()
    peers = [(place ^ other, stage, core) for other in (1, 2, 3)]
    peers += [(place, lax.rem(stage + shift, 4), core) for shift in (1, 2, 3)]
    peers += [(place, stage, 1 - core)]
    for peer in peers:
        pl.semaphore_signal(barrier, inc=1, device_id=peer, device_id_type=MESH)
    pl.semaphore_wait(barrier, len(peers))

    rows = pl.ds(pl.multiple_of(core * half_rows, half_rows), half_rows)
    ours, theirs = tokens.at[seq, rows], tokens.at[1 - seq, rows]

    def send(source, block, target, slot):
        return pltpu.make_async_remote_copy(
            source, sequence.at[block, core], z_send.at[slot], z_recv.at[block],
            device_id=(place, target, core), device_id_type=MESH,
        )

    def arrival(block):
        return pltpu.make_async_remote_copy(
            ours, sequence.at[block, core], z_send.at[0], z_recv.at[block],
            device_id=(place, stage, 1 - core), device_id_type=MESH,
        )

    def share(block):
        return pltpu.make_async_remote_copy(
            sequence.at[block, core], sequence.at[block, core], tp_send.at[block], tp_recv.at[block],
            device_id=(place, stage, 1 - core), device_id_type=MESH,
        )

    def shared(block):
        return pltpu.make_async_remote_copy(
            sequence.at[block, 1 - core], sequence.at[block, 1 - core], tp_send.at[block], tp_recv.at[block],
            device_id=(place, stage, 1 - core), device_id_type=MESH,
        )

    first = send(ours, stage, stage ^ 1, 0)
    ends = ((0, 2, 3), (3, 1, 0))
    mids = ((1, 2, 0), (2, 1, 3))
    for own, near, _ in mids:

        @pl.when(stage == own)
        def _():
            send(theirs, own, near, 1).start()

    first.start()
    for own, near, far in ends:

        @pl.when(stage == own)
        def _():
            send(theirs, own, far, 1).start()
            send(theirs, own, near, 2).start()

    weights = []
    for index, (shard, full) in enumerate(((w_joined, full_joined), (w_out, full_out))):
        for other in (1, 2, 3):
            sem = 3 * index + other - 1
            weights.append(
                pltpu.make_async_remote_copy(
                    shard, full.at[place], w_send.at[sem], w_recv.at[sem],
                    device_id=(place ^ other, stage, core), device_id_type=MESH,
                )
            )
            weights[-1].start()

    units = w_down.shape[1] // 2

    def down_copy(owner, other, which, sem):
        columns = pl.ds(which * units, units)
        source = w_down if owner is place else full_down.at[owner]
        return pltpu.make_async_remote_copy(
            source.at[:, columns], full_down.at[owner, :, columns], down_send.at[sem], down_recv.at[sem],
            device_id=(place ^ other, stage, core), device_id_type=MESH,
        )

    halves = [
        down_copy(place, other, which, 2 * which + other - 1)
        for other, which in ((1, 0), (2, 1), (1, 1), (2, 0))
    ]
    for copy in halves:
        copy.start()
    flags = []
    for shift in (1, 2, 3):
        flags.append(
            pltpu.make_async_remote_copy(
                keep, keep_all.at[stage], keep_send.at[shift - 1], keep_recv.at[shift - 1],
                device_id=(place, lax.rem(stage + shift, 4), core), device_id_type=MESH,
            )
        )
        flags[-1].start()
    local = []
    for index, (source, target) in enumerate(
        (
            (tokens.at[seq, pl.ds(0, half_rows)], sequence.at[stage, 0]),
            (tokens.at[seq, pl.ds(half_rows, half_rows)], sequence.at[stage, 1]),
            (keep, keep_all.at[stage]),
            (w_joined, full_joined.at[place]),
            (w_out, full_out.at[place]),
            (w_down, full_down.at[place]),
        )
    ):
        local.append(pltpu.make_async_copy(source, target, local_sem.at[index]))
        local[-1].start()

    on = [down_copy(place ^ 1, 2, 0, 4), down_copy(place ^ 2, 1, 1, 5)]
    for first_half, second in zip(halves[:2], on):
        first_half.wait_recv()
        second.start()

    for own, near, end in mids:
        far = 3 - end

        @pl.when(stage == own)
        def _():
            arrival(near).wait_recv()
            send(sequence.at[near, core], near, end, 2).start()
            share(near).start()
            arrival(end).wait_recv()
            share(end).start()
            arrival(far).wait_recv()
            share(far).start()
            send(theirs, own, near, 1).wait_send()
            send(sequence.at[near, core], near, end, 2).wait_send()
            for block in (near, end, far):
                share(block).wait_send()
                shared(block).wait_recv()

    for own, near, far in ends:

        @pl.when(stage == own)
        def _():
            inner = 3 - near
            for block in (inner, far, near):
                arrival(block).wait_recv()
                share(block).start()
            send(theirs, own, near, 1).wait_send()
            send(theirs, own, near, 2).wait_send()
            for block in (inner, far, near):
                share(block).wait_send()
                shared(block).wait_recv()

    first.wait_send()
    for copy in weights + flags + halves[2:] + on:
        copy.wait()
    for copy in halves[:2]:
        copy.wait_send()
    for copy in local:
        copy.wait()


def start(tokens, keep, w_joined, w_out, w_down):
    _, block_rows, width = tokens.shape
    dma = pltpu.SemaphoreType.DMA
    return pl.pallas_call(
        start_kernel,
        in_specs=[pl.BlockSpec(memory_space=pltpu.VMEM)] * 5,
        out_specs=[pl.BlockSpec(memory_space=pl.ANY)] * 5,
        out_shape=[
            jax.ShapeDtypeStruct((4, 2, block_rows // 2, width), tokens.dtype),
            jax.ShapeDtypeStruct((4,) + keep.shape, keep.dtype),
            jax.ShapeDtypeStruct((4,) + w_joined.shape, w_joined.dtype),
            jax.ShapeDtypeStruct((4,) + w_out.shape, w_out.dtype),
            jax.ShapeDtypeStruct((4,) + w_down.shape, w_down.dtype),
        ],
        scratch_shapes=[
            dma((3,)), dma((4,)), dma((4,)), dma((4,)), dma((6,)), dma((6,)), dma((6,)), dma((6,)), dma((3,)), dma((3,)), dma((6,)),
        ],
        compiler_params=pltpu.CompilerParams(collective_id=0, has_side_effects=True),
        cost_estimate=pl.CostEstimate(flops=40 << 30, bytes_accessed=16 << 20, transcendentals=0),
        name="start",
    )(tokens, keep, w_joined, w_out, w_down)


def rows_norm(residual):
    centered = residual - jnp.mean(residual, -1, keepdims=True)
    inv_scale = lax.rsqrt(jnp.mean(centered * centered, -1, keepdims=True) + NORM_EPS)
    return centered * inv_scale, inv_scale


def rows_norm_back(grad_out, normed, inv_scale, norm_gain):
    grad_norm = grad_out * norm_gain
    mean_grad = jnp.mean(grad_norm, -1, keepdims=True)
    mean_cross = jnp.mean(grad_norm * normed, -1, keepdims=True)
    return (grad_norm - mean_grad - normed * mean_cross) * inv_scale


def middle_kernel(
    attended, sequence, cotangent, w_out, w_down, up_0, up_1, up_2, vectors,
    out_home, grad_one, grad_heads, early, late, down_sum, sums,
    token_v, mine_v, theirs_v, both_v, cot_v, out_w, down_w, up_w,
    send_a, recv_a, send_b, recv_b, send_c, recv_c,
    normed_v, inv_v, low_v, hidden_v, gate_v, lift_v, grad_v, ffn_v, att_v, result_v, keep_v, away_v, tile_v,
    down_v, down_got, load_sem, far_send, far_recv, pair_send, pair_recv, cot_send, cot_recv, cot_pass, cot_took,
    a_send, a_recv, b_send, b_recv, c_send, c_recv, out_send, out_recv, out_pass, out_took,
    one_sem, keep_sem, away_send, away_recv, tile_sem, down_send, down_recv, down_sem,
):
    place, stage, core = lax.axis_index("fsdp"), lax.axis_index("ctx"), lax.axis_index("tp")
    seq, half = stage // 2, stage % 2
    pair = stage ^ 1
    chunks = token_v.shape[0]
    units = hidden_v.shape[2]
    wide = 512
    quarter = up_0.shape[0]

    barrier = pltpu.get_barrier_semaphore()
    peers = [(place ^ other, stage, core) for other in (1, 2, 3)]
    peers += [(place, lax.rem(stage + shift, 4), core) for shift in (1, 2, 3)]
    peers += [(place, stage, 1 - core)]
    for peer in peers:
        pl.semaphore_signal(barrier, inc=1, device_id=peer, device_id_type=MESH)
    pl.semaphore_wait(barrier, len(peers))

    def remote(source, target, send, recv, device):
        return pltpu.make_async_remote_copy(
            source, target, send, recv, device_id=device, device_id_type=MESH
        )

    partner = (place, pair, core)
    other_core = (place, stage, 1 - core)

    def pair_copy(c):
        return remote(
            attended.at[(1 - half) * chunks + c], theirs_v.at[c], pair_send.at[c], pair_recv.at[c], partner
        )

    for c in range(chunks):
        pair_copy(c).start()

    def far_copy(which):
        source, over = ((up_1, 2), (up_2, 1))[which]
        columns = pl.ds(which * units, units)
        rows = pl.ds(pl.multiple_of((place ^ 3 ^ over) * quarter, quarter), quarter)
        return remote(
            source.at[:, columns], up_w.at[rows, columns], far_send.at[which], far_recv.at[which],
            (place ^ over, stage, core),
        )

    for which in (0, 1):
        far_copy(which).start()

    def cot_owner(which):
        return 2 * which + stage // 2

    def cot_copy(which):
        return remote(
            cotangent.at[which, core], cot_v.at[stage % 2, core],
            cot_send.at[which], cot_recv.at[stage % 2], (place, cot_owner(which), core),
        )

    def cot_local(which):
        return pltpu.make_async_copy(cotangent.at[which], cot_v.at[stage % 2], cot_send.at[which])

    for which in (0, 1):

        @pl.when(cot_owner(which) == stage)
        def _():
            cot_local(which).start()

        @pl.when(cot_owner(which) != stage)
        def _():
            cot_copy(which).start()

    def cot_arrival(block):
        return remote(
            cot_v.at[block, core], cot_v.at[block, core], cot_pass.at[block], cot_recv.at[block], other_core
        )

    def cot_share(block, whose):
        return remote(
            cot_v.at[block, whose], cot_v.at[block, whose], cot_pass.at[block], cot_took.at[block], other_core
        )

    loads = [
        pltpu.make_async_copy(attended.at[pl.ds(half * chunks, chunks)], mine_v, load_sem.at[0]),
        pltpu.make_async_copy(w_out, out_w, load_sem.at[1]),
        pltpu.make_async_copy(sequence.at[pl.ds(half * chunks, chunks)], token_v, load_sem.at[2]),
        pltpu.make_async_copy(w_down, down_w, load_sem.at[3]),
    ]
    for other, shard in enumerate((up_0, up_1, up_2)):
        rows = pl.ds(pl.multiple_of((place ^ other) * quarter, quarter), quarter)
        loads.append(pltpu.make_async_copy(shard, up_w.at[rows], load_sem.at[4 + other]))
    for load in loads:
        load.start()

    def vector(index):
        return vectors[index : index + 1, :]

    b_out, gain_one, shift_one, b_down, gain_two, shift_two = (vector(i) for i in range(6))
    sums[...] = jnp.zeros_like(sums)

    def add_sum(index, rows):
        sums[index : index + 1, :] += jnp.sum(rows, 0, keepdims=True)

    def exchange(c, sent, got, send, recv):
        return remote(sent.at[c], got.at[c], send.at[c], recv.at[c], other_core)

    def total(c, sent, got):
        return sent[c].astype(jnp.float32) + got[c].astype(jnp.float32)

    loads[0].wait()
    loads[1].wait()

    @pl.loop(0, chunks)
    def _(c):
        pair_copy(c).wait_recv()
        first, second = mine_v[c], theirs_v[c]
        both = jnp.where(
            half == 0, jnp.concatenate([first, second], 1), jnp.concatenate([second, first], 1)
        )
        both_v[c] = both
        send_a[c] = dot(both, out_w[...], ((1,), (1,))).astype(jnp.bfloat16)
        exchange(c, send_a, recv_a, a_send, a_recv).start()

    for load in loads[2:]:
        load.wait()
    for which in (0, 1):
        far_copy(which).wait_recv()

    @pl.loop(0, chunks)
    def _(c):
        exchange(c, send_a, recv_a, a_send, a_recv).wait_recv()

        @pl.when(c == chunks - 1)
        def _():
            for block in (0, 1):

                @pl.when(2 * half + block != stage)
                def _():
                    cot_arrival(block).wait_recv()
                    cot_share(block, core).start()

        residual = token_v[c].astype(jnp.float32) + (total(c, send_a, recv_a) + b_out)
        normed, inv_scale = rows_norm(residual)
        normed_v[c] = normed
        inv_v[c] = inv_scale
        low_v[c] = (normed * gain_one + shift_one).astype(jnp.bfloat16)
        for n in range(0, units, wide):
            gate = dot(low_v[c], up_w[:, n : n + wide])
            lift = dot(low_v[c], up_w[:, units + n : units + n + wide])
            chance = 0.5 + 0.5 * lax.erf(gate * 0.7071067811865476)
            density = jnp.exp(gate * gate * -0.5) * 0.3989422804014327
            gelu = gate * chance
            hidden_v[c, :, n : n + wide] = (gelu * lift).astype(jnp.bfloat16)
            gate_v[c, :, n : n + wide] = (lift * (chance + gate * density)).astype(jnp.bfloat16)
            lift_v[c, :, n : n + wide] = gelu.astype(jnp.bfloat16)
        send_b[c] = dot(hidden_v[c], down_w[...], ((1,), (1,))).astype(jnp.bfloat16)
        exchange(c, send_b, recv_b, b_send, b_recv).start()

    for block in (0, 1):

        @pl.when(2 * half + block != stage)
        def _():
            cot_share(block, core).wait_send()
            cot_share(block, 1 - core).wait_recv()

    for which in (0, 1):

        @pl.when(cot_owner(which) == stage)
        def _():
            cot_local(which).wait()

        @pl.when(cot_owner(which) != stage)
        def _():
            cot_copy(which).wait_send()

    def home(c):
        return 2 * half + c // 2

    def out_copy(c):
        return remote(
            result_v.at[c], out_home.at[seq, core], out_send.at[c], out_recv.at[seq], (place, home(c), core)
        )

    def out_local(c):
        return pltpu.make_async_copy(result_v.at[c], out_home.at[seq, c % 2], out_send.at[c])

    @pl.loop(0, chunks)
    def _(c):
        exchange(c, send_b, recv_b, b_send, b_recv).wait_recv()
        normed_one = normed_v[c]
        residual = normed_one * gain_one + shift_one + (total(c, send_b, recv_b) + b_down)
        normed, inv_scale = rows_norm(residual)
        result_v[c] = (normed * gain_two + shift_two).astype(jnp.bfloat16)

        @pl.when(home(c) == stage)
        def _():
            out_local(c).start()

        @pl.when((home(c) != stage) & (c % 2 == core))
        def _():
            out_copy(c).start()

        grad_in = cot_v[c // 2, c % 2].astype(jnp.float32)
        add_sum(0, grad_in * normed)
        add_sum(1, grad_in)
        grad_two = rows_norm_back(grad_in, normed, inv_scale, gain_two)
        grad_v[c] = grad_two
        grad_ffn = grad_two.astype(jnp.bfloat16)
        ffn_v[c] = grad_ffn
        add_sum(2, grad_ffn.astype(jnp.float32))

    tile = tile_v.shape[2]

    def columns(index):
        return pl.ds(pl.multiple_of(index * tile, tile), tile)

    def weight_part(left, right):
        rows = left.shape[0] * left.shape[1]
        return dot(
            left[...].reshape(rows, left.shape[2]), right.reshape(rows, tile), ((0,), (0,))
        ).astype(jnp.bfloat16)

    unit_tiles = units // tile

    def down_copy(i, other):
        rows = pl.ds(pl.multiple_of((place ^ other) * quarter, quarter), quarter)
        return remote(
            down_v.at[rows, columns(i)], down_got.at[other - 1, :, columns(i)],
            down_send.at[i, other - 1], down_recv.at[i, other - 1], (place ^ other, stage, core),
        )

    @pl.loop(0, unit_tiles)
    def _(i):
        down_v[:, columns(i)] = weight_part(ffn_v, hidden_v[:, :, columns(i)])
        for other in (1, 2, 3):
            down_copy(i, other).start()

    @pl.loop(0, chunks)
    def _(c):
        for n in range(0, units, wide):
            grad_hidden = dot(ffn_v[c], down_w[:, n : n + wide])
            gate_v[c, :, n : n + wide] = (grad_hidden * gate_v[c, :, n : n + wide]).astype(jnp.bfloat16)
            lift_v[c, :, n : n + wide] = (grad_hidden * lift_v[c, :, n : n + wide]).astype(jnp.bfloat16)
        send_c[c] = (
            dot(gate_v[c], up_w[:, :units], ((1,), (1,))) + dot(lift_v[c], up_w[:, units:], ((1,), (1,)))
        ).astype(jnp.bfloat16)
        exchange(c, send_c, recv_c, c_send, c_recv).start()

    def one_copy(c):
        return pltpu.make_async_copy(grad_v.at[c], grad_one.at[c], one_sem.at[c])

    def keep_copy(c):
        return pltpu.make_async_copy(keep_v.at[c], grad_heads.at[half * chunks + c], keep_sem.at[c])

    def away_copy(c, whose):
        return remote(
            away_v.at[c], grad_heads.at[whose * chunks + c], away_send.at[c], away_recv.at[c], partner
        )

    @pl.loop(0, chunks)
    def _(c):
        exchange(c, send_c, recv_c, c_send, c_recv).wait_recv()
        grad_first = grad_v[c] + total(c, send_c, recv_c)
        normed = normed_v[c]
        add_sum(3, grad_first * normed)
        add_sum(4, grad_first)
        grad_res = rows_norm_back(grad_first, normed, inv_v[c], gain_one)
        grad_v[c] = grad_res
        one_copy(c).start()
        grad_att = grad_res.astype(jnp.bfloat16)
        att_v[c] = grad_att
        add_sum(5, grad_att.astype(jnp.float32))
        heads = dot(att_v[c], out_w[...]).astype(jnp.bfloat16)
        first, second = heads[:, : heads.shape[1] // 2], heads[:, heads.shape[1] // 2 :]
        keep_v[c] = jnp.where(half == 0, first, second)
        away_v[c] = jnp.where(half == 0, second, first)
        away_copy(c, half).start()
        keep_copy(c).start()

    early_tiles = early.shape[2] // tile

    def tile_copy(slot, row, index):
        target, column = index
        return pltpu.make_async_copy(
            tile_v.at[slot, pl.ds(row * quarter, quarter)],
            target.at[place ^ row, :, columns(column)],
            tile_sem.at[slot, row],
        )

    def weight_tile(count, target, column, left, right):
        slot = lax.rem(count, 2)

        @pl.when(count >= 2)
        def _():
            for row in range(4):
                tile_copy(slot, row, (target, column)).wait()

        tile_v[slot] = weight_part(left, right)
        for row in range(4):
            tile_copy(slot, row, (target, column)).start()

    @pl.loop(0, unit_tiles)
    def _(i):
        weight_tile(i, early, i, low_v, gate_v[:, :, columns(i)])

    @pl.loop(unit_tiles, early_tiles)
    def _(i):
        weight_tile(i, early, i, low_v, lift_v[:, :, columns(i - unit_tiles)])

    late_units = 2 * unit_tiles - early_tiles

    @pl.loop(0, late_units)
    def _(i):
        weight_tile(early_tiles + i, late, i, low_v, lift_v[:, :, columns(early_tiles - unit_tiles + i)])

    weight_tile(2 * unit_tiles, late, late_units, att_v, both_v[...])
    for slot in (0, 1):
        for row in range(4):
            tile_copy(slot, row, (late, 0)).wait()

    for i in range(unit_tiles):
        for other in (1, 2, 3):
            down_copy(i, other).wait_recv()
    own_rows = pl.ds(pl.multiple_of(place * quarter, quarter), quarter)
    down_got[0] = (
        down_v[own_rows, :].astype(jnp.float32)
        + down_got[0].astype(jnp.float32)
        + (down_got[1].astype(jnp.float32) + down_got[2].astype(jnp.float32))
    ).astype(jnp.bfloat16)
    down_out = pltpu.make_async_copy(down_got.at[0], down_sum, down_sem)
    down_out.start()

    def out_arrival(which):
        return remote(
            out_home.at[which, core], out_home.at[which, core], out_pass.at[which], out_recv.at[which], other_core
        )

    def out_share(which, whose):
        return remote(
            out_home.at[which, whose], out_home.at[which, whose], out_pass.at[which], out_took.at[which], other_core
        )

    for which in (0, 1):

        @pl.when(cot_owner(which) != stage)
        def _():
            out_arrival(which).wait_recv()
            out_share(which, core).start()

    down_out.wait()
    for which in (0, 1):
        far_copy(which).wait_send()
    for i in range(unit_tiles):
        for other in (1, 2, 3):
            down_copy(i, other).wait_send()

    @pl.loop(0, chunks)
    def _(c):
        pair_copy(c).wait_send()
        exchange(c, send_a, recv_a, a_send, a_recv).wait_send()
        exchange(c, send_b, recv_b, b_send, b_recv).wait_send()
        exchange(c, send_c, recv_c, c_send, c_recv).wait_send()
        one_copy(c).wait()
        keep_copy(c).wait()
        away_copy(c, half).wait_send()
        away_copy(c, 1 - half).wait_recv()

        @pl.when(home(c) == stage)
        def _():
            out_local(c).wait()

        @pl.when((home(c) != stage) & (c % 2 == core))
        def _():
            out_copy(c).wait_send()

    for which in (0, 1):

        @pl.when(cot_owner(which) != stage)
        def _():
            out_share(which, core).wait_send()
            out_share(which, 1 - core).wait_recv()


def middle(attended, sequence, cotangent, w_out, w_down, up_shards, vectors):
    chunks, rows, width = 4, sequence.shape[1], sequence.shape[2]
    head_width, units = w_out.shape[1], w_down.shape[1]
    tile = head_width
    early, late = 6 * tile, 2 * units + head_width - 6 * tile
    dma, bf16, f32 = pltpu.SemaphoreType.DMA, jnp.bfloat16, jnp.float32

    def vmem(shape, dtype=bf16):
        return pltpu.VMEM(shape, dtype)

    wide = (chunks, rows, width)
    inner = (chunks, rows, units)
    narrow_rows = (chunks, rows, head_width // 2)
    four, two = dma((chunks,)), dma((2,))
    return pl.pallas_call(
        middle_kernel,
        in_specs=[pl.BlockSpec(memory_space=pl.ANY)] * 8 + [pl.BlockSpec(memory_space=pltpu.VMEM)],
        out_specs=[pl.BlockSpec(memory_space=pl.ANY)] * 6 + [pl.BlockSpec(memory_space=pltpu.VMEM)],
        out_shape=[
            jax.ShapeDtypeStruct((2, 2, rows, width), bf16),
            jax.ShapeDtypeStruct(wide, f32),
            jax.ShapeDtypeStruct((2 * chunks, rows, head_width // 2), bf16),
            jax.ShapeDtypeStruct((4, width // 4, early), bf16),
            jax.ShapeDtypeStruct((4, width // 4, late), bf16),
            jax.ShapeDtypeStruct((width // 4, units), bf16),
            jax.ShapeDtypeStruct((8, width), f32),
        ],
        scratch_shapes=[
            vmem(wide), vmem(narrow_rows), vmem(narrow_rows), vmem((chunks, rows, head_width)),
            vmem((2, 2, rows, width)), vmem((width, head_width)), vmem((width, units)), vmem((width, 2 * units)),
            vmem(wide), vmem(wide), vmem(wide), vmem(wide), vmem(wide), vmem(wide),
            vmem(wide, f32), vmem((chunks, rows, 1), f32), vmem(wide),
            vmem(inner), vmem(inner), vmem(inner),
            vmem(wide, f32), vmem(wide), vmem(wide), vmem(wide), vmem(narrow_rows), vmem(narrow_rows),
            vmem((2, width, tile)), vmem((width, units)), vmem((3, width // 4, units)),
            dma((7,)), two, two, four, four, two, two, two, two,
            four, four, four, four, four, four, four, two, two, two,
            four, four, four, four, dma((2, 4)), dma((units // tile, 3)), dma((units // tile, 3)), dma,
        ],
        compiler_params=pltpu.CompilerParams(
            collective_id=1, has_side_effects=True, vmem_limit_bytes=60 << 20
        ),
        cost_estimate=pl.CostEstimate(flops=50 << 30, bytes_accessed=32 << 20, transcendentals=0),
        name="middle",
    )(attended, sequence, cotangent, w_out, w_down, *up_shards, vectors)


def tail_kernel(
    d_query, d_key, d_value, w_joined, sums_in, sequence, grad_one, early, late, moved_1, moved_2, moved_3,
    home, shard, joined, sums,
    token_v, one_v, part_v, late_v, project_v, own_v, tp_sent, tp_got, pair_sent, pair_got, final_v,
    summed_v, end_got, inner_v, mid_got, total_v, joined_v, quarter_got, cross_sent, cross_got, full_v,
    step_v, step_got,
    load_sem, late_send, late_recv, tp_send, tp_recv, pair_send, pair_recv, home_send, home_recv, home_pass, home_took, home_local,
    end_send, end_recv, mid_send, mid_recv, back_send, back_recv, shard_sem,
    quarter_send, quarter_recv, cross_send, cross_recv, half_send, half_recv, half_local, step_send, step_recv,
):
    place, stage, core = lax.axis_index("fsdp"), lax.axis_index("ctx"), lax.axis_index("tp")
    seq, half = stage // 2, stage % 2
    bf16, f32 = jnp.bfloat16, jnp.float32
    pieces = summed_v.shape[0]
    piece = summed_v.shape[2]
    quarter = joined_v.shape[0] // 4
    width = d_query.shape[2]

    barrier = pltpu.get_barrier_semaphore()
    peers = [(place ^ other, stage, core) for other in (1, 2, 3)]
    peers += [(place, lax.rem(stage + shift, 4), core) for shift in (1, 2, 3)]
    peers += [(place, stage, 1 - core)]
    for peer in peers:
        pl.semaphore_signal(barrier, inc=1, device_id=peer, device_id_type=MESH)
    pl.semaphore_wait(barrier, len(peers))

    def remote(source, target, send, recv, device):
        return pltpu.make_async_remote_copy(
            source, target, send, recv, device_id=device, device_id_type=MESH
        )

    other_core = (place, stage, 1 - core)
    partner = (place, stage ^ 1, core)
    at_end = (stage == 0) | (stage == 3)
    across = (place, jnp.where(at_end, stage, 3 - stage), core)
    inward = (place, jnp.where(stage < 2, 1, 2), core)
    outward = (place, jnp.where(stage < 2, 0, 3), core)

    loads = [
        pltpu.make_async_copy(source, part_v.at[index], load_sem.at[index])
        for index, source in enumerate((early.at[0], moved_1, moved_2, moved_3))
    ]
    loads.append(pltpu.make_async_copy(sequence, token_v, load_sem.at[4]))
    loads.append(pltpu.make_async_copy(grad_one, one_v, load_sem.at[5]))
    loads.append(pltpu.make_async_copy(late.at[0], late_v.at[0], load_sem.at[6]))

    def late_copy(other):
        return remote(
            late.at[other], late_v.at[other], late_send.at[other - 1], late_recv.at[other - 1],
            (place ^ other, stage, core),
        )

    for other in (1, 2, 3):
        late_copy(other).start()
    for load in loads:
        load.start()

    def input_share(chunk):
        rows = jnp.concatenate([d_query[chunk], d_key[chunk], d_value[chunk]], 1)
        project_v[chunk] = rows
        return dot(rows, w_joined[...], ((1,), (1,)))

    def block_of(i):
        return jnp.where(i < 2, 2 * (1 - half) + i, 2 * half + i - 2)

    def tp_copy(i):
        return remote(tp_sent.at[i], tp_got.at[i], tp_send.at[i], tp_recv.at[i], other_core)

    @pl.loop(0, 4)
    def _(i):
        block = block_of(i)
        tp_sent[i] = input_share(2 * block + 1 - core).astype(bf16)
        tp_copy(i).start()
        own_v[i] = input_share(2 * block + core)

    def pair_copy(i):
        return remote(pair_sent.at[i], pair_got.at[i], pair_send.at[i], pair_recv.at[i], partner)

    @pl.loop(0, 2)
    def _(i):
        tp_copy(i).wait_recv()
        pair_sent[i] = (own_v[i] + tp_got[i].astype(f32)).astype(bf16)
        pair_copy(i).start()

    def end_copy(j):
        return remote(summed_v.at[j], end_got.at[j], end_send.at[j], end_recv.at[j], inward)

    def mid_copy(j):
        return remote(inner_v.at[j], mid_got.at[j], mid_send.at[j], mid_recv.at[j], across)

    def columns(j):
        return pl.ds(j * piece, piece)

    def back_copy(j):
        return remote(total_v.at[j], shard.at[:, columns(j)], back_send.at[j], back_recv.at[j], outward)

    def shard_copy(j):
        return pltpu.make_async_copy(total_v.at[j], shard.at[:, columns(j)], shard_sem.at[j])

    def sum_piece(j, parts, first):
        terms = [parts[index, :, first : first + piece].astype(f32) for index in range(4)]
        summed_v[j] = (terms[0] + terms[1] + (terms[2] + terms[3])).astype(bf16)

        @pl.when(at_end)
        def _():
            end_copy(j).start()

    for load in loads[:4]:
        load.wait()
    for j in range(pieces - 1):
        sum_piece(j, part_v, j * piece)

    loads[4].wait()
    tokens = token_v[...].reshape(-1, token_v.shape[2])
    project = project_v[...].reshape(-1, project_v.shape[2])
    strip = 256
    for row in range(0, joined_v.shape[0], strip):
        joined_v[row : row + strip, :] = dot(
            tokens[:, row : row + strip], project, ((0,), (0,))
        ).astype(bf16)

    def quarter_copy(other):
        rows = pl.ds(pl.multiple_of((place ^ other) * quarter, quarter), quarter)
        return remote(
            joined_v.at[rows], quarter_got.at[other - 1], quarter_send.at[other - 1], quarter_recv.at[other - 1],
            (place ^ other, stage, core),
        )

    for other in (1, 2, 3):
        quarter_copy(other).start()

    def column_sum(grads):
        return jnp.sum(grads[...].reshape(-1, width).astype(f32), 0, keepdims=True)

    bias_parts = []
    for total in (column_sum(d_query), column_sum(d_value)):
        for which in (0, 1):
            bias_parts.append(jnp.where(half == which, total, 0.0))
    bias = jnp.concatenate(bias_parts, 1)
    step_v[0] = sums_in[...]
    step_v[0, 6:7, :] = bias
    steps = [(place ^ 1, stage, core), (place ^ 2, stage, core), partner, (place, stage ^ 2, core)]

    def step_copy(index):
        return remote(
            step_v.at[index], step_got.at[index], step_send.at[index], step_recv.at[index], steps[index]
        )

    def step_on(index):
        step_copy(index).wait_recv()
        step_v[index + 1] = step_v[index] + step_got[index]
        if index < 3:
            step_copy(index + 1).start()

    step_copy(0).start()
    loads[6].wait()
    for other in (1, 2, 3):
        late_copy(other).wait_recv()
    sum_piece(pieces - 1, late_v, 0)

    loads[5].wait()

    def home_copy(i):
        return remote(
            final_v.at[i], home.at[seq, core], home_send.at[i], home_recv.at[seq], (place, 2 * half + i, core)
        )

    def home_direct(i):
        return remote(final_v.at[i], home.at[seq, core], home_send.at[i], home_took.at[seq], other_core)

    def home_here(i):
        return pltpu.make_async_copy(final_v.at[i], home.at[seq, core], home_local)

    for i in range(2):
        tp_copy(i + 2).wait_recv()
        pair_copy(i).wait_recv()
        final_v[i] = (
            own_v[i + 2] + tp_got[i + 2].astype(f32) + pair_got[i].astype(f32) + one_v[2 * i + core]
        ).astype(bf16)

        @pl.when(2 * half + i == stage)
        def _():
            home_direct(i).start()
            home_here(i).start()

        @pl.when(2 * half + i != stage)
        def _():
            home_copy(i).start()

    step_on(0)
    for other in (1, 2, 3):
        quarter_copy(other).wait_recv()
    own_rows = pl.ds(pl.multiple_of(place * quarter, quarter), quarter)
    cross_sent[...] = (
        joined_v[own_rows, :].astype(f32)
        + quarter_got[0].astype(f32)
        + (quarter_got[1].astype(f32) + quarter_got[2].astype(f32))
    ).astype(bf16)
    cross_copy = remote(cross_sent, cross_got, cross_send, cross_recv, (place, stage ^ 2, core))
    cross_copy.start()
    step_on(1)

    def from_end(j):
        end_copy(j).wait_recv()
        inner_v[j] = (summed_v[j].astype(f32) + end_got[j].astype(f32)).astype(bf16)
        mid_copy(j).start()

    def from_mid(j):
        mid_copy(j).wait_recv()
        total_v[j] = (inner_v[j].astype(f32) + mid_got[j].astype(f32)).astype(bf16)
        back_copy(j).start()
        shard_copy(j).start()

    @pl.when(~at_end)
    def _():
        from_end(0)
        for j in range(1, pieces):
            from_end(j)
            from_mid(j - 1)

    step_on(2)
    cross_copy.wait_recv()
    full_v[...] = (cross_sent[...].astype(f32) + cross_got[...].astype(f32)).astype(bf16)
    half_copy = remote(full_v, joined.at[half], half_send, half_recv, partner)
    half_copy.start()
    half_here = pltpu.make_async_copy(full_v, joined.at[half], half_local)
    half_here.start()
    step_on(3)
    sums[...] = step_v[4]

    def home_arrival(which):
        return remote(
            home.at[which, core], home.at[which, core], home_pass.at[which], home_recv.at[which], other_core
        )

    def home_share(which, whose):
        return remote(
            home.at[which, whose], home.at[which, whose], home_pass.at[which], home_took.at[which], other_core
        )

    for which in (0, 1):

        @pl.when(2 * which + stage // 2 != stage)
        def _():
            home_arrival(which).wait_recv()
            home_share(which, core).start()

    @pl.when(~at_end)
    def _():
        from_mid(pieces - 1)
        for j in range(pieces):
            mid_copy(j).wait_send()
            back_copy(j).wait_send()
            shard_copy(j).wait()

    @pl.when(at_end)
    def _():
        for j in range(pieces):
            end_copy(j).wait_send()
            back_copy(j).wait_recv()

    for i in range(4):
        tp_copy(i).wait_send()
        step_copy(i).wait_send()
    for i in range(2):
        pair_copy(i).wait_send()

        @pl.when(2 * half + i == stage)
        def _():
            home_direct(i).wait_send()
            home_here(i).wait()

        @pl.when(2 * half + i != stage)
        def _():
            home_copy(i).wait_send()

    for which in (0, 1):

        @pl.when(2 * which + stage // 2 != stage)
        def _():
            home_share(which, core).wait_send()

        home_share(which, 1 - core).wait_recv()
    for other in (1, 2, 3):
        quarter_copy(other).wait_send()
        late_copy(other).wait_send()
    cross_copy.wait_send()
    half_here.wait()
    half_copy.wait_send()
    remote(full_v, joined.at[1 - half], half_send, half_recv, partner).wait_recv()


def tail(d_query, d_key, d_value, w_joined, sums, sequence, grad_one, early, late, moved):
    rows, width = sequence.shape[1:]
    quarter, piece = late.shape[1:]
    columns = early.shape[2] + piece
    joined = w_joined.shape[1]
    pieces = columns // piece
    dma, bf16, f32 = pltpu.SemaphoreType.DMA, jnp.bfloat16, jnp.float32

    def vmem(shape, dtype=bf16):
        return pltpu.VMEM(shape, dtype)

    any_spec, vmem_spec = pl.BlockSpec(memory_space=pl.ANY), pl.BlockSpec(memory_space=pltpu.VMEM)
    cut = (pieces, quarter, piece)
    one, two, three, four = dma, dma((2,)), dma((3,)), dma((4,))
    return pl.pallas_call(
        tail_kernel,
        in_specs=[vmem_spec] * 5 + [any_spec] * 7,
        out_specs=[any_spec] * 3 + [vmem_spec],
        out_shape=[
            jax.ShapeDtypeStruct((2, 2, rows, width), bf16),
            jax.ShapeDtypeStruct((quarter, columns), bf16),
            jax.ShapeDtypeStruct((2, quarter, joined), bf16),
            jax.ShapeDtypeStruct(sums.shape, f32),
        ],
        scratch_shapes=[
            vmem(sequence.shape), vmem(grad_one.shape, f32), vmem(early.shape), vmem(late.shape),
            vmem((8, rows, joined)), vmem((4, rows, width), f32),
            vmem((4, rows, width)), vmem((4, rows, width)), vmem((2, rows, width)), vmem((2, rows, width)),
            vmem((2, rows, width)),
            vmem(cut), vmem(cut), vmem(cut), vmem(cut), vmem(cut),
            vmem((width, joined)), vmem((3, quarter, joined)), vmem((quarter, joined)), vmem((quarter, joined)),
            vmem((quarter, joined)),
            vmem((5,) + sums.shape, f32), vmem((4,) + sums.shape, f32),
            dma((7,)), three, three, four, four, two, two, two, two, two, two, one,
            three, three, three, three, three, three, three,
            three, three, one, one, one, one, one, four, four,
        ],
        compiler_params=pltpu.CompilerParams(
            collective_id=2, has_side_effects=True, vmem_limit_bytes=60 << 20
        ),
        cost_estimate=pl.CostEstimate(flops=80 << 30, bytes_accessed=32 << 20, transcendentals=0),
        name="tail",
    )(d_query, d_key, d_value, w_joined, sums, sequence, grad_one, early, late, *moved)


def pick(pair, index):
    return lax.dynamic_index_in_dim(pair, index, 0, keepdims=False)


def per_device_paired(
    tokens,
    doc_lengths,
    keep,
    w_query,
    b_query,
    w_key,
    w_value,
    b_value,
    w_out,
    b_out,
    gain_one,
    shift_one,
    w_up,
    w_down,
    b_down,
    gain_two,
    shift_two,
    cotangent,
):
    _, block_rows, model_width = tokens.shape
    length = 4 * block_rows
    half_rows = block_rows // 2
    local_heads = b_query.shape[0] // HEAD
    heads = local_heads // 2
    width = heads * HEAD
    place = lax.axis_index("fsdp")
    stage = lax.axis_index("ctx")
    core = lax.axis_index("tp")
    seq, half = stage // 2, stage % 2

    def core_half(array):
        return lax.dynamic_slice_in_dim(array, core * half_rows, half_rows, 1)

    def own_columns(array):
        return lax.dynamic_slice_in_dim(array, half * width, width, array.ndim - 1)

    w_joined = jnp.concatenate([own_columns(w_query), own_columns(w_key), own_columns(w_value)], -1)
    sequence, keep_all, full_joined, full_out, full_down = start(tokens, keep, w_joined, w_out, w_down)
    sequence = sequence.reshape(length, model_width)
    full_joined = full_joined.reshape(model_width, 3 * width)
    full_out = full_out.reshape(model_width, 2 * width)
    full_down = full_down.reshape(model_width, -1)
    keep_row = lax.dynamic_index_in_dim(keep_all, seq, 1, keepdims=False).reshape(length)

    bounds = jnp.cumsum(pick(doc_lengths, seq))
    docs = bounds.shape[0]
    positions = jnp.arange(length, dtype=jnp.int32)
    segments = jnp.sum((bounds[None, :] <= positions[:, None]).astype(jnp.int32), -1)
    starts = jnp.concatenate([jnp.zeros((1,), jnp.int32), bounds[:-1]])
    firsts = segments[:: TILE]
    lasts = segments[TILE - 1 :: TILE]
    doc_index = jnp.arange(docs, dtype=jnp.int32)
    span_from = jnp.sum(jnp.where(firsts[:, None] == doc_index, starts, 0), -1) // TILE
    span_to = (jnp.sum(jnp.where(lasts[:, None] == doc_index, bounds, 0), -1) + TILE - 1) // TILE
    spans = jnp.stack([span_from, span_to]).astype(jnp.int32)
    slopes = head_slopes(core * local_heads + half * heads, heads)
    feature = jnp.arange(LANES, dtype=jnp.int32)
    key_doc = jnp.where(segments[:, None] == feature - DOC_ROW, 0.0, MASKED)
    pos_high = (positions // 256 * 256).astype(jnp.float32)[:, None]
    pos_low = (positions % 256).astype(jnp.float32)[:, None]
    key_feat = jnp.where(feature < DOC_ROW, 0.0, 1.0)[None, :]
    key_feat = jnp.where((feature >= DOC_ROW) & (feature < DOC_ROW + docs), key_doc, key_feat)
    key_feat = jnp.where(feature == KEEP_ROW, jnp.where(keep_row == 1, 0.0, MASKED)[:, None], key_feat)
    key_feat = jnp.where((feature >= POS_ROW) & (feature < POS_ROW + 3), pos_high, key_feat)
    key_feat = jnp.where((feature >= POS_ROW + 3) & (feature < LINE_ROW), pos_low, key_feat)
    key_feat = jnp.where(feature >= FEAT_END, 0.0, key_feat).astype(jnp.bfloat16)
    rows = feature[None, :, None]
    query_feat = jnp.where(segments[None, None, :] == rows - DOC_ROW, 1.0, 0.0)
    query_feat = jnp.where(rows == KEEP_ROW, 1.0, query_feat)
    slope_terms = three_terms(slopes[:, None, None], narrow)
    line_terms = three_terms(
        -slopes[:, None, None] * positions.astype(jnp.float32)[None, None, :], narrow
    )
    for term in range(3):
        here = (rows == POS_ROW + term) | (rows == POS_ROW + 3 + term)
        query_feat = jnp.where(here, slope_terms[term], query_feat)
        query_feat = jnp.where(rows == LINE_ROW + term, line_terms[term], query_feat)
    query_feat = query_feat.astype(jnp.bfloat16)

    up_own, full_joined = lax.optimization_barrier((w_up.reshape(w_up.shape[0], -1), full_joined))
    up_shards = [up_own] + [lax.ppermute(up_own, "fsdp", swap) for swap in (X_SWAP, Y_SWAP)]

    bias = jnp.concatenate([own_columns(b_query), jnp.zeros((width,), jnp.float32), own_columns(b_value)])
    pad = -3 * width % LANES
    query_t, queries, keys, keys_t, values, values_t = project(
        sequence,
        jnp.pad(full_joined, ((0, 0), (0, pad))),
        jnp.pad(bias, (0, pad))[None],
        key_feat,
        query_feat,
        heads,
    )
    attended_all, attended_t, lse = attend(spans, slopes, query_t, keys, values_t)

    row_count = length // 2
    vectors = jnp.stack([b_out, gain_one, shift_one, b_down, gain_two, shift_two, b_out, b_out])
    out, grad_one, grad_heads, early, late, down_sum, sums = middle(
        attended_all.reshape(8, half_rows, width),
        sequence.reshape(8, half_rows, model_width),
        cotangent.reshape(2, 2, half_rows, model_width),
        full_out,
        full_down,
        up_shards,
        vectors,
    )
    out = out.reshape(2, block_rows, model_width)
    grad_heads = grad_heads.reshape(length, width)
    moved = [
        lax.ppermute(early[other], "fsdp", swap)
        for other, swap in ((1, X_SWAP), (2, Y_SWAP), (3, D_SWAP))
    ]
    d_query, d_key, d_value = attend_back(
        spans, slopes, query_t, queries, keys, keys_t, values, grad_heads, attended_t, lse
    )
    d_tokens, shard, joined, sums = tail(
        d_query.reshape(8, half_rows, width),
        d_key.reshape(8, half_rows, width),
        d_value.reshape(8, half_rows, width),
        full_joined,
        sums,
        sequence.reshape(8, half_rows, model_width),
        grad_one,
        early,
        late,
        moved,
    )
    d_tokens = d_tokens.reshape(2, block_rows, model_width).astype(jnp.float32)
    sum_up, sum_out = jnp.split(shard.astype(jnp.float32), (2 * w_up.shape[2],), 1)
    sum_up = sum_up.reshape(w_up.shape)
    sum_down = lax.psum(down_sum, "ctx").astype(jnp.float32)
    joined = joined.astype(jnp.float32)

    def both_halves(first):
        return jnp.concatenate(
            [joined[0, :, first : first + width], joined[1, :, first : first + width]], -1
        )

    total_gain_two, total_shift_two, total_b_down, total_gain_one, total_shift_one, total_b_out = sums[:6]
    total_bias = sums[6].reshape(2, 2 * width)
    return (
        out,
        d_tokens,
        both_halves(0),
        total_bias[0],
        both_halves(width),
        both_halves(2 * width),
        total_bias[1],
        sum_out,
        total_b_out,
        total_gain_one,
        total_shift_one,
        sum_up,
        sum_down,
        total_b_down,
        total_gain_two,
        total_shift_two,
    )


def paired(mesh, tokens, doc_lengths, b_query):
    sizes = dict(mesh.shape)
    return (
        sizes == {"fsdp": 4, "ctx": 4, "tp": 2}
        and tokens.shape[0] == 8
        and tokens.shape[1] % (8 * TILE) == 0
        and doc_lengths.shape[1] <= KEEP_ROW - DOC_ROW
        and b_query.shape[0] % (4 * HEAD) == 0
    )


def solution(mesh):
    in_specs = (
        P("fsdp", "ctx", None),
        P("fsdp", None),
        P("fsdp", "ctx"),
        P("fsdp", "tp"),
        P("tp"),
        P("fsdp", "tp"),
        P("fsdp", "tp"),
        P("tp"),
        P("fsdp", "tp"),
        P(),
        P(),
        P(),
        P("fsdp", None, "tp"),
        P("fsdp", "tp"),
        P(),
        P(),
        P(),
        P("fsdp", "ctx", None),
    )
    out_specs = (
        P("fsdp", "ctx", None),
        P("fsdp", "ctx", None),
        P("fsdp", "tp"),
        P("tp"),
        P("fsdp", "tp"),
        P("fsdp", "tp"),
        P("tp"),
        P("fsdp", "tp"),
        P(),
        P(),
        P(),
        P("fsdp", None, "tp"),
        P("fsdp", "tp"),
        P(),
        P(),
        P(),
    )

    def whole(*args):
        body = per_device_paired if paired(mesh, args[0], args[1], args[4]) else per_device_general
        return jax.shard_map(
            body, mesh=mesh, in_specs=in_specs, out_specs=out_specs, check_vma=False
        )(*args)

    return whole
```

```python
import functools

import jax
import jax.numpy as jnp
from jax import lax
from jax.experimental import pallas as pl
from jax.experimental.pallas import tpu as pltpu
from jax.sharding import PartitionSpec as P

HEAD = 64


NORM_EPS = 1e-12
MASKED = -1e30


def layer_norm(residual, norm_gain, norm_shift):
    centered = residual - jnp.mean(residual, -1, keepdims=True)
    inv_scale = lax.rsqrt(jnp.mean(centered * centered, -1, keepdims=True) + NORM_EPS)
    normed = centered * inv_scale
    return (normed * norm_gain + norm_shift, normed, inv_scale)


def norm_back(grad_out, normed, inv_scale, norm_gain):
    grad_norm = grad_out * norm_gain
    mean_grad = jnp.mean(grad_norm, -1, keepdims=True)
    mean_cross = jnp.mean(grad_norm * normed, -1, keepdims=True)
    grad_in = (grad_norm - mean_grad - normed * mean_cross) * inv_scale
    return (grad_in, jnp.sum(grad_out * normed, 0), jnp.sum(grad_out, 0))


def head_slopes(first_head, head_count):
    head_index = first_head + jnp.arange(head_count, dtype=jnp.int32)
    head_float = head_index.astype(jnp.float32)
    return jnp.where(head_index < 8, jnp.exp2(-(head_float + 1.0)), jnp.exp2(-(head_float - 7.5)))


def segment_ids(lengths, positions):
    bounds = jnp.cumsum(lengths, -1)
    return jnp.sum((bounds[:, None, :] <= positions[None, :, None]).astype(jnp.int32), -1)


def score_block(query_heads, query_pos, query_seg, key_heads, key_pos, key_seg, key_keep, slopes):
    scores = (
        jnp.einsum("sqhd,skhd->shqk", query_heads, key_heads, preferred_element_type=jnp.float32)
        * 0.125
    )
    distance = jnp.abs(query_pos[:, None] - key_pos[None, :]).astype(jnp.float32)
    scores = scores - slopes[None, :, None, None] * distance[None, None]
    same_doc = query_seg[:, None, :, None] == key_seg[:, None, None, :]
    visible = (key_keep[:, None, None, :] == 1) | (query_pos[:, None] == key_pos[None, :])[
        None, None
    ]
    return (scores, same_doc & visible)


def grad_block(
    query_heads,
    query_pos,
    query_seg,
    grad_heads,
    log_total,
    delta,
    key_heads,
    value_heads,
    key_pos,
    key_seg,
    key_keep,
    slopes,
):
    scores, allowed = score_block(
        query_heads, query_pos, query_seg, key_heads, key_pos, key_seg, key_keep, slopes
    )
    probs = jnp.where(allowed, jnp.exp(scores - log_total[..., None]), 0.0)
    grad_probs = jnp.einsum(
        "sqhd,skhd->shqk", grad_heads, value_heads, preferred_element_type=jnp.float32
    )
    grad_scores = (probs * (grad_probs - delta[..., None])).astype(jnp.bfloat16)
    grad_query = (
        jnp.einsum("shqk,skhd->sqhd", grad_scores, key_heads, preferred_element_type=jnp.float32)
        * 0.125
    )
    grad_key = (
        jnp.einsum("shqk,sqhd->skhd", grad_scores, query_heads, preferred_element_type=jnp.float32)
        * 0.125
    )
    grad_value = jnp.einsum(
        "shqk,sqhd->skhd",
        probs.astype(jnp.bfloat16),
        grad_heads,
        preferred_element_type=jnp.float32,
    )
    return (grad_query, grad_key, grad_value)


def intersections(query_seg, key_seg):
    return jnp.any((key_seg[:, 0] <= query_seg[:, -1]) & (key_seg[:, -1] >= query_seg[:, 0]))


def guarded(active, update, current):
    return lax.cond(active, update, lambda untouched: untouched, current)


def over_blocks(length, advance, current):
    block_len = 512
    block_count = length // block_len
    return lax.fori_loop(
        0,
        block_count,
        lambda block_index, running: advance(running, block_index * block_len, block_len),
        current,
    )


def per_device_general(
    tokens,
    doc_lengths,
    keep,
    w_query,
    b_query,
    w_key,
    w_value,
    b_value,
    w_out,
    b_out,
    gain_one,
    shift_one,
    w_up,
    w_down,
    b_down,
    gain_two,
    shift_two,
    cotangent,
):
    seq_count, block_rows, model_width = tokens.shape
    local_heads = b_query.shape[0] // HEAD
    head_width = local_heads * HEAD
    row_count = seq_count * block_rows
    slopes = head_slopes(lax.axis_index("tp") * local_heads, local_heads)
    own_pos = lax.axis_index("ctx") * block_rows + jnp.arange(block_rows, dtype=jnp.int32)
    own_seg = segment_ids(doc_lengths, own_pos)
    token_rows = tokens.reshape(row_count, model_width)
    full_query, full_key, full_value, full_out = (
        lax.all_gather(w_query, "fsdp", axis=0, tiled=True),
        lax.all_gather(w_key, "fsdp", axis=0, tiled=True),
        lax.all_gather(w_value, "fsdp", axis=0, tiled=True),
        lax.all_gather(w_out, "fsdp", axis=0, tiled=True),
    )
    queries = (
        jnp.dot(token_rows, full_query, preferred_element_type=jnp.float32) + b_query
    ).astype(jnp.bfloat16)
    key_rows = jnp.dot(token_rows, full_key, preferred_element_type=jnp.float32).astype(
        jnp.bfloat16
    )
    values = (jnp.dot(token_rows, full_value, preferred_element_type=jnp.float32) + b_value).astype(
        jnp.bfloat16
    )
    query_heads = queries.reshape(seq_count, block_rows, local_heads, HEAD)
    key_value = jnp.concatenate([key_rows, values], -1).reshape(
        seq_count, block_rows, 2 * head_width
    )

    def split_pairs(slab_pairs, block_len):
        return (
            slab_pairs[..., :head_width].reshape(seq_count, block_len, local_heads, HEAD),
            slab_pairs[..., head_width:].reshape(seq_count, block_len, local_heads, HEAD),
        )

    def key_slab(pairs, piece_keep, offset, block_len):
        slab_pairs = lax.dynamic_slice_in_dim(pairs, offset, block_len, 1)
        slab_keep = lax.dynamic_slice_in_dim(piece_keep, offset, block_len, 1)
        key_pos = offset + jnp.arange(block_len, dtype=jnp.int32)
        key_seg = segment_ids(doc_lengths, key_pos)
        slab_keys, slab_values = split_pairs(slab_pairs, block_len)
        return (slab_keys, slab_values, slab_keep, key_pos, key_seg)

    start_state = (
        jnp.full((seq_count, local_heads, block_rows), MASKED, jnp.float32),
        jnp.zeros((seq_count, local_heads, block_rows), jnp.float32),
        jnp.zeros((seq_count, local_heads, block_rows, HEAD), jnp.float32),
    )
    pairs = lax.all_gather(key_value, "ctx", axis=1, tiled=True)
    piece_keep = lax.all_gather(keep, "ctx", axis=1, tiled=True)

    def advance(partial_value, offset, block_len):
        slab_keys, slab_values, slab_keep, key_pos, key_seg = key_slab(
            pairs, piece_keep, offset, block_len
        )

        def update(current):
            row_max, row_sum, weighted = current
            scores, allowed = score_block(
                query_heads, own_pos, own_seg, slab_keys, key_pos, key_seg, slab_keep, slopes
            )
            scores = jnp.where(allowed, scores, MASKED)
            new_max = jnp.maximum(row_max, jnp.max(scores, -1))
            factor = jnp.exp(row_max - new_max)
            weights = jnp.where(allowed, jnp.exp(scores - new_max[..., None]), 0.0)
            row_sum = row_sum * factor + jnp.sum(weights, -1)
            weighted = weighted * factor[..., None] + jnp.einsum(
                "shqk,skhd->shqd",
                weights.astype(jnp.bfloat16),
                slab_values,
                preferred_element_type=jnp.float32,
            )
            return (new_max, row_sum, weighted)

        return guarded(intersections(own_seg, key_seg), update, partial_value)

    row_max, row_sum, weighted = over_blocks(pairs.shape[1], advance, start_state)
    attended = (
        (weighted / row_sum[..., None])
        .transpose(0, 2, 1, 3)
        .reshape(row_count, head_width)
        .astype(jnp.bfloat16)
    )
    log_total = row_max + jnp.log(row_sum)
    att_part = jnp.einsum("rh,dh->rd", attended, full_out, preferred_element_type=jnp.float32)
    branch_att = lax.psum(att_part.astype(jnp.bfloat16), "tp").astype(jnp.float32) + b_out
    first_out, normed_one, inv_one = layer_norm(
        token_rows.astype(jnp.float32) + branch_att, gain_one, shift_one
    )
    first_low = first_out.astype(jnp.bfloat16)
    full_up, full_down = (
        lax.all_gather(w_up, "fsdp", axis=0, tiled=True),
        lax.all_gather(w_down, "fsdp", axis=0, tiled=True),
    )
    gate_up = jnp.einsum("rd,dcf->rcf", first_low, full_up, preferred_element_type=jnp.float32)
    product, gelu_back = jax.vjp(
        lambda gate_part, up_part: jax.nn.gelu(gate_part, approximate=False) * up_part,
        gate_up[:, 0],
        gate_up[:, 1],
    )
    hidden = product.astype(jnp.bfloat16)
    ffn_part = jnp.einsum("rf,df->rd", hidden, full_down, preferred_element_type=jnp.float32)
    branch_ffn = lax.psum(ffn_part.astype(jnp.bfloat16), "tp").astype(jnp.float32) + b_down
    result, normed_two, inv_two = layer_norm(first_out + branch_ffn, gain_two, shift_two)
    grad_in = cotangent.reshape(row_count, model_width).astype(jnp.float32)
    grad_two, d_gain_two, d_shift_two = norm_back(grad_in, normed_two, inv_two, gain_two)
    grad_ffn = grad_two.astype(jnp.bfloat16)
    d_b_down = jnp.sum(grad_ffn.astype(jnp.float32), 0)
    d_w_down = jnp.einsum("rd,rf->df", grad_ffn, hidden, preferred_element_type=jnp.float32)
    grad_hidden = jnp.einsum("rd,df->rf", grad_ffn, full_down, preferred_element_type=jnp.float32)
    grad_gate, grad_up = gelu_back(grad_hidden)
    grad_gate_up = jnp.stack([grad_gate, grad_up], 1).astype(jnp.bfloat16)
    d_w_up = jnp.einsum("rd,rcf->dcf", first_low, grad_gate_up, preferred_element_type=jnp.float32)
    first_part = jnp.einsum(
        "rcf,dcf->rd", grad_gate_up, full_up, preferred_element_type=jnp.float32
    )
    grad_first = grad_two + lax.psum(first_part.astype(jnp.bfloat16), "tp").astype(jnp.float32)
    grad_one, d_gain_one, d_shift_one = norm_back(grad_first, normed_one, inv_one, gain_one)
    grad_att = grad_one.astype(jnp.bfloat16)
    d_b_out = jnp.sum(grad_att.astype(jnp.float32), 0)
    d_w_out = jnp.einsum("rd,rh->dh", grad_att, attended, preferred_element_type=jnp.float32)
    grad_attended = jnp.einsum(
        "rd,dh->rh", grad_att, full_out, preferred_element_type=jnp.float32
    ).astype(jnp.bfloat16)
    grad_heads = grad_attended.reshape(seq_count, block_rows, local_heads, HEAD)
    delta = jnp.einsum(
        "sqhd,sqhd->shq",
        grad_heads,
        attended.reshape(seq_count, block_rows, local_heads, HEAD),
        preferred_element_type=jnp.float32,
    )
    query_zero = jnp.zeros((seq_count, block_rows, local_heads, HEAD), jnp.float32)
    full_len = block_rows * lax.axis_size("ctx")
    term_zero = jnp.zeros((seq_count, full_len, 2 * head_width), jnp.float32)
    return_pairs = lax.all_gather(key_value, "ctx", axis=1, tiled=True)
    return_piece_keep = lax.all_gather(keep, "ctx", axis=1, tiled=True)

    def advance(partial_value, offset, block_len):
        slab_keys, slab_values, slab_keep, key_pos, key_seg = key_slab(
            return_pairs, return_piece_keep, offset, block_len
        )

        def update(current):
            query_grad, key_terms = current
            part_query, part_key, part_value = grad_block(
                query_heads,
                own_pos,
                own_seg,
                grad_heads,
                log_total,
                delta,
                slab_keys,
                slab_values,
                key_pos,
                key_seg,
                slab_keep,
                slopes,
            )
            slab_grads = jnp.concatenate(
                [
                    part_key.reshape(seq_count, block_len, head_width),
                    part_value.reshape(seq_count, block_len, head_width),
                ],
                -1,
            )
            return (
                query_grad + part_query,
                lax.dynamic_update_slice_in_dim(key_terms, slab_grads, offset, 1),
            )

        return guarded(intersections(own_seg, key_seg), update, partial_value)

    query_grad, key_terms = over_blocks(return_pairs.shape[1], advance, (query_zero, term_zero))
    pair_grads = lax.psum_scatter(
        key_terms.astype(jnp.bfloat16), "ctx", scatter_dimension=1, tiled=True
    ).astype(jnp.float32)
    query_low = query_grad.reshape(row_count, head_width).astype(jnp.bfloat16)
    pair_low = pair_grads.reshape(row_count, 2 * head_width).astype(jnp.bfloat16)
    grad_project = jnp.concatenate([query_low, pair_low], -1)
    joined_weights = jnp.concatenate([full_query, full_key, full_value], -1)
    joined_grads = jnp.einsum(
        "rd,rh->dh", token_rows, grad_project, preferred_element_type=jnp.float32
    )
    input_part = jnp.einsum(
        "rh,dh->rd", grad_project, joined_weights, preferred_element_type=jnp.float32
    )
    d_tokens = grad_one + lax.psum(input_part.astype(jnp.bfloat16), "tp").astype(jnp.float32)
    d_b_query = jnp.sum(query_low.astype(jnp.float32), 0)
    d_b_value = jnp.sum(pair_low[:, head_width:].astype(jnp.float32), 0)
    d_w_query = joined_grads[:, :head_width]
    d_w_key = joined_grads[:, head_width : 2 * head_width]
    d_w_value = joined_grads[:, 2 * head_width :]
    shard_grads = (
        lax.psum_scatter(
            d_w_query.astype(jnp.bfloat16), "fsdp", scatter_dimension=0, tiled=True
        ).astype(jnp.float32),
        lax.psum_scatter(
            d_w_key.astype(jnp.bfloat16), "fsdp", scatter_dimension=0, tiled=True
        ).astype(jnp.float32),
        lax.psum_scatter(
            d_w_value.astype(jnp.bfloat16), "fsdp", scatter_dimension=0, tiled=True
        ).astype(jnp.float32),
        lax.psum_scatter(
            d_w_out.astype(jnp.bfloat16), "fsdp", scatter_dimension=0, tiled=True
        ).astype(jnp.float32),
        lax.psum_scatter(
            d_w_up.astype(jnp.bfloat16), "fsdp", scatter_dimension=0, tiled=True
        ).astype(jnp.float32),
        lax.psum_scatter(
            d_w_down.astype(jnp.bfloat16), "fsdp", scatter_dimension=0, tiled=True
        ).astype(jnp.float32),
    )
    sum_query, sum_key, sum_value, sum_out, sum_up, sum_down = (
        lax.psum(shard_grads[0].astype(jnp.bfloat16), "ctx").astype(jnp.float32),
        lax.psum(shard_grads[1].astype(jnp.bfloat16), "ctx").astype(jnp.float32),
        lax.psum(shard_grads[2].astype(jnp.bfloat16), "ctx").astype(jnp.float32),
        lax.psum(shard_grads[3].astype(jnp.bfloat16), "ctx").astype(jnp.float32),
        lax.psum(shard_grads[4].astype(jnp.bfloat16), "ctx").astype(jnp.float32),
        lax.psum(shard_grads[5].astype(jnp.bfloat16), "ctx").astype(jnp.float32),
    )
    (
        total_b_query,
        total_b_value,
        total_b_out,
        total_b_down,
        total_gain_one,
        total_shift_one,
        total_gain_two,
        total_shift_two,
    ) = lax.psum(
        (d_b_query, d_b_value, d_b_out, d_b_down, d_gain_one, d_shift_one, d_gain_two, d_shift_two),
        ("fsdp", "ctx"),
    )
    return (
        result.reshape(seq_count, block_rows, model_width).astype(jnp.bfloat16),
        d_tokens.reshape(seq_count, block_rows, model_width),
        sum_query,
        total_b_query,
        sum_key,
        sum_value,
        total_b_value,
        sum_out,
        total_b_out,
        total_gain_one,
        total_shift_one,
        sum_up,
        sum_down,
        total_b_down,
        total_gain_two,
        total_shift_two,
    )


LANES = 128
VMEM_BYTES = 60 << 20
MESH = pl.DeviceIdType.MESH
TILE = 256
DOC_ROW, KEEP_ROW, POS_ROW, LINE_ROW, LOG_ROW, FEAT_END = 64, 72, 73, 79, 82, 85
X_SWAP = [(0, 1), (1, 0), (2, 3), (3, 2)]
Y_SWAP = [(0, 2), (2, 0), (1, 3), (3, 1)]
D_SWAP = [(0, 3), (3, 0), (1, 2), (2, 1)]


def dot(left, right, dims=((1,), (0,))):
    return lax.dot_general(left, right, (dims, ((), ())), preferred_element_type=jnp.float32)


def three_terms(value, low):
    high = low(value)
    middle = low(value - high)
    return high, middle, low(value - high - middle)


def side_signs(rows):
    sub = lax.broadcasted_iota(jnp.int32, (LANES, rows), 0)
    bias_rows = (sub >= POS_ROW) & (sub < LOG_ROW)
    after = jnp.where(bias_rows, -1.0, 1.0).astype(jnp.bfloat16)
    same = jnp.where(bias_rows, 0.0, 1.0).astype(jnp.bfloat16)
    bare = jnp.where(bias_rows | (sub == KEEP_ROW), 0.0, 1.0).astype(jnp.bfloat16)
    return after, same, bare


def diagonal_scores(keys, query_t, same, bare, slope):
    rows = lax.broadcasted_iota(jnp.int32, (TILE, TILE), 0)
    cols = lax.broadcasted_iota(jnp.int32, (TILE, TILE), 1)
    apart = jnp.abs(rows - cols)
    full = dot(keys, query_t * same) - slope * apart.astype(jnp.float32)
    return jnp.where(apart == 0, dot(keys, query_t * bare), full)


def sweep(first, last, step, most=2):
    many = (last - first) // most

    @pl.loop(0, many)
    def _(i):
        step(first + i * most, most)

    @pl.loop(first + many * most, last)
    def _(tile):
        step(tile, 1)


def doc_bounds(docs_ref, seq):
    bounds, total = [], 0
    for index in range(docs_ref.shape[1]):
        total = total + docs_ref[seq, index]
        bounds.append(total)
    return bounds


def tile_span(docs_ref, seq, block):
    first, last = block * TILE, block * TILE + TILE - 1
    begin = end = start = 0
    for bound in doc_bounds(docs_ref, seq):
        begin = jnp.where(bound <= first, bound, begin)
        end = jnp.where(start <= last, bound, end)
        start = bound
    return lax.div(begin, TILE), lax.div(end + TILE - 1, TILE)


def start_kernel(
    docs, slopes, tokens, keep, w_query, w_key, w_value, w_out, w_down, b_query, b_value, w_up,
    sequence, full_joined, full_out, full_down, up_flat, query_t, queries, keys, keys_t, values, values_t,
    tokens_v, own_v, joined_v, keep_v, up_v, qt_v, q_v, k_v, kt_v, v_v, vt_v,
    z_send, z_recv, tp_send, tp_recv, w_send, w_recv, down_send, down_recv, keep_send, keep_recv, local_sem,
    block_sem, joined_sem, up_sem, out_sem,
):
    place, stage, core = lax.axis_index("fsdp"), lax.axis_index("ctx"), lax.axis_index("tp")
    seq, half = stage // 2, stage % 2
    half_rows, model_width = sequence.shape[2:]
    rows_of = 2 * half_rows
    heads = qt_v.shape[1]
    width = heads * HEAD
    f32, bf16 = jnp.float32, jnp.bfloat16
    barrier = pltpu.get_barrier_semaphore()
    peers = [(place ^ other, stage, core) for other in (1, 2, 3)]
    peers += [(place, lax.rem(stage + shift, 4), core) for shift in (1, 2, 3)]
    peers += [(place, stage, 1 - core)]
    for peer in peers:
        pl.semaphore_signal(barrier, inc=1, device_id=peer, device_id_type=MESH)

    def columns_of(weight):
        return jnp.where(half == 0, weight[:, :width], weight[:, width:])

    own_v[...] = jnp.concatenate([columns_of(w[...]) for w in (w_query, w_key, w_value)], 1)
    joined_v[place] = own_v[...]
    tokens_v[stage] = tokens[seq].reshape(2, half_rows, model_width)
    keep_v[stage] = keep[...]
    pl.semaphore_wait(barrier, len(peers))

    def remote(source, target, send, recv, device):
        return pltpu.make_async_remote_copy(
            source, target, send, recv, device_id=device, device_id_type=MESH
        )

    rows = pl.ds(pl.multiple_of(core * half_rows, half_rows), half_rows)
    ours, theirs = tokens.at[seq, rows], tokens.at[1 - seq, rows]
    other_core = (place, stage, 1 - core)
    inner = (stage == 1) | (stage == 2)
    facing, opposite = 3 - stage, stage ^ 2

    def send(source, block, target, slot):
        return remote(source, tokens_v.at[block, core], z_send.at[slot], z_recv.at[block], (place, target, core))

    def arrival(block):
        return remote(ours, tokens_v.at[block, core], z_send.at[0], z_recv.at[block], other_core)

    def share(block, whose):
        half_block = tokens_v.at[block, whose]
        return remote(half_block, half_block, tp_send.at[block], tp_recv.at[block], other_core)

    to_pair = send(ours, stage, stage ^ 1, 0)
    to_facing = send(theirs, stage, facing, 1)
    to_opposite = send(theirs, stage, opposite, 2)
    to_facing.start()
    to_pair.start()

    @pl.when(~inner)
    def _():
        to_opposite.start()

    weights = [
        remote(
            own_v, joined_v.at[place], w_send.at[other - 1], w_recv.at[other - 1], (place ^ other, stage, core)
        )
        for other in (1, 2, 3)
    ]
    flags = [
        remote(
            keep, keep_v.at[stage], keep_send.at[shift - 1], keep_recv.at[shift - 1],
            (place, lax.rem(stage + shift, 4), core),
        )
        for shift in (1, 2, 3)
    ]
    outs = [
        remote(
            w_out, full_out.at[place], w_send.at[other + 2], w_recv.at[other + 2], (place ^ other, stage, core)
        )
        for other in (1, 2, 3)
    ]

    units = w_down.shape[1] // 2

    def down_copy(owner, other, which, sem):
        columns = pl.ds(which * units, units)
        source = w_down if owner is place else full_down.at[owner]
        return remote(
            source.at[:, columns], full_down.at[owner, :, columns], down_send.at[sem], down_recv.at[sem],
            (place ^ other, stage, core),
        )

    halves = [
        down_copy(place, other, which, 2 * which + other - 1)
        for other, which in ((1, 0), (2, 1), (1, 1), (2, 0))
    ]
    on = [down_copy(place ^ 1, 2, 0, 4), down_copy(place ^ 2, 1, 1, 5)]
    for copy in weights + flags + outs + halves:
        copy.start()
    local = [
        pltpu.make_async_copy(w_out, full_out.at[place], local_sem.at[0]),
        pltpu.make_async_copy(w_down, full_down.at[place], local_sem.at[1]),
    ]
    for copy in local:
        copy.start()

    for part in (0, 1):
        up_v[:, pl.ds(part * w_up.shape[2], w_up.shape[2])] = w_up[:, part, :]
    up_out = pltpu.make_async_copy(up_v, up_flat, up_sem)
    up_out.start()

    bounds = doc_bounds(docs, seq)
    third, fourth = 3 - stage, 3 - (stage ^ 1)

    def out_copies(slot, block):
        at = pl.ds(pl.multiple_of(block * rows_of, rows_of), rows_of)
        pairs = (
            (qt_v.at[slot], query_t.at[:, :, at]),
            (q_v.at[slot], queries.at[:, at, :]),
            (k_v.at[slot], keys.at[:, at, :]),
            (kt_v.at[slot], keys_t.at[:, :, at]),
            (v_v.at[slot], values.at[:, at, :]),
            (vt_v.at[slot], values_t.at[:, :, at]),
        )
        return [
            pltpu.make_async_copy(source, target, block_sem.at[slot, index])
            for index, (source, target) in enumerate(pairs)
        ]

    def sequence_copy(block):
        return pltpu.make_async_copy(tokens_v.at[block], sequence.at[block], out_sem.at[block])

    def low(value):
        return value.astype(bf16).astype(f32)

    def project(slot, block):
        x = tokens_v[block].reshape(rows_of, model_width)
        y = dot(x, joined_v[...].reshape(model_width, 3 * width))
        zero = jnp.zeros((1, width), f32)
        biases = [
            jnp.where(half == 0, b[:, :width], b[:, width:])
            for b in (b_query[...].reshape(1, -1), b_value[...].reshape(1, -1))
        ]
        y = low(y + jnp.concatenate([biases[0], zero, biases[1]], 1))
        fill = -y.shape[1] % LANES
        if fill:
            y = jnp.concatenate([y, jnp.zeros((rows_of, fill), f32)], 1)
        lane = lax.broadcasted_iota(jnp.int32, (rows_of, LANES), 1)
        sub = lax.broadcasted_iota(jnp.int32, (LANES, rows_of), 0)
        first = block * rows_of
        key_pos = first + lax.broadcasted_iota(jnp.int32, (rows_of, LANES), 0)
        query_pos = first + lax.broadcasted_iota(jnp.int32, (LANES, rows_of), 1)

        def segments(positions):
            return sum((bound <= positions).astype(jnp.int32) for bound in bounds)

        flag = keep_v[block, pl.ds(seq, 1), :].astype(f32)
        flag = jnp.broadcast_to(flag, (LANES, rows_of)).T
        key_feat = jnp.where(lane < DOC_ROW, 0.0, 1.0)
        key_doc = jnp.where(segments(key_pos) == lane - DOC_ROW, 0.0, MASKED)
        key_feat = jnp.where((lane >= DOC_ROW) & (lane < DOC_ROW + len(bounds)), key_doc, key_feat)
        key_feat = jnp.where(lane == KEEP_ROW, jnp.where(flag > 0.5, 0.0, MASKED), key_feat)
        pos_low = key_pos & 255
        key_feat = jnp.where(
            (lane >= POS_ROW) & (lane < POS_ROW + 3), (key_pos - pos_low).astype(f32), key_feat
        )
        key_feat = jnp.where((lane >= POS_ROW + 3) & (lane < LINE_ROW), pos_low.astype(f32), key_feat)
        key_feat = jnp.where(lane >= FEAT_END, 0.0, key_feat)
        doc_feat = jnp.where(segments(query_pos) == sub - DOC_ROW, 1.0, 0.0)
        doc_feat = jnp.where(sub == KEEP_ROW, 1.0, doc_feat)

        def head_part(index):
            pair = y[:, index // 2 * LANES : (index // 2 + 1) * LANES]
            if index % 2:
                pair = pltpu.roll(pair, HEAD, 1)
            return jnp.where(lane < HEAD, pair, 0.0)

        for head in range(heads):
            query_feat = doc_feat
            slope = jnp.full((1, rows_of), slopes[head], f32)
            slope_terms = three_terms(slope, low)
            line_terms = three_terms(-slope * query_pos[:1].astype(f32), low)
            for term in range(3):
                here = (sub == POS_ROW + term) | (sub == POS_ROW + 3 + term)
                query_feat = jnp.where(here, slope_terms[term], query_feat)
                query_feat = jnp.where(sub == LINE_ROW + term, line_terms[term], query_feat)
            query = head_part(head) * 0.125
            q_v[slot, head] = query[:, :HEAD].astype(bf16)
            qt_v[slot, head] = (query.T + query_feat).astype(bf16)
            key = head_part(heads + head)
            k_v[slot, head] = (key + key_feat).astype(bf16)
            kt_v[slot, head] = key.T[:HEAD].astype(bf16)
            value = head_part(2 * heads + head)
            ones = (lane >= HEAD) & (lane < HEAD + 3)
            v_v[slot, head] = jnp.where(ones, 1.0, value).astype(bf16)
            vt_v[slot, head] = jnp.where(sub == HEAD, 1.0, value.T)[:80].astype(bf16)

    for copy in weights + flags:
        copy.wait_recv()
    joined_out = pltpu.make_async_copy(joined_v, full_joined, joined_sem)
    joined_out.start()

    @pl.loop(0, 4)
    def _(i):
        pair = stage ^ 1
        block = jnp.where(i == 0, stage, jnp.where(i == 1, pair, jnp.where(i == 2, third, fourth)))
        slot = lax.rem(i, 2)

        @pl.when(i == 1)
        def _():
            arrival(pair).wait_recv()
            share(pair, core).start()
            arrival(third).wait_recv()

            @pl.when(inner)
            def _():
                send(tokens_v.at[third, core], third, pair, 2).start()

            share(third, core).start()
            for near, far in zip(halves[:2], on):
                near.wait_recv()
                far.start()

        @pl.when(i == 3)
        def _():
            arrival(fourth).wait_recv()
            share(fourth, core).start()

        @pl.when(i >= 1)
        def _():
            share(block, 1 - core).wait_recv()

        @pl.when(i >= 2)
        def _():
            for copy in out_copies(slot, block):
                copy.wait()

        sequence_copy(block).start()
        project(slot, block)
        for copy in out_copies(slot, block):
            copy.start()

    to_pair.wait_send()
    to_facing.wait_send()
    to_opposite.wait_send()
    for block in (stage ^ 1, third, fourth):
        share(block, core).wait_send()
    for copy in outs + halves[2:] + on:
        copy.wait()
    for copy in weights + flags + halves[:2]:
        copy.wait_send()
    for copy in local + [joined_out, up_out]:
        copy.wait()
    for block in range(4):
        sequence_copy(block).wait()
    for slot in (0, 1):
        for copy in out_copies(slot, 0):
            copy.wait()


def start(docs, slopes, tokens, keep, w_query, w_key, w_value, w_out, w_down, b_query, b_value, w_up):
    _, block_rows, model_width = tokens.shape
    heads = slopes.shape[0]
    width, length = heads * HEAD, 4 * block_rows
    dma, bf16 = pltpu.SemaphoreType.DMA, jnp.bfloat16
    half_rows, quarter = block_rows // 2, w_query.shape[0]
    any_spec = pl.BlockSpec(memory_space=pl.ANY)
    vmem_spec = pl.BlockSpec(memory_space=pltpu.VMEM)
    smem_spec = pl.BlockSpec(memory_space=pltpu.SMEM)

    def parts(rows):
        return [
            (heads, LANES, rows),
            (heads, rows, HEAD),
            (heads, rows, LANES),
            (heads, HEAD, rows),
            (heads, rows, LANES),
            (heads, 80, rows),
        ]

    three, four, six = dma((3,)), dma((4,)), dma((6,))
    return pl.pallas_call(
        start_kernel,
        in_specs=[smem_spec] * 2 + [vmem_spec] * 10,
        out_specs=[any_spec] * 11,
        out_shape=[
            jax.ShapeDtypeStruct(shape, bf16)
            for shape in [
                (4, 2, half_rows, model_width),
                (4, quarter, 3 * width),
                (4,) + w_out.shape,
                (4,) + w_down.shape,
                (quarter, 2 * w_up.shape[2]),
            ]
            + parts(length)
        ],
        scratch_shapes=[
            pltpu.VMEM((4, 2, half_rows, model_width), bf16),
            pltpu.VMEM((quarter, 3 * width), bf16),
            pltpu.VMEM((4, quarter, 3 * width), bf16),
            pltpu.VMEM((4,) + keep.shape, keep.dtype),
            pltpu.VMEM((quarter, 2 * w_up.shape[2]), bf16),
            *[pltpu.VMEM((2,) + shape, bf16) for shape in parts(block_rows)],
            three, four, four, four, six, six, six, six, three, three, dma((2,)), dma((2, 6)), dma, dma, four,
        ],
        compiler_params=pltpu.CompilerParams(
            collective_id=0, has_side_effects=True, vmem_limit_bytes=VMEM_BYTES
        ),
        cost_estimate=pl.CostEstimate(flops=40 << 30, bytes_accessed=16 << 20, transcendentals=0),
        name="start",
    )(docs, slopes, tokens, keep, w_query, w_key, w_value, w_out, w_down, b_query, b_value, w_up)


def attend_kernel(docs_ref, slope_ref, qt_ref, k_ref, vt_ref, o_ref, ot_ref, lse_ref, max_ref, acc_ref):
    heads = qt_ref.shape[0]
    block = pl.program_id(0)
    first_tile, last_tile = tile_span(docs_ref, lax.axis_index("ctx") // 2, block)
    after, same, bare = side_signs(TILE)

    def tile_rows(tile, count=1):
        return pl.ds(pl.multiple_of(tile * TILE, TILE), count * TILE)

    own = tile_rows(block)
    for head in range(heads):
        scores = diagonal_scores(k_ref[head, own, :], qt_ref[head], same, bare, slope_ref[head])
        top = jnp.max(scores, 0, keepdims=True)
        weights = jnp.exp(scores - top).astype(jnp.bfloat16)
        max_ref[head] = top
        acc_ref[head] = dot(vt_ref[head, :, own], weights)

    def step(tile, count, sign):
        each = range(heads)
        keys = [k_ref[head, tile_rows(tile, count), :] for head in each]
        values = [vt_ref[head, :, tile_rows(tile, count)] for head in each]
        queries = [qt_ref[head] if sign is None else qt_ref[head] * sign for head in each]
        old = [max_ref[head] for head in each]
        acc = [acc_ref[head] for head in each]
        scores = [dot(keys[head], queries[head]) for head in each]
        top = [jnp.maximum(old[head], jnp.max(scores[head], 0, keepdims=True)) for head in each]
        weights = [jnp.exp(scores[head] - top[head]).astype(jnp.bfloat16) for head in each]
        parts = [dot(values[head], weights[head]) for head in each]
        for head in each:
            max_ref[head] = top[head]
            acc_ref[head] = acc[head] * jnp.exp(old[head] - top[head]) + parts[head]

    sweep(first_tile, block, lambda tile, count: step(tile, count, None))
    sweep(block + 1, last_tile, lambda tile, count: step(tile, count, after))

    parts = []
    for head in range(heads):
        total = acc_ref[head, HEAD : HEAD + 1, :]
        out_t = acc_ref[head, :HEAD, :] / total
        ot_ref[head] = out_t
        parts.append(out_t)
        lse_ref[head] = max_ref[head] + jnp.log(total)
    o_ref[...] = jnp.concatenate(parts, 0).T.astype(jnp.bfloat16)


def attend(docs, slopes, query_t, keys, value_t):
    heads, _, length = query_t.shape
    blocks = length // TILE
    return pl.pallas_call(
        attend_kernel,
        grid_spec=pltpu.PrefetchScalarGridSpec(
            num_scalar_prefetch=2,
            grid=(blocks,),
            in_specs=[
                pl.BlockSpec((heads, LANES, TILE), lambda i, *_: (0, 0, i)),
                pl.BlockSpec(keys.shape, lambda i, *_: (0, 0, 0)),
                pl.BlockSpec(value_t.shape, lambda i, *_: (0, 0, 0)),
            ],
            out_specs=[
                pl.BlockSpec((TILE, heads * HEAD), lambda i, *_: (i, 0)),
                pl.BlockSpec((heads, HEAD, TILE), lambda i, *_: (0, 0, i)),
                pl.BlockSpec((heads, 1, TILE), lambda i, *_: (0, 0, i)),
            ],
            scratch_shapes=[
                pltpu.VMEM((heads, 1, TILE), jnp.float32),
                pltpu.VMEM((heads, 80, TILE), jnp.float32),
            ],
        ),
        out_shape=[
            jax.ShapeDtypeStruct((length, heads * HEAD), jnp.bfloat16),
            jax.ShapeDtypeStruct((heads, HEAD, length), jnp.float32),
            jax.ShapeDtypeStruct((heads, 1, length), jnp.float32),
        ],
        compiler_params=pltpu.CompilerParams(vmem_limit_bytes=VMEM_BYTES),
        cost_estimate=pl.CostEstimate(
            flops=heads * length * length * 256, bytes_accessed=6 << 20, transcendentals=heads * length * length
        ),
        name="attend",
    )(docs, slopes, query_t, keys, value_t)


def attend_back_kernel(
    docs_ref, slope_ref, qt_ref, q_ref, k_ref, kt_ref, v_ref, g_ref, ot_ref, lse_ref,
    dq_ref, dk_ref, dv_ref, qt_log, grad_heads, grad_t, query_acc, key_acc, value_acc,
):
    heads = qt_ref.shape[0]
    blocks = pl.num_programs(0)
    block = pl.program_id(0)
    length = qt_ref.shape[2]
    first_tile, last_tile = tile_span(docs_ref, lax.axis_index("ctx") // 2, block)
    after, same, bare = side_signs(TILE)

    def low(value):
        return value.astype(jnp.bfloat16).astype(jnp.float32)

    def tile_rows(tile, count=1):
        return pl.ds(pl.multiple_of(tile * TILE, TILE), count * TILE)

    @pl.when(block == 0)
    def _():
        query_acc[...] = jnp.zeros_like(query_acc)
        sub = lax.broadcasted_iota(jnp.int32, (LANES, TILE), 0)

        @pl.loop(0, length // TILE)
        def _(tile):
            rows = tile_rows(tile)
            grad = g_ref[rows, :].astype(jnp.float32)
            turned = grad.T
            for head in range(heads):
                own = turned[head * HEAD : (head + 1) * HEAD]
                delta = jnp.sum(own * ot_ref[head, :, rows], 0, keepdims=True)
                first, second, third = three_terms(-delta, low)
                wide = jnp.concatenate([own, jnp.zeros_like(own)], 0)
                wide = jnp.where(sub == HEAD, first, wide)
                wide = jnp.where(sub == HEAD + 1, second, wide)
                wide = jnp.where(sub == HEAD + 2, third, wide)
                grad_t[head, :, rows] = wide.astype(jnp.bfloat16)
                grad_heads[head, rows, :] = own.T.astype(jnp.bfloat16)
                first, second, third = three_terms(-lse_ref[head, :, rows], low)
                query = qt_ref[head, :, rows].astype(jnp.float32)
                query = jnp.where(sub == LOG_ROW, first, query)
                query = jnp.where(sub == LOG_ROW + 1, second, query)
                query = jnp.where(sub == LOG_ROW + 2, third, query)
                qt_log[head, :, rows] = query.astype(jnp.bfloat16)

    def accumulate(tile, scores, first, count=1):
        each = range(heads)
        rows = tile_rows(tile, count)
        values = [v_ref[head] for head in each]
        turned = [grad_t[head, :, rows] for head in each]
        grads = [grad_heads[head, rows, :] for head in each]
        queries = [q_ref[head, rows, :] for head in each]
        keys_t = [kt_ref[head] for head in each]
        probs = [jnp.exp(scores[head]) for head in each]
        grad_probs = [dot(values[head], turned[head]) for head in each]
        grad_scores = [(probs[head] * grad_probs[head]).astype(jnp.bfloat16) for head in each]
        value_part = [dot(probs[head].astype(jnp.bfloat16), grads[head]) for head in each]
        key_part = [dot(grad_scores[head], queries[head]) for head in each]
        query_part = [dot(keys_t[head], grad_scores[head]) for head in each]
        for head in each:
            if first:
                value_acc[head] = value_part[head]
                key_acc[head] = key_part[head]
            else:
                value_acc[head] += value_part[head]
                key_acc[head] += key_part[head]
            query_acc[head, :, rows] += query_part[head]

    own = [qt_log[head, :, tile_rows(block)] for head in range(heads)]
    accumulate(
        block,
        [
            diagonal_scores(k_ref[head], own[head], same, bare, slope_ref[head])
            for head in range(heads)
        ],
        True,
    )
    after_wide = side_signs(2 * TILE)[0]

    def step(tile, count, sign):
        queries = [qt_log[head, :, tile_rows(tile, count)] for head in range(heads)]
        if sign is not None:
            queries = [query * sign[:, : count * TILE] for query in queries]
        accumulate(tile, [dot(k_ref[head], queries[head]) for head in range(heads)], False, count)

    sweep(first_tile, block, lambda tile, count: step(tile, count, after_wide))
    sweep(block + 1, last_tile, lambda tile, count: step(tile, count, None))

    dk_ref[...] = jnp.concatenate([key_acc[head] for head in range(heads)], 1).astype(jnp.bfloat16)
    dv_ref[...] = jnp.concatenate([value_acc[head] for head in range(heads)], 1).astype(jnp.bfloat16)

    @pl.when(block == blocks - 1)
    def _():
        @pl.loop(0, length // TILE)
        def _(tile):
            rows = tile_rows(tile)
            turned = jnp.concatenate([query_acc[head, :, rows] for head in range(heads)], 0)
            dq_ref[rows, :] = (turned.T * 0.125).astype(jnp.bfloat16)


def attend_back(docs, slopes, query_t, queries, keys, keys_t, values, grads, out_t, lse):
    heads, _, length = query_t.shape
    blocks = length // TILE
    width = heads * HEAD

    def whole(array):
        return pl.BlockSpec(array.shape, lambda i, *_: (0,) * array.ndim)

    return pl.pallas_call(
        attend_back_kernel,
        grid_spec=pltpu.PrefetchScalarGridSpec(
            num_scalar_prefetch=2,
            grid=(blocks,),
            in_specs=[
                whole(query_t),
                whole(queries),
                pl.BlockSpec((heads, TILE, LANES), lambda i, *_: (0, i, 0)),
                pl.BlockSpec((heads, HEAD, TILE), lambda i, *_: (0, 0, i)),
                pl.BlockSpec((heads, TILE, LANES), lambda i, *_: (0, i, 0)),
                whole(grads),
                whole(out_t),
                whole(lse),
            ],
            out_specs=[
                pl.BlockSpec((length, width), lambda i, *_: (0, 0)),
                pl.BlockSpec((TILE, width), lambda i, *_: (i, 0)),
                pl.BlockSpec((TILE, width), lambda i, *_: (i, 0)),
            ],
            scratch_shapes=[
                pltpu.VMEM((heads, LANES, length), jnp.bfloat16),
                pltpu.VMEM((heads, length, HEAD), jnp.bfloat16),
                pltpu.VMEM((heads, LANES, length), jnp.bfloat16),
                pltpu.VMEM((heads, HEAD, length), jnp.float32),
                pltpu.VMEM((heads, TILE, HEAD), jnp.float32),
                pltpu.VMEM((heads, TILE, HEAD), jnp.float32),
            ],
        ),
        out_shape=[jax.ShapeDtypeStruct((length, width), jnp.bfloat16)] * 3,
        compiler_params=pltpu.CompilerParams(vmem_limit_bytes=VMEM_BYTES),
        cost_estimate=pl.CostEstimate(
            flops=heads * length * length * 640, bytes_accessed=12 << 20, transcendentals=heads * length * length
        ),
        name="attend_back",
    )(docs, slopes, query_t, queries, keys, keys_t, values, grads, out_t, lse)


def rows_norm(residual):
    centered = residual - jnp.mean(residual, -1, keepdims=True)
    inv_scale = lax.rsqrt(jnp.mean(centered * centered, -1, keepdims=True) + NORM_EPS)
    return centered * inv_scale, inv_scale


def rows_norm_back(grad_out, normed, inv_scale, norm_gain):
    grad_norm = grad_out * norm_gain
    mean_grad = jnp.mean(grad_norm, -1, keepdims=True)
    mean_cross = jnp.mean(grad_norm * normed, -1, keepdims=True)
    return (grad_norm - mean_grad - normed * mean_cross) * inv_scale


def middle_kernel(
    attended, sequence, cotangent, w_out, w_down, up_0, up_1, up_2, *rest,
):
    vectors, rest = rest[:6], rest[6:]
    (
        out_home, grad_one, grad_heads, early_0, early_1, early_2, early_3, late, down_sum, sums,
        token_v, mine_v, theirs_v, both_v, cot_v, out_w, down_w, up_w,
        send_a, recv_a, send_b, recv_b, send_c, recv_c,
        normed_v, inv_v, low_v, hidden_v, gate_v, lift_v, grad_v, ffn_v, att_v, result_v, keep_v, away_v, tile_v,
        down_v, down_got, load_sem, far_send, far_recv, pair_send, pair_recv, cot_send, cot_recv, cot_pass, cot_took,
        a_send, a_recv, b_send, b_recv, c_send, c_recv, out_send, out_recv, out_pass, out_took,
        one_sem, keep_sem, away_send, away_recv, tile_sem, down_send, down_recv, down_sem,
    ) = rest
    place, stage, core = lax.axis_index("fsdp"), lax.axis_index("ctx"), lax.axis_index("tp")
    seq, half = stage // 2, stage % 2
    pair = stage ^ 1
    chunks = token_v.shape[0]
    units = hidden_v.shape[2]
    wide = 512
    quarter = up_0.shape[0]

    barrier = pltpu.get_barrier_semaphore()
    peers = [(place ^ other, stage, core) for other in (1, 2, 3)]
    peers += [(place, lax.rem(stage + shift, 4), core) for shift in (1, 2, 3)]
    peers += [(place, stage, 1 - core)]
    for peer in peers:
        pl.semaphore_signal(barrier, inc=1, device_id=peer, device_id_type=MESH)
    pl.semaphore_wait(barrier, len(peers))

    def remote(source, target, send, recv, device):
        return pltpu.make_async_remote_copy(
            source, target, send, recv, device_id=device, device_id_type=MESH
        )

    partner = (place, pair, core)
    other_core = (place, stage, 1 - core)

    def pair_copy(c):
        return remote(
            attended.at[(1 - half) * chunks + c], theirs_v.at[c], pair_send.at[c], pair_recv.at[c], partner
        )

    for c in range(chunks):
        pair_copy(c).start()

    def far_copy(which):
        source, over = ((up_1, 2), (up_2, 1))[which]
        columns = pl.ds(which * units, units)
        rows = pl.ds(pl.multiple_of((place ^ 3 ^ over) * quarter, quarter), quarter)
        return remote(
            source.at[:, columns], up_w.at[rows, columns], far_send.at[which], far_recv.at[which],
            (place ^ over, stage, core),
        )

    for which in (0, 1):
        far_copy(which).start()

    def cot_owner(which):
        return 2 * which + stage // 2

    def cot_copy(which):
        return remote(
            cotangent.at[which, core], cot_v.at[stage % 2, core],
            cot_send.at[which], cot_recv.at[stage % 2], (place, cot_owner(which), core),
        )

    def cot_local(which):
        return pltpu.make_async_copy(cotangent.at[which], cot_v.at[stage % 2], cot_send.at[which])

    for which in (0, 1):

        @pl.when(cot_owner(which) == stage)
        def _():
            cot_local(which).start()

        @pl.when(cot_owner(which) != stage)
        def _():
            cot_copy(which).start()

    def cot_arrival(block):
        return remote(
            cot_v.at[block, core], cot_v.at[block, core], cot_pass.at[block], cot_recv.at[block], other_core
        )

    def cot_share(block, whose):
        return remote(
            cot_v.at[block, whose], cot_v.at[block, whose], cot_pass.at[block], cot_took.at[block], other_core
        )

    loads = [
        pltpu.make_async_copy(attended.at[pl.ds(half * chunks, chunks)], mine_v, load_sem.at[0]),
        pltpu.make_async_copy(w_out, out_w, load_sem.at[1]),
        pltpu.make_async_copy(sequence.at[pl.ds(half * chunks, chunks)], token_v, load_sem.at[2]),
        pltpu.make_async_copy(w_down, down_w, load_sem.at[3]),
    ]
    for other, shard in enumerate((up_0, up_1, up_2)):
        rows = pl.ds(pl.multiple_of((place ^ other) * quarter, quarter), quarter)
        loads.append(pltpu.make_async_copy(shard, up_w.at[rows], load_sem.at[4 + other]))
    for load in loads:
        load.start()

    b_out, gain_one, shift_one, b_down, gain_two, shift_two = (v[...].reshape(1, -1) for v in vectors)
    sums[...] = jnp.zeros_like(sums)

    def add_sum(index, rows):
        sums[index : index + 1, :] += jnp.sum(rows, 0, keepdims=True)

    def exchange(c, sent, got, send, recv):
        return remote(sent.at[c], got.at[c], send.at[c], recv.at[c], other_core)

    def total(c, sent, got):
        return sent[c].astype(jnp.float32) + got[c].astype(jnp.float32)

    loads[0].wait()
    loads[1].wait()

    @pl.loop(0, chunks)
    def _(c):
        pair_copy(c).wait_recv()
        first, second = mine_v[c], theirs_v[c]
        both = jnp.where(
            half == 0, jnp.concatenate([first, second], 1), jnp.concatenate([second, first], 1)
        )
        both_v[c] = both
        send_a[c] = dot(both, out_w[...], ((1,), (1,))).astype(jnp.bfloat16)
        exchange(c, send_a, recv_a, a_send, a_recv).start()

    for load in loads[2:]:
        load.wait()
    for which in (0, 1):
        far_copy(which).wait_recv()

    @pl.loop(0, chunks)
    def _(c):
        exchange(c, send_a, recv_a, a_send, a_recv).wait_recv()

        @pl.when(c == chunks - 1)
        def _():
            for block in (0, 1):

                @pl.when(2 * half + block != stage)
                def _():
                    cot_arrival(block).wait_recv()
                    cot_share(block, core).start()

        residual = token_v[c].astype(jnp.float32) + (total(c, send_a, recv_a) + b_out)
        normed, inv_scale = rows_norm(residual)
        normed_v[c] = normed
        inv_v[c] = inv_scale
        low_v[c] = (normed * gain_one + shift_one).astype(jnp.bfloat16)
        for n in range(0, units, wide):
            gate = dot(low_v[c], up_w[:, n : n + wide])
            lift = dot(low_v[c], up_w[:, units + n : units + n + wide])
            chance = 0.5 + 0.5 * lax.erf(gate * 0.7071067811865476)
            density = jnp.exp(gate * gate * -0.5) * 0.3989422804014327
            gelu = gate * chance
            hidden_v[c, :, n : n + wide] = (gelu * lift).astype(jnp.bfloat16)
            gate_v[c, :, n : n + wide] = (lift * (chance + gate * density)).astype(jnp.bfloat16)
            lift_v[c, :, n : n + wide] = gelu.astype(jnp.bfloat16)
        send_b[c] = dot(hidden_v[c], down_w[...], ((1,), (1,))).astype(jnp.bfloat16)
        exchange(c, send_b, recv_b, b_send, b_recv).start()

    for block in (0, 1):

        @pl.when(2 * half + block != stage)
        def _():
            cot_share(block, core).wait_send()
            cot_share(block, 1 - core).wait_recv()

    for which in (0, 1):

        @pl.when(cot_owner(which) == stage)
        def _():
            cot_local(which).wait()

        @pl.when(cot_owner(which) != stage)
        def _():
            cot_copy(which).wait_send()

    def home(c):
        return 2 * half + c // 2

    def out_copy(c):
        return remote(
            result_v.at[c], out_home.at[seq, core], out_send.at[c], out_recv.at[seq], (place, home(c), core)
        )

    def out_local(c):
        return pltpu.make_async_copy(result_v.at[c], out_home.at[seq, c % 2], out_send.at[c])

    @pl.loop(0, chunks)
    def _(c):
        exchange(c, send_b, recv_b, b_send, b_recv).wait_recv()
        normed_one = normed_v[c]
        residual = normed_one * gain_one + shift_one + (total(c, send_b, recv_b) + b_down)
        normed, inv_scale = rows_norm(residual)
        result_v[c] = (normed * gain_two + shift_two).astype(jnp.bfloat16)

        @pl.when(home(c) == stage)
        def _():
            out_local(c).start()

        @pl.when((home(c) != stage) & (c % 2 == core))
        def _():
            out_copy(c).start()

        grad_in = cot_v[c // 2, c % 2].astype(jnp.float32)
        add_sum(0, grad_in * normed)
        add_sum(1, grad_in)
        grad_two = rows_norm_back(grad_in, normed, inv_scale, gain_two)
        grad_v[c] = grad_two
        grad_ffn = grad_two.astype(jnp.bfloat16)
        ffn_v[c] = grad_ffn
        add_sum(2, grad_ffn.astype(jnp.float32))

    tile = tile_v.shape[2]

    def columns(index):
        return pl.ds(pl.multiple_of(index * tile, tile), tile)

    def weight_part(left, right):
        rows = left.shape[0] * left.shape[1]
        return dot(
            left[...].reshape(rows, left.shape[2]), right.reshape(rows, tile), ((0,), (0,))
        ).astype(jnp.bfloat16)

    unit_tiles = units // tile

    def down_copy(i, other):
        rows = pl.ds(pl.multiple_of((place ^ other) * quarter, quarter), quarter)
        return remote(
            down_v.at[rows, columns(i)], down_got.at[other - 1, :, columns(i)],
            down_send.at[i, other - 1], down_recv.at[i, other - 1], (place ^ other, stage, core),
        )

    @pl.loop(0, unit_tiles)
    def _(i):
        down_v[:, columns(i)] = weight_part(ffn_v, hidden_v[:, :, columns(i)])
        for other in (1, 2, 3):
            down_copy(i, other).start()

    @pl.loop(0, chunks)
    def _(c):
        for n in range(0, units, wide):
            grad_hidden = dot(ffn_v[c], down_w[:, n : n + wide])
            gate_v[c, :, n : n + wide] = (grad_hidden * gate_v[c, :, n : n + wide]).astype(jnp.bfloat16)
            lift_v[c, :, n : n + wide] = (grad_hidden * lift_v[c, :, n : n + wide]).astype(jnp.bfloat16)
        send_c[c] = (
            dot(gate_v[c], up_w[:, :units], ((1,), (1,))) + dot(lift_v[c], up_w[:, units:], ((1,), (1,)))
        ).astype(jnp.bfloat16)
        exchange(c, send_c, recv_c, c_send, c_recv).start()

    def one_copy(c):
        return pltpu.make_async_copy(grad_v.at[c], grad_one.at[c], one_sem.at[c])

    def keep_copy(c):
        return pltpu.make_async_copy(keep_v.at[c], grad_heads.at[half * chunks + c], keep_sem.at[c])

    def away_copy(c, whose):
        return remote(
            away_v.at[c], grad_heads.at[whose * chunks + c], away_send.at[c], away_recv.at[c], partner
        )

    @pl.loop(0, chunks)
    def _(c):
        exchange(c, send_c, recv_c, c_send, c_recv).wait_recv()
        grad_first = grad_v[c] + total(c, send_c, recv_c)
        normed = normed_v[c]
        add_sum(3, grad_first * normed)
        add_sum(4, grad_first)
        grad_res = rows_norm_back(grad_first, normed, inv_v[c], gain_one)
        grad_v[c] = grad_res
        one_copy(c).start()
        grad_att = grad_res.astype(jnp.bfloat16)
        att_v[c] = grad_att
        add_sum(5, grad_att.astype(jnp.float32))
        heads = dot(att_v[c], out_w[...]).astype(jnp.bfloat16)
        first, second = heads[:, : heads.shape[1] // 2], heads[:, heads.shape[1] // 2 :]
        keep_v[c] = jnp.where(half == 0, first, second)
        away_v[c] = jnp.where(half == 0, second, first)
        away_copy(c, half).start()
        keep_copy(c).start()

    early = (early_0, early_1, early_2, early_3)
    early_tiles = early_0.shape[1] // tile

    def tile_copy(slot, other, index):
        target, column = index
        rows = pl.ds(pl.multiple_of((place ^ other) * quarter, quarter), quarter)
        place_of = target[other] if isinstance(target, tuple) else target.at[other]
        return pltpu.make_async_copy(
            tile_v.at[slot, rows], place_of.at[:, columns(column)], tile_sem.at[slot, other]
        )

    def weight_tile(count, target, column, left, right):
        slot = lax.rem(count, 2)

        @pl.when(count >= 2)
        def _():
            for row in range(4):
                tile_copy(slot, row, (target, column)).wait()

        tile_v[slot] = weight_part(left, right)
        for row in range(4):
            tile_copy(slot, row, (target, column)).start()

    @pl.loop(0, unit_tiles)
    def _(i):
        weight_tile(i, early, i, low_v, gate_v[:, :, columns(i)])

    @pl.loop(unit_tiles, early_tiles)
    def _(i):
        weight_tile(i, early, i, low_v, lift_v[:, :, columns(i - unit_tiles)])

    late_units = 2 * unit_tiles - early_tiles

    @pl.loop(0, late_units)
    def _(i):
        weight_tile(early_tiles + i, late, i, low_v, lift_v[:, :, columns(early_tiles - unit_tiles + i)])

    weight_tile(2 * unit_tiles, late, late_units, att_v, both_v[...])
    for slot in (0, 1):
        for row in range(4):
            tile_copy(slot, row, (late, 0)).wait()

    for i in range(unit_tiles):
        for other in (1, 2, 3):
            down_copy(i, other).wait_recv()
    own_rows = pl.ds(pl.multiple_of(place * quarter, quarter), quarter)
    down_got[0] = (
        down_v[own_rows, :].astype(jnp.float32)
        + down_got[0].astype(jnp.float32)
        + (down_got[1].astype(jnp.float32) + down_got[2].astype(jnp.float32))
    ).astype(jnp.bfloat16)
    down_out = pltpu.make_async_copy(down_got.at[0], down_sum, down_sem)
    down_out.start()

    def out_arrival(which):
        return remote(
            out_home.at[which, core], out_home.at[which, core], out_pass.at[which], out_recv.at[which], other_core
        )

    def out_share(which, whose):
        return remote(
            out_home.at[which, whose], out_home.at[which, whose], out_pass.at[which], out_took.at[which], other_core
        )

    for which in (0, 1):

        @pl.when(cot_owner(which) != stage)
        def _():
            out_arrival(which).wait_recv()
            out_share(which, core).start()

    down_out.wait()
    for which in (0, 1):
        far_copy(which).wait_send()
    for i in range(unit_tiles):
        for other in (1, 2, 3):
            down_copy(i, other).wait_send()

    @pl.loop(0, chunks)
    def _(c):
        pair_copy(c).wait_send()
        exchange(c, send_a, recv_a, a_send, a_recv).wait_send()
        exchange(c, send_b, recv_b, b_send, b_recv).wait_send()
        exchange(c, send_c, recv_c, c_send, c_recv).wait_send()
        one_copy(c).wait()
        keep_copy(c).wait()
        away_copy(c, half).wait_send()
        away_copy(c, 1 - half).wait_recv()

        @pl.when(home(c) == stage)
        def _():
            out_local(c).wait()

        @pl.when((home(c) != stage) & (c % 2 == core))
        def _():
            out_copy(c).wait_send()

    for which in (0, 1):

        @pl.when(cot_owner(which) != stage)
        def _():
            out_share(which, core).wait_send()
            out_share(which, 1 - core).wait_recv()


def middle(attended, sequence, cotangent, w_out, w_down, up_shards, vectors):
    chunks, rows, width = 4, sequence.shape[1], sequence.shape[2]
    head_width, units = w_out.shape[1], w_down.shape[1]
    tile = head_width
    early, late = 6 * tile, 2 * units + head_width - 6 * tile
    dma, bf16, f32 = pltpu.SemaphoreType.DMA, jnp.bfloat16, jnp.float32

    def vmem(shape, dtype=bf16):
        return pltpu.VMEM(shape, dtype)

    wide = (chunks, rows, width)
    inner = (chunks, rows, units)
    narrow_rows = (chunks, rows, head_width // 2)
    four, two = dma((chunks,)), dma((2,))
    return pl.pallas_call(
        middle_kernel,
        in_specs=[pl.BlockSpec(memory_space=pl.ANY)] * 8 + [pl.BlockSpec(memory_space=pltpu.VMEM)] * 6,
        out_specs=[pl.BlockSpec(memory_space=pl.ANY)] * 9 + [pl.BlockSpec(memory_space=pltpu.VMEM)],
        out_shape=[
            jax.ShapeDtypeStruct((2, 2, rows, width), bf16),
            jax.ShapeDtypeStruct(wide, f32),
            jax.ShapeDtypeStruct((2 * chunks, rows, head_width // 2), bf16),
            *[jax.ShapeDtypeStruct((width // 4, early), bf16)] * 4,
            jax.ShapeDtypeStruct((4, width // 4, late), bf16),
            jax.ShapeDtypeStruct((width // 4, units), bf16),
            jax.ShapeDtypeStruct((8, width), f32),
        ],
        scratch_shapes=[
            vmem(wide), vmem(narrow_rows), vmem(narrow_rows), vmem((chunks, rows, head_width)),
            vmem((2, 2, rows, width)), vmem((width, head_width)), vmem((width, units)), vmem((width, 2 * units)),
            vmem(wide), vmem(wide), vmem(wide), vmem(wide), vmem(wide), vmem(wide),
            vmem(wide, f32), vmem((chunks, rows, 1), f32), vmem(wide),
            vmem(inner), vmem(inner), vmem(inner),
            vmem(wide, f32), vmem(wide), vmem(wide), vmem(wide), vmem(narrow_rows), vmem(narrow_rows),
            vmem((2, width, tile)), vmem((width, units)), vmem((3, width // 4, units)),
            dma((7,)), two, two, four, four, two, two, two, two,
            four, four, four, four, four, four, four, two, two, two,
            four, four, four, four, dma((2, 4)), dma((units // tile, 3)), dma((units // tile, 3)), dma,
        ],
        compiler_params=pltpu.CompilerParams(
            collective_id=1, has_side_effects=True, vmem_limit_bytes=VMEM_BYTES
        ),
        cost_estimate=pl.CostEstimate(flops=50 << 30, bytes_accessed=32 << 20, transcendentals=0),
        name="middle",
    )(attended, sequence, cotangent, w_out, w_down, *up_shards, *vectors)


def tail_kernel(
    d_query, d_key, d_value, w_joined, sums_in, sequence, grad_one, early, late, moved_1, moved_2, moved_3,
    home, shard, joined, sums,
    query_v, key_v, value_v, token_v, one_v, part_v, late_v, project_v, own_v, tp_sent, tp_got, pair_sent, pair_got,
    final_v, summed_v, end_got, inner_v, mid_got, total_v, joined_v, quarter_got, both_sent, both_end, both_inner,
    both_mid, both_total, step_v, step_got,
    load_sem, late_send, late_recv, tp_send, tp_recv, pair_send, pair_recv, home_send, home_recv, home_pass,
    home_took, home_local, end_send, end_recv, mid_send, mid_recv, back_send, back_recv, shard_sem,
    quarter_send, quarter_recv, both_send, both_recv, both_local, step_send, step_recv,
):
    place, stage, core = lax.axis_index("fsdp"), lax.axis_index("ctx"), lax.axis_index("tp")
    seq, half = stage // 2, stage % 2
    bf16, f32 = jnp.bfloat16, jnp.float32
    pieces = summed_v.shape[0]
    piece = summed_v.shape[2]
    early_pieces = early.shape[1] // piece
    quarter = joined_v.shape[0] // 4
    width = d_query.shape[2]

    barrier = pltpu.get_barrier_semaphore()
    peers = [(place ^ other, stage, core) for other in (1, 2, 3)]
    peers += [(place, lax.rem(stage + shift, 4), core) for shift in (1, 2, 3)]
    peers += [(place, stage, 1 - core)]
    for peer in peers:
        pl.semaphore_signal(barrier, inc=1, device_id=peer, device_id_type=MESH)

    loads = [
        pltpu.make_async_copy(source, target, load_sem.at[index])
        for index, (source, target) in enumerate(
            (
                (early, part_v.at[0]),
                (moved_1, part_v.at[1]),
                (moved_2, part_v.at[2]),
                (moved_3, part_v.at[3]),
                (d_query, query_v),
                (d_key, key_v),
                (d_value, value_v),
                (late.at[0], late_v.at[0]),
                (sequence, token_v),
                (grad_one, one_v),
            )
        )
    ]
    for load in loads:
        load.start()
    pl.semaphore_wait(barrier, len(peers))

    def remote(source, target, send, recv, device):
        return pltpu.make_async_remote_copy(
            source, target, send, recv, device_id=device, device_id_type=MESH
        )

    other_core = (place, stage, 1 - core)
    partner = (place, stage ^ 1, core)
    at_end = (stage == 0) | (stage == 3)
    inward = (place, stage ^ 1, core)
    outward = (place, stage ^ 1, core)
    across = (place, 3 - stage, core)

    def late_copy(other):
        return remote(
            late.at[other], late_v.at[other], late_send.at[other - 1], late_recv.at[other - 1],
            (place ^ other, stage, core),
        )

    for other in (1, 2, 3):
        late_copy(other).start()

    def columns(j):
        return pl.ds(j * piece, piece)

    def end_copy(j):
        return remote(summed_v.at[j], end_got.at[j], end_send.at[j], end_recv.at[j], inward)

    def mid_copy(j):
        return remote(inner_v.at[j], mid_got.at[j], mid_send.at[j], mid_recv.at[j], across)

    def back_copy(j):
        return remote(total_v.at[j], shard.at[:, columns(j)], back_send.at[j], back_recv.at[j], outward)

    def shard_copy(j):
        return pltpu.make_async_copy(total_v.at[j], shard.at[:, columns(j)], shard_sem.at[j])

    def sum_piece(j, parts, first):
        terms = [parts[index, :, first : first + piece].astype(f32) for index in range(4)]
        summed_v[j] = (terms[0] + terms[1] + (terms[2] + terms[3])).astype(bf16)

        @pl.when(at_end)
        def _():
            end_copy(j).start()

    def from_end(j):
        end_copy(j).wait_recv()
        inner_v[j] = (summed_v[j].astype(f32) + end_got[j].astype(f32)).astype(bf16)
        mid_copy(j).start()

    def from_mid(j):
        mid_copy(j).wait_recv()
        total_v[j] = (inner_v[j].astype(f32) + mid_got[j].astype(f32)).astype(bf16)
        back_copy(j).start()
        shard_copy(j).start()

    for load in loads[:4]:
        load.wait()
    for j in range(early_pieces):
        sum_piece(j, part_v, j * piece)

    def input_share(chunk):
        rows = jnp.concatenate([query_v[chunk], key_v[chunk], value_v[chunk]], 1)
        project_v[chunk] = rows
        return dot(rows, w_joined[...], ((1,), (1,)))

    def block_of(i):
        return jnp.where(i < 2, 2 * (1 - half) + i, 2 * half + i - 2)

    def tp_copy(i):
        return remote(tp_sent.at[i], tp_got.at[i], tp_send.at[i], tp_recv.at[i], other_core)

    for load in loads[4:7]:
        load.wait()

    @pl.loop(0, 4)
    def _(i):
        block = block_of(i)
        tp_sent[i] = input_share(2 * block + 1 - core).astype(bf16)
        tp_copy(i).start()
        own_v[i] = input_share(2 * block + core)

    def pair_copy(i):
        return remote(pair_sent.at[i], pair_got.at[i], pair_send.at[i], pair_recv.at[i], partner)

    @pl.loop(0, 2)
    def _(i):
        tp_copy(i).wait_recv()
        pair_sent[i] = (own_v[i] + tp_got[i].astype(f32)).astype(bf16)
        pair_copy(i).start()

    @pl.when(~at_end)
    def _():
        for j in range(early_pieces // 2):
            from_end(j)

    loads[8].wait()
    tokens = token_v[...].reshape(-1, token_v.shape[2])
    project = project_v[...].reshape(-1, project_v.shape[2])
    strip = 256
    for row in range(0, joined_v.shape[0], strip):
        joined_v[row : row + strip, :] = dot(
            tokens[:, row : row + strip], project, ((0,), (0,))
        ).astype(bf16)

    def quarter_copy(other):
        rows = pl.ds(pl.multiple_of((place ^ other) * quarter, quarter), quarter)
        return remote(
            joined_v.at[rows], quarter_got.at[other - 1], quarter_send.at[other - 1], quarter_recv.at[other - 1],
            (place ^ other, stage, core),
        )

    for other in (1, 2, 3):
        quarter_copy(other).start()

    def column_sum(grads):
        return jnp.sum(grads[...].reshape(-1, width).astype(f32), 0, keepdims=True)

    bias_parts = []
    for total in (column_sum(query_v), column_sum(value_v)):
        for which in (0, 1):
            bias_parts.append(jnp.where(half == which, total, 0.0))
    bias = jnp.concatenate(bias_parts, 1)
    step_v[0] = sums_in[...]
    step_v[0, 6:7, :] = bias
    steps = [(place ^ 1, stage, core), (place ^ 2, stage, core), partner, (place, stage ^ 2, core)]

    def step_copy(index):
        return remote(
            step_v.at[index], step_got.at[index], step_send.at[index], step_recv.at[index], steps[index]
        )

    def step_on(index):
        step_copy(index).wait_recv()
        step_v[index + 1] = step_v[index] + step_got[index]
        if index < 3:
            step_copy(index + 1).start()

    step_copy(0).start()

    @pl.when(~at_end)
    def _():
        for j in range(early_pieces // 2, early_pieces):
            from_end(j)
            from_mid(j - early_pieces // 2)

    loads[7].wait()
    for other in (1, 2, 3):
        late_copy(other).wait_recv()
    for j in range(early_pieces, pieces):
        sum_piece(j, late_v, (j - early_pieces) * piece)
    step_on(0)

    def both_end_copy():
        return remote(both_sent, both_end, both_send.at[0], both_recv.at[0], inward)

    def both_mid_copy():
        return remote(both_inner, both_mid, both_send.at[1], both_recv.at[1], across)

    def both_back_copy():
        return remote(both_total, joined, both_send.at[2], both_recv.at[2], outward)

    def both_here():
        return pltpu.make_async_copy(both_total, joined, both_local)

    for other in (1, 2, 3):
        quarter_copy(other).wait_recv()
    own_rows = pl.ds(pl.multiple_of(place * quarter, quarter), quarter)
    both_sent[...] = (
        joined_v[own_rows, :].astype(f32)
        + quarter_got[0].astype(f32)
        + (quarter_got[1].astype(f32) + quarter_got[2].astype(f32))
    ).astype(bf16)

    @pl.when(at_end)
    def _():
        both_end_copy().start()

    step_on(1)

    loads[9].wait()

    def home_copy(i):
        return remote(
            final_v.at[i], home.at[seq, core], home_send.at[i], home_recv.at[seq], (place, 2 * half + i, core)
        )

    def home_direct(i):
        return remote(final_v.at[i], home.at[seq, core], home_send.at[i], home_took.at[seq], other_core)

    def home_here(i):
        return pltpu.make_async_copy(final_v.at[i], home.at[seq, core], home_local)

    for i in range(2):
        tp_copy(i + 2).wait_recv()
        pair_copy(i).wait_recv()
        final_v[i] = (
            own_v[i + 2] + tp_got[i + 2].astype(f32) + pair_got[i].astype(f32) + one_v[2 * i + core]
        ).astype(bf16)

        @pl.when(2 * half + i == stage)
        def _():
            home_direct(i).start()
            home_here(i).start()

        @pl.when(2 * half + i != stage)
        def _():
            home_copy(i).start()

    @pl.when(~at_end)
    def _():
        for j in range(early_pieces, pieces):
            from_end(j)
            from_mid(j - early_pieces // 2)
        both_end_copy().wait_recv()
        both_inner[half] = both_sent[...]
        both_inner[1 - half] = both_end[...]
        both_mid_copy().start()
        for j in range(pieces - early_pieces // 2, pieces):
            from_mid(j)
        both_mid_copy().wait_recv()
        both_total[...] = (both_inner[...].astype(f32) + both_mid[...].astype(f32)).astype(bf16)
        both_back_copy().start()
        both_here().start()

    step_on(2)
    step_on(3)
    sums[...] = step_v[4]

    def home_arrival(which):
        return remote(
            home.at[which, core], home.at[which, core], home_pass.at[which], home_recv.at[which], other_core
        )

    def home_share(which, whose):
        return remote(
            home.at[which, whose], home.at[which, whose], home_pass.at[which], home_took.at[which], other_core
        )

    for which in (0, 1):

        @pl.when(2 * which + stage // 2 != stage)
        def _():
            home_arrival(which).wait_recv()
            home_share(which, core).start()

    @pl.when(~at_end)
    def _():
        for j in range(pieces):
            mid_copy(j).wait_send()
            back_copy(j).wait_send()
            shard_copy(j).wait()
        both_mid_copy().wait_send()
        both_back_copy().wait_send()
        both_here().wait()

    @pl.when(at_end)
    def _():
        for j in range(pieces):
            end_copy(j).wait_send()
            back_copy(j).wait_recv()
        both_end_copy().wait_send()
        both_back_copy().wait_recv()

    for i in range(4):
        tp_copy(i).wait_send()
        step_copy(i).wait_send()
    for i in range(2):
        pair_copy(i).wait_send()

        @pl.when(2 * half + i == stage)
        def _():
            home_direct(i).wait_send()
            home_here(i).wait()

        @pl.when(2 * half + i != stage)
        def _():
            home_copy(i).wait_send()

    for which in (0, 1):

        @pl.when(2 * which + stage // 2 != stage)
        def _():
            home_share(which, core).wait_send()

        home_share(which, 1 - core).wait_recv()
    for other in (1, 2, 3):
        quarter_copy(other).wait_send()
        late_copy(other).wait_send()


def tail(d_query, d_key, d_value, w_joined, sums, sequence, grad_one, early, late, moved):
    rows, width = sequence.shape[1:]
    quarter = early.shape[0]
    joined = w_joined.shape[1]
    piece = 3 * LANES
    columns = early.shape[1] + late.shape[2]
    pieces = columns // piece
    dma, bf16, f32 = pltpu.SemaphoreType.DMA, jnp.bfloat16, jnp.float32

    def vmem(shape, dtype=bf16):
        return pltpu.VMEM(shape, dtype)

    any_spec, vmem_spec = pl.BlockSpec(memory_space=pl.ANY), pl.BlockSpec(memory_space=pltpu.VMEM)
    cut = (pieces, quarter, piece)
    both = (2, quarter, joined)
    one, two, three, four, many = dma, dma((2,)), dma((3,)), dma((4,)), dma((pieces,))
    return pl.pallas_call(
        tail_kernel,
        in_specs=[any_spec] * 3 + [vmem_spec] * 2 + [any_spec] * 7,
        out_specs=[any_spec] * 3 + [vmem_spec],
        out_shape=[
            jax.ShapeDtypeStruct((2, 2, rows, width), bf16),
            jax.ShapeDtypeStruct((quarter, columns), bf16),
            jax.ShapeDtypeStruct(both, bf16),
            jax.ShapeDtypeStruct(sums.shape, f32),
        ],
        scratch_shapes=[
            vmem(d_query.shape), vmem(d_query.shape), vmem(d_query.shape),
            vmem(sequence.shape), vmem(grad_one.shape, f32), vmem((4,) + early.shape), vmem(late.shape),
            vmem((8, rows, joined)), vmem((4, rows, width), f32),
            vmem((4, rows, width)), vmem((4, rows, width)), vmem((2, rows, width)), vmem((2, rows, width)),
            vmem((2, rows, width)),
            vmem(cut), vmem(cut), vmem(cut), vmem(cut), vmem(cut),
            vmem((width, joined)), vmem((3, quarter, joined)), vmem((quarter, joined)), vmem((quarter, joined)),
            vmem(both), vmem(both), vmem(both),
            vmem((5,) + sums.shape, f32), vmem((4,) + sums.shape, f32),
            dma((10,)), three, three, four, four, two, two, two, two, two, two, one,
            many, many, many, many, many, many, many,
            three, three, three, three, one, four, four,
        ],
        compiler_params=pltpu.CompilerParams(
            collective_id=2, has_side_effects=True, vmem_limit_bytes=VMEM_BYTES
        ),
        cost_estimate=pl.CostEstimate(flops=80 << 30, bytes_accessed=32 << 20, transcendentals=0),
        name="tail",
    )(d_query, d_key, d_value, w_joined, sums, sequence, grad_one, early, late, *moved)


def pick(pair, index):
    return lax.dynamic_index_in_dim(pair, index, 0, keepdims=False)


def finish_kernel(
    tokens_ref, shard_ref, joined_ref, down_ref, sums_ref,
    d_tokens, d_query, d_key, d_value, d_out, d_up, d_down, *vectors,
):
    f32 = jnp.float32
    for index in range(6):
        vectors[index][...] = sums_ref[index]
    biases = sums_ref[6]
    vectors[6][...] = biases[: biases.shape[0] // 2]
    vectors[7][...] = biases[biases.shape[0] // 2 :]
    d_tokens[...] = tokens_ref[...].astype(f32)
    units = d_up.shape[2]
    d_up[:, 0, :] = shard_ref[:, :units].astype(f32)
    d_up[:, 1, :] = shard_ref[:, units : 2 * units].astype(f32)
    d_out[...] = shard_ref[:, 2 * units :].astype(f32)
    d_down[...] = down_ref[...].astype(f32)
    width = d_query.shape[1] // 2
    for index, target in enumerate((d_query, d_key, d_value)):
        columns = slice(index * width, (index + 1) * width)
        target[...] = jnp.concatenate(
            [joined_ref[0, :, columns], joined_ref[1, :, columns]], 1
        ).astype(f32)


def finish(tokens, shard, joined, down, sums):
    steps = 4
    quarter, units = down.shape
    head_width = shard.shape[1] - 2 * units
    row, some = tokens.shape[0] // steps, quarter // steps
    sizes = [sums.shape[1]] * 6 + [head_width] * 2
    f32 = jnp.float32

    def rows(width):
        return pl.BlockSpec((some, width), lambda i: (i, 0))

    return pl.pallas_call(
        finish_kernel,
        grid=(steps,),
        in_specs=[
            pl.BlockSpec((row, tokens.shape[1]), lambda i: (i, 0)),
            rows(shard.shape[1]),
            pl.BlockSpec((2, some, joined.shape[2]), lambda i: (0, i, 0)),
            rows(units),
            pl.BlockSpec(sums.shape, lambda i: (0, 0)),
        ],
        out_specs=[
            pl.BlockSpec((row, tokens.shape[1]), lambda i: (i, 0)),
            rows(head_width), rows(head_width), rows(head_width), rows(head_width),
            pl.BlockSpec((some, 2, units), lambda i: (i, 0, 0)),
            rows(units),
            *[pl.BlockSpec((size,), lambda i: (0,)) for size in sizes],
        ],
        out_shape=[
            jax.ShapeDtypeStruct(tokens.shape, f32),
            *[jax.ShapeDtypeStruct((quarter, head_width), f32)] * 4,
            jax.ShapeDtypeStruct((quarter, 2, units), f32),
            jax.ShapeDtypeStruct((quarter, units), f32),
            *[jax.ShapeDtypeStruct((size,), f32) for size in sizes],
        ],
        compiler_params=pltpu.CompilerParams(vmem_limit_bytes=VMEM_BYTES),
        name="finish",
    )(tokens, shard, joined, down, sums)


def per_device_paired(
    tokens,
    doc_lengths,
    keep,
    w_query,
    b_query,
    w_key,
    w_value,
    b_value,
    w_out,
    b_out,
    gain_one,
    shift_one,
    w_up,
    w_down,
    b_down,
    gain_two,
    shift_two,
    cotangent,
):
    _, block_rows, model_width = tokens.shape
    length = 4 * block_rows
    half_rows = block_rows // 2
    local_heads = b_query.shape[0] // HEAD
    heads = local_heads // 2
    width = heads * HEAD
    half = lax.axis_index("ctx") % 2
    core = lax.axis_index("tp")
    slopes = head_slopes(core * local_heads + half * heads, heads)
    (
        sequence, full_joined, full_out, full_down, up_own, query_t, queries, keys, keys_t, values, values_t,
    ) = start(
        doc_lengths, slopes, tokens, keep, w_query, w_key, w_value, w_out, w_down,
        b_query, b_value, w_up,
    )
    full_joined = full_joined.reshape(model_width, 3 * width)
    full_out = full_out.reshape(model_width, 2 * width)
    full_down = full_down.reshape(model_width, -1)
    up_shards = [up_own] + [lax.ppermute(up_own, "fsdp", swap) for swap in (X_SWAP, Y_SWAP)]
    attended_all, attended_t, lse = attend(doc_lengths, slopes, query_t, keys, values_t)

    vectors = (b_out, gain_one, shift_one, b_down, gain_two, shift_two)
    out, grad_one, grad_heads, *early, late, down_sum, sums = middle(
        attended_all.reshape(8, half_rows, width),
        sequence.reshape(8, half_rows, model_width),
        cotangent.reshape(2, 2, half_rows, model_width),
        full_out,
        full_down,
        up_shards,
        vectors,
    )
    out = out.reshape(2, block_rows, model_width)
    grad_heads = grad_heads.reshape(length, width)
    moved = [
        lax.ppermute(early[other], "fsdp", swap)
        for other, swap in ((1, X_SWAP), (2, Y_SWAP), (3, D_SWAP))
    ]
    d_query, d_key, d_value = attend_back(
        doc_lengths, slopes, query_t, queries, keys, keys_t, values, grad_heads, attended_t, lse
    )
    d_tokens, shard, joined, sums = tail(
        d_query.reshape(8, half_rows, width),
        d_key.reshape(8, half_rows, width),
        d_value.reshape(8, half_rows, width),
        full_joined,
        sums,
        sequence.reshape(8, half_rows, model_width),
        grad_one,
        early[0],
        late,
        moved,
    )
    (
        d_tokens, d_w_query, d_w_key, d_w_value, sum_out, sum_up, sum_down,
        total_gain_two, total_shift_two, total_b_down, total_gain_one, total_shift_one, total_b_out,
        total_b_query, total_b_value,
    ) = finish(
        d_tokens.reshape(2 * block_rows, model_width), shard, joined, lax.psum(down_sum, "ctx"), sums
    )
    d_tokens = d_tokens.reshape(2, block_rows, model_width)
    return (
        out,
        d_tokens,
        d_w_query,
        total_b_query,
        d_w_key,
        d_w_value,
        total_b_value,
        sum_out,
        total_b_out,
        total_gain_one,
        total_shift_one,
        sum_up,
        sum_down,
        total_b_down,
        total_gain_two,
        total_shift_two,
    )


def paired(mesh, tokens, doc_lengths, b_query):
    sizes = dict(mesh.shape)
    return (
        sizes == {"fsdp": 4, "ctx": 4, "tp": 2}
        and tokens.shape[0] == 8
        and tokens.shape[1] % (8 * TILE) == 0
        and doc_lengths.shape[1] <= KEEP_ROW - DOC_ROW
        and b_query.shape[0] % (4 * HEAD) == 0
    )


def solution(mesh):
    in_specs = (
        P("fsdp", "ctx", None),
        P("fsdp", None),
        P("fsdp", "ctx"),
        P("fsdp", "tp"),
        P("tp"),
        P("fsdp", "tp"),
        P("fsdp", "tp"),
        P("tp"),
        P("fsdp", "tp"),
        P(),
        P(),
        P(),
        P("fsdp", None, "tp"),
        P("fsdp", "tp"),
        P(),
        P(),
        P(),
        P("fsdp", "ctx", None),
    )
    out_specs = (
        P("fsdp", "ctx", None),
        P("fsdp", "ctx", None),
        P("fsdp", "tp"),
        P("tp"),
        P("fsdp", "tp"),
        P("fsdp", "tp"),
        P("tp"),
        P("fsdp", "tp"),
        P(),
        P(),
        P(),
        P("fsdp", None, "tp"),
        P("fsdp", "tp"),
        P(),
        P(),
        P(),
    )

    def whole(*args):
        body = per_device_paired if paired(mesh, args[0], args[1], args[4]) else per_device_general
        return jax.shard_map(
            body, mesh=mesh, in_specs=in_specs, out_specs=out_specs, check_vma=False
        )(*args)

    return whole
```

```python
import functools

import jax
import jax.numpy as jnp
from jax import lax
from jax.experimental import pallas as pl
from jax.experimental.pallas import tpu as pltpu
from jax.sharding import PartitionSpec as P

HEAD = 64


NORM_EPS = 1e-12
MASKED = -1e30


def layer_norm(residual, norm_gain, norm_shift):
    centered = residual - jnp.mean(residual, -1, keepdims=True)
    inv_scale = lax.rsqrt(jnp.mean(centered * centered, -1, keepdims=True) + NORM_EPS)
    normed = centered * inv_scale
    return (normed * norm_gain + norm_shift, normed, inv_scale)


def norm_back(grad_out, normed, inv_scale, norm_gain):
    grad_norm = grad_out * norm_gain
    mean_grad = jnp.mean(grad_norm, -1, keepdims=True)
    mean_cross = jnp.mean(grad_norm * normed, -1, keepdims=True)
    grad_in = (grad_norm - mean_grad - normed * mean_cross) * inv_scale
    return (grad_in, jnp.sum(grad_out * normed, 0), jnp.sum(grad_out, 0))


def head_slopes(first_head, head_count):
    head_index = first_head + jnp.arange(head_count, dtype=jnp.int32)
    head_float = head_index.astype(jnp.float32)
    return jnp.where(head_index < 8, jnp.exp2(-(head_float + 1.0)), jnp.exp2(-(head_float - 7.5)))


def segment_ids(lengths, positions):
    bounds = jnp.cumsum(lengths, -1)
    return jnp.sum((bounds[:, None, :] <= positions[None, :, None]).astype(jnp.int32), -1)


def score_block(query_heads, query_pos, query_seg, key_heads, key_pos, key_seg, key_keep, slopes):
    scores = (
        jnp.einsum("sqhd,skhd->shqk", query_heads, key_heads, preferred_element_type=jnp.float32)
        * 0.125
    )
    distance = jnp.abs(query_pos[:, None] - key_pos[None, :]).astype(jnp.float32)
    scores = scores - slopes[None, :, None, None] * distance[None, None]
    same_doc = query_seg[:, None, :, None] == key_seg[:, None, None, :]
    visible = (key_keep[:, None, None, :] == 1) | (query_pos[:, None] == key_pos[None, :])[
        None, None
    ]
    return (scores, same_doc & visible)


def grad_block(
    query_heads,
    query_pos,
    query_seg,
    grad_heads,
    log_total,
    delta,
    key_heads,
    value_heads,
    key_pos,
    key_seg,
    key_keep,
    slopes,
):
    scores, allowed = score_block(
        query_heads, query_pos, query_seg, key_heads, key_pos, key_seg, key_keep, slopes
    )
    probs = jnp.where(allowed, jnp.exp(scores - log_total[..., None]), 0.0)
    grad_probs = jnp.einsum(
        "sqhd,skhd->shqk", grad_heads, value_heads, preferred_element_type=jnp.float32
    )
    grad_scores = (probs * (grad_probs - delta[..., None])).astype(jnp.bfloat16)
    grad_query = (
        jnp.einsum("shqk,skhd->sqhd", grad_scores, key_heads, preferred_element_type=jnp.float32)
        * 0.125
    )
    grad_key = (
        jnp.einsum("shqk,sqhd->skhd", grad_scores, query_heads, preferred_element_type=jnp.float32)
        * 0.125
    )
    grad_value = jnp.einsum(
        "shqk,sqhd->skhd",
        probs.astype(jnp.bfloat16),
        grad_heads,
        preferred_element_type=jnp.float32,
    )
    return (grad_query, grad_key, grad_value)


def intersections(query_seg, key_seg):
    return jnp.any((key_seg[:, 0] <= query_seg[:, -1]) & (key_seg[:, -1] >= query_seg[:, 0]))


def guarded(active, update, current):
    return lax.cond(active, update, lambda untouched: untouched, current)


def over_blocks(length, advance, current):
    block_len = 512
    block_count = length // block_len
    return lax.fori_loop(
        0,
        block_count,
        lambda block_index, running: advance(running, block_index * block_len, block_len),
        current,
    )


def per_device_general(
    tokens,
    doc_lengths,
    keep,
    w_query,
    b_query,
    w_key,
    w_value,
    b_value,
    w_out,
    b_out,
    gain_one,
    shift_one,
    w_up,
    w_down,
    b_down,
    gain_two,
    shift_two,
    cotangent,
):
    seq_count, block_rows, model_width = tokens.shape
    local_heads = b_query.shape[0] // HEAD
    head_width = local_heads * HEAD
    row_count = seq_count * block_rows
    slopes = head_slopes(lax.axis_index("tp") * local_heads, local_heads)
    own_pos = lax.axis_index("ctx") * block_rows + jnp.arange(block_rows, dtype=jnp.int32)
    own_seg = segment_ids(doc_lengths, own_pos)
    token_rows = tokens.reshape(row_count, model_width)
    full_query, full_key, full_value, full_out = (
        lax.all_gather(w_query, "fsdp", axis=0, tiled=True),
        lax.all_gather(w_key, "fsdp", axis=0, tiled=True),
        lax.all_gather(w_value, "fsdp", axis=0, tiled=True),
        lax.all_gather(w_out, "fsdp", axis=0, tiled=True),
    )
    queries = (
        jnp.dot(token_rows, full_query, preferred_element_type=jnp.float32) + b_query
    ).astype(jnp.bfloat16)
    key_rows = jnp.dot(token_rows, full_key, preferred_element_type=jnp.float32).astype(
        jnp.bfloat16
    )
    values = (jnp.dot(token_rows, full_value, preferred_element_type=jnp.float32) + b_value).astype(
        jnp.bfloat16
    )
    query_heads = queries.reshape(seq_count, block_rows, local_heads, HEAD)
    key_value = jnp.concatenate([key_rows, values], -1).reshape(
        seq_count, block_rows, 2 * head_width
    )

    def split_pairs(slab_pairs, block_len):
        return (
            slab_pairs[..., :head_width].reshape(seq_count, block_len, local_heads, HEAD),
            slab_pairs[..., head_width:].reshape(seq_count, block_len, local_heads, HEAD),
        )

    def key_slab(pairs, piece_keep, offset, block_len):
        slab_pairs = lax.dynamic_slice_in_dim(pairs, offset, block_len, 1)
        slab_keep = lax.dynamic_slice_in_dim(piece_keep, offset, block_len, 1)
        key_pos = offset + jnp.arange(block_len, dtype=jnp.int32)
        key_seg = segment_ids(doc_lengths, key_pos)
        slab_keys, slab_values = split_pairs(slab_pairs, block_len)
        return (slab_keys, slab_values, slab_keep, key_pos, key_seg)

    start_state = (
        jnp.full((seq_count, local_heads, block_rows), MASKED, jnp.float32),
        jnp.zeros((seq_count, local_heads, block_rows), jnp.float32),
        jnp.zeros((seq_count, local_heads, block_rows, HEAD), jnp.float32),
    )
    pairs = lax.all_gather(key_value, "ctx", axis=1, tiled=True)
    piece_keep = lax.all_gather(keep, "ctx", axis=1, tiled=True)

    def advance(partial_value, offset, block_len):
        slab_keys, slab_values, slab_keep, key_pos, key_seg = key_slab(
            pairs, piece_keep, offset, block_len
        )

        def update(current):
            row_max, row_sum, weighted = current
            scores, allowed = score_block(
                query_heads, own_pos, own_seg, slab_keys, key_pos, key_seg, slab_keep, slopes
            )
            scores = jnp.where(allowed, scores, MASKED)
            new_max = jnp.maximum(row_max, jnp.max(scores, -1))
            factor = jnp.exp(row_max - new_max)
            weights = jnp.where(allowed, jnp.exp(scores - new_max[..., None]), 0.0)
            row_sum = row_sum * factor + jnp.sum(weights, -1)
            weighted = weighted * factor[..., None] + jnp.einsum(
                "shqk,skhd->shqd",
                weights.astype(jnp.bfloat16),
                slab_values,
                preferred_element_type=jnp.float32,
            )
            return (new_max, row_sum, weighted)

        return guarded(intersections(own_seg, key_seg), update, partial_value)

    row_max, row_sum, weighted = over_blocks(pairs.shape[1], advance, start_state)
    attended = (
        (weighted / row_sum[..., None])
        .transpose(0, 2, 1, 3)
        .reshape(row_count, head_width)
        .astype(jnp.bfloat16)
    )
    log_total = row_max + jnp.log(row_sum)
    att_part = jnp.einsum("rh,dh->rd", attended, full_out, preferred_element_type=jnp.float32)
    branch_att = lax.psum(att_part.astype(jnp.bfloat16), "tp").astype(jnp.float32) + b_out
    first_out, normed_one, inv_one = layer_norm(
        token_rows.astype(jnp.float32) + branch_att, gain_one, shift_one
    )
    first_low = first_out.astype(jnp.bfloat16)
    full_up, full_down = (
        lax.all_gather(w_up, "fsdp", axis=0, tiled=True),
        lax.all_gather(w_down, "fsdp", axis=0, tiled=True),
    )
    gate_up = jnp.einsum("rd,dcf->rcf", first_low, full_up, preferred_element_type=jnp.float32)
    product, gelu_back = jax.vjp(
        lambda gate_part, up_part: jax.nn.gelu(gate_part, approximate=False) * up_part,
        gate_up[:, 0],
        gate_up[:, 1],
    )
    hidden = product.astype(jnp.bfloat16)
    ffn_part = jnp.einsum("rf,df->rd", hidden, full_down, preferred_element_type=jnp.float32)
    branch_ffn = lax.psum(ffn_part.astype(jnp.bfloat16), "tp").astype(jnp.float32) + b_down
    result, normed_two, inv_two = layer_norm(first_out + branch_ffn, gain_two, shift_two)
    grad_in = cotangent.reshape(row_count, model_width).astype(jnp.float32)
    grad_two, d_gain_two, d_shift_two = norm_back(grad_in, normed_two, inv_two, gain_two)
    grad_ffn = grad_two.astype(jnp.bfloat16)
    d_b_down = jnp.sum(grad_ffn.astype(jnp.float32), 0)
    d_w_down = jnp.einsum("rd,rf->df", grad_ffn, hidden, preferred_element_type=jnp.float32)
    grad_hidden = jnp.einsum("rd,df->rf", grad_ffn, full_down, preferred_element_type=jnp.float32)
    grad_gate, grad_up = gelu_back(grad_hidden)
    grad_gate_up = jnp.stack([grad_gate, grad_up], 1).astype(jnp.bfloat16)
    d_w_up = jnp.einsum("rd,rcf->dcf", first_low, grad_gate_up, preferred_element_type=jnp.float32)
    first_part = jnp.einsum(
        "rcf,dcf->rd", grad_gate_up, full_up, preferred_element_type=jnp.float32
    )
    grad_first = grad_two + lax.psum(first_part.astype(jnp.bfloat16), "tp").astype(jnp.float32)
    grad_one, d_gain_one, d_shift_one = norm_back(grad_first, normed_one, inv_one, gain_one)
    grad_att = grad_one.astype(jnp.bfloat16)
    d_b_out = jnp.sum(grad_att.astype(jnp.float32), 0)
    d_w_out = jnp.einsum("rd,rh->dh", grad_att, attended, preferred_element_type=jnp.float32)
    grad_attended = jnp.einsum(
        "rd,dh->rh", grad_att, full_out, preferred_element_type=jnp.float32
    ).astype(jnp.bfloat16)
    grad_heads = grad_attended.reshape(seq_count, block_rows, local_heads, HEAD)
    delta = jnp.einsum(
        "sqhd,sqhd->shq",
        grad_heads,
        attended.reshape(seq_count, block_rows, local_heads, HEAD),
        preferred_element_type=jnp.float32,
    )
    query_zero = jnp.zeros((seq_count, block_rows, local_heads, HEAD), jnp.float32)
    full_len = block_rows * lax.axis_size("ctx")
    term_zero = jnp.zeros((seq_count, full_len, 2 * head_width), jnp.float32)
    return_pairs = lax.all_gather(key_value, "ctx", axis=1, tiled=True)
    return_piece_keep = lax.all_gather(keep, "ctx", axis=1, tiled=True)

    def advance(partial_value, offset, block_len):
        slab_keys, slab_values, slab_keep, key_pos, key_seg = key_slab(
            return_pairs, return_piece_keep, offset, block_len
        )

        def update(current):
            query_grad, key_terms = current
            part_query, part_key, part_value = grad_block(
                query_heads,
                own_pos,
                own_seg,
                grad_heads,
                log_total,
                delta,
                slab_keys,
                slab_values,
                key_pos,
                key_seg,
                slab_keep,
                slopes,
            )
            slab_grads = jnp.concatenate(
                [
                    part_key.reshape(seq_count, block_len, head_width),
                    part_value.reshape(seq_count, block_len, head_width),
                ],
                -1,
            )
            return (
                query_grad + part_query,
                lax.dynamic_update_slice_in_dim(key_terms, slab_grads, offset, 1),
            )

        return guarded(intersections(own_seg, key_seg), update, partial_value)

    query_grad, key_terms = over_blocks(return_pairs.shape[1], advance, (query_zero, term_zero))
    pair_grads = lax.psum_scatter(
        key_terms.astype(jnp.bfloat16), "ctx", scatter_dimension=1, tiled=True
    ).astype(jnp.float32)
    query_low = query_grad.reshape(row_count, head_width).astype(jnp.bfloat16)
    pair_low = pair_grads.reshape(row_count, 2 * head_width).astype(jnp.bfloat16)
    grad_project = jnp.concatenate([query_low, pair_low], -1)
    joined_weights = jnp.concatenate([full_query, full_key, full_value], -1)
    joined_grads = jnp.einsum(
        "rd,rh->dh", token_rows, grad_project, preferred_element_type=jnp.float32
    )
    input_part = jnp.einsum(
        "rh,dh->rd", grad_project, joined_weights, preferred_element_type=jnp.float32
    )
    d_tokens = grad_one + lax.psum(input_part.astype(jnp.bfloat16), "tp").astype(jnp.float32)
    d_b_query = jnp.sum(query_low.astype(jnp.float32), 0)
    d_b_value = jnp.sum(pair_low[:, head_width:].astype(jnp.float32), 0)
    d_w_query = joined_grads[:, :head_width]
    d_w_key = joined_grads[:, head_width : 2 * head_width]
    d_w_value = joined_grads[:, 2 * head_width :]
    shard_grads = (
        lax.psum_scatter(
            d_w_query.astype(jnp.bfloat16), "fsdp", scatter_dimension=0, tiled=True
        ).astype(jnp.float32),
        lax.psum_scatter(
            d_w_key.astype(jnp.bfloat16), "fsdp", scatter_dimension=0, tiled=True
        ).astype(jnp.float32),
        lax.psum_scatter(
            d_w_value.astype(jnp.bfloat16), "fsdp", scatter_dimension=0, tiled=True
        ).astype(jnp.float32),
        lax.psum_scatter(
            d_w_out.astype(jnp.bfloat16), "fsdp", scatter_dimension=0, tiled=True
        ).astype(jnp.float32),
        lax.psum_scatter(
            d_w_up.astype(jnp.bfloat16), "fsdp", scatter_dimension=0, tiled=True
        ).astype(jnp.float32),
        lax.psum_scatter(
            d_w_down.astype(jnp.bfloat16), "fsdp", scatter_dimension=0, tiled=True
        ).astype(jnp.float32),
    )
    sum_query, sum_key, sum_value, sum_out, sum_up, sum_down = (
        lax.psum(shard_grads[0].astype(jnp.bfloat16), "ctx").astype(jnp.float32),
        lax.psum(shard_grads[1].astype(jnp.bfloat16), "ctx").astype(jnp.float32),
        lax.psum(shard_grads[2].astype(jnp.bfloat16), "ctx").astype(jnp.float32),
        lax.psum(shard_grads[3].astype(jnp.bfloat16), "ctx").astype(jnp.float32),
        lax.psum(shard_grads[4].astype(jnp.bfloat16), "ctx").astype(jnp.float32),
        lax.psum(shard_grads[5].astype(jnp.bfloat16), "ctx").astype(jnp.float32),
    )
    (
        total_b_query,
        total_b_value,
        total_b_out,
        total_b_down,
        total_gain_one,
        total_shift_one,
        total_gain_two,
        total_shift_two,
    ) = lax.psum(
        (d_b_query, d_b_value, d_b_out, d_b_down, d_gain_one, d_shift_one, d_gain_two, d_shift_two),
        ("fsdp", "ctx"),
    )
    return (
        result.reshape(seq_count, block_rows, model_width).astype(jnp.bfloat16),
        d_tokens.reshape(seq_count, block_rows, model_width),
        sum_query,
        total_b_query,
        sum_key,
        sum_value,
        total_b_value,
        sum_out,
        total_b_out,
        total_gain_one,
        total_shift_one,
        sum_up,
        sum_down,
        total_b_down,
        total_gain_two,
        total_shift_two,
    )


LANES = 128
VMEM_BYTES = 60 << 20
MESH = pl.DeviceIdType.MESH
TILE = 256
DOC_ROW, KEEP_ROW, POS_ROW, LINE_ROW, LOG_ROW, FEAT_END = 64, 72, 73, 79, 82, 85
X_SWAP = [(0, 1), (1, 0), (2, 3), (3, 2)]
Y_SWAP = [(0, 2), (2, 0), (1, 3), (3, 1)]
D_SWAP = [(0, 3), (3, 0), (1, 2), (2, 1)]


def dot(left, right, dims=((1,), (0,))):
    return lax.dot_general(left, right, (dims, ((), ())), preferred_element_type=jnp.float32)


def three_terms(value, low):
    high = low(value)
    middle = low(value - high)
    return high, middle, low(value - high - middle)


def side_signs(rows):
    sub = lax.broadcasted_iota(jnp.int32, (LANES, rows), 0)
    bias_rows = (sub >= POS_ROW) & (sub < LOG_ROW)
    after = jnp.where(bias_rows, -1.0, 1.0).astype(jnp.bfloat16)
    same = jnp.where(bias_rows, 0.0, 1.0).astype(jnp.bfloat16)
    bare = jnp.where(bias_rows | (sub == KEEP_ROW), 0.0, 1.0).astype(jnp.bfloat16)
    return after, same, bare


def diagonal_scores(keys, queries_t, same, bare, slopes):
    rows = lax.broadcasted_iota(jnp.int32, (TILE, TILE), 0)
    cols = lax.broadcasted_iota(jnp.int32, (TILE, TILE), 1)
    apart = jnp.abs(rows - cols).astype(jnp.float32)
    own = rows == cols
    full = [dot(key, query_t * same) for key, query_t in zip(keys, queries_t)]
    alone = [dot(key, query_t * bare) for key, query_t in zip(keys, queries_t)]
    return [
        jnp.where(own, single, scores - slope * apart)
        for scores, single, slope in zip(full, alone, slopes)
    ]


def sweep(first, last, step, most=2):
    many = (last - first) // most

    @pl.loop(0, many)
    def _(i):
        step(first + i * most, most)

    @pl.loop(first + many * most, last)
    def _(tile):
        step(tile, 1)


def doc_bounds(docs_ref, seq):
    bounds, total = [], 0
    for index in range(docs_ref.shape[1]):
        total = total + docs_ref[seq, index]
        bounds.append(total)
    return bounds


def tile_span(docs_ref, seq, block):
    first, last = block * TILE, block * TILE + TILE - 1
    begin = end = start = 0
    for bound in doc_bounds(docs_ref, seq):
        begin = jnp.where(bound <= first, bound, begin)
        end = jnp.where(start <= last, bound, end)
        start = bound
    return lax.div(begin, TILE), lax.div(end + TILE - 1, TILE)


def start_kernel(
    docs, slopes, tokens, keep, w_query, w_key, w_value, w_out, w_up, b_query, b_value, cotangent,
    sequence, full_joined, full_out, full_gate, up_lift, cot_far, cot_near, query_t, queries, keys, keys_t, values, values_t,
    tokens_v, own_v, joined_v, keep_v, gate_v, lift_v, qt_v, q_v, k_v, kt_v, v_v, vt_v,
    z_send, z_recv, tp_send, tp_recv, w_send, w_recv, gate_send, gate_recv, keep_send, keep_recv, local_sem,
    block_sem, joined_sem, lift_sem, gate_sem, cot_sem, out_sem,
):
    place, stage, core = lax.axis_index("fsdp"), lax.axis_index("ctx"), lax.axis_index("tp")
    seq, half = stage // 2, stage % 2
    half_rows, model_width = sequence.shape[2:]
    rows_of = 2 * half_rows
    heads = qt_v.shape[1]
    width = heads * HEAD
    f32, bf16 = jnp.float32, jnp.bfloat16
    barrier = pltpu.get_barrier_semaphore()
    peers = [(place ^ other, stage, core) for other in (1, 2, 3)]
    peers += [(place, lax.rem(stage + shift, 4), core) for shift in (1, 2, 3)]
    peers += [(place, stage, 1 - core)]
    for peer in peers:
        pl.semaphore_signal(barrier, inc=1, device_id=peer, device_id_type=MESH)

    def columns_of(weight):
        return jnp.where(half == 0, weight[:, :width], weight[:, width:])

    own_v[...] = jnp.concatenate([columns_of(w[...]) for w in (w_query, w_key, w_value)], 1)
    joined_v[place] = own_v[...]
    tokens_v[stage] = tokens[seq].reshape(2, half_rows, model_width)
    keep_v[stage] = keep[...]
    pl.semaphore_wait(barrier, len(peers))

    def remote(source, target, send, recv, device):
        return pltpu.make_async_remote_copy(
            source, target, send, recv, device_id=device, device_id_type=MESH
        )

    rows = pl.ds(pl.multiple_of(core * half_rows, half_rows), half_rows)
    ours, theirs = tokens.at[seq, rows], tokens.at[1 - seq, rows]
    other_core = (place, stage, 1 - core)
    inner = (stage == 1) | (stage == 2)
    facing, opposite = 3 - stage, stage ^ 2
    third, fourth = jnp.where(inner, facing, opposite), jnp.where(inner, opposite, facing)

    def send(source, block, target, slot):
        return remote(source, tokens_v.at[block, core], z_send.at[slot], z_recv.at[block], (place, target, core))

    def arrival(block):
        return remote(ours, tokens_v.at[block, core], z_send.at[0], z_recv.at[block], other_core)

    def share(block, whose):
        half_block = tokens_v.at[block, whose]
        return remote(half_block, half_block, tp_send.at[block], tp_recv.at[block], other_core)

    to_pair = send(ours, stage, stage ^ 1, 0)
    to_across = send(theirs, stage, third, 1)
    to_pair.start()

    @pl.when(inner)
    def _():
        to_across.start()

    weights = [
        remote(
            own_v, joined_v.at[place], w_send.at[other - 1], w_recv.at[other - 1], (place ^ other, stage, core)
        )
        for other in (1, 2, 3)
    ]
    flags = [
        remote(
            keep, keep_v.at[stage], keep_send.at[shift - 1], keep_recv.at[shift - 1],
            (place, lax.rem(stage + shift, 4), core),
        )
        for shift in (1, 2, 3)
    ]
    outs = [
        remote(
            w_out, full_out.at[place], w_send.at[other + 2], w_recv.at[other + 2], (place ^ other, stage, core)
        )
        for other in (1, 2, 3)
    ]

    units = w_up.shape[2] // 2

    def gate_copy(owner, other, which, sem):
        block = gate_v.at[owner, :, pl.ds(which * units, units)]
        return remote(block, block, gate_send.at[sem], gate_recv.at[sem], (place ^ other, stage, core))

    halves = [
        gate_copy(place, other, which, 2 * which + other - 1)
        for other, which in ((1, 0), (2, 1), (1, 1), (2, 0))
    ]
    on = [gate_copy(place ^ 1, 2, 0, 4), gate_copy(place ^ 2, 1, 1, 5)]
    for copy in weights + flags + outs:
        copy.start()
    gate_v[place] = w_up[:, 0, :]
    for copy in halves:
        copy.start()
    lift_v[...] = w_up[:, 1, :]
    lift_out = pltpu.make_async_copy(lift_v, up_lift, lift_sem)
    lift_out.start()
    own_out = pltpu.make_async_copy(w_out, full_out.at[place], local_sem)
    own_out.start()
    odd = stage % 2
    cot_outs = [
        pltpu.make_async_copy(cotangent.at[1 - odd, core], cot_far, cot_sem.at[0]),
        pltpu.make_async_copy(cotangent.at[odd, core], cot_near, cot_sem.at[1]),
    ]
    for copy in cot_outs:
        copy.start()

    bounds = doc_bounds(docs, seq)

    def out_copies(slot, block):
        at = pl.ds(pl.multiple_of(block * rows_of, rows_of), rows_of)
        pairs = (
            (qt_v.at[slot], query_t.at[:, :, at]),
            (q_v.at[slot], queries.at[:, at, :]),
            (k_v.at[slot], keys.at[:, at, :]),
            (kt_v.at[slot], keys_t.at[:, :, at]),
            (v_v.at[slot], values.at[:, at, :]),
            (vt_v.at[slot], values_t.at[:, :, at]),
        )
        return [
            pltpu.make_async_copy(source, target, block_sem.at[slot, index])
            for index, (source, target) in enumerate(pairs)
        ]

    def sequence_copy(block):
        return pltpu.make_async_copy(tokens_v.at[block], sequence.at[block], out_sem.at[block])

    def low(value):
        return value.astype(bf16).astype(f32)

    def project(slot, block):
        x = tokens_v[block].reshape(rows_of, model_width)
        y = dot(x, joined_v[...].reshape(model_width, 3 * width))
        zero = jnp.zeros((1, width), f32)
        biases = [
            jnp.where(half == 0, b[:, :width], b[:, width:])
            for b in (b_query[...].reshape(1, -1), b_value[...].reshape(1, -1))
        ]
        y = low(y + jnp.concatenate([biases[0], zero, biases[1]], 1))
        fill = -y.shape[1] % LANES
        if fill:
            y = jnp.concatenate([y, jnp.zeros((rows_of, fill), f32)], 1)
        lane = lax.broadcasted_iota(jnp.int32, (rows_of, LANES), 1)
        sub = lax.broadcasted_iota(jnp.int32, (LANES, rows_of), 0)
        first = block * rows_of
        key_pos = first + lax.broadcasted_iota(jnp.int32, (rows_of, LANES), 0)
        query_pos = first + lax.broadcasted_iota(jnp.int32, (LANES, rows_of), 1)

        def segments(positions):
            return sum((bound <= positions).astype(jnp.int32) for bound in bounds)

        flag = keep_v[block, pl.ds(seq, 1), :].astype(f32)
        flag = jnp.broadcast_to(flag, (LANES, rows_of)).T
        key_feat = jnp.where(lane < DOC_ROW, 0.0, 1.0)
        key_doc = jnp.where(segments(key_pos) == lane - DOC_ROW, 0.0, MASKED)
        key_feat = jnp.where((lane >= DOC_ROW) & (lane < DOC_ROW + len(bounds)), key_doc, key_feat)
        key_feat = jnp.where(lane == KEEP_ROW, jnp.where(flag > 0.5, 0.0, MASKED), key_feat)
        pos_low = key_pos & 255
        key_feat = jnp.where(
            (lane >= POS_ROW) & (lane < POS_ROW + 3), (key_pos - pos_low).astype(f32), key_feat
        )
        key_feat = jnp.where((lane >= POS_ROW + 3) & (lane < LINE_ROW), pos_low.astype(f32), key_feat)
        key_feat = jnp.where(lane >= FEAT_END, 0.0, key_feat)
        doc_feat = jnp.where(segments(query_pos) == sub - DOC_ROW, 1.0, 0.0)
        doc_feat = jnp.where(sub == KEEP_ROW, 1.0, doc_feat)

        def head_part(index):
            pair = y[:, index // 2 * LANES : (index // 2 + 1) * LANES]
            if index % 2:
                pair = pltpu.roll(pair, HEAD, 1)
            return jnp.where(lane < HEAD, pair, 0.0)

        for head in range(heads):
            query_feat = doc_feat
            slope = jnp.full((1, rows_of), slopes[head], f32)
            slope_terms = three_terms(slope, low)
            line_terms = three_terms(-slope * query_pos[:1].astype(f32), low)
            for term in range(3):
                here = (sub == POS_ROW + term) | (sub == POS_ROW + 3 + term)
                query_feat = jnp.where(here, slope_terms[term], query_feat)
                query_feat = jnp.where(sub == LINE_ROW + term, line_terms[term], query_feat)
            query = head_part(head) * 0.125
            q_v[slot, head] = query[:, :HEAD].astype(bf16)
            qt_v[slot, head] = (query.T + query_feat).astype(bf16)
            key = head_part(heads + head)
            k_v[slot, head] = (key + key_feat).astype(bf16)
            kt_v[slot, head] = key.T[:HEAD].astype(bf16)
            value = head_part(2 * heads + head)
            ones = (lane >= HEAD) & (lane < HEAD + 3)
            v_v[slot, head] = jnp.where(ones, 1.0, value).astype(bf16)
            vt_v[slot, head] = jnp.where(sub == HEAD, 1.0, value.T)[:80].astype(bf16)

    for copy in weights + flags:
        copy.wait_recv()
    joined_out = pltpu.make_async_copy(joined_v, full_joined, joined_sem)
    joined_out.start()

    @pl.when(~inner)
    def _():
        to_pair.wait_send()
        to_across.start()

    @pl.loop(0, 4)
    def _(i):
        pair = stage ^ 1
        block = jnp.where(i == 0, stage, jnp.where(i == 1, pair, jnp.where(i == 2, third, fourth)))
        slot = lax.rem(i, 2)

        @pl.when(i == 1)
        def _():
            arrival(pair).wait_recv()
            share(pair, core).start()
            arrival(third).wait_recv()

            @pl.when(inner)
            def _():
                send(tokens_v.at[third, core], third, pair, 2).start()

            share(third, core).start()
            for near, far in zip(halves[:2], on):
                near.wait_recv()
                far.start()

        @pl.when(i == 3)
        def _():
            arrival(fourth).wait_recv()

            @pl.when(inner)
            def _():
                send(tokens_v.at[fourth, core], fourth, pair, 3).start()

            share(fourth, core).start()

        @pl.when(i >= 1)
        def _():
            share(block, 1 - core).wait_recv()

        @pl.when(i >= 2)
        def _():
            for copy in out_copies(slot, block):
                copy.wait()

        sequence_copy(block).start()
        project(slot, block)
        for copy in out_copies(slot, block):
            copy.start()

    @pl.when(inner)
    def _():
        to_pair.wait_send()

    to_across.wait_send()

    @pl.when(inner)
    def _():
        for block, slot in ((third, 2), (fourth, 3)):
            send(tokens_v.at[block, core], block, stage ^ 1, slot).wait_send()

    for block in (stage ^ 1, third, fourth):
        share(block, core).wait_send()
    for copy in outs + halves[2:] + on:
        copy.wait()
    gate_out = pltpu.make_async_copy(gate_v, full_gate, gate_sem)
    gate_out.start()
    for copy in weights + flags + halves[:2]:
        copy.wait_send()
    for copy in [own_out, joined_out, lift_out, gate_out] + cot_outs:
        copy.wait()
    for block in range(4):
        sequence_copy(block).wait()
    for slot in (0, 1):
        for copy in out_copies(slot, 0):
            copy.wait()


def start(docs, slopes, tokens, keep, w_query, w_key, w_value, w_out, w_up, b_query, b_value, cotangent):
    _, block_rows, model_width = tokens.shape
    heads = slopes.shape[0]
    width, length = heads * HEAD, 4 * block_rows
    dma, bf16 = pltpu.SemaphoreType.DMA, jnp.bfloat16
    half_rows, quarter = block_rows // 2, w_query.shape[0]
    any_spec = pl.BlockSpec(memory_space=pl.ANY)
    vmem_spec = pl.BlockSpec(memory_space=pltpu.VMEM)
    smem_spec = pl.BlockSpec(memory_space=pltpu.SMEM)

    def parts(rows):
        return [
            (heads, LANES, rows),
            (heads, rows, HEAD),
            (heads, rows, LANES),
            (heads, HEAD, rows),
            (heads, rows, LANES),
            (heads, 80, rows),
        ]

    three, four, six = dma((3,)), dma((4,)), dma((6,))
    return pl.pallas_call(
        start_kernel,
        in_specs=[smem_spec] * 2 + [vmem_spec] * 10,
        out_specs=[any_spec] * 13,
        out_shape=[
            jax.ShapeDtypeStruct(shape, bf16)
            for shape in [
                (4, 2, half_rows, model_width),
                (4, quarter, 3 * width),
                (4,) + w_out.shape,
                (4, quarter, w_up.shape[2]),
                (quarter, w_up.shape[2]),
                (half_rows, model_width),
                (half_rows, model_width),
            ]
            + parts(length)
        ],
        scratch_shapes=[
            pltpu.VMEM((4, 2, half_rows, model_width), bf16),
            pltpu.VMEM((quarter, 3 * width), bf16),
            pltpu.VMEM((4, quarter, 3 * width), bf16),
            pltpu.VMEM((4,) + keep.shape, keep.dtype),
            pltpu.VMEM((4, quarter, w_up.shape[2]), bf16),
            pltpu.VMEM((quarter, w_up.shape[2]), bf16),
            *[pltpu.VMEM((2,) + shape, bf16) for shape in parts(block_rows)],
            four, four, four, four, six, six, six, six, three, three, dma, dma((2, 6)), dma, dma, dma, dma((2,)), four,
        ],
        compiler_params=pltpu.CompilerParams(
            collective_id=0, has_side_effects=True, vmem_limit_bytes=VMEM_BYTES
        ),
        cost_estimate=pl.CostEstimate(flops=40 << 30, bytes_accessed=16 << 20, transcendentals=0),
        name="start",
    )(docs, slopes, tokens, keep, w_query, w_key, w_value, w_out, w_up, b_query, b_value, cotangent)


def attend_kernel(docs_ref, slope_ref, qt_ref, k_ref, vt_ref, o_ref, ot_ref, lse_ref, max_ref, acc_ref):
    heads = qt_ref.shape[0]
    block = pl.program_id(0)
    first_tile, last_tile = tile_span(docs_ref, lax.axis_index("ctx") // 2, block)
    after, same, bare = side_signs(TILE)

    def tile_rows(tile, count=1):
        return pl.ds(pl.multiple_of(tile * TILE, TILE), count * TILE)

    own = tile_rows(block)
    each = range(heads)
    scores = diagonal_scores(
        [k_ref[head, own, :] for head in each], [qt_ref[head] for head in each], same, bare,
        [slope_ref[head] for head in each],
    )
    tops = [jnp.max(scores[head], 0, keepdims=True) for head in each]
    weights = [jnp.exp(scores[head] - tops[head]).astype(jnp.bfloat16) for head in each]
    parts = [dot(vt_ref[head, :, own], weights[head]) for head in each]
    for head in each:
        max_ref[head] = tops[head]
        acc_ref[head] = parts[head]

    def step(tile, count, sign):
        each = range(heads)
        keys = [k_ref[head, tile_rows(tile, count), :] for head in each]
        values = [vt_ref[head, :, tile_rows(tile, count)] for head in each]
        queries = [qt_ref[head] if sign is None else qt_ref[head] * sign for head in each]
        old = [max_ref[head] for head in each]
        acc = [acc_ref[head] for head in each]
        scores = [dot(keys[head], queries[head]) for head in each]
        top = [jnp.maximum(old[head], jnp.max(scores[head], 0, keepdims=True)) for head in each]
        weights = [jnp.exp(scores[head] - top[head]).astype(jnp.bfloat16) for head in each]
        parts = [dot(values[head], weights[head]) for head in each]
        for head in each:
            max_ref[head] = top[head]
            acc_ref[head] = acc[head] * jnp.exp(old[head] - top[head]) + parts[head]

    sweep(first_tile, block, lambda tile, count: step(tile, count, None))
    sweep(block + 1, last_tile, lambda tile, count: step(tile, count, after))

    parts = []
    for head in range(heads):
        total = acc_ref[head, HEAD : HEAD + 1, :]
        out_t = acc_ref[head, :HEAD, :] / total
        ot_ref[head] = out_t
        parts.append(out_t)
        lse_ref[head] = max_ref[head] + jnp.log(total)
    o_ref[...] = jnp.concatenate(parts, 0).T.astype(jnp.bfloat16)


def attend(docs, slopes, query_t, keys, value_t):
    heads, _, length = query_t.shape
    blocks = length // TILE
    return pl.pallas_call(
        attend_kernel,
        grid_spec=pltpu.PrefetchScalarGridSpec(
            num_scalar_prefetch=2,
            grid=(blocks,),
            in_specs=[
                pl.BlockSpec((heads, LANES, TILE), lambda i, *_: (0, 0, i)),
                pl.BlockSpec(keys.shape, lambda i, *_: (0, 0, 0)),
                pl.BlockSpec(value_t.shape, lambda i, *_: (0, 0, 0)),
            ],
            out_specs=[
                pl.BlockSpec((TILE, heads * HEAD), lambda i, *_: (i, 0)),
                pl.BlockSpec((heads, HEAD, TILE), lambda i, *_: (0, 0, i)),
                pl.BlockSpec((heads, 1, TILE), lambda i, *_: (0, 0, i)),
            ],
            scratch_shapes=[
                pltpu.VMEM((heads, 1, TILE), jnp.float32),
                pltpu.VMEM((heads, 80, TILE), jnp.float32),
            ],
        ),
        out_shape=[
            jax.ShapeDtypeStruct((length, heads * HEAD), jnp.bfloat16),
            jax.ShapeDtypeStruct((heads, HEAD, length), jnp.float32),
            jax.ShapeDtypeStruct((heads, 1, length), jnp.float32),
        ],
        compiler_params=pltpu.CompilerParams(vmem_limit_bytes=VMEM_BYTES),
        cost_estimate=pl.CostEstimate(
            flops=heads * length * length * 256, bytes_accessed=6 << 20, transcendentals=heads * length * length
        ),
        name="attend",
    )(docs, slopes, query_t, keys, value_t)


def attend_back_kernel(
    docs_ref, slope_ref, qt_ref, q_ref, k_ref, kt_ref, v_ref, g_ref, ot_ref, lse_ref,
    dq_ref, dk_ref, dv_ref, qt_log, grad_heads, grad_t, query_acc, key_acc, value_acc,
):
    heads = qt_ref.shape[0]
    blocks = pl.num_programs(0)
    block = pl.program_id(0)
    length = qt_ref.shape[2]
    first_tile, last_tile = tile_span(docs_ref, lax.axis_index("ctx") // 2, block)
    after, same, bare = side_signs(TILE)

    def low(value):
        return value.astype(jnp.bfloat16).astype(jnp.float32)

    def tile_rows(tile, count=1):
        return pl.ds(pl.multiple_of(tile * TILE, TILE), count * TILE)

    @pl.when(block == 0)
    def _():
        query_acc[...] = jnp.zeros_like(query_acc)
        sub = lax.broadcasted_iota(jnp.int32, (LANES, TILE), 0)

        @pl.loop(0, length // TILE)
        def _(tile):
            rows = tile_rows(tile)
            grad = g_ref[rows, :].astype(jnp.float32)
            turned = grad.T
            for head in range(heads):
                own = turned[head * HEAD : (head + 1) * HEAD]
                delta = jnp.sum(own * ot_ref[head, :, rows], 0, keepdims=True)
                first, second, third = three_terms(-delta, low)
                wide = jnp.concatenate([own, jnp.zeros_like(own)], 0)
                wide = jnp.where(sub == HEAD, first, wide)
                wide = jnp.where(sub == HEAD + 1, second, wide)
                wide = jnp.where(sub == HEAD + 2, third, wide)
                grad_t[head, :, rows] = wide.astype(jnp.bfloat16)
                grad_heads[head, rows, :] = own.T.astype(jnp.bfloat16)
                first, second, third = three_terms(-lse_ref[head, :, rows], low)
                query = qt_ref[head, :, rows].astype(jnp.float32)
                query = jnp.where(sub == LOG_ROW, first, query)
                query = jnp.where(sub == LOG_ROW + 1, second, query)
                query = jnp.where(sub == LOG_ROW + 2, third, query)
                qt_log[head, :, rows] = query.astype(jnp.bfloat16)

    def accumulate(tile, scores, first, count=1):
        each = range(heads)
        rows = tile_rows(tile, count)
        values = [v_ref[head] for head in each]
        turned = [grad_t[head, :, rows] for head in each]
        grads = [grad_heads[head, rows, :] for head in each]
        queries = [q_ref[head, rows, :] for head in each]
        keys_t = [kt_ref[head] for head in each]
        probs = [jnp.exp(scores[head]) for head in each]
        grad_probs = [dot(values[head], turned[head]) for head in each]
        grad_scores = [(probs[head] * grad_probs[head]).astype(jnp.bfloat16) for head in each]
        value_part = [dot(probs[head].astype(jnp.bfloat16), grads[head]) for head in each]
        key_part = [dot(grad_scores[head], queries[head]) for head in each]
        query_part = [dot(keys_t[head], grad_scores[head]) for head in each]
        for head in each:
            if first:
                value_acc[head] = value_part[head]
                key_acc[head] = key_part[head]
            else:
                value_acc[head] += value_part[head]
                key_acc[head] += key_part[head]
            query_acc[head, :, rows] += query_part[head]

    own = [qt_log[head, :, tile_rows(block)] for head in range(heads)]
    accumulate(
        block,
        diagonal_scores(
            [k_ref[head] for head in range(heads)], own, same, bare,
            [slope_ref[head] for head in range(heads)],
        ),
        True,
    )
    after_wide = side_signs(2 * TILE)[0]

    def step(tile, count, sign):
        queries = [qt_log[head, :, tile_rows(tile, count)] for head in range(heads)]
        if sign is not None:
            queries = [query * sign[:, : count * TILE] for query in queries]
        accumulate(tile, [dot(k_ref[head], queries[head]) for head in range(heads)], False, count)

    sweep(first_tile, block, lambda tile, count: step(tile, count, after_wide))
    sweep(block + 1, last_tile, lambda tile, count: step(tile, count, None))

    dk_ref[...] = jnp.concatenate([key_acc[head] for head in range(heads)], 1).astype(jnp.bfloat16)
    dv_ref[...] = jnp.concatenate([value_acc[head] for head in range(heads)], 1).astype(jnp.bfloat16)

    @pl.when(block == blocks - 1)
    def _():
        @pl.loop(0, length // TILE)
        def _(tile):
            rows = tile_rows(tile)
            turned = jnp.concatenate([query_acc[head, :, rows] for head in range(heads)], 0)
            dq_ref[rows, :] = (turned.T * 0.125).astype(jnp.bfloat16)


def attend_back(docs, slopes, query_t, queries, keys, keys_t, values, grads, out_t, lse):
    heads, _, length = query_t.shape
    blocks = length // TILE
    width = heads * HEAD

    def whole(array):
        return pl.BlockSpec(array.shape, lambda i, *_: (0,) * array.ndim)

    return pl.pallas_call(
        attend_back_kernel,
        grid_spec=pltpu.PrefetchScalarGridSpec(
            num_scalar_prefetch=2,
            grid=(blocks,),
            in_specs=[
                whole(query_t),
                whole(queries),
                pl.BlockSpec((heads, TILE, LANES), lambda i, *_: (0, i, 0)),
                pl.BlockSpec((heads, HEAD, TILE), lambda i, *_: (0, 0, i)),
                pl.BlockSpec((heads, TILE, LANES), lambda i, *_: (0, i, 0)),
                whole(grads),
                whole(out_t),
                whole(lse),
            ],
            out_specs=[
                pl.BlockSpec((length, width), lambda i, *_: (0, 0)),
                pl.BlockSpec((TILE, width), lambda i, *_: (i, 0)),
                pl.BlockSpec((TILE, width), lambda i, *_: (i, 0)),
            ],
            scratch_shapes=[
                pltpu.VMEM((heads, LANES, length), jnp.bfloat16),
                pltpu.VMEM((heads, length, HEAD), jnp.bfloat16),
                pltpu.VMEM((heads, LANES, length), jnp.bfloat16),
                pltpu.VMEM((heads, HEAD, length), jnp.float32),
                pltpu.VMEM((heads, TILE, HEAD), jnp.float32),
                pltpu.VMEM((heads, TILE, HEAD), jnp.float32),
            ],
        ),
        out_shape=[jax.ShapeDtypeStruct((length, width), jnp.bfloat16)] * 3,
        compiler_params=pltpu.CompilerParams(vmem_limit_bytes=VMEM_BYTES),
        cost_estimate=pl.CostEstimate(
            flops=heads * length * length * 640, bytes_accessed=12 << 20, transcendentals=heads * length * length
        ),
        name="attend_back",
    )(docs, slopes, query_t, queries, keys, keys_t, values, grads, out_t, lse)


def rows_norm(residual):
    centered = residual - jnp.mean(residual, -1, keepdims=True)
    inv_scale = lax.rsqrt(jnp.mean(centered * centered, -1, keepdims=True) + NORM_EPS)
    return centered * inv_scale, inv_scale


def rows_norm_back(grad_out, normed, inv_scale, norm_gain):
    grad_norm = grad_out * norm_gain
    mean_grad = jnp.mean(grad_norm, -1, keepdims=True)
    mean_cross = jnp.mean(grad_norm * normed, -1, keepdims=True)
    return (grad_norm - mean_grad - normed * mean_cross) * inv_scale


def middle_kernel(
    attended, sequence, cotangent, cot_far, cot_near, w_out, gate_full, w_down, lift_0, lift_1, lift_2, lift_3, *rest,
):
    vectors, rest = rest[:6], rest[6:]
    (
        out_home, grad_one, grad_heads, early_0, early_1, early_2, early_3, late, down_sum, sums,
        token_v, mine_v, theirs_v, both_v, cot_v, out_w, down_w, up_w,
        send_a, recv_a, send_b, recv_b, send_c, recv_c,
        normed_v, inv_v, low_v, hidden_v, gate_v, lift_v, grad_v, ffn_v, att_v, result_v, keep_v, away_v, tile_v,
        down_v, down_got, home_v, load_sem, near_send, near_recv, pair_send, pair_recv, cot_send, cot_pass, cot_took,
        a_send, a_recv, b_send, b_recv, c_send, c_recv, out_send, out_recv, out_pass, out_took,
        one_sem, keep_sem, away_send, away_recv, tile_sem, down_send, down_recv, down_sem, home_sem,
    ) = rest
    place, stage, core = lax.axis_index("fsdp"), lax.axis_index("ctx"), lax.axis_index("tp")
    seq, half = stage // 2, stage % 2
    pair = stage ^ 1
    chunks = token_v.shape[0]
    units = hidden_v.shape[2]
    wide = 512
    quarter = lift_0.shape[0]

    barrier = pltpu.get_barrier_semaphore()
    peers = [(place ^ other, stage, core) for other in (1, 2, 3)]
    peers += [(place, lax.rem(stage + shift, 4), core) for shift in (1, 2, 3)]
    peers += [(place, stage, 1 - core)]
    for peer in peers:
        pl.semaphore_signal(barrier, inc=1, device_id=peer, device_id_type=MESH)
    pl.semaphore_wait(barrier, len(peers))

    def remote(source, target, send, recv, device):
        return pltpu.make_async_remote_copy(
            source, target, send, recv, device_id=device, device_id_type=MESH
        )

    partner = (place, pair, core)
    other_core = (place, stage, 1 - core)

    def pair_copy(c):
        return remote(
            attended.at[(1 - half) * chunks + c], theirs_v.at[c], pair_send.at[c], pair_recv.at[c], partner
        )

    for c in range(chunks):
        pair_copy(c).start()

    def rows_of(owner):
        return pl.ds(pl.multiple_of(owner * quarter, quarter), quarter)

    def near_copy(owner, other, which, sem):
        columns = pl.ds(which * (units // 2), units // 2)
        block = down_w.at[rows_of(owner), columns]
        source = w_down.at[:, columns] if owner is place else block
        return remote(source, block, near_send.at[sem], near_recv.at[sem], (place ^ other, stage, core))

    halves = [
        near_copy(place, other, which, 2 * which + other - 1)
        for other, which in ((1, 0), (2, 1), (1, 1), (2, 0))
    ]
    on = [near_copy(place ^ 1, 2, 0, 4), near_copy(place ^ 2, 1, 1, 5)]
    for copy in halves:
        copy.start()

    def cot_owner(which):
        return 2 * which + stage // 2

    near_block = jnp.where(stage < 2, 0, 1)
    far_block = 1 - near_block
    facing = (stage == 1) | (stage == 2)
    far_load = pltpu.make_async_copy(cot_far, cot_v.at[far_block, core], cot_send.at[0])
    near_load = pltpu.make_async_copy(cot_near, cot_v.at[near_block, core], cot_send.at[1])
    own_load = pltpu.make_async_copy(cotangent.at[stage // 2], cot_v.at[near_block], cot_send.at[1])
    far_load.start()

    @pl.when(facing)
    def _():
        near_load.start()

    @pl.when(~facing)
    def _():
        own_load.start()

    def cot_share(block, whose):
        return remote(
            cot_v.at[block, whose], cot_v.at[block, whose], cot_pass.at[block], cot_took.at[block], other_core
        )

    loads = [
        pltpu.make_async_copy(attended.at[pl.ds(half * chunks, chunks)], mine_v, load_sem.at[0]),
        pltpu.make_async_copy(w_out, out_w, load_sem.at[1]),
        pltpu.make_async_copy(sequence.at[pl.ds(half * chunks, chunks)], token_v, load_sem.at[2]),
        pltpu.make_async_copy(w_down, down_w.at[rows_of(place)], load_sem.at[3]),
        pltpu.make_async_copy(gate_full, up_w.at[:, pl.ds(0, units)], load_sem.at[4]),
    ]
    for other, shard in enumerate((lift_0, lift_1, lift_2, lift_3)):
        target = up_w.at[rows_of(place ^ other), pl.ds(units, units)]
        loads.append(pltpu.make_async_copy(shard, target, load_sem.at[5 + other]))
    for load in loads:
        load.start()

    b_out, gain_one, shift_one, b_down, gain_two, shift_two = (v[...].reshape(1, -1) for v in vectors)
    sums[...] = jnp.zeros_like(sums)

    def add_sum(index, rows):
        sums[index : index + 1, :] += jnp.sum(rows, 0, keepdims=True)

    def exchange(c, sent, got, send, recv):
        return remote(sent.at[c], got.at[c], send.at[c], recv.at[c], other_core)

    def total(c, sent, got):
        return sent[c].astype(jnp.float32) + got[c].astype(jnp.float32)

    loads[0].wait()
    loads[1].wait()

    def attention_branch(c):
        pair_copy(c).wait_recv()
        first, second = mine_v[c], theirs_v[c]
        both = jnp.where(
            half == 0, jnp.concatenate([first, second], 1), jnp.concatenate([second, first], 1)
        )
        both_v[c] = both
        send_a[c] = dot(both, out_w[...], ((1,), (1,))).astype(jnp.bfloat16)
        exchange(c, send_a, recv_a, a_send, a_recv).start()

    attention_branch(0)
    far_load.wait()
    cot_share(far_block, core).start()

    @pl.when(facing)
    def _():
        near_load.wait()
        cot_share(near_block, core).start()

    @pl.when(~facing)
    def _():
        own_load.wait()

    for load in loads[2:]:
        load.wait()
    @pl.loop(0, chunks)
    def _(c):
        @pl.when(c + 1 < chunks)
        def _():
            attention_branch(c + 1)

        @pl.when(c == 1)
        def _():
            for near, far in zip(halves[:2], on):
                near.wait_recv()
                far.start()

        exchange(c, send_a, recv_a, a_send, a_recv).wait_recv()

        residual = token_v[c].astype(jnp.float32) + (total(c, send_a, recv_a) + b_out)
        normed, inv_scale = rows_norm(residual)
        normed_v[c] = normed
        inv_v[c] = inv_scale
        low_v[c] = (normed * gain_one + shift_one).astype(jnp.bfloat16)
        for n in range(0, units, wide):
            gate = dot(low_v[c], up_w[:, n : n + wide])
            lift = dot(low_v[c], up_w[:, units + n : units + n + wide])
            chance = 0.5 + 0.5 * lax.erf(gate * 0.7071067811865476)
            density = jnp.exp(gate * gate * -0.5) * 0.3989422804014327
            gelu = gate * chance
            hidden_v[c, :, n : n + wide] = (gelu * lift).astype(jnp.bfloat16)
            gate_v[c, :, n : n + wide] = (lift * (chance + gate * density)).astype(jnp.bfloat16)
            lift_v[c, :, n : n + wide] = gelu.astype(jnp.bfloat16)

    for copy in halves[2:] + on:
        copy.wait_recv()
    @pl.loop(0, chunks)
    def _(c):
        send_b[c] = dot(hidden_v[c], down_w[...], ((1,), (1,))).astype(jnp.bfloat16)
        exchange(c, send_b, recv_b, b_send, b_recv).start()

    cot_share(far_block, core).wait_send()
    cot_share(far_block, 1 - core).wait_recv()

    @pl.when(facing)
    def _():
        cot_share(near_block, core).wait_send()
        cot_share(near_block, 1 - core).wait_recv()

    def home(c):
        return 2 * half + c // 2

    def out_copy(c):
        return remote(
            result_v.at[c], home_v.at[seq], out_send.at[c], out_recv.at[seq], (place, home(c), core)
        )

    def out_local(c):
        return pltpu.make_async_copy(result_v.at[c], out_home.at[seq, c % 2], out_send.at[c])

    @pl.loop(0, chunks)
    def _(c):
        exchange(c, send_b, recv_b, b_send, b_recv).wait_recv()
        normed_one = normed_v[c]
        residual = normed_one * gain_one + shift_one + (total(c, send_b, recv_b) + b_down)
        normed, inv_scale = rows_norm(residual)
        result_v[c] = (normed * gain_two + shift_two).astype(jnp.bfloat16)

        @pl.when(home(c) == stage)
        def _():
            out_local(c).start()

        @pl.when((home(c) != stage) & (c % 2 == core))
        def _():
            out_copy(c).start()

        grad_in = cot_v[c // 2, c % 2].astype(jnp.float32)
        add_sum(0, grad_in * normed)
        add_sum(1, grad_in)
        grad_two = rows_norm_back(grad_in, normed, inv_scale, gain_two)
        grad_v[c] = grad_two
        grad_ffn = grad_two.astype(jnp.bfloat16)
        ffn_v[c] = grad_ffn
        add_sum(2, grad_ffn.astype(jnp.float32))

    tile = tile_v.shape[2]

    def columns(index):
        return pl.ds(pl.multiple_of(index * tile, tile), tile)

    def weight_part(left, right):
        rows = left.shape[0] * left.shape[1]
        return dot(
            left[...].reshape(rows, left.shape[2]), right.reshape(rows, tile), ((0,), (0,))
        ).astype(jnp.bfloat16)

    unit_tiles = units // tile

    def down_copy(i, other):
        rows = pl.ds(pl.multiple_of((place ^ other) * quarter, quarter), quarter)
        return remote(
            down_v.at[rows, columns(i)], down_got.at[other - 1, :, columns(i)],
            down_send.at[i, other - 1], down_recv.at[i, other - 1], (place ^ other, stage, core),
        )

    @pl.loop(0, unit_tiles)
    def _(i):
        down_v[:, columns(i)] = weight_part(ffn_v, hidden_v[:, :, columns(i)])
        for other in (1, 2, 3):
            down_copy(i, other).start()

    @pl.loop(0, chunks)
    def _(c):
        for n in range(0, units, wide):
            grad_hidden = dot(ffn_v[c], down_w[:, n : n + wide])
            gate_v[c, :, n : n + wide] = (grad_hidden * gate_v[c, :, n : n + wide]).astype(jnp.bfloat16)
            lift_v[c, :, n : n + wide] = (grad_hidden * lift_v[c, :, n : n + wide]).astype(jnp.bfloat16)
        send_c[c] = (
            dot(gate_v[c], up_w[:, :units], ((1,), (1,))) + dot(lift_v[c], up_w[:, units:], ((1,), (1,)))
        ).astype(jnp.bfloat16)
        exchange(c, send_c, recv_c, c_send, c_recv).start()

    def one_copy(c):
        return pltpu.make_async_copy(grad_v.at[c], grad_one.at[c], one_sem.at[c])

    def keep_copy(c):
        return pltpu.make_async_copy(keep_v.at[c], grad_heads.at[half * chunks + c], keep_sem.at[c])

    def away_copy(c, whose):
        return remote(
            away_v.at[c], grad_heads.at[whose * chunks + c], away_send.at[c], away_recv.at[c], partner
        )

    @pl.loop(0, chunks)
    def _(c):
        exchange(c, send_c, recv_c, c_send, c_recv).wait_recv()
        grad_first = grad_v[c] + total(c, send_c, recv_c)
        normed = normed_v[c]
        add_sum(3, grad_first * normed)
        add_sum(4, grad_first)
        grad_res = rows_norm_back(grad_first, normed, inv_v[c], gain_one)
        grad_v[c] = grad_res
        one_copy(c).start()
        grad_att = grad_res.astype(jnp.bfloat16)
        att_v[c] = grad_att
        add_sum(5, grad_att.astype(jnp.float32))
        heads = dot(att_v[c], out_w[...]).astype(jnp.bfloat16)
        first, second = heads[:, : heads.shape[1] // 2], heads[:, heads.shape[1] // 2 :]
        keep_v[c] = jnp.where(half == 0, first, second)
        away_v[c] = jnp.where(half == 0, second, first)
        away_copy(c, half).start()
        keep_copy(c).start()

    early = (early_0, early_1, early_2, early_3)
    early_tiles = early_0.shape[1] // tile

    def tile_copy(slot, other, index):
        target, column = index
        rows = pl.ds(pl.multiple_of((place ^ other) * quarter, quarter), quarter)
        place_of = target[other] if isinstance(target, tuple) else target.at[other]
        return pltpu.make_async_copy(
            tile_v.at[slot, rows], place_of.at[:, columns(column)], tile_sem.at[slot, other]
        )

    def weight_tile(count, target, column, left, right):
        slot = lax.rem(count, 2)

        @pl.when(count >= 2)
        def _():
            for row in range(4):
                tile_copy(slot, row, (target, column)).wait()

        tile_v[slot] = weight_part(left, right)
        for row in range(4):
            tile_copy(slot, row, (target, column)).start()

    @pl.loop(0, unit_tiles)
    def _(i):
        weight_tile(i, early, i, low_v, gate_v[:, :, columns(i)])

    @pl.loop(unit_tiles, early_tiles)
    def _(i):
        weight_tile(i, early, i, low_v, lift_v[:, :, columns(i - unit_tiles)])

    late_units = 2 * unit_tiles - early_tiles

    @pl.loop(0, late_units)
    def _(i):
        weight_tile(early_tiles + i, late, i, low_v, lift_v[:, :, columns(early_tiles - unit_tiles + i)])

    weight_tile(2 * unit_tiles, late, late_units, att_v, both_v[...])
    for slot in (0, 1):
        for row in range(4):
            tile_copy(slot, row, (late, 0)).wait()

    for i in range(unit_tiles):
        for other in (1, 2, 3):
            down_copy(i, other).wait_recv()
    own_rows = pl.ds(pl.multiple_of(place * quarter, quarter), quarter)
    down_got[0] = (
        down_v[own_rows, :].astype(jnp.float32)
        + down_got[0].astype(jnp.float32)
        + (down_got[1].astype(jnp.float32) + down_got[2].astype(jnp.float32))
    ).astype(jnp.bfloat16)
    down_out = pltpu.make_async_copy(down_got.at[0], down_sum, down_sem)
    down_out.start()

    def out_arrival(which):
        return remote(
            home_v.at[which], home_v.at[which], out_pass.at[which], out_recv.at[which], other_core
        )

    def out_share(which, whose):
        return remote(
            home_v.at[which], out_home.at[which, whose], out_pass.at[which], out_took.at[which], other_core
        )

    def out_here(which):
        return pltpu.make_async_copy(home_v.at[which], out_home.at[which, core], home_sem.at[which])

    for which in (0, 1):

        @pl.when(cot_owner(which) != stage)
        def _():
            out_arrival(which).wait_recv()
            out_share(which, core).start()
            out_here(which).start()

    down_out.wait()
    for copy in halves + on:
        copy.wait_send()
    for i in range(unit_tiles):
        for other in (1, 2, 3):
            down_copy(i, other).wait_send()

    @pl.loop(0, chunks)
    def _(c):
        pair_copy(c).wait_send()
        exchange(c, send_a, recv_a, a_send, a_recv).wait_send()
        exchange(c, send_b, recv_b, b_send, b_recv).wait_send()
        exchange(c, send_c, recv_c, c_send, c_recv).wait_send()
        one_copy(c).wait()
        keep_copy(c).wait()
        away_copy(c, half).wait_send()
        away_copy(c, 1 - half).wait_recv()

        @pl.when(home(c) == stage)
        def _():
            out_local(c).wait()

        @pl.when((home(c) != stage) & (c % 2 == core))
        def _():
            out_copy(c).wait_send()

    for which in (0, 1):

        @pl.when(cot_owner(which) != stage)
        def _():
            out_share(which, core).wait_send()
            out_share(which, 1 - core).wait_recv()
            out_here(which).wait()


def middle(attended, sequence, cotangents, w_out, w_gate, w_down, lift_shards, vectors):
    chunks, rows, width = 4, sequence.shape[1], sequence.shape[2]
    head_width, units = w_out.shape[1], w_down.shape[1]
    tile = head_width
    early, late = 6 * tile, 2 * units + head_width - 6 * tile
    dma, bf16, f32 = pltpu.SemaphoreType.DMA, jnp.bfloat16, jnp.float32

    def vmem(shape, dtype=bf16):
        return pltpu.VMEM(shape, dtype)

    wide = (chunks, rows, width)
    inner = (chunks, rows, units)
    narrow_rows = (chunks, rows, head_width // 2)
    four, two = dma((chunks,)), dma((2,))
    return pl.pallas_call(
        middle_kernel,
        in_specs=[pl.BlockSpec(memory_space=pl.ANY)] * 12 + [pl.BlockSpec(memory_space=pltpu.VMEM)] * 6,
        out_specs=[pl.BlockSpec(memory_space=pl.ANY)] * 9 + [pl.BlockSpec(memory_space=pltpu.VMEM)],
        out_shape=[
            jax.ShapeDtypeStruct((2, 2, rows, width), bf16),
            jax.ShapeDtypeStruct(wide, f32),
            jax.ShapeDtypeStruct((2 * chunks, rows, head_width // 2), bf16),
            *[jax.ShapeDtypeStruct((width // 4, early), bf16)] * 4,
            jax.ShapeDtypeStruct((4, width // 4, late), bf16),
            jax.ShapeDtypeStruct((width // 4, units), bf16),
            jax.ShapeDtypeStruct((8, width), f32),
        ],
        scratch_shapes=[
            vmem(wide), vmem(narrow_rows), vmem(narrow_rows), vmem((chunks, rows, head_width)),
            vmem((2, 2, rows, width)), vmem((width, head_width)), vmem((width, units)), vmem((width, 2 * units)),
            vmem(wide), vmem(wide), vmem(wide), vmem(wide), vmem(wide), vmem(wide),
            vmem(wide, f32), vmem((chunks, rows, 1), f32), vmem(wide),
            vmem(inner), vmem(inner), vmem(inner),
            vmem(wide, f32), vmem(wide), vmem(wide), vmem(wide), vmem(narrow_rows), vmem(narrow_rows),
            vmem((2, width, tile)), vmem((width, units)), vmem((3, width // 4, units)), vmem((2, rows, width)),
            dma((9,)), dma((6,)), dma((6,)), four, four, two, two, two,
            four, four, four, four, four, four, four, two, two, two,
            four, four, four, four, dma((2, 4)), dma((units // tile, 3)), dma((units // tile, 3)), dma, two,
        ],
        compiler_params=pltpu.CompilerParams(
            collective_id=1, has_side_effects=True, vmem_limit_bytes=VMEM_BYTES
        ),
        cost_estimate=pl.CostEstimate(flops=50 << 30, bytes_accessed=32 << 20, transcendentals=0),
        name="middle",
    )(attended, sequence, *cotangents, w_out, w_gate, w_down, *lift_shards, *vectors)


def tail_kernel(
    d_query, d_key, d_value, w_joined, sums_in, sequence, grad_one, early, late, moved_1, moved_2, moved_3,
    down_own, down_in,
    home, shard, joined, down, sums,
    query_v, key_v, value_v, token_v, one_v, part_v, late_v, project_v, own_v, tp_sent, tp_got, pair_sent, pair_got,
    final_v, summed_v, end_got, inner_v, mid_got, total_v, joined_v, quarter_got, both_sent, both_end, both_inner,
    both_mid, both_total, step_v, step_got, home_v, down_v, down_inner, down_got, down_total,
    load_sem, late_send, late_recv, tp_send, tp_recv, pair_send, pair_recv, home_send, home_recv, home_pass,
    home_took, home_local, end_send, end_recv, mid_send, mid_recv, back_send, back_recv, shard_sem,
    quarter_send, quarter_recv, both_send, both_recv, both_local, step_send, step_recv, home_sem, down_sem, down_mid_send, down_mid_recv, down_back_send, down_back_recv,
):
    place, stage, core = lax.axis_index("fsdp"), lax.axis_index("ctx"), lax.axis_index("tp")
    seq, half = stage // 2, stage % 2
    bf16, f32 = jnp.bfloat16, jnp.float32
    pieces = summed_v.shape[0]
    piece = summed_v.shape[2]
    early_pieces = early.shape[1] // piece
    quarter = joined_v.shape[0] // 4
    width = d_query.shape[2]

    barrier = pltpu.get_barrier_semaphore()
    peers = [(place ^ other, stage, core) for other in (1, 2, 3)]
    peers += [(place, lax.rem(stage + shift, 4), core) for shift in (1, 2, 3)]
    peers += [(place, stage, 1 - core)]
    for peer in peers:
        pl.semaphore_signal(barrier, inc=1, device_id=peer, device_id_type=MESH)

    loads = [
        pltpu.make_async_copy(source, target, load_sem.at[index])
        for index, (source, target) in enumerate(
            (
                (early, part_v.at[0]),
                (moved_1, part_v.at[1]),
                (moved_2, part_v.at[2]),
                (moved_3, part_v.at[3]),
                (d_query, query_v),
                (d_key, key_v),
                (d_value, value_v),
                (late.at[0], late_v.at[0]),
                (sequence, token_v),
                (grad_one, one_v),
            )
        )
    ]
    down_loads = [
        pltpu.make_async_copy(source, down_v.at[index], down_sem.at[index])
        for index, source in enumerate((down_own, down_in))
    ]
    for load in down_loads + loads:
        load.start()
    pl.semaphore_wait(barrier, len(peers))

    def remote(source, target, send, recv, device):
        return pltpu.make_async_remote_copy(
            source, target, send, recv, device_id=device, device_id_type=MESH
        )

    other_core = (place, stage, 1 - core)
    partner = (place, stage ^ 1, core)
    at_end = (stage == 0) | (stage == 3)
    inward = (place, stage ^ 1, core)
    outward = (place, stage ^ 1, core)
    across = (place, 3 - stage, core)

    def late_copy(other):
        return remote(
            late.at[other], late_v.at[other], late_send.at[other - 1], late_recv.at[other - 1],
            (place ^ other, stage, core),
        )

    for other in (1, 2, 3):
        late_copy(other).start()

    def columns(j):
        return pl.ds(j * piece, piece)

    def end_copy(j):
        return remote(summed_v.at[j], end_got.at[j], end_send.at[j], end_recv.at[j], inward)

    def mid_copy(j):
        return remote(inner_v.at[j], mid_got.at[j], mid_send.at[j], mid_recv.at[j], across)

    def back_copy(j):
        return remote(total_v.at[j], shard.at[:, columns(j)], back_send.at[j], back_recv.at[j], outward)

    def shard_copy(j):
        return pltpu.make_async_copy(total_v.at[j], shard.at[:, columns(j)], shard_sem.at[j])

    def sum_piece(j, parts, first):
        terms = [parts[index, :, first : first + piece].astype(f32) for index in range(4)]
        summed_v[j] = (terms[0] + terms[1] + (terms[2] + terms[3])).astype(bf16)

        @pl.when(at_end)
        def _():
            end_copy(j).start()

    def from_end(j):
        end_copy(j).wait_recv()
        inner_v[j] = (summed_v[j].astype(f32) + end_got[j].astype(f32)).astype(bf16)
        mid_copy(j).start()

    def from_mid(j):
        mid_copy(j).wait_recv()
        total_v[j] = (inner_v[j].astype(f32) + mid_got[j].astype(f32)).astype(bf16)
        back_copy(j).start()
        shard_copy(j).start()

    down_pieces = down_mid_send.shape[0]
    down_size = down_v.shape[2] // down_pieces

    def down_part(ref, j):
        return ref.at[:, pl.ds(j * down_size, down_size)]

    def down_mid(j):
        return remote(
            down_part(down_inner, j), down_part(down_got, j), down_mid_send.at[j], down_mid_recv.at[j], across
        )

    def down_back(j):
        return remote(
            down_part(down_total, j), down_part(down, j), down_back_send.at[j], down_back_recv.at[j], outward
        )

    def down_here(j):
        return pltpu.make_async_copy(down_part(down_total, j), down_part(down, j), down_sem.at[j])

    def down_from_mid(j):
        down_mid(j).wait_recv()
        part = slice(j * down_size, (j + 1) * down_size)
        down_total[:, part] = (
            down_inner[:, part].astype(f32) + down_got[:, part].astype(f32)
        ).astype(bf16)
        down_back(j).start()
        down_here(j).start()

    for load in down_loads:
        load.wait()

    @pl.when(~at_end)
    def _():
        down_inner[...] = (down_v[0].astype(f32) + down_v[1].astype(f32)).astype(bf16)
        for j in range(down_pieces):
            down_mid(j).start()

    for load in loads[:4]:
        load.wait()
    for j in range(early_pieces):
        sum_piece(j, part_v, j * piece)

    def input_share(chunk):
        rows = jnp.concatenate([query_v[chunk], key_v[chunk], value_v[chunk]], 1)
        project_v[chunk] = rows
        return dot(rows, w_joined[...], ((1,), (1,)))

    def block_of(i):
        return jnp.where(i < 2, 2 * (1 - half) + i, 2 * half + i - 2)

    def tp_copy(i):
        return remote(tp_sent.at[i], tp_got.at[i], tp_send.at[i], tp_recv.at[i], other_core)

    for load in loads[4:7]:
        load.wait()

    @pl.loop(0, 4)
    def _(i):
        block = block_of(i)
        tp_sent[i] = input_share(2 * block + 1 - core).astype(bf16)
        tp_copy(i).start()
        own_v[i] = input_share(2 * block + core)

    def pair_copy(i):
        return remote(pair_sent.at[i], pair_got.at[i], pair_send.at[i], pair_recv.at[i], partner)

    @pl.loop(0, 2)
    def _(i):
        tp_copy(i).wait_recv()
        pair_sent[i] = (own_v[i] + tp_got[i].astype(f32)).astype(bf16)
        pair_copy(i).start()

    @pl.when(~at_end)
    def _():
        for j in range(early_pieces // 2):
            from_end(j)

    @pl.when(~at_end)
    def _():
        for j in range(down_pieces):
            down_from_mid(j)

    loads[8].wait()
    tokens = token_v[...].reshape(-1, token_v.shape[2])
    project = project_v[...].reshape(-1, project_v.shape[2])
    strip = 256
    for row in range(0, joined_v.shape[0], strip):
        joined_v[row : row + strip, :] = dot(
            tokens[:, row : row + strip], project, ((0,), (0,))
        ).astype(bf16)

    def quarter_copy(other):
        rows = pl.ds(pl.multiple_of((place ^ other) * quarter, quarter), quarter)
        return remote(
            joined_v.at[rows], quarter_got.at[other - 1], quarter_send.at[other - 1], quarter_recv.at[other - 1],
            (place ^ other, stage, core),
        )

    for other in (1, 2, 3):
        quarter_copy(other).start()

    def column_sum(grads):
        return jnp.sum(grads[...].reshape(-1, width).astype(f32), 0, keepdims=True)

    bias_parts = []
    for total in (column_sum(query_v), column_sum(value_v)):
        for which in (0, 1):
            bias_parts.append(jnp.where(half == which, total, 0.0))
    bias = jnp.concatenate(bias_parts, 1)
    step_v[0] = sums_in[...]
    step_v[0, 6:7, :] = bias
    steps = [(place ^ 1, stage, core), (place ^ 2, stage, core), partner, (place, stage ^ 2, core)]

    def step_copy(index):
        return remote(
            step_v.at[index], step_got.at[index], step_send.at[index], step_recv.at[index], steps[index]
        )

    def step_on(index):
        step_copy(index).wait_recv()
        step_v[index + 1] = step_v[index] + step_got[index]
        if index < 3:
            step_copy(index + 1).start()

    step_copy(0).start()

    @pl.when(~at_end)
    def _():
        for j in range(early_pieces // 2, early_pieces):
            from_end(j)
            from_mid(j - early_pieces // 2)

    loads[7].wait()
    for other in (1, 2, 3):
        late_copy(other).wait_recv()
    for j in range(early_pieces, pieces):
        sum_piece(j, late_v, (j - early_pieces) * piece)
    step_on(0)

    def both_end_copy():
        return remote(both_sent, both_end, both_send.at[0], both_recv.at[0], inward)

    def both_mid_copy():
        return remote(both_inner, both_mid, both_send.at[1], both_recv.at[1], across)

    def both_back_copy():
        return remote(both_total, joined, both_send.at[2], both_recv.at[2], outward)

    def both_here():
        return pltpu.make_async_copy(both_total, joined, both_local)

    for other in (1, 2, 3):
        quarter_copy(other).wait_recv()
    own_rows = pl.ds(pl.multiple_of(place * quarter, quarter), quarter)
    both_sent[...] = (
        joined_v[own_rows, :].astype(f32)
        + quarter_got[0].astype(f32)
        + (quarter_got[1].astype(f32) + quarter_got[2].astype(f32))
    ).astype(bf16)

    @pl.when(at_end)
    def _():
        both_end_copy().start()

    step_on(1)

    loads[9].wait()

    def home_copy(i):
        return remote(
            final_v.at[i], home_v.at[seq], home_send.at[i], home_recv.at[seq], (place, 2 * half + i, core)
        )

    def home_direct(i):
        return remote(final_v.at[i], home.at[seq, core], home_send.at[i], home_took.at[seq], other_core)

    def home_here(i):
        return pltpu.make_async_copy(final_v.at[i], home.at[seq, core], home_local)

    for i in range(2):
        tp_copy(i + 2).wait_recv()
        pair_copy(i).wait_recv()
        final_v[i] = (
            own_v[i + 2] + tp_got[i + 2].astype(f32) + pair_got[i].astype(f32) + one_v[2 * i + core]
        ).astype(bf16)

        @pl.when(2 * half + i == stage)
        def _():
            home_direct(i).start()
            home_here(i).start()

        @pl.when(2 * half + i != stage)
        def _():
            home_copy(i).start()

    @pl.when(~at_end)
    def _():
        for j in range(early_pieces, pieces):
            from_end(j)
            from_mid(j - early_pieces // 2)
        both_end_copy().wait_recv()
        both_inner[half] = both_sent[...]
        both_inner[1 - half] = both_end[...]
        both_mid_copy().start()
        for j in range(pieces - early_pieces // 2, pieces):
            from_mid(j)
        both_mid_copy().wait_recv()
        both_total[...] = (both_inner[...].astype(f32) + both_mid[...].astype(f32)).astype(bf16)
        both_back_copy().start()
        both_here().start()

    step_on(2)
    step_on(3)
    sums[...] = step_v[4]

    def home_arrival(which):
        return remote(
            home_v.at[which], home_v.at[which], home_pass.at[which], home_recv.at[which], other_core
        )

    def home_share(which, whose):
        return remote(
            home_v.at[which], home.at[which, whose], home_pass.at[which], home_took.at[which], other_core
        )

    def home_keep(which):
        return pltpu.make_async_copy(home_v.at[which], home.at[which, core], home_sem.at[which])

    for which in (0, 1):

        @pl.when(2 * which + stage // 2 != stage)
        def _():
            home_arrival(which).wait_recv()
            home_share(which, core).start()
            home_keep(which).start()

    @pl.when(~at_end)
    def _():
        for j in range(pieces):
            mid_copy(j).wait_send()
            back_copy(j).wait_send()
            shard_copy(j).wait()
        both_mid_copy().wait_send()
        both_back_copy().wait_send()
        both_here().wait()

    @pl.when(~at_end)
    def _():
        for j in range(down_pieces):
            down_mid(j).wait_send()
            down_back(j).wait_send()
            down_here(j).wait()

    @pl.when(at_end)
    def _():
        for j in range(down_pieces):
            down_back(j).wait_recv()
        for j in range(pieces):
            end_copy(j).wait_send()
            back_copy(j).wait_recv()
        both_end_copy().wait_send()
        both_back_copy().wait_recv()

    for i in range(4):
        tp_copy(i).wait_send()
        step_copy(i).wait_send()
    for i in range(2):
        pair_copy(i).wait_send()

        @pl.when(2 * half + i == stage)
        def _():
            home_direct(i).wait_send()
            home_here(i).wait()

        @pl.when(2 * half + i != stage)
        def _():
            home_copy(i).wait_send()

    for which in (0, 1):

        @pl.when(2 * which + stage // 2 != stage)
        def _():
            home_share(which, core).wait_send()
            home_keep(which).wait()

        home_share(which, 1 - core).wait_recv()
    for other in (1, 2, 3):
        quarter_copy(other).wait_send()
        late_copy(other).wait_send()


def tail(d_query, d_key, d_value, w_joined, sums, sequence, grad_one, early, late, moved, downs):
    rows, width = sequence.shape[1:]
    quarter = early.shape[0]
    joined = w_joined.shape[1]
    piece = 3 * LANES
    columns = early.shape[1] + late.shape[2]
    pieces = columns // piece
    dma, bf16, f32 = pltpu.SemaphoreType.DMA, jnp.bfloat16, jnp.float32

    def vmem(shape, dtype=bf16):
        return pltpu.VMEM(shape, dtype)

    any_spec, vmem_spec = pl.BlockSpec(memory_space=pl.ANY), pl.BlockSpec(memory_space=pltpu.VMEM)
    cut = (pieces, quarter, piece)
    both = (2, quarter, joined)
    one, two, three, four, many = dma, dma((2,)), dma((3,)), dma((4,)), dma((pieces,))
    return pl.pallas_call(
        tail_kernel,
        in_specs=[any_spec] * 3 + [vmem_spec] * 2 + [any_spec] * 9,
        out_specs=[any_spec] * 4 + [vmem_spec],
        out_shape=[
            jax.ShapeDtypeStruct((2, 2, rows, width), bf16),
            jax.ShapeDtypeStruct((quarter, columns), bf16),
            jax.ShapeDtypeStruct(both, bf16),
            jax.ShapeDtypeStruct(downs[0].shape, bf16),
            jax.ShapeDtypeStruct(sums.shape, f32),
        ],
        scratch_shapes=[
            vmem(d_query.shape), vmem(d_query.shape), vmem(d_query.shape),
            vmem(sequence.shape), vmem(grad_one.shape, f32), vmem((4,) + early.shape), vmem(late.shape),
            vmem((8, rows, joined)), vmem((4, rows, width), f32),
            vmem((4, rows, width)), vmem((4, rows, width)), vmem((2, rows, width)), vmem((2, rows, width)),
            vmem((2, rows, width)),
            vmem(cut), vmem(cut), vmem(cut), vmem(cut), vmem(cut),
            vmem((width, joined)), vmem((3, quarter, joined)), vmem((quarter, joined)), vmem((quarter, joined)),
            vmem(both), vmem(both), vmem(both),
            vmem((5,) + sums.shape, f32), vmem((4,) + sums.shape, f32), vmem((2, rows, width)),
            vmem((2,) + downs[0].shape), vmem(downs[0].shape), vmem(downs[0].shape), vmem(downs[0].shape),
            dma((10,)), three, three, four, four, two, two, two, two, two, two, one,
            many, many, many, many, many, many, many,
            three, three, three, three, one, four, four, two, two, two, two, two, two,
        ],
        compiler_params=pltpu.CompilerParams(
            collective_id=2, has_side_effects=True, vmem_limit_bytes=VMEM_BYTES
        ),
        cost_estimate=pl.CostEstimate(flops=80 << 30, bytes_accessed=32 << 20, transcendentals=0),
        name="tail",
    )(d_query, d_key, d_value, w_joined, sums, sequence, grad_one, early, late, *moved, *downs)


def pick(pair, index):
    return lax.dynamic_index_in_dim(pair, index, 0, keepdims=False)


def finish_kernel(
    tokens_ref, shard_ref, joined_ref, down_ref, sums_ref,
    d_tokens, d_query, d_key, d_value, d_out, d_up, d_down, *vectors,
):
    f32 = jnp.float32
    for index in range(6):
        vectors[index][...] = sums_ref[index]
    biases = sums_ref[6]
    vectors[6][...] = biases[: biases.shape[0] // 2]
    vectors[7][...] = biases[biases.shape[0] // 2 :]
    d_tokens[...] = tokens_ref[...].astype(f32)
    units = d_up.shape[2]
    d_up[:, 0, :] = shard_ref[:, :units].astype(f32)
    d_up[:, 1, :] = shard_ref[:, units : 2 * units].astype(f32)
    d_out[...] = shard_ref[:, 2 * units :].astype(f32)
    d_down[...] = down_ref[...].astype(f32)
    width = d_query.shape[1] // 2
    for index, target in enumerate((d_query, d_key, d_value)):
        columns = slice(index * width, (index + 1) * width)
        target[...] = jnp.concatenate(
            [joined_ref[0, :, columns], joined_ref[1, :, columns]], 1
        ).astype(f32)


def finish(tokens, shard, joined, down, sums):
    steps = 4
    quarter, units = down.shape
    head_width = shard.shape[1] - 2 * units
    row, some = tokens.shape[0] // steps, quarter // steps
    sizes = [sums.shape[1]] * 6 + [head_width] * 2
    f32 = jnp.float32

    def rows(width):
        return pl.BlockSpec((some, width), lambda i: (i, 0))

    return pl.pallas_call(
        finish_kernel,
        grid=(steps,),
        in_specs=[
            pl.BlockSpec((row, tokens.shape[1]), lambda i: (i, 0)),
            rows(shard.shape[1]),
            pl.BlockSpec((2, some, joined.shape[2]), lambda i: (0, i, 0)),
            rows(units),
            pl.BlockSpec(sums.shape, lambda i: (0, 0)),
        ],
        out_specs=[
            pl.BlockSpec((row, tokens.shape[1]), lambda i: (i, 0)),
            rows(head_width), rows(head_width), rows(head_width), rows(head_width),
            pl.BlockSpec((some, 2, units), lambda i: (i, 0, 0)),
            rows(units),
            *[pl.BlockSpec((size,), lambda i: (0,)) for size in sizes],
        ],
        out_shape=[
            jax.ShapeDtypeStruct(tokens.shape, f32),
            *[jax.ShapeDtypeStruct((quarter, head_width), f32)] * 4,
            jax.ShapeDtypeStruct((quarter, 2, units), f32),
            jax.ShapeDtypeStruct((quarter, units), f32),
            *[jax.ShapeDtypeStruct((size,), f32) for size in sizes],
        ],
        compiler_params=pltpu.CompilerParams(vmem_limit_bytes=VMEM_BYTES),
        name="finish",
    )(tokens, shard, joined, down, sums)


def per_device_paired(
    tokens,
    doc_lengths,
    keep,
    w_query,
    b_query,
    w_key,
    w_value,
    b_value,
    w_out,
    b_out,
    gain_one,
    shift_one,
    w_up,
    w_down,
    b_down,
    gain_two,
    shift_two,
    cotangent,
):
    _, block_rows, model_width = tokens.shape
    length = 4 * block_rows
    half_rows = block_rows // 2
    local_heads = b_query.shape[0] // HEAD
    heads = local_heads // 2
    width = heads * HEAD
    cotangent = cotangent.reshape(2, 2, half_rows, model_width)
    half = lax.axis_index("ctx") % 2
    core = lax.axis_index("tp")
    slopes = head_slopes(core * local_heads + half * heads, heads)
    (
        sequence, full_joined, full_out, full_gate, up_lift, cot_far, cot_near, query_t, queries, keys, keys_t, values, values_t,
    ) = start(
        doc_lengths, slopes, tokens, keep, w_query, w_key, w_value, w_out, w_up, b_query, b_value,
        cotangent,
    )
    full_joined = full_joined.reshape(model_width, 3 * width)
    full_out = full_out.reshape(model_width, 2 * width)
    full_gate = full_gate.reshape(model_width, -1)
    lift_shards = [up_lift] + [
        lax.ppermute(up_lift, "fsdp", swap) for swap in (X_SWAP, Y_SWAP, D_SWAP)
    ]
    cotangents = (
        cotangent,
        lax.ppermute(cot_far, "ctx", [(3, 1), (0, 2), (1, 0), (2, 3)]),
        lax.ppermute(cot_near, "ctx", [(1, 2), (2, 1)]),
    )
    attended_all, attended_t, lse = attend(doc_lengths, slopes, query_t, keys, values_t)

    vectors = (b_out, gain_one, shift_one, b_down, gain_two, shift_two)
    out, grad_one, grad_heads, *early, late, down_sum, sums = middle(
        attended_all.reshape(8, half_rows, width),
        sequence.reshape(8, half_rows, model_width),
        cotangents,
        full_out,
        full_gate,
        w_down,
        lift_shards,
        vectors,
    )
    out = out.reshape(2, block_rows, model_width)
    grad_heads = grad_heads.reshape(length, width)
    moved = [
        lax.ppermute(early[other], "fsdp", swap)
        for other, swap in ((1, X_SWAP), (2, Y_SWAP), (3, D_SWAP))
    ]
    downs = (down_sum, lax.ppermute(down_sum, "ctx", [(0, 1), (3, 2)]))
    d_query, d_key, d_value = attend_back(
        doc_lengths, slopes, query_t, queries, keys, keys_t, values, grad_heads, attended_t, lse
    )
    d_tokens, shard, joined, down, sums = tail(
        d_query.reshape(8, half_rows, width),
        d_key.reshape(8, half_rows, width),
        d_value.reshape(8, half_rows, width),
        full_joined,
        sums,
        sequence.reshape(8, half_rows, model_width),
        grad_one,
        early[0],
        late,
        moved,
        downs,
    )
    (
        d_tokens, d_w_query, d_w_key, d_w_value, sum_out, sum_up, sum_down,
        total_gain_two, total_shift_two, total_b_down, total_gain_one, total_shift_one, total_b_out,
        total_b_query, total_b_value,
    ) = finish(
        d_tokens.reshape(2 * block_rows, model_width), shard, joined, down, sums
    )
    d_tokens = d_tokens.reshape(2, block_rows, model_width)
    return (
        out,
        d_tokens,
        d_w_query,
        total_b_query,
        d_w_key,
        d_w_value,
        total_b_value,
        sum_out,
        total_b_out,
        total_gain_one,
        total_shift_one,
        sum_up,
        sum_down,
        total_b_down,
        total_gain_two,
        total_shift_two,
    )


def paired(mesh, tokens, doc_lengths, b_query):
    sizes = dict(mesh.shape)
    return (
        sizes == {"fsdp": 4, "ctx": 4, "tp": 2}
        and tokens.shape[0] == 8
        and tokens.shape[1] % (8 * TILE) == 0
        and doc_lengths.shape[1] <= KEEP_ROW - DOC_ROW
        and b_query.shape[0] % (4 * HEAD) == 0
    )


def solution(mesh):
    in_specs = (
        P("fsdp", "ctx", None),
        P("fsdp", None),
        P("fsdp", "ctx"),
        P("fsdp", "tp"),
        P("tp"),
        P("fsdp", "tp"),
        P("fsdp", "tp"),
        P("tp"),
        P("fsdp", "tp"),
        P(),
        P(),
        P(),
        P("fsdp", None, "tp"),
        P("fsdp", "tp"),
        P(),
        P(),
        P(),
        P("fsdp", "ctx", None),
    )
    out_specs = (
        P("fsdp", "ctx", None),
        P("fsdp", "ctx", None),
        P("fsdp", "tp"),
        P("tp"),
        P("fsdp", "tp"),
        P("fsdp", "tp"),
        P("tp"),
        P("fsdp", "tp"),
        P(),
        P(),
        P(),
        P("fsdp", None, "tp"),
        P("fsdp", "tp"),
        P(),
        P(),
        P(),
    )

    def whole(*args):
        body = per_device_paired if paired(mesh, args[0], args[1], args[4]) else per_device_general
        return jax.shard_map(
            body, mesh=mesh, in_specs=in_specs, out_specs=out_specs, check_vma=False
        )(*args)

    return whole
```

```python
import functools

import jax
import jax.numpy as jnp
from jax import lax
from jax.experimental import pallas as pl
from jax.experimental.pallas import tpu as pltpu
from jax.sharding import PartitionSpec as P

HEAD = 64


NORM_EPS = 1e-12
MASKED = -1e30


def layer_norm(residual, norm_gain, norm_shift):
    centered = residual - jnp.mean(residual, -1, keepdims=True)
    inv_scale = lax.rsqrt(jnp.mean(centered * centered, -1, keepdims=True) + NORM_EPS)
    normed = centered * inv_scale
    return (normed * norm_gain + norm_shift, normed, inv_scale)


def norm_back(grad_out, normed, inv_scale, norm_gain):
    grad_norm = grad_out * norm_gain
    mean_grad = jnp.mean(grad_norm, -1, keepdims=True)
    mean_cross = jnp.mean(grad_norm * normed, -1, keepdims=True)
    grad_in = (grad_norm - mean_grad - normed * mean_cross) * inv_scale
    return (grad_in, jnp.sum(grad_out * normed, 0), jnp.sum(grad_out, 0))


def head_slopes(first_head, head_count):
    head_index = first_head + jnp.arange(head_count, dtype=jnp.int32)
    head_float = head_index.astype(jnp.float32)
    return jnp.where(head_index < 8, jnp.exp2(-(head_float + 1.0)), jnp.exp2(-(head_float - 7.5)))


def segment_ids(lengths, positions):
    bounds = jnp.cumsum(lengths, -1)
    return jnp.sum((bounds[:, None, :] <= positions[None, :, None]).astype(jnp.int32), -1)


def score_block(query_heads, query_pos, query_seg, key_heads, key_pos, key_seg, key_keep, slopes):
    scores = (
        jnp.einsum("sqhd,skhd->shqk", query_heads, key_heads, preferred_element_type=jnp.float32)
        * 0.125
    )
    distance = jnp.abs(query_pos[:, None] - key_pos[None, :]).astype(jnp.float32)
    scores = scores - slopes[None, :, None, None] * distance[None, None]
    same_doc = query_seg[:, None, :, None] == key_seg[:, None, None, :]
    visible = (key_keep[:, None, None, :] == 1) | (query_pos[:, None] == key_pos[None, :])[
        None, None
    ]
    return (scores, same_doc & visible)


def grad_block(
    query_heads,
    query_pos,
    query_seg,
    grad_heads,
    log_total,
    delta,
    key_heads,
    value_heads,
    key_pos,
    key_seg,
    key_keep,
    slopes,
):
    scores, allowed = score_block(
        query_heads, query_pos, query_seg, key_heads, key_pos, key_seg, key_keep, slopes
    )
    probs = jnp.where(allowed, jnp.exp(scores - log_total[..., None]), 0.0)
    grad_probs = jnp.einsum(
        "sqhd,skhd->shqk", grad_heads, value_heads, preferred_element_type=jnp.float32
    )
    grad_scores = (probs * (grad_probs - delta[..., None])).astype(jnp.bfloat16)
    grad_query = (
        jnp.einsum("shqk,skhd->sqhd", grad_scores, key_heads, preferred_element_type=jnp.float32)
        * 0.125
    )
    grad_key = (
        jnp.einsum("shqk,sqhd->skhd", grad_scores, query_heads, preferred_element_type=jnp.float32)
        * 0.125
    )
    grad_value = jnp.einsum(
        "shqk,sqhd->skhd",
        probs.astype(jnp.bfloat16),
        grad_heads,
        preferred_element_type=jnp.float32,
    )
    return (grad_query, grad_key, grad_value)


def intersections(query_seg, key_seg):
    return jnp.any((key_seg[:, 0] <= query_seg[:, -1]) & (key_seg[:, -1] >= query_seg[:, 0]))


def guarded(active, update, current):
    return lax.cond(active, update, lambda untouched: untouched, current)


def over_blocks(length, advance, current):
    block_len = 512
    block_count = length // block_len
    return lax.fori_loop(
        0,
        block_count,
        lambda block_index, running: advance(running, block_index * block_len, block_len),
        current,
    )


def per_device_general(
    tokens,
    doc_lengths,
    keep,
    w_query,
    b_query,
    w_key,
    w_value,
    b_value,
    w_out,
    b_out,
    gain_one,
    shift_one,
    w_up,
    w_down,
    b_down,
    gain_two,
    shift_two,
    cotangent,
):
    seq_count, block_rows, model_width = tokens.shape
    local_heads = b_query.shape[0] // HEAD
    head_width = local_heads * HEAD
    row_count = seq_count * block_rows
    slopes = head_slopes(lax.axis_index("tp") * local_heads, local_heads)
    own_pos = lax.axis_index("ctx") * block_rows + jnp.arange(block_rows, dtype=jnp.int32)
    own_seg = segment_ids(doc_lengths, own_pos)
    token_rows = tokens.reshape(row_count, model_width)
    full_query, full_key, full_value, full_out = (
        lax.all_gather(w_query, "fsdp", axis=0, tiled=True),
        lax.all_gather(w_key, "fsdp", axis=0, tiled=True),
        lax.all_gather(w_value, "fsdp", axis=0, tiled=True),
        lax.all_gather(w_out, "fsdp", axis=0, tiled=True),
    )
    queries = (
        jnp.dot(token_rows, full_query, preferred_element_type=jnp.float32) + b_query
    ).astype(jnp.bfloat16)
    key_rows = jnp.dot(token_rows, full_key, preferred_element_type=jnp.float32).astype(
        jnp.bfloat16
    )
    values = (jnp.dot(token_rows, full_value, preferred_element_type=jnp.float32) + b_value).astype(
        jnp.bfloat16
    )
    query_heads = queries.reshape(seq_count, block_rows, local_heads, HEAD)
    key_value = jnp.concatenate([key_rows, values], -1).reshape(
        seq_count, block_rows, 2 * head_width
    )

    def split_pairs(slab_pairs, block_len):
        return (
            slab_pairs[..., :head_width].reshape(seq_count, block_len, local_heads, HEAD),
            slab_pairs[..., head_width:].reshape(seq_count, block_len, local_heads, HEAD),
        )

    def key_slab(pairs, piece_keep, offset, block_len):
        slab_pairs = lax.dynamic_slice_in_dim(pairs, offset, block_len, 1)
        slab_keep = lax.dynamic_slice_in_dim(piece_keep, offset, block_len, 1)
        key_pos = offset + jnp.arange(block_len, dtype=jnp.int32)
        key_seg = segment_ids(doc_lengths, key_pos)
        slab_keys, slab_values = split_pairs(slab_pairs, block_len)
        return (slab_keys, slab_values, slab_keep, key_pos, key_seg)

    start_state = (
        jnp.full((seq_count, local_heads, block_rows), MASKED, jnp.float32),
        jnp.zeros((seq_count, local_heads, block_rows), jnp.float32),
        jnp.zeros((seq_count, local_heads, block_rows, HEAD), jnp.float32),
    )
    pairs = lax.all_gather(key_value, "ctx", axis=1, tiled=True)
    piece_keep = lax.all_gather(keep, "ctx", axis=1, tiled=True)

    def advance(partial_value, offset, block_len):
        slab_keys, slab_values, slab_keep, key_pos, key_seg = key_slab(
            pairs, piece_keep, offset, block_len
        )

        def update(current):
            row_max, row_sum, weighted = current
            scores, allowed = score_block(
                query_heads, own_pos, own_seg, slab_keys, key_pos, key_seg, slab_keep, slopes
            )
            scores = jnp.where(allowed, scores, MASKED)
            new_max = jnp.maximum(row_max, jnp.max(scores, -1))
            factor = jnp.exp(row_max - new_max)
            weights = jnp.where(allowed, jnp.exp(scores - new_max[..., None]), 0.0)
            row_sum = row_sum * factor + jnp.sum(weights, -1)
            weighted = weighted * factor[..., None] + jnp.einsum(
                "shqk,skhd->shqd",
                weights.astype(jnp.bfloat16),
                slab_values,
                preferred_element_type=jnp.float32,
            )
            return (new_max, row_sum, weighted)

        return guarded(intersections(own_seg, key_seg), update, partial_value)

    row_max, row_sum, weighted = over_blocks(pairs.shape[1], advance, start_state)
    attended = (
        (weighted / row_sum[..., None])
        .transpose(0, 2, 1, 3)
        .reshape(row_count, head_width)
        .astype(jnp.bfloat16)
    )
    log_total = row_max + jnp.log(row_sum)
    att_part = jnp.einsum("rh,dh->rd", attended, full_out, preferred_element_type=jnp.float32)
    branch_att = lax.psum(att_part.astype(jnp.bfloat16), "tp").astype(jnp.float32) + b_out
    first_out, normed_one, inv_one = layer_norm(
        token_rows.astype(jnp.float32) + branch_att, gain_one, shift_one
    )
    first_low = first_out.astype(jnp.bfloat16)
    full_up, full_down = (
        lax.all_gather(w_up, "fsdp", axis=0, tiled=True),
        lax.all_gather(w_down, "fsdp", axis=0, tiled=True),
    )
    gate_up = jnp.einsum("rd,dcf->rcf", first_low, full_up, preferred_element_type=jnp.float32)
    product, gelu_back = jax.vjp(
        lambda gate_part, up_part: jax.nn.gelu(gate_part, approximate=False) * up_part,
        gate_up[:, 0],
        gate_up[:, 1],
    )
    hidden = product.astype(jnp.bfloat16)
    ffn_part = jnp.einsum("rf,df->rd", hidden, full_down, preferred_element_type=jnp.float32)
    branch_ffn = lax.psum(ffn_part.astype(jnp.bfloat16), "tp").astype(jnp.float32) + b_down
    result, normed_two, inv_two = layer_norm(first_out + branch_ffn, gain_two, shift_two)
    grad_in = cotangent.reshape(row_count, model_width).astype(jnp.float32)
    grad_two, d_gain_two, d_shift_two = norm_back(grad_in, normed_two, inv_two, gain_two)
    grad_ffn = grad_two.astype(jnp.bfloat16)
    d_b_down = jnp.sum(grad_ffn.astype(jnp.float32), 0)
    d_w_down = jnp.einsum("rd,rf->df", grad_ffn, hidden, preferred_element_type=jnp.float32)
    grad_hidden = jnp.einsum("rd,df->rf", grad_ffn, full_down, preferred_element_type=jnp.float32)
    grad_gate, grad_up = gelu_back(grad_hidden)
    grad_gate_up = jnp.stack([grad_gate, grad_up], 1).astype(jnp.bfloat16)
    d_w_up = jnp.einsum("rd,rcf->dcf", first_low, grad_gate_up, preferred_element_type=jnp.float32)
    first_part = jnp.einsum(
        "rcf,dcf->rd", grad_gate_up, full_up, preferred_element_type=jnp.float32
    )
    grad_first = grad_two + lax.psum(first_part.astype(jnp.bfloat16), "tp").astype(jnp.float32)
    grad_one, d_gain_one, d_shift_one = norm_back(grad_first, normed_one, inv_one, gain_one)
    grad_att = grad_one.astype(jnp.bfloat16)
    d_b_out = jnp.sum(grad_att.astype(jnp.float32), 0)
    d_w_out = jnp.einsum("rd,rh->dh", grad_att, attended, preferred_element_type=jnp.float32)
    grad_attended = jnp.einsum(
        "rd,dh->rh", grad_att, full_out, preferred_element_type=jnp.float32
    ).astype(jnp.bfloat16)
    grad_heads = grad_attended.reshape(seq_count, block_rows, local_heads, HEAD)
    delta = jnp.einsum(
        "sqhd,sqhd->shq",
        grad_heads,
        attended.reshape(seq_count, block_rows, local_heads, HEAD),
        preferred_element_type=jnp.float32,
    )
    query_zero = jnp.zeros((seq_count, block_rows, local_heads, HEAD), jnp.float32)
    full_len = block_rows * lax.axis_size("ctx")
    term_zero = jnp.zeros((seq_count, full_len, 2 * head_width), jnp.float32)
    return_pairs = lax.all_gather(key_value, "ctx", axis=1, tiled=True)
    return_piece_keep = lax.all_gather(keep, "ctx", axis=1, tiled=True)

    def advance(partial_value, offset, block_len):
        slab_keys, slab_values, slab_keep, key_pos, key_seg = key_slab(
            return_pairs, return_piece_keep, offset, block_len
        )

        def update(current):
            query_grad, key_terms = current
            part_query, part_key, part_value = grad_block(
                query_heads,
                own_pos,
                own_seg,
                grad_heads,
                log_total,
                delta,
                slab_keys,
                slab_values,
                key_pos,
                key_seg,
                slab_keep,
                slopes,
            )
            slab_grads = jnp.concatenate(
                [
                    part_key.reshape(seq_count, block_len, head_width),
                    part_value.reshape(seq_count, block_len, head_width),
                ],
                -1,
            )
            return (
                query_grad + part_query,
                lax.dynamic_update_slice_in_dim(key_terms, slab_grads, offset, 1),
            )

        return guarded(intersections(own_seg, key_seg), update, partial_value)

    query_grad, key_terms = over_blocks(return_pairs.shape[1], advance, (query_zero, term_zero))
    pair_grads = lax.psum_scatter(
        key_terms.astype(jnp.bfloat16), "ctx", scatter_dimension=1, tiled=True
    ).astype(jnp.float32)
    query_low = query_grad.reshape(row_count, head_width).astype(jnp.bfloat16)
    pair_low = pair_grads.reshape(row_count, 2 * head_width).astype(jnp.bfloat16)
    grad_project = jnp.concatenate([query_low, pair_low], -1)
    joined_weights = jnp.concatenate([full_query, full_key, full_value], -1)
    joined_grads = jnp.einsum(
        "rd,rh->dh", token_rows, grad_project, preferred_element_type=jnp.float32
    )
    input_part = jnp.einsum(
        "rh,dh->rd", grad_project, joined_weights, preferred_element_type=jnp.float32
    )
    d_tokens = grad_one + lax.psum(input_part.astype(jnp.bfloat16), "tp").astype(jnp.float32)
    d_b_query = jnp.sum(query_low.astype(jnp.float32), 0)
    d_b_value = jnp.sum(pair_low[:, head_width:].astype(jnp.float32), 0)
    d_w_query = joined_grads[:, :head_width]
    d_w_key = joined_grads[:, head_width : 2 * head_width]
    d_w_value = joined_grads[:, 2 * head_width :]
    shard_grads = (
        lax.psum_scatter(
            d_w_query.astype(jnp.bfloat16), "fsdp", scatter_dimension=0, tiled=True
        ).astype(jnp.float32),
        lax.psum_scatter(
            d_w_key.astype(jnp.bfloat16), "fsdp", scatter_dimension=0, tiled=True
        ).astype(jnp.float32),
        lax.psum_scatter(
            d_w_value.astype(jnp.bfloat16), "fsdp", scatter_dimension=0, tiled=True
        ).astype(jnp.float32),
        lax.psum_scatter(
            d_w_out.astype(jnp.bfloat16), "fsdp", scatter_dimension=0, tiled=True
        ).astype(jnp.float32),
        lax.psum_scatter(
            d_w_up.astype(jnp.bfloat16), "fsdp", scatter_dimension=0, tiled=True
        ).astype(jnp.float32),
        lax.psum_scatter(
            d_w_down.astype(jnp.bfloat16), "fsdp", scatter_dimension=0, tiled=True
        ).astype(jnp.float32),
    )
    sum_query, sum_key, sum_value, sum_out, sum_up, sum_down = (
        lax.psum(shard_grads[0].astype(jnp.bfloat16), "ctx").astype(jnp.float32),
        lax.psum(shard_grads[1].astype(jnp.bfloat16), "ctx").astype(jnp.float32),
        lax.psum(shard_grads[2].astype(jnp.bfloat16), "ctx").astype(jnp.float32),
        lax.psum(shard_grads[3].astype(jnp.bfloat16), "ctx").astype(jnp.float32),
        lax.psum(shard_grads[4].astype(jnp.bfloat16), "ctx").astype(jnp.float32),
        lax.psum(shard_grads[5].astype(jnp.bfloat16), "ctx").astype(jnp.float32),
    )
    (
        total_b_query,
        total_b_value,
        total_b_out,
        total_b_down,
        total_gain_one,
        total_shift_one,
        total_gain_two,
        total_shift_two,
    ) = lax.psum(
        (d_b_query, d_b_value, d_b_out, d_b_down, d_gain_one, d_shift_one, d_gain_two, d_shift_two),
        ("fsdp", "ctx"),
    )
    return (
        result.reshape(seq_count, block_rows, model_width).astype(jnp.bfloat16),
        d_tokens.reshape(seq_count, block_rows, model_width),
        sum_query,
        total_b_query,
        sum_key,
        sum_value,
        total_b_value,
        sum_out,
        total_b_out,
        total_gain_one,
        total_shift_one,
        sum_up,
        sum_down,
        total_b_down,
        total_gain_two,
        total_shift_two,
    )


LANES = 128
VMEM_BYTES = 60 << 20
MESH = pl.DeviceIdType.MESH
TILE = 256
DOC_ROW, KEEP_ROW, POS_ROW, LINE_ROW, LOG_ROW, FEAT_END = 64, 72, 73, 79, 82, 85
X_SWAP = [(0, 1), (1, 0), (2, 3), (3, 2)]
Y_SWAP = [(0, 2), (2, 0), (1, 3), (3, 1)]
D_SWAP = [(0, 3), (3, 0), (1, 2), (2, 1)]


def dot(left, right, dims=((1,), (0,))):
    return lax.dot_general(left, right, (dims, ((), ())), preferred_element_type=jnp.float32)


def three_terms(value, low):
    high = low(value)
    middle = low(value - high)
    return high, middle, low(value - high - middle)


def side_signs(rows):
    sub = lax.broadcasted_iota(jnp.int32, (LANES, rows), 0)
    bias_rows = (sub >= POS_ROW) & (sub < LOG_ROW)
    after = jnp.where(bias_rows, -1.0, 1.0).astype(jnp.bfloat16)
    same = jnp.where(bias_rows, 0.0, 1.0).astype(jnp.bfloat16)
    bare = jnp.where(bias_rows | (sub == KEEP_ROW), 0.0, 1.0).astype(jnp.bfloat16)
    return after, same, bare


def diagonal_scores(keys, queries_t, same, bare, slopes):
    rows = lax.broadcasted_iota(jnp.int32, (TILE, TILE), 0)
    cols = lax.broadcasted_iota(jnp.int32, (TILE, TILE), 1)
    apart = jnp.abs(rows - cols).astype(jnp.float32)
    own = rows == cols
    full = [dot(key, query_t * same) for key, query_t in zip(keys, queries_t)]
    alone = [dot(key, query_t * bare) for key, query_t in zip(keys, queries_t)]
    return [
        jnp.where(own, single, scores - slope * apart)
        for scores, single, slope in zip(full, alone, slopes)
    ]


def sweep(first, last, step, most=2):
    many = (last - first) // most

    @pl.loop(0, many)
    def _(i):
        step(first + i * most, most)

    @pl.loop(first + many * most, last)
    def _(tile):
        step(tile, 1)


def doc_bounds(docs_ref, seq):
    bounds, total = [], 0
    for index in range(docs_ref.shape[1]):
        total = total + docs_ref[seq, index]
        bounds.append(total)
    return bounds


def tile_span(docs_ref, seq, block):
    first, last = block * TILE, block * TILE + TILE - 1
    begin = end = start = 0
    for bound in doc_bounds(docs_ref, seq):
        begin = jnp.where(bound <= first, bound, begin)
        end = jnp.where(start <= last, bound, end)
        start = bound
    return lax.div(begin, TILE), lax.div(end + TILE - 1, TILE)


def start_kernel(
    docs, slopes, tokens, keep, w_query, w_key, w_value, w_out, w_up, b_query, b_value, cotangent,
    sequence, full_joined, full_out, full_gate, up_lift, cot_far, cot_near, query_t, queries, keys, keys_t, values, values_t,
    tokens_v, own_v, joined_v, keep_v, gate_v, lift_v, qt_v, q_v, k_v, kt_v, v_v, vt_v,
    z_send, z_recv, tp_send, tp_recv, w_send, w_recv, gate_send, gate_recv, keep_send, keep_recv, local_sem,
    block_sem, joined_sem, lift_sem, gate_sem, cot_sem, out_sem,
):
    place, stage, core = lax.axis_index("fsdp"), lax.axis_index("ctx"), lax.axis_index("tp")
    seq, half = stage // 2, stage % 2
    half_rows, model_width = sequence.shape[2:]
    rows_of = 2 * half_rows
    heads = qt_v.shape[1]
    width = heads * HEAD
    f32, bf16 = jnp.float32, jnp.bfloat16
    barrier = pltpu.get_barrier_semaphore()
    peers = [(place ^ other, stage, core) for other in (1, 2, 3)]
    peers += [(place, lax.rem(stage + shift, 4), core) for shift in (1, 2, 3)]
    peers += [(place, stage, 1 - core)]
    for peer in peers:
        pl.semaphore_signal(barrier, inc=1, device_id=peer, device_id_type=MESH)

    def columns_of(weight):
        return jnp.where(half == 0, weight[:, :width], weight[:, width:])

    own_v[...] = jnp.concatenate([columns_of(w[...]) for w in (w_query, w_key, w_value)], 1)
    joined_v[place] = own_v[...]
    tokens_v[stage] = tokens[seq].reshape(2, half_rows, model_width)
    keep_v[stage] = keep[...]
    pl.semaphore_wait(barrier, len(peers))

    def remote(source, target, send, recv, device):
        return pltpu.make_async_remote_copy(
            source, target, send, recv, device_id=device, device_id_type=MESH
        )

    rows = pl.ds(pl.multiple_of(core * half_rows, half_rows), half_rows)
    ours, theirs = tokens.at[seq, rows], tokens.at[1 - seq, rows]
    other_core = (place, stage, 1 - core)
    inner = (stage == 1) | (stage == 2)
    facing, opposite = 3 - stage, stage ^ 2
    third, fourth = jnp.where(inner, facing, opposite), jnp.where(inner, opposite, facing)

    def send(source, block, target, slot):
        return remote(source, tokens_v.at[block, core], z_send.at[slot], z_recv.at[block], (place, target, core))

    def arrival(block):
        return remote(ours, tokens_v.at[block, core], z_send.at[0], z_recv.at[block], other_core)

    def share(block, whose):
        half_block = tokens_v.at[block, whose]
        return remote(half_block, half_block, tp_send.at[block], tp_recv.at[block], other_core)

    to_pair = send(ours, stage, stage ^ 1, 0)
    to_across = send(theirs, stage, third, 1)
    to_pair.start()

    @pl.when(inner)
    def _():
        to_across.start()

    weights = [
        remote(
            own_v, joined_v.at[place], w_send.at[other - 1], w_recv.at[other - 1], (place ^ other, stage, core)
        )
        for other in (1, 2, 3)
    ]
    flags = [
        remote(
            keep, keep_v.at[stage], keep_send.at[shift - 1], keep_recv.at[shift - 1],
            (place, lax.rem(stage + shift, 4), core),
        )
        for shift in (1, 2, 3)
    ]
    outs = [
        remote(
            w_out, full_out.at[place], w_send.at[other + 2], w_recv.at[other + 2], (place ^ other, stage, core)
        )
        for other in (1, 2, 3)
    ]

    units = w_up.shape[2] // 2

    def gate_copy(owner, other, which, sem):
        block = gate_v.at[owner, :, pl.ds(which * units, units)]
        return remote(block, block, gate_send.at[sem], gate_recv.at[sem], (place ^ other, stage, core))

    halves = [
        gate_copy(place, other, which, 2 * which + other - 1)
        for other, which in ((1, 0), (2, 1), (1, 1), (2, 0))
    ]
    on = [gate_copy(place ^ 1, 2, 0, 4), gate_copy(place ^ 2, 1, 1, 5)]
    for copy in weights + flags + outs:
        copy.start()
    gate_v[place] = w_up[:, 0, :]
    for copy in halves:
        copy.start()
    lift_v[...] = w_up[:, 1, :]
    lift_out = pltpu.make_async_copy(lift_v, up_lift, lift_sem)
    lift_out.start()
    own_out = pltpu.make_async_copy(w_out, full_out.at[place], local_sem)
    own_out.start()
    odd = stage % 2
    cot_outs = [
        pltpu.make_async_copy(cotangent.at[1 - odd, core], cot_far, cot_sem.at[0]),
        pltpu.make_async_copy(cotangent.at[odd, core], cot_near, cot_sem.at[1]),
    ]
    for copy in cot_outs:
        copy.start()

    bounds = doc_bounds(docs, seq)

    def out_copies(slot, block):
        at = pl.ds(pl.multiple_of(block * rows_of, rows_of), rows_of)
        pairs = (
            (qt_v.at[slot], query_t.at[:, :, at]),
            (q_v.at[slot], queries.at[:, at, :]),
            (k_v.at[slot], keys.at[:, at, :]),
            (kt_v.at[slot], keys_t.at[:, :, at]),
            (v_v.at[slot], values.at[:, at, :]),
            (vt_v.at[slot], values_t.at[:, :, at]),
        )
        return [
            pltpu.make_async_copy(source, target, block_sem.at[slot, index])
            for index, (source, target) in enumerate(pairs)
        ]

    def sequence_copy(block):
        return pltpu.make_async_copy(tokens_v.at[block], sequence.at[block], out_sem.at[block])

    def low(value):
        return value.astype(bf16).astype(f32)

    def project(slot, block):
        x = tokens_v[block].reshape(rows_of, model_width)
        y = dot(x, joined_v[...].reshape(model_width, 3 * width))
        zero = jnp.zeros((1, width), f32)
        biases = [
            jnp.where(half == 0, b[:, :width], b[:, width:])
            for b in (b_query[...].reshape(1, -1), b_value[...].reshape(1, -1))
        ]
        y = low(y + jnp.concatenate([biases[0], zero, biases[1]], 1))
        fill = -y.shape[1] % LANES
        if fill:
            y = jnp.concatenate([y, jnp.zeros((rows_of, fill), f32)], 1)
        lane = lax.broadcasted_iota(jnp.int32, (rows_of, LANES), 1)
        sub = lax.broadcasted_iota(jnp.int32, (LANES, rows_of), 0)
        first = block * rows_of
        key_pos = first + lax.broadcasted_iota(jnp.int32, (rows_of, LANES), 0)
        query_pos = first + lax.broadcasted_iota(jnp.int32, (LANES, rows_of), 1)

        def segments(positions):
            return sum((bound <= positions).astype(jnp.int32) for bound in bounds)

        flag = keep_v[block, pl.ds(seq, 1), :].astype(f32)
        flag = jnp.broadcast_to(flag, (LANES, rows_of)).T
        key_feat = jnp.where(lane < DOC_ROW, 0.0, 1.0)
        key_doc = jnp.where(segments(key_pos) == lane - DOC_ROW, 0.0, MASKED)
        key_feat = jnp.where((lane >= DOC_ROW) & (lane < DOC_ROW + len(bounds)), key_doc, key_feat)
        key_feat = jnp.where(lane == KEEP_ROW, jnp.where(flag > 0.5, 0.0, MASKED), key_feat)
        pos_low = key_pos & 255
        key_feat = jnp.where(
            (lane >= POS_ROW) & (lane < POS_ROW + 3), (key_pos - pos_low).astype(f32), key_feat
        )
        key_feat = jnp.where((lane >= POS_ROW + 3) & (lane < LINE_ROW), pos_low.astype(f32), key_feat)
        key_feat = jnp.where(lane >= FEAT_END, 0.0, key_feat)
        doc_feat = jnp.where(segments(query_pos) == sub - DOC_ROW, 1.0, 0.0)
        doc_feat = jnp.where(sub == KEEP_ROW, 1.0, doc_feat)

        def head_part(index):
            pair = y[:, index // 2 * LANES : (index // 2 + 1) * LANES]
            if index % 2:
                pair = pltpu.roll(pair, HEAD, 1)
            return jnp.where(lane < HEAD, pair, 0.0)

        for head in range(heads):
            query_feat = doc_feat
            slope = jnp.full((1, rows_of), slopes[head], f32)
            slope_terms = three_terms(slope, low)
            line_terms = three_terms(-slope * query_pos[:1].astype(f32), low)
            for term in range(3):
                here = (sub == POS_ROW + term) | (sub == POS_ROW + 3 + term)
                query_feat = jnp.where(here, slope_terms[term], query_feat)
                query_feat = jnp.where(sub == LINE_ROW + term, line_terms[term], query_feat)
            query = head_part(head) * 0.125
            q_v[slot, head] = query[:, :HEAD].astype(bf16)
            qt_v[slot, head] = (query.T + query_feat).astype(bf16)
            key = head_part(heads + head)
            k_v[slot, head] = (key + key_feat).astype(bf16)
            kt_v[slot, head] = key.T[:HEAD].astype(bf16)
            value = head_part(2 * heads + head)
            ones = (lane >= HEAD) & (lane < HEAD + 3)
            v_v[slot, head] = jnp.where(ones, 1.0, value).astype(bf16)
            vt_v[slot, head] = jnp.where(sub == HEAD, 1.0, value.T)[:80].astype(bf16)

    for copy in weights + flags:
        copy.wait_recv()
    joined_out = pltpu.make_async_copy(joined_v, full_joined, joined_sem)
    joined_out.start()

    @pl.when(~inner)
    def _():
        to_pair.wait_send()
        to_across.start()

    @pl.loop(0, 4)
    def _(i):
        pair = stage ^ 1
        block = jnp.where(i == 0, stage, jnp.where(i == 1, pair, jnp.where(i == 2, third, fourth)))
        slot = lax.rem(i, 2)

        @pl.when(i == 1)
        def _():
            arrival(pair).wait_recv()
            share(pair, core).start()
            arrival(third).wait_recv()

            @pl.when(inner)
            def _():
                send(tokens_v.at[third, core], third, pair, 2).start()

            share(third, core).start()
            for near, far in zip(halves[:2], on):
                near.wait_recv()
                far.start()

        @pl.when(i == 3)
        def _():
            arrival(fourth).wait_recv()

            @pl.when(inner)
            def _():
                send(tokens_v.at[fourth, core], fourth, pair, 3).start()

            share(fourth, core).start()

        @pl.when(i >= 1)
        def _():
            share(block, 1 - core).wait_recv()

        @pl.when(i >= 2)
        def _():
            for copy in out_copies(slot, block):
                copy.wait()

        sequence_copy(block).start()
        project(slot, block)
        for copy in out_copies(slot, block):
            copy.start()

    @pl.when(inner)
    def _():
        to_pair.wait_send()

    to_across.wait_send()

    @pl.when(inner)
    def _():
        for block, slot in ((third, 2), (fourth, 3)):
            send(tokens_v.at[block, core], block, stage ^ 1, slot).wait_send()

    for block in (stage ^ 1, third, fourth):
        share(block, core).wait_send()
    for copy in outs + halves[2:] + on:
        copy.wait()
    gate_out = pltpu.make_async_copy(gate_v, full_gate, gate_sem)
    gate_out.start()
    for copy in weights + flags + halves[:2]:
        copy.wait_send()
    for copy in [own_out, joined_out, lift_out, gate_out] + cot_outs:
        copy.wait()
    for block in range(4):
        sequence_copy(block).wait()
    for slot in (0, 1):
        for copy in out_copies(slot, 0):
            copy.wait()


def start(docs, slopes, tokens, keep, w_query, w_key, w_value, w_out, w_up, b_query, b_value, cotangent):
    _, block_rows, model_width = tokens.shape
    heads = slopes.shape[0]
    width, length = heads * HEAD, 4 * block_rows
    dma, bf16 = pltpu.SemaphoreType.DMA, jnp.bfloat16
    half_rows, quarter = block_rows // 2, w_query.shape[0]
    any_spec = pl.BlockSpec(memory_space=pl.ANY)
    vmem_spec = pl.BlockSpec(memory_space=pltpu.VMEM)
    smem_spec = pl.BlockSpec(memory_space=pltpu.SMEM)

    def parts(rows):
        return [
            (heads, LANES, rows),
            (heads, rows, HEAD),
            (heads, rows, LANES),
            (heads, HEAD, rows),
            (heads, rows, LANES),
            (heads, 80, rows),
        ]

    three, four, six = dma((3,)), dma((4,)), dma((6,))
    return pl.pallas_call(
        start_kernel,
        in_specs=[smem_spec] * 2 + [vmem_spec] * 10,
        out_specs=[any_spec] * 13,
        out_shape=[
            jax.ShapeDtypeStruct(shape, bf16)
            for shape in [
                (4, 2, half_rows, model_width),
                (4, quarter, 3 * width),
                (4,) + w_out.shape,
                (4, quarter, w_up.shape[2]),
                (quarter, w_up.shape[2]),
                (half_rows, model_width),
                (half_rows, model_width),
            ]
            + parts(length)
        ],
        scratch_shapes=[
            pltpu.VMEM((4, 2, half_rows, model_width), bf16),
            pltpu.VMEM((quarter, 3 * width), bf16),
            pltpu.VMEM((4, quarter, 3 * width), bf16),
            pltpu.VMEM((4,) + keep.shape, keep.dtype),
            pltpu.VMEM((4, quarter, w_up.shape[2]), bf16),
            pltpu.VMEM((quarter, w_up.shape[2]), bf16),
            *[pltpu.VMEM((2,) + shape, bf16) for shape in parts(block_rows)],
            four, four, four, four, six, six, six, six, three, three, dma, dma((2, 6)), dma, dma, dma, dma((2,)), four,
        ],
        compiler_params=pltpu.CompilerParams(
            collective_id=0, has_side_effects=True, vmem_limit_bytes=VMEM_BYTES
        ),
        cost_estimate=pl.CostEstimate(flops=40 << 30, bytes_accessed=16 << 20, transcendentals=0),
        name="start",
    )(docs, slopes, tokens, keep, w_query, w_key, w_value, w_out, w_up, b_query, b_value, cotangent)


def attend_kernel(docs_ref, slope_ref, qt_ref, k_ref, vt_ref, o_ref, ot_ref, lse_ref, max_ref, acc_ref):
    heads = qt_ref.shape[0]
    block = pl.program_id(0)
    first_tile, last_tile = tile_span(docs_ref, lax.axis_index("ctx") // 2, block)
    after, same, bare = side_signs(TILE)

    def tile_rows(tile, count=1):
        return pl.ds(pl.multiple_of(tile * TILE, TILE), count * TILE)

    own = tile_rows(block)
    each = range(heads)
    scores = diagonal_scores(
        [k_ref[head, own, :] for head in each], [qt_ref[head] for head in each], same, bare,
        [slope_ref[head] for head in each],
    )
    tops = [jnp.max(scores[head], 0, keepdims=True) for head in each]
    weights = [jnp.exp(scores[head] - tops[head]).astype(jnp.bfloat16) for head in each]
    parts = [dot(vt_ref[head, :, own], weights[head]) for head in each]
    for head in each:
        max_ref[head] = tops[head]
        acc_ref[head] = parts[head]

    def step(tile, count, sign):
        each = range(heads)
        keys = [k_ref[head, tile_rows(tile, count), :] for head in each]
        values = [vt_ref[head, :, tile_rows(tile, count)] for head in each]
        queries = [qt_ref[head] if sign is None else qt_ref[head] * sign for head in each]
        old = [max_ref[head] for head in each]
        acc = [acc_ref[head] for head in each]
        scores = [dot(keys[head], queries[head]) for head in each]
        top = [jnp.maximum(old[head], jnp.max(scores[head], 0, keepdims=True)) for head in each]
        weights = [jnp.exp(scores[head] - top[head]).astype(jnp.bfloat16) for head in each]
        parts = [dot(values[head], weights[head]) for head in each]
        for head in each:
            max_ref[head] = top[head]
            acc_ref[head] = acc[head] * jnp.exp(old[head] - top[head]) + parts[head]

    sweep(first_tile, block, lambda tile, count: step(tile, count, None))
    sweep(block + 1, last_tile, lambda tile, count: step(tile, count, after))

    parts = []
    for head in range(heads):
        total = acc_ref[head, HEAD : HEAD + 1, :]
        out_t = acc_ref[head, :HEAD, :] / total
        ot_ref[head] = out_t
        parts.append(out_t)
        lse_ref[head] = max_ref[head] + jnp.log(total)
    o_ref[...] = jnp.concatenate(parts, 0).T.astype(jnp.bfloat16)


def attend(docs, slopes, query_t, keys, value_t):
    heads, _, length = query_t.shape
    blocks = length // TILE
    return pl.pallas_call(
        attend_kernel,
        grid_spec=pltpu.PrefetchScalarGridSpec(
            num_scalar_prefetch=2,
            grid=(blocks,),
            in_specs=[
                pl.BlockSpec((heads, LANES, TILE), lambda i, *_: (0, 0, i)),
                pl.BlockSpec(keys.shape, lambda i, *_: (0, 0, 0)),
                pl.BlockSpec(value_t.shape, lambda i, *_: (0, 0, 0)),
            ],
            out_specs=[
                pl.BlockSpec((TILE, heads * HEAD), lambda i, *_: (i, 0)),
                pl.BlockSpec((heads, HEAD, TILE), lambda i, *_: (0, 0, i)),
                pl.BlockSpec((heads, 1, TILE), lambda i, *_: (0, 0, i)),
            ],
            scratch_shapes=[
                pltpu.VMEM((heads, 1, TILE), jnp.float32),
                pltpu.VMEM((heads, 80, TILE), jnp.float32),
            ],
        ),
        out_shape=[
            jax.ShapeDtypeStruct((length, heads * HEAD), jnp.bfloat16),
            jax.ShapeDtypeStruct((heads, HEAD, length), jnp.float32),
            jax.ShapeDtypeStruct((heads, 1, length), jnp.float32),
        ],
        compiler_params=pltpu.CompilerParams(vmem_limit_bytes=VMEM_BYTES),
        cost_estimate=pl.CostEstimate(
            flops=heads * length * length * 256, bytes_accessed=6 << 20, transcendentals=heads * length * length
        ),
        name="attend",
    )(docs, slopes, query_t, keys, value_t)


def attend_back_kernel(
    docs_ref, slope_ref, qt_ref, q_ref, k_ref, kt_ref, v_ref, g_ref, ot_ref, lse_ref,
    dq_ref, dk_ref, dv_ref, qt_log, grad_heads, grad_t, query_acc, key_acc, value_acc,
):
    heads = qt_ref.shape[0]
    blocks = pl.num_programs(0)
    block = pl.program_id(0)
    length = qt_ref.shape[2]
    first_tile, last_tile = tile_span(docs_ref, lax.axis_index("ctx") // 2, block)
    after, same, bare = side_signs(TILE)

    def low(value):
        return value.astype(jnp.bfloat16).astype(jnp.float32)

    def tile_rows(tile, count=1):
        return pl.ds(pl.multiple_of(tile * TILE, TILE), count * TILE)

    @pl.when(block == 0)
    def _():
        query_acc[...] = jnp.zeros_like(query_acc)
        sub = lax.broadcasted_iota(jnp.int32, (LANES, TILE), 0)

        @pl.loop(0, length // TILE)
        def _(tile):
            rows = tile_rows(tile)
            grad = g_ref[rows, :].astype(jnp.float32)
            turned = grad.T
            for head in range(heads):
                own = turned[head * HEAD : (head + 1) * HEAD]
                delta = jnp.sum(own * ot_ref[head, :, rows], 0, keepdims=True)
                first, second, third = three_terms(-delta, low)
                wide = jnp.concatenate([own, jnp.zeros_like(own)], 0)
                wide = jnp.where(sub == HEAD, first, wide)
                wide = jnp.where(sub == HEAD + 1, second, wide)
                wide = jnp.where(sub == HEAD + 2, third, wide)
                grad_t[head, :, rows] = wide.astype(jnp.bfloat16)
                grad_heads[head, rows, :] = own.T.astype(jnp.bfloat16)
                first, second, third = three_terms(-lse_ref[head, :, rows], low)
                query = qt_ref[head, :, rows].astype(jnp.float32)
                query = jnp.where(sub == LOG_ROW, first, query)
                query = jnp.where(sub == LOG_ROW + 1, second, query)
                query = jnp.where(sub == LOG_ROW + 2, third, query)
                qt_log[head, :, rows] = query.astype(jnp.bfloat16)

    def accumulate(tile, scores, first, count=1):
        each = range(heads)
        rows = tile_rows(tile, count)
        values = [v_ref[head] for head in each]
        turned = [grad_t[head, :, rows] for head in each]
        grads = [grad_heads[head, rows, :] for head in each]
        queries = [q_ref[head, rows, :] for head in each]
        keys_t = [kt_ref[head] for head in each]
        probs = [jnp.exp(scores[head]) for head in each]
        grad_probs = [dot(values[head], turned[head]) for head in each]
        grad_scores = [(probs[head] * grad_probs[head]).astype(jnp.bfloat16) for head in each]
        value_part = [dot(probs[head].astype(jnp.bfloat16), grads[head]) for head in each]
        key_part = [dot(grad_scores[head], queries[head]) for head in each]
        query_part = [dot(keys_t[head], grad_scores[head]) for head in each]
        for head in each:
            if first:
                value_acc[head] = value_part[head]
                key_acc[head] = key_part[head]
            else:
                value_acc[head] += value_part[head]
                key_acc[head] += key_part[head]
            query_acc[head, :, rows] += query_part[head]

    own = [qt_log[head, :, tile_rows(block)] for head in range(heads)]
    accumulate(
        block,
        diagonal_scores(
            [k_ref[head] for head in range(heads)], own, same, bare,
            [slope_ref[head] for head in range(heads)],
        ),
        True,
    )
    after_wide = side_signs(2 * TILE)[0]

    def step(tile, count, sign):
        queries = [qt_log[head, :, tile_rows(tile, count)] for head in range(heads)]
        if sign is not None:
            queries = [query * sign[:, : count * TILE] for query in queries]
        accumulate(tile, [dot(k_ref[head], queries[head]) for head in range(heads)], False, count)

    sweep(first_tile, block, lambda tile, count: step(tile, count, after_wide))
    sweep(block + 1, last_tile, lambda tile, count: step(tile, count, None))

    dk_ref[...] = jnp.concatenate([key_acc[head] for head in range(heads)], 1).astype(jnp.bfloat16)
    dv_ref[...] = jnp.concatenate([value_acc[head] for head in range(heads)], 1).astype(jnp.bfloat16)

    @pl.when(block == blocks - 1)
    def _():
        @pl.loop(0, length // TILE)
        def _(tile):
            rows = tile_rows(tile)
            turned = jnp.concatenate([query_acc[head, :, rows] for head in range(heads)], 0)
            dq_ref[rows, :] = (turned.T * 0.125).astype(jnp.bfloat16)


def attend_back(docs, slopes, query_t, queries, keys, keys_t, values, grads, out_t, lse):
    heads, _, length = query_t.shape
    blocks = length // TILE
    width = heads * HEAD

    def whole(array):
        return pl.BlockSpec(array.shape, lambda i, *_: (0,) * array.ndim)

    return pl.pallas_call(
        attend_back_kernel,
        grid_spec=pltpu.PrefetchScalarGridSpec(
            num_scalar_prefetch=2,
            grid=(blocks,),
            in_specs=[
                whole(query_t),
                whole(queries),
                pl.BlockSpec((heads, TILE, LANES), lambda i, *_: (0, i, 0)),
                pl.BlockSpec((heads, HEAD, TILE), lambda i, *_: (0, 0, i)),
                pl.BlockSpec((heads, TILE, LANES), lambda i, *_: (0, i, 0)),
                whole(grads),
                whole(out_t),
                whole(lse),
            ],
            out_specs=[
                pl.BlockSpec((length, width), lambda i, *_: (0, 0)),
                pl.BlockSpec((TILE, width), lambda i, *_: (i, 0)),
                pl.BlockSpec((TILE, width), lambda i, *_: (i, 0)),
            ],
            scratch_shapes=[
                pltpu.VMEM((heads, LANES, length), jnp.bfloat16),
                pltpu.VMEM((heads, length, HEAD), jnp.bfloat16),
                pltpu.VMEM((heads, LANES, length), jnp.bfloat16),
                pltpu.VMEM((heads, HEAD, length), jnp.float32),
                pltpu.VMEM((heads, TILE, HEAD), jnp.float32),
                pltpu.VMEM((heads, TILE, HEAD), jnp.float32),
            ],
        ),
        out_shape=[jax.ShapeDtypeStruct((length, width), jnp.bfloat16)] * 3,
        compiler_params=pltpu.CompilerParams(vmem_limit_bytes=VMEM_BYTES),
        cost_estimate=pl.CostEstimate(
            flops=heads * length * length * 640, bytes_accessed=12 << 20, transcendentals=heads * length * length
        ),
        name="attend_back",
    )(docs, slopes, query_t, queries, keys, keys_t, values, grads, out_t, lse)


def rows_norm(residual):
    centered = residual - jnp.mean(residual, -1, keepdims=True)
    inv_scale = lax.rsqrt(jnp.mean(centered * centered, -1, keepdims=True) + NORM_EPS)
    return centered * inv_scale, inv_scale


def rows_norm_back(grad_out, normed, inv_scale, norm_gain):
    grad_norm = grad_out * norm_gain
    mean_grad = jnp.mean(grad_norm, -1, keepdims=True)
    mean_cross = jnp.mean(grad_norm * normed, -1, keepdims=True)
    return (grad_norm - mean_grad - normed * mean_cross) * inv_scale


def middle_kernel(
    attended, sequence, cotangent, cot_far, cot_near, w_out, gate_full, w_down, lift_0, lift_1, lift_2, lift_3, *rest,
):
    vectors, rest = rest[:6], rest[6:]
    (
        out_home, grad_one, grad_heads, early_0, early_1, early_2, early_3, late, down_sum, sums,
        token_v, mine_v, theirs_v, both_v, cot_v, out_w, down_w, up_w,
        send_a, recv_a, send_b, recv_b, send_c, recv_c,
        normed_v, inv_v, low_v, hidden_v, gate_v, lift_v, grad_v, ffn_v, att_v, result_v, keep_v, away_v, tile_v,
        down_v, down_got, home_v, load_sem, near_send, near_recv, pair_send, pair_recv, cot_send, cot_pass, cot_took,
        a_send, a_recv, b_send, b_recv, c_send, c_recv, out_send, out_recv, out_pass, out_took,
        one_sem, keep_sem, away_send, away_recv, tile_sem, down_send, down_recv, down_sem, home_sem,
    ) = rest
    place, stage, core = lax.axis_index("fsdp"), lax.axis_index("ctx"), lax.axis_index("tp")
    seq, half = stage // 2, stage % 2
    pair = stage ^ 1
    chunks = token_v.shape[0]
    units = hidden_v.shape[2]
    wide = 512
    quarter = lift_0.shape[0]

    barrier = pltpu.get_barrier_semaphore()
    peers = [(place ^ other, stage, core) for other in (1, 2, 3)]
    peers += [(place, lax.rem(stage + shift, 4), core) for shift in (1, 2, 3)]
    peers += [(place, stage, 1 - core)]
    for peer in peers:
        pl.semaphore_signal(barrier, inc=1, device_id=peer, device_id_type=MESH)
    pl.semaphore_wait(barrier, len(peers))

    def remote(source, target, send, recv, device):
        return pltpu.make_async_remote_copy(
            source, target, send, recv, device_id=device, device_id_type=MESH
        )

    partner = (place, pair, core)
    other_core = (place, stage, 1 - core)

    def pair_copy(c):
        return remote(
            attended.at[(1 - half) * chunks + c], theirs_v.at[c], pair_send.at[c], pair_recv.at[c], partner
        )

    for c in range(chunks):
        pair_copy(c).start()

    def rows_of(owner):
        return pl.ds(pl.multiple_of(owner * quarter, quarter), quarter)

    def near_copy(owner, other, which, sem):
        columns = pl.ds(which * (units // 2), units // 2)
        block = down_w.at[rows_of(owner), columns]
        source = w_down.at[:, columns] if owner is place else block
        return remote(source, block, near_send.at[sem], near_recv.at[sem], (place ^ other, stage, core))

    halves = [
        near_copy(place, other, which, 2 * which + other - 1)
        for other, which in ((1, 0), (2, 1), (1, 1), (2, 0))
    ]
    on = [near_copy(place ^ 1, 2, 0, 4), near_copy(place ^ 2, 1, 1, 5)]
    for copy in halves:
        copy.start()

    def cot_owner(which):
        return 2 * which + stage // 2

    near_block = jnp.where(stage < 2, 0, 1)
    far_block = 1 - near_block
    facing = (stage == 1) | (stage == 2)
    far_load = pltpu.make_async_copy(cot_far, cot_v.at[far_block, core], cot_send.at[0])
    near_load = pltpu.make_async_copy(cot_near, cot_v.at[near_block, core], cot_send.at[1])
    own_load = pltpu.make_async_copy(cotangent.at[stage // 2], cot_v.at[near_block], cot_send.at[1])
    far_load.start()

    @pl.when(facing)
    def _():
        near_load.start()

    @pl.when(~facing)
    def _():
        own_load.start()

    def cot_share(block, whose):
        return remote(
            cot_v.at[block, whose], cot_v.at[block, whose], cot_pass.at[block], cot_took.at[block], other_core
        )

    loads = [
        pltpu.make_async_copy(attended.at[pl.ds(half * chunks, chunks)], mine_v, load_sem.at[0]),
        pltpu.make_async_copy(w_out, out_w, load_sem.at[1]),
        pltpu.make_async_copy(sequence.at[pl.ds(half * chunks, chunks)], token_v, load_sem.at[2]),
        pltpu.make_async_copy(w_down, down_w.at[rows_of(place)], load_sem.at[3]),
        pltpu.make_async_copy(gate_full, up_w.at[:, pl.ds(0, units)], load_sem.at[4]),
    ]
    for other, shard in enumerate((lift_0, lift_1, lift_2, lift_3)):
        target = up_w.at[rows_of(place ^ other), pl.ds(units, units)]
        loads.append(pltpu.make_async_copy(shard, target, load_sem.at[5 + other]))
    for load in loads:
        load.start()

    b_out, gain_one, shift_one, b_down, gain_two, shift_two = (v[...].reshape(1, -1) for v in vectors)
    sums[...] = jnp.zeros_like(sums)

    def add_sum(index, rows):
        sums[index : index + 1, :] += jnp.sum(rows, 0, keepdims=True)

    def exchange(c, sent, got, send, recv):
        return remote(sent.at[c], got.at[c], send.at[c], recv.at[c], other_core)

    def total(c, sent, got):
        return sent[c].astype(jnp.float32) + got[c].astype(jnp.float32)

    loads[0].wait()
    loads[1].wait()

    def attention_branch(c):
        pair_copy(c).wait_recv()
        first, second = mine_v[c], theirs_v[c]
        both = jnp.where(
            half == 0, jnp.concatenate([first, second], 1), jnp.concatenate([second, first], 1)
        )
        both_v[c] = both
        send_a[c] = dot(both, out_w[...], ((1,), (1,))).astype(jnp.bfloat16)
        exchange(c, send_a, recv_a, a_send, a_recv).start()

    attention_branch(0)
    far_load.wait()
    cot_share(far_block, core).start()

    @pl.when(facing)
    def _():
        near_load.wait()
        cot_share(near_block, core).start()

    @pl.when(~facing)
    def _():
        own_load.wait()

    for load in loads[2:]:
        load.wait()
    @pl.loop(0, chunks)
    def _(c):
        @pl.when(c + 1 < chunks)
        def _():
            attention_branch(c + 1)

        @pl.when(c == 1)
        def _():
            for near, far in zip(halves[:2], on):
                near.wait_recv()
                far.start()

        exchange(c, send_a, recv_a, a_send, a_recv).wait_recv()

        residual = token_v[c].astype(jnp.float32) + (total(c, send_a, recv_a) + b_out)
        normed, inv_scale = rows_norm(residual)
        normed_v[c] = normed
        inv_v[c] = inv_scale
        low_v[c] = (normed * gain_one + shift_one).astype(jnp.bfloat16)
        for n in range(0, units, wide):
            gate = dot(low_v[c], up_w[:, n : n + wide])
            lift = dot(low_v[c], up_w[:, units + n : units + n + wide])
            chance = 0.5 + 0.5 * lax.erf(gate * 0.7071067811865476)
            density = jnp.exp(gate * gate * -0.5) * 0.3989422804014327
            gelu = gate * chance
            hidden_v[c, :, n : n + wide] = (gelu * lift).astype(jnp.bfloat16)
            gate_v[c, :, n : n + wide] = (lift * (chance + gate * density)).astype(jnp.bfloat16)
            lift_v[c, :, n : n + wide] = gelu.astype(jnp.bfloat16)

    for copy in halves[2:] + on:
        copy.wait_recv()
    @pl.loop(0, chunks)
    def _(c):
        send_b[c] = dot(hidden_v[c], down_w[...], ((1,), (1,))).astype(jnp.bfloat16)
        exchange(c, send_b, recv_b, b_send, b_recv).start()

    cot_share(far_block, core).wait_send()
    cot_share(far_block, 1 - core).wait_recv()

    @pl.when(facing)
    def _():
        cot_share(near_block, core).wait_send()
        cot_share(near_block, 1 - core).wait_recv()

    def home(c):
        return 2 * half + c // 2

    def out_copy(c):
        return remote(
            result_v.at[c], home_v.at[seq], out_send.at[c], out_recv.at[seq], (place, home(c), core)
        )

    def out_local(c):
        return pltpu.make_async_copy(result_v.at[c], out_home.at[seq, c % 2], out_send.at[c])

    @pl.loop(0, chunks)
    def _(c):
        exchange(c, send_b, recv_b, b_send, b_recv).wait_recv()
        normed_one = normed_v[c]
        residual = normed_one * gain_one + shift_one + (total(c, send_b, recv_b) + b_down)
        normed, inv_scale = rows_norm(residual)
        result_v[c] = (normed * gain_two + shift_two).astype(jnp.bfloat16)

        @pl.when(home(c) == stage)
        def _():
            out_local(c).start()

        @pl.when((home(c) != stage) & (c % 2 == core))
        def _():
            out_copy(c).start()

        grad_in = cot_v[c // 2, c % 2].astype(jnp.float32)
        add_sum(0, grad_in * normed)
        add_sum(1, grad_in)
        grad_two = rows_norm_back(grad_in, normed, inv_scale, gain_two)
        grad_v[c] = grad_two
        grad_ffn = grad_two.astype(jnp.bfloat16)
        ffn_v[c] = grad_ffn
        add_sum(2, grad_ffn.astype(jnp.float32))

    tile = tile_v.shape[2]

    def columns(index):
        return pl.ds(pl.multiple_of(index * tile, tile), tile)

    def weight_part(left, right):
        rows = left.shape[0] * left.shape[1]
        return dot(
            left[...].reshape(rows, left.shape[2]), right.reshape(rows, tile), ((0,), (0,))
        ).astype(jnp.bfloat16)

    unit_tiles = units // tile

    def down_copy(i, other):
        rows = pl.ds(pl.multiple_of((place ^ other) * quarter, quarter), quarter)
        return remote(
            down_v.at[rows, columns(i)], down_got.at[other - 1, :, columns(i)],
            down_send.at[i, other - 1], down_recv.at[i, other - 1], (place ^ other, stage, core),
        )

    @pl.loop(0, unit_tiles)
    def _(i):
        down_v[:, columns(i)] = weight_part(ffn_v, hidden_v[:, :, columns(i)])
        for other in (1, 2, 3):
            down_copy(i, other).start()

    @pl.loop(0, chunks)
    def _(c):
        for n in range(0, units, wide):
            grad_hidden = dot(ffn_v[c], down_w[:, n : n + wide])
            gate_v[c, :, n : n + wide] = (grad_hidden * gate_v[c, :, n : n + wide]).astype(jnp.bfloat16)
            lift_v[c, :, n : n + wide] = (grad_hidden * lift_v[c, :, n : n + wide]).astype(jnp.bfloat16)
        send_c[c] = (
            dot(gate_v[c], up_w[:, :units], ((1,), (1,))) + dot(lift_v[c], up_w[:, units:], ((1,), (1,)))
        ).astype(jnp.bfloat16)
        exchange(c, send_c, recv_c, c_send, c_recv).start()

    def one_copy(c):
        return pltpu.make_async_copy(grad_v.at[c], grad_one.at[c], one_sem.at[c])

    def keep_copy(c):
        return pltpu.make_async_copy(keep_v.at[c], grad_heads.at[half * chunks + c], keep_sem.at[c])

    def away_copy(c, whose):
        return remote(
            away_v.at[c], grad_heads.at[whose * chunks + c], away_send.at[c], away_recv.at[c], partner
        )

    @pl.loop(0, chunks)
    def _(c):
        exchange(c, send_c, recv_c, c_send, c_recv).wait_recv()
        grad_first = grad_v[c] + total(c, send_c, recv_c)
        normed = normed_v[c]
        add_sum(3, grad_first * normed)
        add_sum(4, grad_first)
        grad_res = rows_norm_back(grad_first, normed, inv_v[c], gain_one)
        grad_v[c] = grad_res
        one_copy(c).start()
        grad_att = grad_res.astype(jnp.bfloat16)
        att_v[c] = grad_att
        add_sum(5, grad_att.astype(jnp.float32))
        heads = dot(att_v[c], out_w[...]).astype(jnp.bfloat16)
        first, second = heads[:, : heads.shape[1] // 2], heads[:, heads.shape[1] // 2 :]
        keep_v[c] = jnp.where(half == 0, first, second)
        away_v[c] = jnp.where(half == 0, second, first)
        away_copy(c, half).start()
        keep_copy(c).start()

    early = (early_0, early_1, early_2, early_3)
    early_tiles = early_0.shape[1] // tile

    def tile_copy(slot, other, index):
        target, column = index
        rows = pl.ds(pl.multiple_of((place ^ other) * quarter, quarter), quarter)
        place_of = target[other] if isinstance(target, tuple) else target.at[other]
        return pltpu.make_async_copy(
            tile_v.at[slot, rows], place_of.at[:, columns(column)], tile_sem.at[slot, other]
        )

    def weight_tile(count, target, column, left, right):
        slot = lax.rem(count, 2)

        @pl.when(count >= 2)
        def _():
            for row in range(4):
                tile_copy(slot, row, (target, column)).wait()

        tile_v[slot] = weight_part(left, right)
        for row in range(4):
            tile_copy(slot, row, (target, column)).start()

    @pl.loop(0, unit_tiles)
    def _(i):
        weight_tile(i, early, i, low_v, gate_v[:, :, columns(i)])

    @pl.loop(unit_tiles, early_tiles)
    def _(i):
        weight_tile(i, early, i, low_v, lift_v[:, :, columns(i - unit_tiles)])

    late_units = 2 * unit_tiles - early_tiles

    @pl.loop(0, late_units)
    def _(i):
        weight_tile(early_tiles + i, late, i, low_v, lift_v[:, :, columns(early_tiles - unit_tiles + i)])

    weight_tile(2 * unit_tiles, late, late_units, att_v, both_v[...])
    for slot in (0, 1):
        for row in range(4):
            tile_copy(slot, row, (late, 0)).wait()

    for i in range(unit_tiles):
        for other in (1, 2, 3):
            down_copy(i, other).wait_recv()
    own_rows = pl.ds(pl.multiple_of(place * quarter, quarter), quarter)
    down_got[0] = (
        down_v[own_rows, :].astype(jnp.float32)
        + down_got[0].astype(jnp.float32)
        + (down_got[1].astype(jnp.float32) + down_got[2].astype(jnp.float32))
    ).astype(jnp.bfloat16)
    down_out = pltpu.make_async_copy(down_got.at[0], down_sum, down_sem)
    down_out.start()

    def out_arrival(which):
        return remote(
            home_v.at[which], home_v.at[which], out_pass.at[which], out_recv.at[which], other_core
        )

    def out_share(which, whose):
        return remote(
            home_v.at[which], out_home.at[which, whose], out_pass.at[which], out_took.at[which], other_core
        )

    def out_here(which):
        return pltpu.make_async_copy(home_v.at[which], out_home.at[which, core], home_sem.at[which])

    for which in (0, 1):

        @pl.when(cot_owner(which) != stage)
        def _():
            out_arrival(which).wait_recv()
            out_share(which, core).start()
            out_here(which).start()

    down_out.wait()
    for copy in halves + on:
        copy.wait_send()
    for i in range(unit_tiles):
        for other in (1, 2, 3):
            down_copy(i, other).wait_send()

    @pl.loop(0, chunks)
    def _(c):
        pair_copy(c).wait_send()
        exchange(c, send_a, recv_a, a_send, a_recv).wait_send()
        exchange(c, send_b, recv_b, b_send, b_recv).wait_send()
        exchange(c, send_c, recv_c, c_send, c_recv).wait_send()
        one_copy(c).wait()
        keep_copy(c).wait()
        away_copy(c, half).wait_send()
        away_copy(c, 1 - half).wait_recv()

        @pl.when(home(c) == stage)
        def _():
            out_local(c).wait()

        @pl.when((home(c) != stage) & (c % 2 == core))
        def _():
            out_copy(c).wait_send()

    for which in (0, 1):

        @pl.when(cot_owner(which) != stage)
        def _():
            out_share(which, core).wait_send()
            out_share(which, 1 - core).wait_recv()
            out_here(which).wait()


def middle(attended, sequence, cotangents, w_out, w_gate, w_down, lift_shards, vectors):
    chunks, rows, width = 4, sequence.shape[1], sequence.shape[2]
    head_width, units = w_out.shape[1], w_down.shape[1]
    tile = head_width
    early, late = 6 * tile, 2 * units + head_width - 6 * tile
    dma, bf16, f32 = pltpu.SemaphoreType.DMA, jnp.bfloat16, jnp.float32

    def vmem(shape, dtype=bf16):
        return pltpu.VMEM(shape, dtype)

    wide = (chunks, rows, width)
    inner = (chunks, rows, units)
    narrow_rows = (chunks, rows, head_width // 2)
    four, two = dma((chunks,)), dma((2,))
    return pl.pallas_call(
        middle_kernel,
        in_specs=[pl.BlockSpec(memory_space=pl.ANY)] * 12 + [pl.BlockSpec(memory_space=pltpu.VMEM)] * 6,
        out_specs=[pl.BlockSpec(memory_space=pl.ANY)] * 9 + [pl.BlockSpec(memory_space=pltpu.VMEM)],
        out_shape=[
            jax.ShapeDtypeStruct((2, 2, rows, width), bf16),
            jax.ShapeDtypeStruct(wide, f32),
            jax.ShapeDtypeStruct((2 * chunks, rows, head_width // 2), bf16),
            *[jax.ShapeDtypeStruct((width // 4, early), bf16)] * 4,
            jax.ShapeDtypeStruct((4, width // 4, late), bf16),
            jax.ShapeDtypeStruct((width // 4, units), bf16),
            jax.ShapeDtypeStruct((8, width), f32),
        ],
        scratch_shapes=[
            vmem(wide), vmem(narrow_rows), vmem(narrow_rows), vmem((chunks, rows, head_width)),
            vmem((2, 2, rows, width)), vmem((width, head_width)), vmem((width, units)), vmem((width, 2 * units)),
            vmem(wide), vmem(wide), vmem(wide), vmem(wide), vmem(wide), vmem(wide),
            vmem(wide, f32), vmem((chunks, rows, 1), f32), vmem(wide),
            vmem(inner), vmem(inner), vmem(inner),
            vmem(wide, f32), vmem(wide), vmem(wide), vmem(wide), vmem(narrow_rows), vmem(narrow_rows),
            vmem((2, width, tile)), vmem((width, units)), vmem((3, width // 4, units)), vmem((2, rows, width)),
            dma((9,)), dma((6,)), dma((6,)), four, four, two, two, two,
            four, four, four, four, four, four, four, two, two, two,
            four, four, four, four, dma((2, 4)), dma((units // tile, 3)), dma((units // tile, 3)), dma, two,
        ],
        compiler_params=pltpu.CompilerParams(
            collective_id=1, has_side_effects=True, vmem_limit_bytes=VMEM_BYTES
        ),
        cost_estimate=pl.CostEstimate(flops=50 << 30, bytes_accessed=32 << 20, transcendentals=0),
        name="middle",
    )(attended, sequence, *cotangents, w_out, w_gate, w_down, *lift_shards, *vectors)


def tail_kernel(
    d_query, d_key, d_value, w_joined, sums_in, sequence, grad_one, early, late, moved_1, moved_2, moved_3,
    down_own, down_in,
    home, shard, joined, down, sums,
    query_v, key_v, value_v, token_v, one_v, part_v, late_v, project_v, own_v, tp_sent, tp_got, pair_sent, pair_got,
    final_v, summed_v, end_got, inner_v, mid_got, total_v, joined_v, quarter_got, both_sent, both_end, both_inner,
    both_mid, both_total, step_v, step_got, home_v, down_v, down_inner, down_got, down_total,
    load_sem, late_send, late_recv, tp_send, tp_recv, pair_send, pair_recv, home_send, home_recv, home_pass,
    home_took, home_local, end_send, end_recv, mid_send, mid_recv, back_send, back_recv, shard_sem,
    quarter_send, quarter_recv, both_send, both_recv, both_local, step_send, step_recv, home_sem, down_sem, down_mid_send, down_mid_recv, down_back_send, down_back_recv,
):
    place, stage, core = lax.axis_index("fsdp"), lax.axis_index("ctx"), lax.axis_index("tp")
    seq, half = stage // 2, stage % 2
    bf16, f32 = jnp.bfloat16, jnp.float32
    pieces = summed_v.shape[0]
    piece = summed_v.shape[2]
    early_pieces = early.shape[1] // piece
    quarter = joined_v.shape[0] // 4
    width = d_query.shape[2]

    barrier = pltpu.get_barrier_semaphore()
    peers = [(place ^ other, stage, core) for other in (1, 2, 3)]
    peers += [(place, lax.rem(stage + shift, 4), core) for shift in (1, 2, 3)]
    peers += [(place, stage, 1 - core)]
    for peer in peers:
        pl.semaphore_signal(barrier, inc=1, device_id=peer, device_id_type=MESH)

    loads = [
        pltpu.make_async_copy(source, target, load_sem.at[index])
        for index, (source, target) in enumerate(
            (
                (early, part_v.at[0]),
                (moved_1, part_v.at[1]),
                (moved_2, part_v.at[2]),
                (moved_3, part_v.at[3]),
                (d_query, query_v),
                (d_key, key_v),
                (d_value, value_v),
                (late.at[0], late_v.at[0]),
                (sequence, token_v),
                (grad_one, one_v),
            )
        )
    ]
    down_loads = [
        pltpu.make_async_copy(source, down_v.at[index], down_sem.at[index])
        for index, source in enumerate((down_own, down_in))
    ]
    for load in down_loads + loads:
        load.start()
    pl.semaphore_wait(barrier, len(peers))

    def remote(source, target, send, recv, device):
        return pltpu.make_async_remote_copy(
            source, target, send, recv, device_id=device, device_id_type=MESH
        )

    other_core = (place, stage, 1 - core)
    partner = (place, stage ^ 1, core)
    at_end = (stage == 0) | (stage == 3)
    inward = (place, stage ^ 1, core)
    outward = (place, stage ^ 1, core)
    across = (place, 3 - stage, core)

    def late_copy(other):
        return remote(
            late.at[other], late_v.at[other], late_send.at[other - 1], late_recv.at[other - 1],
            (place ^ other, stage, core),
        )

    for other in (1, 2, 3):
        late_copy(other).start()

    def columns(j):
        return pl.ds(j * piece, piece)

    def end_copy(j):
        return remote(summed_v.at[j], end_got.at[j], end_send.at[j], end_recv.at[j], inward)

    def mid_copy(j):
        return remote(inner_v.at[j], mid_got.at[j], mid_send.at[j], mid_recv.at[j], across)

    def back_copy(j):
        return remote(total_v.at[j], shard.at[:, columns(j)], back_send.at[j], back_recv.at[j], outward)

    def shard_copy(j):
        return pltpu.make_async_copy(total_v.at[j], shard.at[:, columns(j)], shard_sem.at[j])

    def sum_piece(j, parts, first):
        terms = [parts[index, :, first : first + piece].astype(f32) for index in range(4)]
        summed_v[j] = (terms[0] + terms[1] + (terms[2] + terms[3])).astype(bf16)

        @pl.when(at_end)
        def _():
            end_copy(j).start()

    def from_end(j):
        end_copy(j).wait_recv()
        inner_v[j] = (summed_v[j].astype(f32) + end_got[j].astype(f32)).astype(bf16)
        mid_copy(j).start()

    def from_mid(j):
        mid_copy(j).wait_recv()
        total_v[j] = (inner_v[j].astype(f32) + mid_got[j].astype(f32)).astype(bf16)
        back_copy(j).start()
        shard_copy(j).start()

    down_pieces = down_mid_send.shape[0]
    down_size = down_v.shape[2] // down_pieces

    def down_part(ref, j):
        return ref.at[:, pl.ds(j * down_size, down_size)]

    def down_mid(j):
        return remote(
            down_part(down_inner, j), down_part(down_got, j), down_mid_send.at[j], down_mid_recv.at[j], across
        )

    def down_back(j):
        return remote(
            down_part(down_total, j), down_part(down, j), down_back_send.at[j], down_back_recv.at[j], outward
        )

    def down_here(j):
        return pltpu.make_async_copy(down_part(down_total, j), down_part(down, j), down_sem.at[j])

    def down_from_mid(j):
        down_mid(j).wait_recv()
        part = slice(j * down_size, (j + 1) * down_size)
        down_total[:, part] = (
            down_inner[:, part].astype(f32) + down_got[:, part].astype(f32)
        ).astype(bf16)
        down_back(j).start()
        down_here(j).start()

    for load in down_loads:
        load.wait()

    @pl.when(~at_end)
    def _():
        down_inner[...] = (down_v[0].astype(f32) + down_v[1].astype(f32)).astype(bf16)
        for j in range(down_pieces):
            down_mid(j).start()

    for load in loads[:4]:
        load.wait()
    for j in range(early_pieces):
        sum_piece(j, part_v, j * piece)

    def input_share(chunk):
        rows = jnp.concatenate([query_v[chunk], key_v[chunk], value_v[chunk]], 1)
        project_v[chunk] = rows
        return dot(rows, w_joined[...], ((1,), (1,)))

    def block_of(i):
        left = jnp.where(stage == 0, 3 - i, jnp.where(i == 0, 0, 4 - i))
        right = jnp.where(stage == 3, i, jnp.where(i == 0, 3, i - 1))
        return jnp.where(stage < 2, left, right)

    def tp_copy(i):
        return remote(tp_sent.at[i], tp_got.at[i], tp_send.at[i], tp_recv.at[i], other_core)

    for load in loads[4:7]:
        load.wait()

    @pl.loop(0, 4)
    def _(i):
        block = block_of(i)
        tp_sent[i] = input_share(2 * block + 1 - core).astype(bf16)
        tp_copy(i).start()
        own_v[i] = input_share(2 * block + core)

    def pair_copy(i):
        return remote(pair_sent.at[i], pair_got.at[i], pair_send.at[i], pair_recv.at[i], partner)

    def share_of(i):
        return own_v[i] + tp_got[i].astype(f32)

    def residual(i):
        return one_v[2 * (block_of(i) - 2 * half) + core]

    tp_copy(0).wait_recv()
    pair_sent[0] = share_of(0).astype(bf16)
    pair_copy(0).start()
    loads[9].wait()

    @pl.when(at_end)
    def _():
        for i in (1, 2):
            tp_copy(i).wait_recv()
            part = share_of(i) + residual(i) if i == 2 else share_of(i)
            pair_sent[i] = part.astype(bf16)
            pair_copy(i).start()

    @pl.when(~at_end)
    def _():
        for j in range(early_pieces // 2):
            from_end(j)

    @pl.when(~at_end)
    def _():
        for j in range(down_pieces):
            down_from_mid(j)

    loads[8].wait()
    tokens = token_v[...].reshape(-1, token_v.shape[2])
    project = project_v[...].reshape(-1, project_v.shape[2])
    strip = 256
    for row in range(0, joined_v.shape[0], strip):
        joined_v[row : row + strip, :] = dot(
            tokens[:, row : row + strip], project, ((0,), (0,))
        ).astype(bf16)

    def quarter_copy(other):
        rows = pl.ds(pl.multiple_of((place ^ other) * quarter, quarter), quarter)
        return remote(
            joined_v.at[rows], quarter_got.at[other - 1], quarter_send.at[other - 1], quarter_recv.at[other - 1],
            (place ^ other, stage, core),
        )

    for other in (1, 2, 3):
        quarter_copy(other).start()

    def column_sum(grads):
        return jnp.sum(grads[...].reshape(-1, width).astype(f32), 0, keepdims=True)

    bias_parts = []
    for total in (column_sum(query_v), column_sum(value_v)):
        for which in (0, 1):
            bias_parts.append(jnp.where(half == which, total, 0.0))
    bias = jnp.concatenate(bias_parts, 1)
    step_v[0] = sums_in[...]
    step_v[0, 6:7, :] = bias
    steps = [(place ^ 1, stage, core), (place ^ 2, stage, core), partner, (place, stage ^ 2, core)]

    def step_copy(index):
        return remote(
            step_v.at[index], step_got.at[index], step_send.at[index], step_recv.at[index], steps[index]
        )

    def step_on(index):
        step_copy(index).wait_recv()
        step_v[index + 1] = step_v[index] + step_got[index]
        if index < 3:
            step_copy(index + 1).start()

    step_copy(0).start()

    @pl.when(~at_end)
    def _():
        for j in range(early_pieces // 2, early_pieces):
            from_end(j)
            from_mid(j - early_pieces // 2)

    def home_copy(i):
        return remote(
            final_v.at[i - 1], home_v, home_send.at[i - 1], home_recv, (place, block_of(i), core)
        )

    @pl.when(~at_end)
    def _():
        for i in (1, 2):
            tp_copy(i).wait_recv()
            pair_copy(i - 1).wait_recv()
            final_v[i - 1] = (share_of(i) + pair_got[i - 1].astype(f32) + residual(i)).astype(bf16)
            home_copy(i).start()

    loads[7].wait()
    for other in (1, 2, 3):
        late_copy(other).wait_recv()
    for j in range(early_pieces, pieces):
        sum_piece(j, late_v, (j - early_pieces) * piece)
    step_on(0)

    def both_end_copy():
        return remote(both_sent, both_end, both_send.at[0], both_recv.at[0], inward)

    def both_mid_copy():
        return remote(both_inner, both_mid, both_send.at[1], both_recv.at[1], across)

    def both_back_copy():
        return remote(both_total, joined, both_send.at[2], both_recv.at[2], outward)

    def both_here():
        return pltpu.make_async_copy(both_total, joined, both_local)

    for other in (1, 2, 3):
        quarter_copy(other).wait_recv()
    own_rows = pl.ds(pl.multiple_of(place * quarter, quarter), quarter)
    both_sent[...] = (
        joined_v[own_rows, :].astype(f32)
        + quarter_got[0].astype(f32)
        + (quarter_got[1].astype(f32) + quarter_got[2].astype(f32))
    ).astype(bf16)

    @pl.when(at_end)
    def _():
        both_end_copy().start()

    step_on(1)

    tp_copy(3).wait_recv()

    @pl.when(at_end)
    def _():
        pair_copy(0).wait_recv()
        final_v[2] = (share_of(3) + pair_got[0].astype(f32) + residual(3)).astype(bf16)

    @pl.when(~at_end)
    def _():
        pair_copy(2).wait_recv()
        final_v[2] = (share_of(3) + pair_got[2].astype(f32)).astype(bf16)

    home_direct = remote(final_v.at[2], home.at[seq, core], home_send.at[2], home_took.at[seq], other_core)
    home_here = pltpu.make_async_copy(final_v.at[2], home.at[seq, core], home_local)
    home_direct.start()
    home_here.start()

    @pl.when(~at_end)
    def _():
        for j in range(early_pieces, pieces):
            from_end(j)
            from_mid(j - early_pieces // 2)
        both_end_copy().wait_recv()
        both_inner[half] = both_sent[...]
        both_inner[1 - half] = both_end[...]
        both_mid_copy().start()
        for j in range(pieces - early_pieces // 2, pieces):
            from_mid(j)
        both_mid_copy().wait_recv()
        both_total[...] = (both_inner[...].astype(f32) + both_mid[...].astype(f32)).astype(bf16)
        both_back_copy().start()
        both_here().start()

    step_on(2)
    step_on(3)
    sums[...] = step_v[4]

    def home_share(whose):
        return remote(home_v, home.at[1 - seq, whose], home_pass, home_took.at[1 - seq], other_core)

    home_keep = pltpu.make_async_copy(home_v, home.at[1 - seq, core], home_sem)
    remote(home_v, home_v, home_pass, home_recv, other_core).wait_recv()
    home_share(core).start()
    home_keep.start()

    @pl.when(~at_end)
    def _():
        for j in range(pieces):
            mid_copy(j).wait_send()
            back_copy(j).wait_send()
            shard_copy(j).wait()
        both_mid_copy().wait_send()
        both_back_copy().wait_send()
        both_here().wait()

    @pl.when(~at_end)
    def _():
        for j in range(down_pieces):
            down_mid(j).wait_send()
            down_back(j).wait_send()
            down_here(j).wait()

    @pl.when(at_end)
    def _():
        for j in range(down_pieces):
            down_back(j).wait_recv()
        for j in range(pieces):
            end_copy(j).wait_send()
            back_copy(j).wait_recv()
        both_end_copy().wait_send()
        both_back_copy().wait_recv()

    for i in range(4):
        tp_copy(i).wait_send()
        step_copy(i).wait_send()
    pair_copy(0).wait_send()

    @pl.when(at_end)
    def _():
        for i in (1, 2):
            pair_copy(i).wait_send()

    @pl.when(~at_end)
    def _():
        for i in (1, 2):
            home_copy(i).wait_send()

    home_direct.wait_send()
    home_here.wait()
    home_share(core).wait_send()
    home_keep.wait()
    home_share(1 - core).wait_recv()
    remote(final_v.at[2], home.at[seq, 1 - core], home_send.at[2], home_took.at[seq], other_core).wait_recv()
    for other in (1, 2, 3):
        quarter_copy(other).wait_send()
        late_copy(other).wait_send()


def tail(d_query, d_key, d_value, w_joined, sums, sequence, grad_one, early, late, moved, downs):
    rows, width = sequence.shape[1:]
    quarter = early.shape[0]
    joined = w_joined.shape[1]
    piece = 3 * LANES
    columns = early.shape[1] + late.shape[2]
    pieces = columns // piece
    dma, bf16, f32 = pltpu.SemaphoreType.DMA, jnp.bfloat16, jnp.float32

    def vmem(shape, dtype=bf16):
        return pltpu.VMEM(shape, dtype)

    any_spec, vmem_spec = pl.BlockSpec(memory_space=pl.ANY), pl.BlockSpec(memory_space=pltpu.VMEM)
    cut = (pieces, quarter, piece)
    both = (2, quarter, joined)
    one, two, three, four, many = dma, dma((2,)), dma((3,)), dma((4,)), dma((pieces,))
    return pl.pallas_call(
        tail_kernel,
        in_specs=[any_spec] * 3 + [vmem_spec] * 2 + [any_spec] * 9,
        out_specs=[any_spec] * 4 + [vmem_spec],
        out_shape=[
            jax.ShapeDtypeStruct((2, 2, rows, width), bf16),
            jax.ShapeDtypeStruct((quarter, columns), bf16),
            jax.ShapeDtypeStruct(both, bf16),
            jax.ShapeDtypeStruct(downs[0].shape, bf16),
            jax.ShapeDtypeStruct(sums.shape, f32),
        ],
        scratch_shapes=[
            vmem(d_query.shape), vmem(d_query.shape), vmem(d_query.shape),
            vmem(sequence.shape), vmem(grad_one.shape, f32), vmem((4,) + early.shape), vmem(late.shape),
            vmem((8, rows, joined)), vmem((4, rows, width), f32),
            vmem((4, rows, width)), vmem((4, rows, width)), vmem((3, rows, width)), vmem((3, rows, width)),
            vmem((3, rows, width)),
            vmem(cut), vmem(cut), vmem(cut), vmem(cut), vmem(cut),
            vmem((width, joined)), vmem((3, quarter, joined)), vmem((quarter, joined)), vmem((quarter, joined)),
            vmem(both), vmem(both), vmem(both),
            vmem((5,) + sums.shape, f32), vmem((4,) + sums.shape, f32), vmem((rows, width)),
            vmem((2,) + downs[0].shape), vmem(downs[0].shape), vmem(downs[0].shape), vmem(downs[0].shape),
            dma((10,)), three, three, four, four, three, three, three, one, one, two, one,
            many, many, many, many, many, many, many,
            three, three, three, three, one, four, four, one, two, two, two, two, two,
        ],
        compiler_params=pltpu.CompilerParams(
            collective_id=2, has_side_effects=True, vmem_limit_bytes=VMEM_BYTES
        ),
        cost_estimate=pl.CostEstimate(flops=80 << 30, bytes_accessed=32 << 20, transcendentals=0),
        name="tail",
    )(d_query, d_key, d_value, w_joined, sums, sequence, grad_one, early, late, *moved, *downs)


def pick(pair, index):
    return lax.dynamic_index_in_dim(pair, index, 0, keepdims=False)


def finish_kernel(
    tokens_ref, shard_ref, joined_ref, down_ref, sums_ref,
    d_tokens, d_query, d_key, d_value, d_out, d_up, d_down, *vectors,
):
    f32 = jnp.float32
    for index in range(6):
        vectors[index][...] = sums_ref[index]
    biases = sums_ref[6]
    vectors[6][...] = biases[: biases.shape[0] // 2]
    vectors[7][...] = biases[biases.shape[0] // 2 :]
    d_tokens[...] = tokens_ref[...].astype(f32)
    units = d_up.shape[2]
    d_up[:, 0, :] = shard_ref[:, :units].astype(f32)
    d_up[:, 1, :] = shard_ref[:, units : 2 * units].astype(f32)
    d_out[...] = shard_ref[:, 2 * units :].astype(f32)
    d_down[...] = down_ref[...].astype(f32)
    width = d_query.shape[1] // 2
    for index, target in enumerate((d_query, d_key, d_value)):
        columns = slice(index * width, (index + 1) * width)
        target[...] = jnp.concatenate(
            [joined_ref[0, :, columns], joined_ref[1, :, columns]], 1
        ).astype(f32)


def finish(tokens, shard, joined, down, sums):
    steps = 4
    quarter, units = down.shape
    head_width = shard.shape[1] - 2 * units
    row, some = tokens.shape[0] // steps, quarter // steps
    sizes = [sums.shape[1]] * 6 + [head_width] * 2
    f32 = jnp.float32

    def rows(width):
        return pl.BlockSpec((some, width), lambda i: (i, 0))

    return pl.pallas_call(
        finish_kernel,
        grid=(steps,),
        in_specs=[
            pl.BlockSpec((row, tokens.shape[1]), lambda i: (i, 0)),
            rows(shard.shape[1]),
            pl.BlockSpec((2, some, joined.shape[2]), lambda i: (0, i, 0)),
            rows(units),
            pl.BlockSpec(sums.shape, lambda i: (0, 0)),
        ],
        out_specs=[
            pl.BlockSpec((row, tokens.shape[1]), lambda i: (i, 0)),
            rows(head_width), rows(head_width), rows(head_width), rows(head_width),
            pl.BlockSpec((some, 2, units), lambda i: (i, 0, 0)),
            rows(units),
            *[pl.BlockSpec((size,), lambda i: (0,)) for size in sizes],
        ],
        out_shape=[
            jax.ShapeDtypeStruct(tokens.shape, f32),
            *[jax.ShapeDtypeStruct((quarter, head_width), f32)] * 4,
            jax.ShapeDtypeStruct((quarter, 2, units), f32),
            jax.ShapeDtypeStruct((quarter, units), f32),
            *[jax.ShapeDtypeStruct((size,), f32) for size in sizes],
        ],
        compiler_params=pltpu.CompilerParams(vmem_limit_bytes=VMEM_BYTES),
        name="finish",
    )(tokens, shard, joined, down, sums)


def per_device_paired(
    tokens,
    doc_lengths,
    keep,
    w_query,
    b_query,
    w_key,
    w_value,
    b_value,
    w_out,
    b_out,
    gain_one,
    shift_one,
    w_up,
    w_down,
    b_down,
    gain_two,
    shift_two,
    cotangent,
):
    _, block_rows, model_width = tokens.shape
    length = 4 * block_rows
    half_rows = block_rows // 2
    local_heads = b_query.shape[0] // HEAD
    heads = local_heads // 2
    width = heads * HEAD
    cotangent = cotangent.reshape(2, 2, half_rows, model_width)
    half = lax.axis_index("ctx") % 2
    core = lax.axis_index("tp")
    slopes = head_slopes(core * local_heads + half * heads, heads)
    (
        sequence, full_joined, full_out, full_gate, up_lift, cot_far, cot_near, query_t, queries, keys, keys_t, values, values_t,
    ) = start(
        doc_lengths, slopes, tokens, keep, w_query, w_key, w_value, w_out, w_up, b_query, b_value,
        cotangent,
    )
    full_joined = full_joined.reshape(model_width, 3 * width)
    full_out = full_out.reshape(model_width, 2 * width)
    full_gate = full_gate.reshape(model_width, -1)
    lift_shards = [up_lift] + [
        lax.ppermute(up_lift, "fsdp", swap) for swap in (X_SWAP, Y_SWAP, D_SWAP)
    ]
    cotangents = (
        cotangent,
        lax.ppermute(cot_far, "ctx", [(3, 1), (0, 2), (1, 0), (2, 3)]),
        lax.ppermute(cot_near, "ctx", [(1, 2), (2, 1)]),
    )
    attended_all, attended_t, lse = attend(doc_lengths, slopes, query_t, keys, values_t)

    vectors = (b_out, gain_one, shift_one, b_down, gain_two, shift_two)
    out, grad_one, grad_heads, *early, late, down_sum, sums = middle(
        attended_all.reshape(8, half_rows, width),
        sequence.reshape(8, half_rows, model_width),
        cotangents,
        full_out,
        full_gate,
        w_down,
        lift_shards,
        vectors,
    )
    out = out.reshape(2, block_rows, model_width)
    grad_heads = grad_heads.reshape(length, width)
    moved = [
        lax.ppermute(early[other], "fsdp", swap)
        for other, swap in ((1, X_SWAP), (2, Y_SWAP), (3, D_SWAP))
    ]
    downs = (down_sum, lax.ppermute(down_sum, "ctx", [(0, 1), (3, 2)]))
    d_query, d_key, d_value = attend_back(
        doc_lengths, slopes, query_t, queries, keys, keys_t, values, grad_heads, attended_t, lse
    )
    d_tokens, shard, joined, down, sums = tail(
        d_query.reshape(8, half_rows, width),
        d_key.reshape(8, half_rows, width),
        d_value.reshape(8, half_rows, width),
        full_joined,
        sums,
        sequence.reshape(8, half_rows, model_width),
        grad_one,
        early[0],
        late,
        moved,
        downs,
    )
    (
        d_tokens, d_w_query, d_w_key, d_w_value, sum_out, sum_up, sum_down,
        total_gain_two, total_shift_two, total_b_down, total_gain_one, total_shift_one, total_b_out,
        total_b_query, total_b_value,
    ) = finish(
        d_tokens.reshape(2 * block_rows, model_width), shard, joined, down, sums
    )
    d_tokens = d_tokens.reshape(2, block_rows, model_width)
    return (
        out,
        d_tokens,
        d_w_query,
        total_b_query,
        d_w_key,
        d_w_value,
        total_b_value,
        sum_out,
        total_b_out,
        total_gain_one,
        total_shift_one,
        sum_up,
        sum_down,
        total_b_down,
        total_gain_two,
        total_shift_two,
    )


def paired(mesh, tokens, doc_lengths, b_query):
    sizes = dict(mesh.shape)
    return (
        sizes == {"fsdp": 4, "ctx": 4, "tp": 2}
        and tokens.shape[0] == 8
        and tokens.shape[1] % (8 * TILE) == 0
        and doc_lengths.shape[1] <= KEEP_ROW - DOC_ROW
        and b_query.shape[0] % (4 * HEAD) == 0
    )


def solution(mesh):
    in_specs = (
        P("fsdp", "ctx", None),
        P("fsdp", None),
        P("fsdp", "ctx"),
        P("fsdp", "tp"),
        P("tp"),
        P("fsdp", "tp"),
        P("fsdp", "tp"),
        P("tp"),
        P("fsdp", "tp"),
        P(),
        P(),
        P(),
        P("fsdp", None, "tp"),
        P("fsdp", "tp"),
        P(),
        P(),
        P(),
        P("fsdp", "ctx", None),
    )
    out_specs = (
        P("fsdp", "ctx", None),
        P("fsdp", "ctx", None),
        P("fsdp", "tp"),
        P("tp"),
        P("fsdp", "tp"),
        P("fsdp", "tp"),
        P("tp"),
        P("fsdp", "tp"),
        P(),
        P(),
        P(),
        P("fsdp", None, "tp"),
        P("fsdp", "tp"),
        P(),
        P(),
        P(),
    )

    def whole(*args):
        body = per_device_paired if paired(mesh, args[0], args[1], args[4]) else per_device_general
        return jax.shard_map(
            body, mesh=mesh, in_specs=in_specs, out_specs=out_specs, check_vma=False
        )(*args)

    return whole
```

```python
import functools

import jax
import jax.numpy as jnp
from jax import lax
from jax.experimental import pallas as pl
from jax.experimental.pallas import tpu as pltpu
from jax.sharding import PartitionSpec as P

HEAD = 64


NORM_EPS = 1e-12
MASKED = -1e30


def layer_norm(residual, norm_gain, norm_shift):
    centered = residual - jnp.mean(residual, -1, keepdims=True)
    inv_scale = lax.rsqrt(jnp.mean(centered * centered, -1, keepdims=True) + NORM_EPS)
    normed = centered * inv_scale
    return (normed * norm_gain + norm_shift, normed, inv_scale)


def norm_back(grad_out, normed, inv_scale, norm_gain):
    grad_norm = grad_out * norm_gain
    mean_grad = jnp.mean(grad_norm, -1, keepdims=True)
    mean_cross = jnp.mean(grad_norm * normed, -1, keepdims=True)
    grad_in = (grad_norm - mean_grad - normed * mean_cross) * inv_scale
    return (grad_in, jnp.sum(grad_out * normed, 0), jnp.sum(grad_out, 0))


def head_slopes(first_head, head_count):
    head_index = first_head + jnp.arange(head_count, dtype=jnp.int32)
    head_float = head_index.astype(jnp.float32)
    return jnp.where(head_index < 8, jnp.exp2(-(head_float + 1.0)), jnp.exp2(-(head_float - 7.5)))


def segment_ids(lengths, positions):
    bounds = jnp.cumsum(lengths, -1)
    return jnp.sum((bounds[:, None, :] <= positions[None, :, None]).astype(jnp.int32), -1)


def score_block(query_heads, query_pos, query_seg, key_heads, key_pos, key_seg, key_keep, slopes):
    scores = (
        jnp.einsum("sqhd,skhd->shqk", query_heads, key_heads, preferred_element_type=jnp.float32)
        * 0.125
    )
    distance = jnp.abs(query_pos[:, None] - key_pos[None, :]).astype(jnp.float32)
    scores = scores - slopes[None, :, None, None] * distance[None, None]
    same_doc = query_seg[:, None, :, None] == key_seg[:, None, None, :]
    visible = (key_keep[:, None, None, :] == 1) | (query_pos[:, None] == key_pos[None, :])[
        None, None
    ]
    return (scores, same_doc & visible)


def grad_block(
    query_heads,
    query_pos,
    query_seg,
    grad_heads,
    log_total,
    delta,
    key_heads,
    value_heads,
    key_pos,
    key_seg,
    key_keep,
    slopes,
):
    scores, allowed = score_block(
        query_heads, query_pos, query_seg, key_heads, key_pos, key_seg, key_keep, slopes
    )
    probs = jnp.where(allowed, jnp.exp(scores - log_total[..., None]), 0.0)
    grad_probs = jnp.einsum(
        "sqhd,skhd->shqk", grad_heads, value_heads, preferred_element_type=jnp.float32
    )
    grad_scores = (probs * (grad_probs - delta[..., None])).astype(jnp.bfloat16)
    grad_query = (
        jnp.einsum("shqk,skhd->sqhd", grad_scores, key_heads, preferred_element_type=jnp.float32)
        * 0.125
    )
    grad_key = (
        jnp.einsum("shqk,sqhd->skhd", grad_scores, query_heads, preferred_element_type=jnp.float32)
        * 0.125
    )
    grad_value = jnp.einsum(
        "shqk,sqhd->skhd",
        probs.astype(jnp.bfloat16),
        grad_heads,
        preferred_element_type=jnp.float32,
    )
    return (grad_query, grad_key, grad_value)


def intersections(query_seg, key_seg):
    return jnp.any((key_seg[:, 0] <= query_seg[:, -1]) & (key_seg[:, -1] >= query_seg[:, 0]))


def guarded(active, update, current):
    return lax.cond(active, update, lambda untouched: untouched, current)


def over_blocks(length, advance, current):
    block_len = 512
    block_count = length // block_len
    return lax.fori_loop(
        0,
        block_count,
        lambda block_index, running: advance(running, block_index * block_len, block_len),
        current,
    )


def per_device_general(
    tokens,
    doc_lengths,
    keep,
    w_query,
    b_query,
    w_key,
    w_value,
    b_value,
    w_out,
    b_out,
    gain_one,
    shift_one,
    w_up,
    w_down,
    b_down,
    gain_two,
    shift_two,
    cotangent,
):
    seq_count, block_rows, model_width = tokens.shape
    local_heads = b_query.shape[0] // HEAD
    head_width = local_heads * HEAD
    row_count = seq_count * block_rows
    slopes = head_slopes(lax.axis_index("tp") * local_heads, local_heads)
    own_pos = lax.axis_index("ctx") * block_rows + jnp.arange(block_rows, dtype=jnp.int32)
    own_seg = segment_ids(doc_lengths, own_pos)
    token_rows = tokens.reshape(row_count, model_width)
    full_query, full_key, full_value, full_out = (
        lax.all_gather(w_query, "fsdp", axis=0, tiled=True),
        lax.all_gather(w_key, "fsdp", axis=0, tiled=True),
        lax.all_gather(w_value, "fsdp", axis=0, tiled=True),
        lax.all_gather(w_out, "fsdp", axis=0, tiled=True),
    )
    queries = (
        jnp.dot(token_rows, full_query, preferred_element_type=jnp.float32) + b_query
    ).astype(jnp.bfloat16)
    key_rows = jnp.dot(token_rows, full_key, preferred_element_type=jnp.float32).astype(
        jnp.bfloat16
    )
    values = (jnp.dot(token_rows, full_value, preferred_element_type=jnp.float32) + b_value).astype(
        jnp.bfloat16
    )
    query_heads = queries.reshape(seq_count, block_rows, local_heads, HEAD)
    key_value = jnp.concatenate([key_rows, values], -1).reshape(
        seq_count, block_rows, 2 * head_width
    )

    def split_pairs(slab_pairs, block_len):
        return (
            slab_pairs[..., :head_width].reshape(seq_count, block_len, local_heads, HEAD),
            slab_pairs[..., head_width:].reshape(seq_count, block_len, local_heads, HEAD),
        )

    def key_slab(pairs, piece_keep, offset, block_len):
        slab_pairs = lax.dynamic_slice_in_dim(pairs, offset, block_len, 1)
        slab_keep = lax.dynamic_slice_in_dim(piece_keep, offset, block_len, 1)
        key_pos = offset + jnp.arange(block_len, dtype=jnp.int32)
        key_seg = segment_ids(doc_lengths, key_pos)
        slab_keys, slab_values = split_pairs(slab_pairs, block_len)
        return (slab_keys, slab_values, slab_keep, key_pos, key_seg)

    start_state = (
        jnp.full((seq_count, local_heads, block_rows), MASKED, jnp.float32),
        jnp.zeros((seq_count, local_heads, block_rows), jnp.float32),
        jnp.zeros((seq_count, local_heads, block_rows, HEAD), jnp.float32),
    )
    pairs = lax.all_gather(key_value, "ctx", axis=1, tiled=True)
    piece_keep = lax.all_gather(keep, "ctx", axis=1, tiled=True)

    def advance(partial_value, offset, block_len):
        slab_keys, slab_values, slab_keep, key_pos, key_seg = key_slab(
            pairs, piece_keep, offset, block_len
        )

        def update(current):
            row_max, row_sum, weighted = current
            scores, allowed = score_block(
                query_heads, own_pos, own_seg, slab_keys, key_pos, key_seg, slab_keep, slopes
            )
            scores = jnp.where(allowed, scores, MASKED)
            new_max = jnp.maximum(row_max, jnp.max(scores, -1))
            factor = jnp.exp(row_max - new_max)
            weights = jnp.where(allowed, jnp.exp(scores - new_max[..., None]), 0.0)
            row_sum = row_sum * factor + jnp.sum(weights, -1)
            weighted = weighted * factor[..., None] + jnp.einsum(
                "shqk,skhd->shqd",
                weights.astype(jnp.bfloat16),
                slab_values,
                preferred_element_type=jnp.float32,
            )
            return (new_max, row_sum, weighted)

        return guarded(intersections(own_seg, key_seg), update, partial_value)

    row_max, row_sum, weighted = over_blocks(pairs.shape[1], advance, start_state)
    attended = (
        (weighted / row_sum[..., None])
        .transpose(0, 2, 1, 3)
        .reshape(row_count, head_width)
        .astype(jnp.bfloat16)
    )
    log_total = row_max + jnp.log(row_sum)
    att_part = jnp.einsum("rh,dh->rd", attended, full_out, preferred_element_type=jnp.float32)
    branch_att = lax.psum(att_part.astype(jnp.bfloat16), "tp").astype(jnp.float32) + b_out
    first_out, normed_one, inv_one = layer_norm(
        token_rows.astype(jnp.float32) + branch_att, gain_one, shift_one
    )
    first_low = first_out.astype(jnp.bfloat16)
    full_up, full_down = (
        lax.all_gather(w_up, "fsdp", axis=0, tiled=True),
        lax.all_gather(w_down, "fsdp", axis=0, tiled=True),
    )
    gate_up = jnp.einsum("rd,dcf->rcf", first_low, full_up, preferred_element_type=jnp.float32)
    product, gelu_back = jax.vjp(
        lambda gate_part, up_part: jax.nn.gelu(gate_part, approximate=False) * up_part,
        gate_up[:, 0],
        gate_up[:, 1],
    )
    hidden = product.astype(jnp.bfloat16)
    ffn_part = jnp.einsum("rf,df->rd", hidden, full_down, preferred_element_type=jnp.float32)
    branch_ffn = lax.psum(ffn_part.astype(jnp.bfloat16), "tp").astype(jnp.float32) + b_down
    result, normed_two, inv_two = layer_norm(first_out + branch_ffn, gain_two, shift_two)
    grad_in = cotangent.reshape(row_count, model_width).astype(jnp.float32)
    grad_two, d_gain_two, d_shift_two = norm_back(grad_in, normed_two, inv_two, gain_two)
    grad_ffn = grad_two.astype(jnp.bfloat16)
    d_b_down = jnp.sum(grad_ffn.astype(jnp.float32), 0)
    d_w_down = jnp.einsum("rd,rf->df", grad_ffn, hidden, preferred_element_type=jnp.float32)
    grad_hidden = jnp.einsum("rd,df->rf", grad_ffn, full_down, preferred_element_type=jnp.float32)
    grad_gate, grad_up = gelu_back(grad_hidden)
    grad_gate_up = jnp.stack([grad_gate, grad_up], 1).astype(jnp.bfloat16)
    d_w_up = jnp.einsum("rd,rcf->dcf", first_low, grad_gate_up, preferred_element_type=jnp.float32)
    first_part = jnp.einsum(
        "rcf,dcf->rd", grad_gate_up, full_up, preferred_element_type=jnp.float32
    )
    grad_first = grad_two + lax.psum(first_part.astype(jnp.bfloat16), "tp").astype(jnp.float32)
    grad_one, d_gain_one, d_shift_one = norm_back(grad_first, normed_one, inv_one, gain_one)
    grad_att = grad_one.astype(jnp.bfloat16)
    d_b_out = jnp.sum(grad_att.astype(jnp.float32), 0)
    d_w_out = jnp.einsum("rd,rh->dh", grad_att, attended, preferred_element_type=jnp.float32)
    grad_attended = jnp.einsum(
        "rd,dh->rh", grad_att, full_out, preferred_element_type=jnp.float32
    ).astype(jnp.bfloat16)
    grad_heads = grad_attended.reshape(seq_count, block_rows, local_heads, HEAD)
    delta = jnp.einsum(
        "sqhd,sqhd->shq",
        grad_heads,
        attended.reshape(seq_count, block_rows, local_heads, HEAD),
        preferred_element_type=jnp.float32,
    )
    query_zero = jnp.zeros((seq_count, block_rows, local_heads, HEAD), jnp.float32)
    full_len = block_rows * lax.axis_size("ctx")
    term_zero = jnp.zeros((seq_count, full_len, 2 * head_width), jnp.float32)
    return_pairs = lax.all_gather(key_value, "ctx", axis=1, tiled=True)
    return_piece_keep = lax.all_gather(keep, "ctx", axis=1, tiled=True)

    def advance(partial_value, offset, block_len):
        slab_keys, slab_values, slab_keep, key_pos, key_seg = key_slab(
            return_pairs, return_piece_keep, offset, block_len
        )

        def update(current):
            query_grad, key_terms = current
            part_query, part_key, part_value = grad_block(
                query_heads,
                own_pos,
                own_seg,
                grad_heads,
                log_total,
                delta,
                slab_keys,
                slab_values,
                key_pos,
                key_seg,
                slab_keep,
                slopes,
            )
            slab_grads = jnp.concatenate(
                [
                    part_key.reshape(seq_count, block_len, head_width),
                    part_value.reshape(seq_count, block_len, head_width),
                ],
                -1,
            )
            return (
                query_grad + part_query,
                lax.dynamic_update_slice_in_dim(key_terms, slab_grads, offset, 1),
            )

        return guarded(intersections(own_seg, key_seg), update, partial_value)

    query_grad, key_terms = over_blocks(return_pairs.shape[1], advance, (query_zero, term_zero))
    pair_grads = lax.psum_scatter(
        key_terms.astype(jnp.bfloat16), "ctx", scatter_dimension=1, tiled=True
    ).astype(jnp.float32)
    query_low = query_grad.reshape(row_count, head_width).astype(jnp.bfloat16)
    pair_low = pair_grads.reshape(row_count, 2 * head_width).astype(jnp.bfloat16)
    grad_project = jnp.concatenate([query_low, pair_low], -1)
    joined_weights = jnp.concatenate([full_query, full_key, full_value], -1)
    joined_grads = jnp.einsum(
        "rd,rh->dh", token_rows, grad_project, preferred_element_type=jnp.float32
    )
    input_part = jnp.einsum(
        "rh,dh->rd", grad_project, joined_weights, preferred_element_type=jnp.float32
    )
    d_tokens = grad_one + lax.psum(input_part.astype(jnp.bfloat16), "tp").astype(jnp.float32)
    d_b_query = jnp.sum(query_low.astype(jnp.float32), 0)
    d_b_value = jnp.sum(pair_low[:, head_width:].astype(jnp.float32), 0)
    d_w_query = joined_grads[:, :head_width]
    d_w_key = joined_grads[:, head_width : 2 * head_width]
    d_w_value = joined_grads[:, 2 * head_width :]
    shard_grads = (
        lax.psum_scatter(
            d_w_query.astype(jnp.bfloat16), "fsdp", scatter_dimension=0, tiled=True
        ).astype(jnp.float32),
        lax.psum_scatter(
            d_w_key.astype(jnp.bfloat16), "fsdp", scatter_dimension=0, tiled=True
        ).astype(jnp.float32),
        lax.psum_scatter(
            d_w_value.astype(jnp.bfloat16), "fsdp", scatter_dimension=0, tiled=True
        ).astype(jnp.float32),
        lax.psum_scatter(
            d_w_out.astype(jnp.bfloat16), "fsdp", scatter_dimension=0, tiled=True
        ).astype(jnp.float32),
        lax.psum_scatter(
            d_w_up.astype(jnp.bfloat16), "fsdp", scatter_dimension=0, tiled=True
        ).astype(jnp.float32),
        lax.psum_scatter(
            d_w_down.astype(jnp.bfloat16), "fsdp", scatter_dimension=0, tiled=True
        ).astype(jnp.float32),
    )
    sum_query, sum_key, sum_value, sum_out, sum_up, sum_down = (
        lax.psum(shard_grads[0].astype(jnp.bfloat16), "ctx").astype(jnp.float32),
        lax.psum(shard_grads[1].astype(jnp.bfloat16), "ctx").astype(jnp.float32),
        lax.psum(shard_grads[2].astype(jnp.bfloat16), "ctx").astype(jnp.float32),
        lax.psum(shard_grads[3].astype(jnp.bfloat16), "ctx").astype(jnp.float32),
        lax.psum(shard_grads[4].astype(jnp.bfloat16), "ctx").astype(jnp.float32),
        lax.psum(shard_grads[5].astype(jnp.bfloat16), "ctx").astype(jnp.float32),
    )
    (
        total_b_query,
        total_b_value,
        total_b_out,
        total_b_down,
        total_gain_one,
        total_shift_one,
        total_gain_two,
        total_shift_two,
    ) = lax.psum(
        (d_b_query, d_b_value, d_b_out, d_b_down, d_gain_one, d_shift_one, d_gain_two, d_shift_two),
        ("fsdp", "ctx"),
    )
    return (
        result.reshape(seq_count, block_rows, model_width).astype(jnp.bfloat16),
        d_tokens.reshape(seq_count, block_rows, model_width),
        sum_query,
        total_b_query,
        sum_key,
        sum_value,
        total_b_value,
        sum_out,
        total_b_out,
        total_gain_one,
        total_shift_one,
        sum_up,
        sum_down,
        total_b_down,
        total_gain_two,
        total_shift_two,
    )


LANES = 128
VMEM_BYTES = 60 << 20
MESH = pl.DeviceIdType.MESH
TILE = 256
DOC_ROW, KEEP_ROW, POS_ROW, LINE_ROW, LOG_ROW, FEAT_END = 64, 72, 73, 79, 82, 85
X_SWAP = [(0, 1), (1, 0), (2, 3), (3, 2)]
Y_SWAP = [(0, 2), (2, 0), (1, 3), (3, 1)]
D_SWAP = [(0, 3), (3, 0), (1, 2), (2, 1)]


def dot(left, right, dims=((1,), (0,))):
    return lax.dot_general(left, right, (dims, ((), ())), preferred_element_type=jnp.float32)


def three_terms(value, low):
    high = low(value)
    middle = low(value - high)
    return high, middle, low(value - high - middle)


def side_signs(rows):
    sub = lax.broadcasted_iota(jnp.int32, (LANES, rows), 0)
    bias_rows = (sub >= POS_ROW) & (sub < LOG_ROW)
    after = jnp.where(bias_rows, -1.0, 1.0).astype(jnp.bfloat16)
    same = jnp.where(bias_rows, 0.0, 1.0).astype(jnp.bfloat16)
    bare = jnp.where(bias_rows | (sub == KEEP_ROW), 0.0, 1.0).astype(jnp.bfloat16)
    return after, same, bare


def diagonal_scores(keys, queries_t, same, bare, slopes):
    rows = lax.broadcasted_iota(jnp.int32, (TILE, TILE), 0)
    cols = lax.broadcasted_iota(jnp.int32, (TILE, TILE), 1)
    apart = jnp.abs(rows - cols).astype(jnp.float32)
    own = rows == cols
    full = [dot(key, query_t * same) for key, query_t in zip(keys, queries_t)]
    alone = [dot(key, query_t * bare) for key, query_t in zip(keys, queries_t)]
    return [
        jnp.where(own, single, scores - slope * apart)
        for scores, single, slope in zip(full, alone, slopes)
    ]


def sweep(first, last, step, most=2):
    many = (last - first) // most

    @pl.loop(0, many)
    def _(i):
        step(first + i * most, most)

    @pl.loop(first + many * most, last)
    def _(tile):
        step(tile, 1)


def doc_bounds(docs_ref, seq):
    bounds, total = [], 0
    for index in range(docs_ref.shape[1]):
        total = total + docs_ref[seq, index]
        bounds.append(total)
    return bounds


def tile_span(docs_ref, seq, block):
    first, last = block * TILE, block * TILE + TILE - 1
    begin = end = start = 0
    for bound in doc_bounds(docs_ref, seq):
        begin = jnp.where(bound <= first, bound, begin)
        end = jnp.where(start <= last, bound, end)
        start = bound
    return lax.div(begin, TILE), lax.div(end + TILE - 1, TILE)


def start_kernel(
    docs, slopes, tokens, keep, w_query, w_key, w_value, w_out, w_up, b_query, b_value, cotangent,
    sequence, full_joined, full_out, full_gate, up_lift, cot_far, cot_near, query_t, queries, keys, keys_t, values, values_t,
    tokens_v, own_v, joined_v, keep_v, gate_v, lift_v, qt_v, q_v, k_v, kt_v, v_v, vt_v,
    z_send, z_recv, tp_send, tp_recv, w_send, w_recv, gate_send, gate_recv, keep_send, keep_recv, local_sem,
    block_sem, joined_sem, lift_sem, gate_sem, cot_sem, out_sem,
):
    place, stage, core = lax.axis_index("fsdp"), lax.axis_index("ctx"), lax.axis_index("tp")
    seq, half = stage // 2, stage % 2
    half_rows, model_width = sequence.shape[2:]
    rows_of = 2 * half_rows
    heads = qt_v.shape[1]
    width = heads * HEAD
    f32, bf16 = jnp.float32, jnp.bfloat16
    barrier = pltpu.get_barrier_semaphore()
    peers = [(place ^ other, stage, core) for other in (1, 2, 3)]
    peers += [(place, lax.rem(stage + shift, 4), core) for shift in (1, 2, 3)]
    peers += [(place, stage, 1 - core)]
    for peer in peers:
        pl.semaphore_signal(barrier, inc=1, device_id=peer, device_id_type=MESH)

    def columns_of(weight):
        return jnp.where(half == 0, weight[:, :width], weight[:, width:])

    own_v[...] = jnp.concatenate([columns_of(w[...]) for w in (w_query, w_key, w_value)], 1)
    joined_v[place] = own_v[...]
    tokens_v[stage] = tokens[seq].reshape(2, half_rows, model_width)
    keep_v[stage] = keep[...]
    pl.semaphore_wait(barrier, len(peers))

    def remote(source, target, send, recv, device):
        return pltpu.make_async_remote_copy(
            source, target, send, recv, device_id=device, device_id_type=MESH
        )

    rows = pl.ds(pl.multiple_of(core * half_rows, half_rows), half_rows)
    ours, theirs = tokens.at[seq, rows], tokens.at[1 - seq, rows]
    other_core = (place, stage, 1 - core)
    inner = (stage == 1) | (stage == 2)
    facing, opposite = 3 - stage, stage ^ 2
    third, fourth = jnp.where(inner, facing, opposite), jnp.where(inner, opposite, facing)

    def send(source, block, target, slot):
        return remote(source, tokens_v.at[block, core], z_send.at[slot], z_recv.at[block], (place, target, core))

    def arrival(block):
        return remote(ours, tokens_v.at[block, core], z_send.at[0], z_recv.at[block], other_core)

    def share(block, whose):
        half_block = tokens_v.at[block, whose]
        return remote(half_block, half_block, tp_send.at[block], tp_recv.at[block], other_core)

    to_pair = send(ours, stage, stage ^ 1, 0)
    to_across = send(theirs, stage, third, 1)
    to_pair.start()

    @pl.when(inner)
    def _():
        to_across.start()

    weights = [
        remote(
            own_v, joined_v.at[place], w_send.at[other - 1], w_recv.at[other - 1], (place ^ other, stage, core)
        )
        for other in (1, 2, 3)
    ]
    flags = [
        remote(
            keep, keep_v.at[stage], keep_send.at[shift - 1], keep_recv.at[shift - 1],
            (place, lax.rem(stage + shift, 4), core),
        )
        for shift in (1, 2, 3)
    ]
    outs = [
        remote(
            w_out, full_out.at[place], w_send.at[other + 2], w_recv.at[other + 2], (place ^ other, stage, core)
        )
        for other in (1, 2, 3)
    ]

    units = w_up.shape[2] // 2

    def gate_copy(owner, other, which, sem):
        block = gate_v.at[owner, :, pl.ds(which * units, units)]
        return remote(block, block, gate_send.at[sem], gate_recv.at[sem], (place ^ other, stage, core))

    halves = [
        gate_copy(place, other, which, 2 * which + other - 1)
        for other, which in ((1, 0), (2, 1), (1, 1), (2, 0))
    ]
    on = [gate_copy(place ^ 1, 2, 0, 4), gate_copy(place ^ 2, 1, 1, 5)]
    for copy in weights + flags + outs:
        copy.start()
    gate_v[place] = w_up[:, 0, :]
    for copy in halves:
        copy.start()
    lift_v[...] = w_up[:, 1, :]
    lift_out = pltpu.make_async_copy(lift_v, up_lift, lift_sem)
    lift_out.start()
    own_out = pltpu.make_async_copy(w_out, full_out.at[place], local_sem)
    own_out.start()
    odd = stage % 2
    cot_outs = [
        pltpu.make_async_copy(cotangent.at[1 - odd, core], cot_far, cot_sem.at[0]),
        pltpu.make_async_copy(cotangent.at[odd, core], cot_near, cot_sem.at[1]),
    ]
    for copy in cot_outs:
        copy.start()

    bounds = doc_bounds(docs, seq)

    def out_copies(slot, block):
        at = pl.ds(pl.multiple_of(block * rows_of, rows_of), rows_of)
        pairs = (
            (qt_v.at[slot], query_t.at[:, :, at]),
            (q_v.at[slot], queries.at[:, at, :]),
            (k_v.at[slot], keys.at[:, at, :]),
            (kt_v.at[slot], keys_t.at[:, :, at]),
            (v_v.at[slot], values.at[:, at, :]),
            (vt_v.at[slot], values_t.at[:, :, at]),
        )
        return [
            pltpu.make_async_copy(source, target, block_sem.at[slot, index])
            for index, (source, target) in enumerate(pairs)
        ]

    def sequence_copy(block):
        return pltpu.make_async_copy(tokens_v.at[block], sequence.at[block], out_sem.at[block])

    def low(value):
        return value.astype(bf16).astype(f32)

    def project(slot, block):
        x = tokens_v[block].reshape(rows_of, model_width)
        y = dot(x, joined_v[...].reshape(model_width, 3 * width))
        zero = jnp.zeros((1, width), f32)
        biases = [
            jnp.where(half == 0, b[:, :width], b[:, width:])
            for b in (b_query[...].reshape(1, -1), b_value[...].reshape(1, -1))
        ]
        y = low(y + jnp.concatenate([biases[0], zero, biases[1]], 1))
        fill = -y.shape[1] % LANES
        if fill:
            y = jnp.concatenate([y, jnp.zeros((rows_of, fill), f32)], 1)
        lane = lax.broadcasted_iota(jnp.int32, (rows_of, LANES), 1)
        sub = lax.broadcasted_iota(jnp.int32, (LANES, rows_of), 0)
        first = block * rows_of
        key_pos = first + lax.broadcasted_iota(jnp.int32, (rows_of, LANES), 0)
        query_pos = first + lax.broadcasted_iota(jnp.int32, (LANES, rows_of), 1)

        def segments(positions):
            return sum((bound <= positions).astype(jnp.int32) for bound in bounds)

        flag = keep_v[block, pl.ds(seq, 1), :].astype(f32)
        flag = jnp.broadcast_to(flag, (LANES, rows_of)).T
        key_feat = jnp.where(lane < DOC_ROW, 0.0, 1.0)
        key_doc = jnp.where(segments(key_pos) == lane - DOC_ROW, 0.0, MASKED)
        key_feat = jnp.where((lane >= DOC_ROW) & (lane < DOC_ROW + len(bounds)), key_doc, key_feat)
        key_feat = jnp.where(lane == KEEP_ROW, jnp.where(flag > 0.5, 0.0, MASKED), key_feat)
        pos_low = key_pos & 255
        key_feat = jnp.where(
            (lane >= POS_ROW) & (lane < POS_ROW + 3), (key_pos - pos_low).astype(f32), key_feat
        )
        key_feat = jnp.where((lane >= POS_ROW + 3) & (lane < LINE_ROW), pos_low.astype(f32), key_feat)
        key_feat = jnp.where(lane >= FEAT_END, 0.0, key_feat)
        doc_feat = jnp.where(segments(query_pos) == sub - DOC_ROW, 1.0, 0.0)
        doc_feat = jnp.where(sub == KEEP_ROW, 1.0, doc_feat)

        def head_part(index):
            pair = y[:, index // 2 * LANES : (index // 2 + 1) * LANES]
            if index % 2:
                pair = pltpu.roll(pair, HEAD, 1)
            return jnp.where(lane < HEAD, pair, 0.0)

        for head in range(heads):
            query_feat = doc_feat
            slope = jnp.full((1, rows_of), slopes[head], f32)
            slope_terms = three_terms(slope, low)
            line_terms = three_terms(-slope * query_pos[:1].astype(f32), low)
            for term in range(3):
                here = (sub == POS_ROW + term) | (sub == POS_ROW + 3 + term)
                query_feat = jnp.where(here, slope_terms[term], query_feat)
                query_feat = jnp.where(sub == LINE_ROW + term, line_terms[term], query_feat)
            query = head_part(head) * 0.125
            q_v[slot, head] = query[:, :HEAD].astype(bf16)
            qt_v[slot, head] = (query.T + query_feat).astype(bf16)
            key = head_part(heads + head)
            k_v[slot, head] = (key + key_feat).astype(bf16)
            kt_v[slot, head] = key.T[:HEAD].astype(bf16)
            value = head_part(2 * heads + head)
            ones = (lane >= HEAD) & (lane < HEAD + 3)
            v_v[slot, head] = jnp.where(ones, 1.0, value).astype(bf16)
            vt_v[slot, head] = jnp.where(sub == HEAD, 1.0, value.T)[:80].astype(bf16)

    for copy in weights + flags:
        copy.wait_recv()
    joined_out = pltpu.make_async_copy(joined_v, full_joined, joined_sem)
    joined_out.start()

    @pl.when(~inner)
    def _():
        to_pair.wait_send()
        to_across.start()

    @pl.loop(0, 4)
    def _(i):
        pair = stage ^ 1
        block = jnp.where(i == 0, stage, jnp.where(i == 1, pair, jnp.where(i == 2, third, fourth)))
        slot = lax.rem(i, 2)

        @pl.when(i == 1)
        def _():
            arrival(pair).wait_recv()
            share(pair, core).start()
            arrival(third).wait_recv()

            @pl.when(inner)
            def _():
                send(tokens_v.at[third, core], third, pair, 2).start()

            share(third, core).start()
            for near, far in zip(halves[:2], on):
                near.wait_recv()
                far.start()

        @pl.when(i == 3)
        def _():
            arrival(fourth).wait_recv()

            @pl.when(inner)
            def _():
                send(tokens_v.at[fourth, core], fourth, pair, 3).start()

            share(fourth, core).start()

        @pl.when(i >= 1)
        def _():
            share(block, 1 - core).wait_recv()

        @pl.when(i >= 2)
        def _():
            for copy in out_copies(slot, block):
                copy.wait()

        sequence_copy(block).start()
        project(slot, block)
        for copy in out_copies(slot, block):
            copy.start()

    @pl.when(inner)
    def _():
        to_pair.wait_send()

    to_across.wait_send()

    @pl.when(inner)
    def _():
        for block, slot in ((third, 2), (fourth, 3)):
            send(tokens_v.at[block, core], block, stage ^ 1, slot).wait_send()

    for block in (stage ^ 1, third, fourth):
        share(block, core).wait_send()
    for copy in outs + halves[2:] + on:
        copy.wait()
    gate_out = pltpu.make_async_copy(gate_v, full_gate, gate_sem)
    gate_out.start()
    for copy in weights + flags + halves[:2]:
        copy.wait_send()
    for copy in [own_out, joined_out, lift_out, gate_out] + cot_outs:
        copy.wait()
    for block in range(4):
        sequence_copy(block).wait()
    for slot in (0, 1):
        for copy in out_copies(slot, 0):
            copy.wait()


def start(docs, slopes, tokens, keep, w_query, w_key, w_value, w_out, w_up, b_query, b_value, cotangent):
    _, block_rows, model_width = tokens.shape
    heads = slopes.shape[0]
    width, length = heads * HEAD, 4 * block_rows
    dma, bf16 = pltpu.SemaphoreType.DMA, jnp.bfloat16
    half_rows, quarter = block_rows // 2, w_query.shape[0]
    any_spec = pl.BlockSpec(memory_space=pl.ANY)
    vmem_spec = pl.BlockSpec(memory_space=pltpu.VMEM)
    smem_spec = pl.BlockSpec(memory_space=pltpu.SMEM)

    def parts(rows):
        return [
            (heads, LANES, rows),
            (heads, rows, HEAD),
            (heads, rows, LANES),
            (heads, HEAD, rows),
            (heads, rows, LANES),
            (heads, 80, rows),
        ]

    three, four, six = dma((3,)), dma((4,)), dma((6,))
    return pl.pallas_call(
        start_kernel,
        in_specs=[smem_spec] * 2 + [vmem_spec] * 10,
        out_specs=[any_spec] * 13,
        out_shape=[
            jax.ShapeDtypeStruct(shape, bf16)
            for shape in [
                (4, 2, half_rows, model_width),
                (4, quarter, 3 * width),
                (4,) + w_out.shape,
                (4, quarter, w_up.shape[2]),
                (quarter, w_up.shape[2]),
                (half_rows, model_width),
                (half_rows, model_width),
            ]
            + parts(length)
        ],
        scratch_shapes=[
            pltpu.VMEM((4, 2, half_rows, model_width), bf16),
            pltpu.VMEM((quarter, 3 * width), bf16),
            pltpu.VMEM((4, quarter, 3 * width), bf16),
            pltpu.VMEM((4,) + keep.shape, keep.dtype),
            pltpu.VMEM((4, quarter, w_up.shape[2]), bf16),
            pltpu.VMEM((quarter, w_up.shape[2]), bf16),
            *[pltpu.VMEM((2,) + shape, bf16) for shape in parts(block_rows)],
            four, four, four, four, six, six, six, six, three, three, dma, dma((2, 6)), dma, dma, dma, dma((2,)), four,
        ],
        compiler_params=pltpu.CompilerParams(
            collective_id=0, has_side_effects=True, vmem_limit_bytes=VMEM_BYTES
        ),
        cost_estimate=pl.CostEstimate(flops=40 << 30, bytes_accessed=16 << 20, transcendentals=0),
        name="start",
    )(docs, slopes, tokens, keep, w_query, w_key, w_value, w_out, w_up, b_query, b_value, cotangent)


def attend_kernel(docs_ref, slope_ref, qt_ref, k_ref, vt_ref, o_ref, ot_ref, lse_ref, max_ref, acc_ref):
    heads = qt_ref.shape[0]
    block = pl.program_id(0)
    first_tile, last_tile = tile_span(docs_ref, lax.axis_index("ctx") // 2, block)
    after, same, bare = side_signs(TILE)

    def tile_rows(tile, count=1):
        return pl.ds(pl.multiple_of(tile * TILE, TILE), count * TILE)

    own = tile_rows(block)
    each = range(heads)
    scores = diagonal_scores(
        [k_ref[head, own, :] for head in each], [qt_ref[head] for head in each], same, bare,
        [slope_ref[head] for head in each],
    )
    tops = [jnp.max(scores[head], 0, keepdims=True) for head in each]
    weights = [jnp.exp(scores[head] - tops[head]).astype(jnp.bfloat16) for head in each]
    parts = [dot(vt_ref[head, :, own], weights[head]) for head in each]
    for head in each:
        max_ref[head] = tops[head]
        acc_ref[head] = parts[head]

    def step(tile, count, sign):
        each = range(heads)
        keys = [k_ref[head, tile_rows(tile, count), :] for head in each]
        values = [vt_ref[head, :, tile_rows(tile, count)] for head in each]
        queries = [qt_ref[head] if sign is None else qt_ref[head] * sign for head in each]
        old = [max_ref[head] for head in each]
        acc = [acc_ref[head] for head in each]
        scores = [dot(keys[head], queries[head]) for head in each]
        top = [jnp.maximum(old[head], jnp.max(scores[head], 0, keepdims=True)) for head in each]
        weights = [jnp.exp(scores[head] - top[head]).astype(jnp.bfloat16) for head in each]
        parts = [dot(values[head], weights[head]) for head in each]
        for head in each:
            max_ref[head] = top[head]
            acc_ref[head] = acc[head] * jnp.exp(old[head] - top[head]) + parts[head]

    sweep(first_tile, block, lambda tile, count: step(tile, count, None))
    sweep(block + 1, last_tile, lambda tile, count: step(tile, count, after))

    parts = []
    for head in range(heads):
        total = acc_ref[head, HEAD : HEAD + 1, :]
        out_t = acc_ref[head, :HEAD, :] / total
        ot_ref[head] = out_t
        parts.append(out_t)
        lse_ref[head] = max_ref[head] + jnp.log(total)
    o_ref[...] = jnp.concatenate(parts, 0).T.astype(jnp.bfloat16)


def attend(docs, slopes, query_t, keys, value_t):
    heads, _, length = query_t.shape
    blocks = length // TILE
    return pl.pallas_call(
        attend_kernel,
        grid_spec=pltpu.PrefetchScalarGridSpec(
            num_scalar_prefetch=2,
            grid=(blocks,),
            in_specs=[
                pl.BlockSpec((heads, LANES, TILE), lambda i, *_: (0, 0, i)),
                pl.BlockSpec(keys.shape, lambda i, *_: (0, 0, 0)),
                pl.BlockSpec(value_t.shape, lambda i, *_: (0, 0, 0)),
            ],
            out_specs=[
                pl.BlockSpec((TILE, heads * HEAD), lambda i, *_: (i, 0)),
                pl.BlockSpec((heads, HEAD, TILE), lambda i, *_: (0, 0, i)),
                pl.BlockSpec((heads, 1, TILE), lambda i, *_: (0, 0, i)),
            ],
            scratch_shapes=[
                pltpu.VMEM((heads, 1, TILE), jnp.float32),
                pltpu.VMEM((heads, 80, TILE), jnp.float32),
            ],
        ),
        out_shape=[
            jax.ShapeDtypeStruct((length, heads * HEAD), jnp.bfloat16),
            jax.ShapeDtypeStruct((heads, HEAD, length), jnp.float32),
            jax.ShapeDtypeStruct((heads, 1, length), jnp.float32),
        ],
        compiler_params=pltpu.CompilerParams(vmem_limit_bytes=VMEM_BYTES),
        cost_estimate=pl.CostEstimate(
            flops=heads * length * length * 256, bytes_accessed=6 << 20, transcendentals=heads * length * length
        ),
        name="attend",
    )(docs, slopes, query_t, keys, value_t)


def attend_back_kernel(
    docs_ref, slope_ref, qt_ref, q_ref, k_ref, kt_ref, v_ref, g_ref, ot_ref, lse_ref,
    dq_ref, dk_ref, dv_ref, qt_log, grad_heads, grad_t, query_acc, key_acc, value_acc,
):
    heads = qt_ref.shape[0]
    blocks = pl.num_programs(0)
    block = pl.program_id(0)
    length = qt_ref.shape[2]
    first_tile, last_tile = tile_span(docs_ref, lax.axis_index("ctx") // 2, block)
    after, same, bare = side_signs(TILE)

    def low(value):
        return value.astype(jnp.bfloat16).astype(jnp.float32)

    def tile_rows(tile, count=1):
        return pl.ds(pl.multiple_of(tile * TILE, TILE), count * TILE)

    @pl.when(block == 0)
    def _():
        query_acc[...] = jnp.zeros_like(query_acc)
        sub = lax.broadcasted_iota(jnp.int32, (LANES, TILE), 0)

        @pl.loop(0, length // TILE)
        def _(tile):
            rows = tile_rows(tile)
            grad = g_ref[rows, :].astype(jnp.float32)
            turned = grad.T
            for head in range(heads):
                own = turned[head * HEAD : (head + 1) * HEAD]
                delta = jnp.sum(own * ot_ref[head, :, rows], 0, keepdims=True)
                first, second, third = three_terms(-delta, low)
                wide = jnp.concatenate([own, jnp.zeros_like(own)], 0)
                wide = jnp.where(sub == HEAD, first, wide)
                wide = jnp.where(sub == HEAD + 1, second, wide)
                wide = jnp.where(sub == HEAD + 2, third, wide)
                grad_t[head, :, rows] = wide.astype(jnp.bfloat16)
                grad_heads[head, rows, :] = own.T.astype(jnp.bfloat16)
                first, second, third = three_terms(-lse_ref[head, :, rows], low)
                query = qt_ref[head, :, rows].astype(jnp.float32)
                query = jnp.where(sub == LOG_ROW, first, query)
                query = jnp.where(sub == LOG_ROW + 1, second, query)
                query = jnp.where(sub == LOG_ROW + 2, third, query)
                qt_log[head, :, rows] = query.astype(jnp.bfloat16)

    def accumulate(tile, scores, first, count=1):
        each = range(heads)
        rows = tile_rows(tile, count)
        values = [v_ref[head] for head in each]
        turned = [grad_t[head, :, rows] for head in each]
        grads = [grad_heads[head, rows, :] for head in each]
        queries = [q_ref[head, rows, :] for head in each]
        keys_t = [kt_ref[head] for head in each]
        probs = [jnp.exp(scores[head]) for head in each]
        grad_probs = [dot(values[head], turned[head]) for head in each]
        grad_scores = [(probs[head] * grad_probs[head]).astype(jnp.bfloat16) for head in each]
        value_part = [dot(probs[head].astype(jnp.bfloat16), grads[head]) for head in each]
        key_part = [dot(grad_scores[head], queries[head]) for head in each]
        query_part = [dot(keys_t[head], grad_scores[head]) for head in each]
        for head in each:
            if first:
                value_acc[head] = value_part[head]
                key_acc[head] = key_part[head]
            else:
                value_acc[head] += value_part[head]
                key_acc[head] += key_part[head]
            query_acc[head, :, rows] += query_part[head]

    own = [qt_log[head, :, tile_rows(block)] for head in range(heads)]
    accumulate(
        block,
        diagonal_scores(
            [k_ref[head] for head in range(heads)], own, same, bare,
            [slope_ref[head] for head in range(heads)],
        ),
        True,
    )
    after_wide = side_signs(2 * TILE)[0]

    def step(tile, count, sign):
        queries = [qt_log[head, :, tile_rows(tile, count)] for head in range(heads)]
        if sign is not None:
            queries = [query * sign[:, : count * TILE] for query in queries]
        accumulate(tile, [dot(k_ref[head], queries[head]) for head in range(heads)], False, count)

    sweep(first_tile, block, lambda tile, count: step(tile, count, after_wide))
    sweep(block + 1, last_tile, lambda tile, count: step(tile, count, None))

    dk_ref[...] = jnp.concatenate([key_acc[head] for head in range(heads)], 1).astype(jnp.bfloat16)
    dv_ref[...] = jnp.concatenate([value_acc[head] for head in range(heads)], 1).astype(jnp.bfloat16)

    @pl.when(block == blocks - 1)
    def _():
        @pl.loop(0, length // TILE)
        def _(tile):
            rows = tile_rows(tile)
            turned = jnp.concatenate([query_acc[head, :, rows] for head in range(heads)], 0)
            dq_ref[rows, :] = (turned.T * 0.125).astype(jnp.bfloat16)


def attend_back(docs, slopes, query_t, queries, keys, keys_t, values, grads, out_t, lse):
    heads, _, length = query_t.shape
    blocks = length // TILE
    width = heads * HEAD

    def whole(array):
        return pl.BlockSpec(array.shape, lambda i, *_: (0,) * array.ndim)

    return pl.pallas_call(
        attend_back_kernel,
        grid_spec=pltpu.PrefetchScalarGridSpec(
            num_scalar_prefetch=2,
            grid=(blocks,),
            in_specs=[
                whole(query_t),
                whole(queries),
                pl.BlockSpec((heads, TILE, LANES), lambda i, *_: (0, i, 0)),
                pl.BlockSpec((heads, HEAD, TILE), lambda i, *_: (0, 0, i)),
                pl.BlockSpec((heads, TILE, LANES), lambda i, *_: (0, i, 0)),
                whole(grads),
                whole(out_t),
                whole(lse),
            ],
            out_specs=[
                pl.BlockSpec((length, width), lambda i, *_: (0, 0)),
                pl.BlockSpec((TILE, width), lambda i, *_: (i, 0)),
                pl.BlockSpec((TILE, width), lambda i, *_: (i, 0)),
            ],
            scratch_shapes=[
                pltpu.VMEM((heads, LANES, length), jnp.bfloat16),
                pltpu.VMEM((heads, length, HEAD), jnp.bfloat16),
                pltpu.VMEM((heads, LANES, length), jnp.bfloat16),
                pltpu.VMEM((heads, HEAD, length), jnp.float32),
                pltpu.VMEM((heads, TILE, HEAD), jnp.float32),
                pltpu.VMEM((heads, TILE, HEAD), jnp.float32),
            ],
        ),
        out_shape=[jax.ShapeDtypeStruct((length, width), jnp.bfloat16)] * 3,
        compiler_params=pltpu.CompilerParams(vmem_limit_bytes=VMEM_BYTES),
        cost_estimate=pl.CostEstimate(
            flops=heads * length * length * 640, bytes_accessed=12 << 20, transcendentals=heads * length * length
        ),
        name="attend_back",
    )(docs, slopes, query_t, queries, keys, keys_t, values, grads, out_t, lse)


def rows_norm(residual):
    centered = residual - jnp.mean(residual, -1, keepdims=True)
    inv_scale = lax.rsqrt(jnp.mean(centered * centered, -1, keepdims=True) + NORM_EPS)
    return centered * inv_scale, inv_scale


def rows_norm_back(grad_out, normed, inv_scale, norm_gain):
    grad_norm = grad_out * norm_gain
    mean_grad = jnp.mean(grad_norm, -1, keepdims=True)
    mean_cross = jnp.mean(grad_norm * normed, -1, keepdims=True)
    return (grad_norm - mean_grad - normed * mean_cross) * inv_scale


def middle_kernel(
    attended, sequence, cotangent, cot_far, cot_near, w_out, gate_full, w_down, lift_0, lift_1, lift_2, lift_3, *rest,
):
    vectors, rest = rest[:6], rest[6:]
    (
        out_home, grad_one, grad_heads, early_0, early_1, early_2, early_3, late, down_sum, sums,
        token_v, mine_v, theirs_v, both_v, cot_v, out_w, down_w, up_w,
        send_a, recv_a, send_b, recv_b, send_c, recv_c,
        normed_v, inv_v, low_v, hidden_v, gate_v, lift_v, grad_v, ffn_v, att_v, result_v, keep_v, away_v, tile_v,
        down_v, down_got, home_v, load_sem, near_send, near_recv, pair_send, pair_recv, cot_send, cot_pass, cot_took,
        a_send, a_recv, b_send, b_recv, c_send, c_recv, out_send, out_recv, out_pass, out_took,
        one_sem, keep_sem, away_send, away_recv, tile_sem, down_send, down_recv, down_sem, home_sem,
    ) = rest
    place, stage, core = lax.axis_index("fsdp"), lax.axis_index("ctx"), lax.axis_index("tp")
    seq, half = stage // 2, stage % 2
    pair = stage ^ 1
    chunks = token_v.shape[0]
    units = hidden_v.shape[2]
    wide = 512
    quarter = lift_0.shape[0]

    barrier = pltpu.get_barrier_semaphore()
    peers = [(place ^ other, stage, core) for other in (1, 2, 3)]
    peers += [(place, lax.rem(stage + shift, 4), core) for shift in (1, 2, 3)]
    peers += [(place, stage, 1 - core)]
    for peer in peers:
        pl.semaphore_signal(barrier, inc=1, device_id=peer, device_id_type=MESH)
    pl.semaphore_wait(barrier, len(peers))

    def remote(source, target, send, recv, device):
        return pltpu.make_async_remote_copy(
            source, target, send, recv, device_id=device, device_id_type=MESH
        )

    partner = (place, pair, core)
    other_core = (place, stage, 1 - core)

    def pair_copy(c):
        return remote(
            attended.at[(1 - half) * chunks + c], theirs_v.at[c], pair_send.at[c], pair_recv.at[c], partner
        )

    for c in range(chunks):
        pair_copy(c).start()

    def rows_of(owner):
        return pl.ds(pl.multiple_of(owner * quarter, quarter), quarter)

    def near_copy(owner, other, which, sem):
        columns = pl.ds(which * (units // 2), units // 2)
        block = down_w.at[rows_of(owner), columns]
        source = w_down.at[:, columns] if owner is place else block
        return remote(source, block, near_send.at[sem], near_recv.at[sem], (place ^ other, stage, core))

    halves = [
        near_copy(place, other, which, 2 * which + other - 1)
        for other, which in ((1, 0), (2, 1), (1, 1), (2, 0))
    ]
    on = [near_copy(place ^ 1, 2, 0, 4), near_copy(place ^ 2, 1, 1, 5)]
    for copy in halves:
        copy.start()

    def cot_owner(which):
        return 2 * which + stage // 2

    near_block = jnp.where(stage < 2, 0, 1)
    far_block = 1 - near_block
    facing = (stage == 1) | (stage == 2)
    far_load = pltpu.make_async_copy(cot_far, cot_v.at[far_block, core], cot_send.at[0])
    near_load = pltpu.make_async_copy(cot_near, cot_v.at[near_block, core], cot_send.at[1])
    own_load = pltpu.make_async_copy(cotangent.at[stage // 2], cot_v.at[near_block], cot_send.at[1])
    far_load.start()

    @pl.when(facing)
    def _():
        near_load.start()

    @pl.when(~facing)
    def _():
        own_load.start()

    def cot_share(block, whose):
        return remote(
            cot_v.at[block, whose], cot_v.at[block, whose], cot_pass.at[block], cot_took.at[block], other_core
        )

    loads = [
        pltpu.make_async_copy(attended.at[pl.ds(half * chunks, chunks)], mine_v, load_sem.at[0]),
        pltpu.make_async_copy(w_out, out_w, load_sem.at[1]),
        pltpu.make_async_copy(sequence.at[pl.ds(half * chunks, chunks)], token_v, load_sem.at[2]),
        pltpu.make_async_copy(w_down, down_w.at[rows_of(place)], load_sem.at[3]),
        pltpu.make_async_copy(gate_full, up_w.at[:, pl.ds(0, units)], load_sem.at[4]),
    ]
    for other, shard in enumerate((lift_0, lift_1, lift_2, lift_3)):
        target = up_w.at[rows_of(place ^ other), pl.ds(units, units)]
        loads.append(pltpu.make_async_copy(shard, target, load_sem.at[5 + other]))
    for load in loads:
        load.start()

    b_out, gain_one, shift_one, b_down, gain_two, shift_two = (v[...].reshape(1, -1) for v in vectors)
    sums[...] = jnp.zeros_like(sums)

    def add_sum(index, rows):
        sums[index : index + 1, :] += jnp.sum(rows, 0, keepdims=True)

    def exchange(c, sent, got, send, recv):
        return remote(sent.at[c], got.at[c], send.at[c], recv.at[c], other_core)

    def total(c, sent, got):
        return sent[c].astype(jnp.float32) + got[c].astype(jnp.float32)

    loads[0].wait()
    loads[1].wait()

    def attention_branch(c):
        pair_copy(c).wait_recv()
        first, second = mine_v[c], theirs_v[c]
        both = jnp.where(
            half == 0, jnp.concatenate([first, second], 1), jnp.concatenate([second, first], 1)
        )
        both_v[c] = both
        send_a[c] = dot(both, out_w[...], ((1,), (1,))).astype(jnp.bfloat16)
        exchange(c, send_a, recv_a, a_send, a_recv).start()

    attention_branch(0)
    far_load.wait()
    cot_share(far_block, core).start()

    @pl.when(facing)
    def _():
        near_load.wait()
        cot_share(near_block, core).start()

    @pl.when(~facing)
    def _():
        own_load.wait()

    for load in loads[2:]:
        load.wait()
    @pl.loop(0, chunks)
    def _(c):
        @pl.when(c + 1 < chunks)
        def _():
            attention_branch(c + 1)

        @pl.when(c == 1)
        def _():
            for near, far in zip(halves[:2], on):
                near.wait_recv()
                far.start()

        exchange(c, send_a, recv_a, a_send, a_recv).wait_recv()

        residual = token_v[c].astype(jnp.float32) + (total(c, send_a, recv_a) + b_out)
        normed, inv_scale = rows_norm(residual)
        normed_v[c] = normed
        inv_v[c] = inv_scale
        low_v[c] = (normed * gain_one + shift_one).astype(jnp.bfloat16)
        for n in range(0, units, wide):
            gate = dot(low_v[c], up_w[:, n : n + wide])
            lift = dot(low_v[c], up_w[:, units + n : units + n + wide])
            chance = 0.5 + 0.5 * lax.erf(gate * 0.7071067811865476)
            density = jnp.exp(gate * gate * -0.5) * 0.3989422804014327
            gelu = gate * chance
            hidden_v[c, :, n : n + wide] = (gelu * lift).astype(jnp.bfloat16)
            gate_v[c, :, n : n + wide] = (lift * (chance + gate * density)).astype(jnp.bfloat16)
            lift_v[c, :, n : n + wide] = gelu.astype(jnp.bfloat16)

    for copy in halves[2:] + on:
        copy.wait_recv()
    @pl.loop(0, chunks)
    def _(c):
        send_b[c] = dot(hidden_v[c], down_w[...], ((1,), (1,))).astype(jnp.bfloat16)
        exchange(c, send_b, recv_b, b_send, b_recv).start()

    cot_share(far_block, core).wait_send()
    cot_share(far_block, 1 - core).wait_recv()

    @pl.when(facing)
    def _():
        cot_share(near_block, core).wait_send()
        cot_share(near_block, 1 - core).wait_recv()

    def home(c):
        return 2 * half + c // 2

    def out_copy(c):
        return remote(
            result_v.at[c], home_v.at[seq], out_send.at[c], out_recv.at[seq], (place, home(c), core)
        )

    def out_local(c):
        return pltpu.make_async_copy(result_v.at[c], out_home.at[seq, c % 2], out_send.at[c])

    @pl.loop(0, chunks)
    def _(c):
        exchange(c, send_b, recv_b, b_send, b_recv).wait_recv()
        normed_one = normed_v[c]
        residual = normed_one * gain_one + shift_one + (total(c, send_b, recv_b) + b_down)
        normed, inv_scale = rows_norm(residual)
        result_v[c] = (normed * gain_two + shift_two).astype(jnp.bfloat16)

        @pl.when(home(c) == stage)
        def _():
            out_local(c).start()

        @pl.when((home(c) != stage) & (c % 2 == core))
        def _():
            out_copy(c).start()

        grad_in = cot_v[c // 2, c % 2].astype(jnp.float32)
        add_sum(0, grad_in * normed)
        add_sum(1, grad_in)
        grad_two = rows_norm_back(grad_in, normed, inv_scale, gain_two)
        grad_v[c] = grad_two
        grad_ffn = grad_two.astype(jnp.bfloat16)
        ffn_v[c] = grad_ffn
        add_sum(2, grad_ffn.astype(jnp.float32))

    tile = tile_v.shape[2]

    def columns(index):
        return pl.ds(pl.multiple_of(index * tile, tile), tile)

    def weight_part(left, right):
        rows = left.shape[0] * left.shape[1]
        return dot(
            left[...].reshape(rows, left.shape[2]), right.reshape(rows, tile), ((0,), (0,))
        ).astype(jnp.bfloat16)

    unit_tiles = units // tile

    def down_copy(i, other):
        rows = pl.ds(pl.multiple_of((place ^ other) * quarter, quarter), quarter)
        return remote(
            down_v.at[rows, columns(i)], down_got.at[other - 1, :, columns(i)],
            down_send.at[i, other - 1], down_recv.at[i, other - 1], (place ^ other, stage, core),
        )

    @pl.loop(0, unit_tiles)
    def _(i):
        down_v[:, columns(i)] = weight_part(ffn_v, hidden_v[:, :, columns(i)])
        for other in (1, 2, 3):
            down_copy(i, other).start()

    @pl.loop(0, chunks)
    def _(c):
        for n in range(0, units, wide):
            grad_hidden = dot(ffn_v[c], down_w[:, n : n + wide])
            gate_v[c, :, n : n + wide] = (grad_hidden * gate_v[c, :, n : n + wide]).astype(jnp.bfloat16)
            lift_v[c, :, n : n + wide] = (grad_hidden * lift_v[c, :, n : n + wide]).astype(jnp.bfloat16)
        send_c[c] = (
            dot(gate_v[c], up_w[:, :units], ((1,), (1,))) + dot(lift_v[c], up_w[:, units:], ((1,), (1,)))
        ).astype(jnp.bfloat16)
        exchange(c, send_c, recv_c, c_send, c_recv).start()

    def one_copy(c):
        return pltpu.make_async_copy(grad_v.at[c], grad_one.at[c], one_sem.at[c])

    def keep_copy(c):
        return pltpu.make_async_copy(keep_v.at[c], grad_heads.at[half * chunks + c], keep_sem.at[c])

    def away_copy(c, whose):
        return remote(
            away_v.at[c], grad_heads.at[whose * chunks + c], away_send.at[c], away_recv.at[c], partner
        )

    @pl.loop(0, chunks)
    def _(c):
        exchange(c, send_c, recv_c, c_send, c_recv).wait_recv()
        grad_first = grad_v[c] + total(c, send_c, recv_c)
        normed = normed_v[c]
        add_sum(3, grad_first * normed)
        add_sum(4, grad_first)
        grad_res = rows_norm_back(grad_first, normed, inv_v[c], gain_one)
        grad_v[c] = grad_res
        one_copy(c).start()
        grad_att = grad_res.astype(jnp.bfloat16)
        att_v[c] = grad_att
        add_sum(5, grad_att.astype(jnp.float32))
        heads = dot(att_v[c], out_w[...]).astype(jnp.bfloat16)
        first, second = heads[:, : heads.shape[1] // 2], heads[:, heads.shape[1] // 2 :]
        keep_v[c] = jnp.where(half == 0, first, second)
        away_v[c] = jnp.where(half == 0, second, first)
        away_copy(c, half).start()
        keep_copy(c).start()

    early = (early_0, early_1, early_2, early_3)
    early_tiles = early_0.shape[1] // tile

    def tile_copy(slot, other, index):
        target, column = index
        rows = pl.ds(pl.multiple_of((place ^ other) * quarter, quarter), quarter)
        place_of = target[other] if isinstance(target, tuple) else target.at[other]
        return pltpu.make_async_copy(
            tile_v.at[slot, rows], place_of.at[:, columns(column)], tile_sem.at[slot, other]
        )

    def weight_tile(count, target, column, left, right):
        slot = lax.rem(count, 2)

        @pl.when(count >= 2)
        def _():
            for row in range(4):
                tile_copy(slot, row, (target, column)).wait()

        tile_v[slot] = weight_part(left, right)
        for row in range(4):
            tile_copy(slot, row, (target, column)).start()

    @pl.loop(0, unit_tiles)
    def _(i):
        weight_tile(i, early, i, low_v, gate_v[:, :, columns(i)])

    @pl.loop(unit_tiles, early_tiles)
    def _(i):
        weight_tile(i, early, i, low_v, lift_v[:, :, columns(i - unit_tiles)])

    late_units = 2 * unit_tiles - early_tiles

    @pl.loop(0, late_units)
    def _(i):
        weight_tile(early_tiles + i, late, i, low_v, lift_v[:, :, columns(early_tiles - unit_tiles + i)])

    weight_tile(2 * unit_tiles, late, late_units, att_v, both_v[...])
    for slot in (0, 1):
        for row in range(4):
            tile_copy(slot, row, (late, 0)).wait()

    for i in range(unit_tiles):
        for other in (1, 2, 3):
            down_copy(i, other).wait_recv()
    own_rows = pl.ds(pl.multiple_of(place * quarter, quarter), quarter)
    down_got[0] = (
        down_v[own_rows, :].astype(jnp.float32)
        + down_got[0].astype(jnp.float32)
        + (down_got[1].astype(jnp.float32) + down_got[2].astype(jnp.float32))
    ).astype(jnp.bfloat16)
    down_out = pltpu.make_async_copy(down_got.at[0], down_sum, down_sem)
    down_out.start()

    def out_arrival(which):
        return remote(
            home_v.at[which], home_v.at[which], out_pass.at[which], out_recv.at[which], other_core
        )

    def out_share(which, whose):
        return remote(
            home_v.at[which], out_home.at[which, whose], out_pass.at[which], out_took.at[which], other_core
        )

    def out_here(which):
        return pltpu.make_async_copy(home_v.at[which], out_home.at[which, core], home_sem.at[which])

    for which in (0, 1):

        @pl.when(cot_owner(which) != stage)
        def _():
            out_arrival(which).wait_recv()
            out_share(which, core).start()
            out_here(which).start()

    down_out.wait()
    for copy in halves + on:
        copy.wait_send()
    for i in range(unit_tiles):
        for other in (1, 2, 3):
            down_copy(i, other).wait_send()

    @pl.loop(0, chunks)
    def _(c):
        pair_copy(c).wait_send()
        exchange(c, send_a, recv_a, a_send, a_recv).wait_send()
        exchange(c, send_b, recv_b, b_send, b_recv).wait_send()
        exchange(c, send_c, recv_c, c_send, c_recv).wait_send()
        one_copy(c).wait()
        keep_copy(c).wait()
        away_copy(c, half).wait_send()
        away_copy(c, 1 - half).wait_recv()

        @pl.when(home(c) == stage)
        def _():
            out_local(c).wait()

        @pl.when((home(c) != stage) & (c % 2 == core))
        def _():
            out_copy(c).wait_send()

    for which in (0, 1):

        @pl.when(cot_owner(which) != stage)
        def _():
            out_share(which, core).wait_send()
            out_share(which, 1 - core).wait_recv()
            out_here(which).wait()


def middle(attended, sequence, cotangents, w_out, w_gate, w_down, lift_shards, vectors):
    chunks, rows, width = 4, sequence.shape[1], sequence.shape[2]
    head_width, units = w_out.shape[1], w_down.shape[1]
    tile = head_width
    early, late = 7 * tile, 2 * units + head_width - 7 * tile
    dma, bf16, f32 = pltpu.SemaphoreType.DMA, jnp.bfloat16, jnp.float32

    def vmem(shape, dtype=bf16):
        return pltpu.VMEM(shape, dtype)

    wide = (chunks, rows, width)
    inner = (chunks, rows, units)
    narrow_rows = (chunks, rows, head_width // 2)
    four, two = dma((chunks,)), dma((2,))
    return pl.pallas_call(
        middle_kernel,
        in_specs=[pl.BlockSpec(memory_space=pl.ANY)] * 12 + [pl.BlockSpec(memory_space=pltpu.VMEM)] * 6,
        out_specs=[pl.BlockSpec(memory_space=pl.ANY)] * 9 + [pl.BlockSpec(memory_space=pltpu.VMEM)],
        out_shape=[
            jax.ShapeDtypeStruct((2, 2, rows, width), bf16),
            jax.ShapeDtypeStruct(wide, f32),
            jax.ShapeDtypeStruct((2 * chunks, rows, head_width // 2), bf16),
            *[jax.ShapeDtypeStruct((width // 4, early), bf16)] * 4,
            jax.ShapeDtypeStruct((4, width // 4, late), bf16),
            jax.ShapeDtypeStruct((width // 4, units), bf16),
            jax.ShapeDtypeStruct((8, width), f32),
        ],
        scratch_shapes=[
            vmem(wide), vmem(narrow_rows), vmem(narrow_rows), vmem((chunks, rows, head_width)),
            vmem((2, 2, rows, width)), vmem((width, head_width)), vmem((width, units)), vmem((width, 2 * units)),
            vmem(wide), vmem(wide), vmem(wide), vmem(wide), vmem(wide), vmem(wide),
            vmem(wide, f32), vmem((chunks, rows, 1), f32), vmem(wide),
            vmem(inner), vmem(inner), vmem(inner),
            vmem(wide, f32), vmem(wide), vmem(wide), vmem(wide), vmem(narrow_rows), vmem(narrow_rows),
            vmem((2, width, tile)), vmem((width, units)), vmem((3, width // 4, units)), vmem((2, rows, width)),
            dma((9,)), dma((6,)), dma((6,)), four, four, two, two, two,
            four, four, four, four, four, four, four, two, two, two,
            four, four, four, four, dma((2, 4)), dma((units // tile, 3)), dma((units // tile, 3)), dma, two,
        ],
        compiler_params=pltpu.CompilerParams(
            collective_id=1, has_side_effects=True, vmem_limit_bytes=VMEM_BYTES
        ),
        cost_estimate=pl.CostEstimate(flops=50 << 30, bytes_accessed=32 << 20, transcendentals=0),
        name="middle",
    )(attended, sequence, *cotangents, w_out, w_gate, w_down, *lift_shards, *vectors)


def tail_kernel(
    d_query, d_key, d_value, w_joined, sums_in, sequence, grad_one, early, late, moved_1, moved_2, moved_3,
    down_own, down_in,
    home, shard, joined, down, sums,
    query_v, key_v, value_v, token_v, one_v, part_v, late_v, project_v, own_v, tp_sent, tp_got, pair_sent, pair_got,
    final_v, summed_v, end_got, inner_v, mid_got, total_v, joined_v, quarter_got, both_sent, both_end, both_inner,
    both_mid, both_total, step_v, step_got, home_v, down_v, down_inner, down_got, down_total,
    load_sem, late_send, late_recv, tp_send, tp_recv, pair_send, pair_recv, home_send, home_recv, home_pass,
    home_took, home_local, end_send, end_recv, mid_send, mid_recv, back_send, back_recv, shard_sem,
    quarter_send, quarter_recv, both_send, both_recv, both_local, step_send, step_recv, home_sem, down_sem, down_mid_send, down_mid_recv, down_back_send, down_back_recv,
):
    place, stage, core = lax.axis_index("fsdp"), lax.axis_index("ctx"), lax.axis_index("tp")
    seq, half = stage // 2, stage % 2
    bf16, f32 = jnp.bfloat16, jnp.float32
    pieces = summed_v.shape[0]
    piece = summed_v.shape[2]
    early_pieces = early.shape[1] // piece
    quarter = joined_v.shape[0] // 4
    width = d_query.shape[2]

    barrier = pltpu.get_barrier_semaphore()
    peers = [(place ^ other, stage, core) for other in (1, 2, 3)]
    peers += [(place, lax.rem(stage + shift, 4), core) for shift in (1, 2, 3)]
    peers += [(place, stage, 1 - core)]
    for peer in peers:
        pl.semaphore_signal(barrier, inc=1, device_id=peer, device_id_type=MESH)

    loads = [
        pltpu.make_async_copy(source, target, load_sem.at[index])
        for index, (source, target) in enumerate(
            (
                (early, part_v.at[0]),
                (moved_1, part_v.at[1]),
                (moved_2, part_v.at[2]),
                (moved_3, part_v.at[3]),
                (d_query, query_v),
                (d_key, key_v),
                (d_value, value_v),
                (late.at[0], late_v.at[0]),
                (sequence, token_v),
                (grad_one, one_v),
            )
        )
    ]
    down_loads = [
        pltpu.make_async_copy(source, down_v.at[index], down_sem.at[index])
        for index, source in enumerate((down_own, down_in))
    ]
    for load in down_loads + loads:
        load.start()
    pl.semaphore_wait(barrier, len(peers))

    def remote(source, target, send, recv, device):
        return pltpu.make_async_remote_copy(
            source, target, send, recv, device_id=device, device_id_type=MESH
        )

    other_core = (place, stage, 1 - core)
    partner = (place, stage ^ 1, core)
    at_end = (stage == 0) | (stage == 3)
    inward = (place, stage ^ 1, core)
    outward = (place, stage ^ 1, core)
    across = (place, 3 - stage, core)

    def late_copy(other):
        return remote(
            late.at[other], late_v.at[other], late_send.at[other - 1], late_recv.at[other - 1],
            (place ^ other, stage, core),
        )

    for other in (1, 2, 3):
        late_copy(other).start()

    def columns(j):
        return pl.ds(j * piece, piece)

    def end_copy(j):
        return remote(summed_v.at[j], end_got.at[j], end_send.at[j], end_recv.at[j], inward)

    def mid_copy(j):
        return remote(inner_v.at[j], mid_got.at[j], mid_send.at[j], mid_recv.at[j], across)

    def back_copy(j):
        return remote(total_v.at[j], shard.at[:, columns(j)], back_send.at[j], back_recv.at[j], outward)

    def shard_copy(j):
        return pltpu.make_async_copy(total_v.at[j], shard.at[:, columns(j)], shard_sem.at[j])

    def sum_piece(j, parts, first):
        terms = [parts[index, :, first : first + piece].astype(f32) for index in range(4)]
        summed_v[j] = (terms[0] + terms[1] + (terms[2] + terms[3])).astype(bf16)

        @pl.when(at_end)
        def _():
            end_copy(j).start()

    def from_end(j):
        end_copy(j).wait_recv()
        inner_v[j] = (summed_v[j].astype(f32) + end_got[j].astype(f32)).astype(bf16)
        mid_copy(j).start()

    def from_mid(j):
        mid_copy(j).wait_recv()
        total_v[j] = (inner_v[j].astype(f32) + mid_got[j].astype(f32)).astype(bf16)
        back_copy(j).start()
        shard_copy(j).start()

    down_pieces = down_mid_send.shape[0]
    down_size = down_v.shape[2] // down_pieces

    def down_part(ref, j):
        return ref.at[:, pl.ds(j * down_size, down_size)]

    def down_mid(j):
        return remote(
            down_part(down_inner, j), down_part(down_got, j), down_mid_send.at[j], down_mid_recv.at[j], across
        )

    def down_back(j):
        return remote(
            down_part(down_total, j), down_part(down, j), down_back_send.at[j], down_back_recv.at[j], outward
        )

    def down_here(j):
        return pltpu.make_async_copy(down_part(down_total, j), down_part(down, j), down_sem.at[j])

    def down_from_mid(j):
        down_mid(j).wait_recv()
        part = slice(j * down_size, (j + 1) * down_size)
        down_total[:, part] = (
            down_inner[:, part].astype(f32) + down_got[:, part].astype(f32)
        ).astype(bf16)
        down_back(j).start()
        down_here(j).start()

    for load in down_loads:
        load.wait()

    @pl.when(~at_end)
    def _():
        down_inner[...] = (down_v[0].astype(f32) + down_v[1].astype(f32)).astype(bf16)
        for j in range(down_pieces):
            down_mid(j).start()

    for load in loads[:4]:
        load.wait()
    for j in range(early_pieces):
        sum_piece(j, part_v, j * piece)

    def input_share(chunk):
        rows = jnp.concatenate([query_v[chunk], key_v[chunk], value_v[chunk]], 1)
        project_v[chunk] = rows
        return dot(rows, w_joined[...], ((1,), (1,)))

    def block_of(i):
        return jnp.where(i < 2, 2 * (1 - half) + i, 2 * half + i - 2)

    def tp_copy(i):
        return remote(tp_sent.at[i], tp_got.at[i], tp_send.at[i], tp_recv.at[i], other_core)

    for load in loads[4:7]:
        load.wait()

    @pl.loop(0, 4)
    def _(i):
        block = block_of(i)
        tp_sent[i] = input_share(2 * block + 1 - core).astype(bf16)
        tp_copy(i).start()
        own_v[i] = input_share(2 * block + core)

    def pair_copy(i):
        return remote(pair_sent.at[i], pair_got.at[i], pair_send.at[i], pair_recv.at[i], partner)

    @pl.loop(0, 2)
    def _(i):
        tp_copy(i).wait_recv()
        pair_sent[i] = (own_v[i] + tp_got[i].astype(f32)).astype(bf16)
        pair_copy(i).start()

    @pl.when(~at_end)
    def _():
        for j in range(early_pieces // 2):
            from_end(j)

    @pl.when(~at_end)
    def _():
        for j in range(down_pieces):
            down_from_mid(j)

    loads[8].wait()
    tokens = token_v[...].reshape(-1, token_v.shape[2])
    project = project_v[...].reshape(-1, project_v.shape[2])
    strip = 256
    for row in range(0, joined_v.shape[0], strip):
        joined_v[row : row + strip, :] = dot(
            tokens[:, row : row + strip], project, ((0,), (0,))
        ).astype(bf16)

    def quarter_copy(other):
        rows = pl.ds(pl.multiple_of((place ^ other) * quarter, quarter), quarter)
        return remote(
            joined_v.at[rows], quarter_got.at[other - 1], quarter_send.at[other - 1], quarter_recv.at[other - 1],
            (place ^ other, stage, core),
        )

    for other in (1, 2, 3):
        quarter_copy(other).start()

    def column_sum(grads):
        return jnp.sum(grads[...].reshape(-1, width).astype(f32), 0, keepdims=True)

    bias_parts = []
    for total in (column_sum(query_v), column_sum(value_v)):
        for which in (0, 1):
            bias_parts.append(jnp.where(half == which, total, 0.0))
    bias = jnp.concatenate(bias_parts, 1)
    step_v[0] = sums_in[...]
    step_v[0, 6:7, :] = bias
    steps = [(place ^ 1, stage, core), (place ^ 2, stage, core), partner, (place, stage ^ 2, core)]

    def step_copy(index):
        return remote(
            step_v.at[index], step_got.at[index], step_send.at[index], step_recv.at[index], steps[index]
        )

    def step_on(index):
        step_copy(index).wait_recv()
        step_v[index + 1] = step_v[index] + step_got[index]
        if index < 3:
            step_copy(index + 1).start()

    step_copy(0).start()

    @pl.when(~at_end)
    def _():
        for j in range(early_pieces // 2, early_pieces):
            from_end(j)
            from_mid(j - early_pieces // 2)

    loads[7].wait()
    for other in (1, 2, 3):
        late_copy(other).wait_recv()
    for j in range(early_pieces, pieces):
        sum_piece(j, late_v, (j - early_pieces) * piece)
    step_on(0)

    def both_end_copy():
        return remote(both_sent, both_end, both_send.at[0], both_recv.at[0], inward)

    def both_mid_copy():
        return remote(both_inner, both_mid, both_send.at[1], both_recv.at[1], across)

    def both_back_copy():
        return remote(both_total, joined, both_send.at[2], both_recv.at[2], outward)

    def both_here():
        return pltpu.make_async_copy(both_total, joined, both_local)

    for other in (1, 2, 3):
        quarter_copy(other).wait_recv()
    own_rows = pl.ds(pl.multiple_of(place * quarter, quarter), quarter)
    both_sent[...] = (
        joined_v[own_rows, :].astype(f32)
        + quarter_got[0].astype(f32)
        + (quarter_got[1].astype(f32) + quarter_got[2].astype(f32))
    ).astype(bf16)

    @pl.when(at_end)
    def _():
        both_end_copy().start()

    step_on(1)

    loads[9].wait()

    def home_copy(i):
        return remote(
            final_v.at[i], home_v.at[seq], home_send.at[i], home_recv.at[seq], (place, 2 * half + i, core)
        )

    def home_direct(i):
        return remote(final_v.at[i], home.at[seq, core], home_send.at[i], home_took.at[seq], other_core)

    def home_here(i):
        return pltpu.make_async_copy(final_v.at[i], home.at[seq, core], home_local)

    for i in range(2):
        tp_copy(i + 2).wait_recv()
        pair_copy(i).wait_recv()
        final_v[i] = (
            own_v[i + 2] + tp_got[i + 2].astype(f32) + pair_got[i].astype(f32) + one_v[2 * i + core]
        ).astype(bf16)

        @pl.when(2 * half + i == stage)
        def _():
            home_direct(i).start()
            home_here(i).start()

        @pl.when(2 * half + i != stage)
        def _():
            home_copy(i).start()

    @pl.when(~at_end)
    def _():
        for j in range(early_pieces, pieces):
            from_end(j)
            from_mid(j - early_pieces // 2)
        both_end_copy().wait_recv()
        both_inner[half] = both_sent[...]
        both_inner[1 - half] = both_end[...]
        both_mid_copy().start()
        for j in range(pieces - early_pieces // 2, pieces):
            from_mid(j)
        both_mid_copy().wait_recv()
        both_total[...] = (both_inner[...].astype(f32) + both_mid[...].astype(f32)).astype(bf16)
        both_back_copy().start()
        both_here().start()

    step_on(2)
    step_on(3)
    sums[...] = step_v[4]

    def home_arrival(which):
        return remote(
            home_v.at[which], home_v.at[which], home_pass.at[which], home_recv.at[which], other_core
        )

    def home_share(which, whose):
        return remote(
            home_v.at[which], home.at[which, whose], home_pass.at[which], home_took.at[which], other_core
        )

    def home_keep(which):
        return pltpu.make_async_copy(home_v.at[which], home.at[which, core], home_sem.at[which])

    for which in (0, 1):

        @pl.when(2 * which + stage // 2 != stage)
        def _():
            home_arrival(which).wait_recv()
            home_share(which, core).start()
            home_keep(which).start()

    @pl.when(~at_end)
    def _():
        for j in range(pieces):
            mid_copy(j).wait_send()
            back_copy(j).wait_send()
            shard_copy(j).wait()
        both_mid_copy().wait_send()
        both_back_copy().wait_send()
        both_here().wait()

    @pl.when(~at_end)
    def _():
        for j in range(down_pieces):
            down_mid(j).wait_send()
            down_back(j).wait_send()
            down_here(j).wait()

    @pl.when(at_end)
    def _():
        for j in range(down_pieces):
            down_back(j).wait_recv()
        for j in range(pieces):
            end_copy(j).wait_send()
            back_copy(j).wait_recv()
        both_end_copy().wait_send()
        both_back_copy().wait_recv()

    for i in range(4):
        tp_copy(i).wait_send()
        step_copy(i).wait_send()
    for i in range(2):
        pair_copy(i).wait_send()

        @pl.when(2 * half + i == stage)
        def _():
            home_direct(i).wait_send()
            home_here(i).wait()

        @pl.when(2 * half + i != stage)
        def _():
            home_copy(i).wait_send()

    for which in (0, 1):

        @pl.when(2 * which + stage // 2 != stage)
        def _():
            home_share(which, core).wait_send()
            home_keep(which).wait()

        home_share(which, 1 - core).wait_recv()
    for other in (1, 2, 3):
        quarter_copy(other).wait_send()
        late_copy(other).wait_send()


def tail(d_query, d_key, d_value, w_joined, sums, sequence, grad_one, early, late, moved, downs):
    rows, width = sequence.shape[1:]
    quarter = early.shape[0]
    joined = w_joined.shape[1]
    piece = 3 * LANES
    columns = early.shape[1] + late.shape[2]
    pieces = columns // piece
    dma, bf16, f32 = pltpu.SemaphoreType.DMA, jnp.bfloat16, jnp.float32

    def vmem(shape, dtype=bf16):
        return pltpu.VMEM(shape, dtype)

    any_spec, vmem_spec = pl.BlockSpec(memory_space=pl.ANY), pl.BlockSpec(memory_space=pltpu.VMEM)
    cut = (pieces, quarter, piece)
    both = (2, quarter, joined)
    one, two, three, four, many = dma, dma((2,)), dma((3,)), dma((4,)), dma((pieces,))
    return pl.pallas_call(
        tail_kernel,
        in_specs=[any_spec] * 3 + [vmem_spec] * 2 + [any_spec] * 9,
        out_specs=[any_spec] * 4 + [vmem_spec],
        out_shape=[
            jax.ShapeDtypeStruct((2, 2, rows, width), bf16),
            jax.ShapeDtypeStruct((quarter, columns), bf16),
            jax.ShapeDtypeStruct(both, bf16),
            jax.ShapeDtypeStruct(downs[0].shape, bf16),
            jax.ShapeDtypeStruct(sums.shape, f32),
        ],
        scratch_shapes=[
            vmem(d_query.shape), vmem(d_query.shape), vmem(d_query.shape),
            vmem(sequence.shape), vmem(grad_one.shape, f32), vmem((4,) + early.shape), vmem(late.shape),
            vmem((8, rows, joined)), vmem((4, rows, width), f32),
            vmem((4, rows, width)), vmem((4, rows, width)), vmem((2, rows, width)), vmem((2, rows, width)),
            vmem((2, rows, width)),
            vmem(cut), vmem(cut), vmem(cut), vmem(cut), vmem(cut),
            vmem((width, joined)), vmem((3, quarter, joined)), vmem((quarter, joined)), vmem((quarter, joined)),
            vmem(both), vmem(both), vmem(both),
            vmem((5,) + sums.shape, f32), vmem((4,) + sums.shape, f32), vmem((2, rows, width)),
            vmem((2,) + downs[0].shape), vmem(downs[0].shape), vmem(downs[0].shape), vmem(downs[0].shape),
            dma((10,)), three, three, four, four, two, two, two, two, two, two, one,
            many, many, many, many, many, many, many,
            three, three, three, three, one, four, four, two, two, two, two, two, two,
        ],
        compiler_params=pltpu.CompilerParams(
            collective_id=2, has_side_effects=True, vmem_limit_bytes=VMEM_BYTES
        ),
        cost_estimate=pl.CostEstimate(flops=80 << 30, bytes_accessed=32 << 20, transcendentals=0),
        name="tail",
    )(d_query, d_key, d_value, w_joined, sums, sequence, grad_one, early, late, *moved, *downs)


def pick(pair, index):
    return lax.dynamic_index_in_dim(pair, index, 0, keepdims=False)


def finish_kernel(
    tokens_ref, shard_ref, joined_ref, down_ref, sums_ref,
    d_tokens, d_query, d_key, d_value, d_out, d_up, d_down, *vectors,
):
    f32 = jnp.float32
    for index in range(6):
        vectors[index][...] = sums_ref[index]
    biases = sums_ref[6]
    vectors[6][...] = biases[: biases.shape[0] // 2]
    vectors[7][...] = biases[biases.shape[0] // 2 :]
    d_tokens[...] = tokens_ref[...].astype(f32)
    units = d_up.shape[2]
    d_up[:, 0, :] = shard_ref[:, :units].astype(f32)
    d_up[:, 1, :] = shard_ref[:, units : 2 * units].astype(f32)
    d_out[...] = shard_ref[:, 2 * units :].astype(f32)
    d_down[...] = down_ref[...].astype(f32)
    width = d_query.shape[1] // 2
    for index, target in enumerate((d_query, d_key, d_value)):
        columns = slice(index * width, (index + 1) * width)
        target[...] = jnp.concatenate(
            [joined_ref[0, :, columns], joined_ref[1, :, columns]], 1
        ).astype(f32)


def finish(tokens, shard, joined, down, sums):
    steps = 4
    quarter, units = down.shape
    head_width = shard.shape[1] - 2 * units
    row, some = tokens.shape[0] // steps, quarter // steps
    sizes = [sums.shape[1]] * 6 + [head_width] * 2
    f32 = jnp.float32

    def rows(width):
        return pl.BlockSpec((some, width), lambda i: (i, 0))

    return pl.pallas_call(
        finish_kernel,
        grid=(steps,),
        in_specs=[
            pl.BlockSpec((row, tokens.shape[1]), lambda i: (i, 0)),
            rows(shard.shape[1]),
            pl.BlockSpec((2, some, joined.shape[2]), lambda i: (0, i, 0)),
            rows(units),
            pl.BlockSpec(sums.shape, lambda i: (0, 0)),
        ],
        out_specs=[
            pl.BlockSpec((row, tokens.shape[1]), lambda i: (i, 0)),
            rows(head_width), rows(head_width), rows(head_width), rows(head_width),
            pl.BlockSpec((some, 2, units), lambda i: (i, 0, 0)),
            rows(units),
            *[pl.BlockSpec((size,), lambda i: (0,)) for size in sizes],
        ],
        out_shape=[
            jax.ShapeDtypeStruct(tokens.shape, f32),
            *[jax.ShapeDtypeStruct((quarter, head_width), f32)] * 4,
            jax.ShapeDtypeStruct((quarter, 2, units), f32),
            jax.ShapeDtypeStruct((quarter, units), f32),
            *[jax.ShapeDtypeStruct((size,), f32) for size in sizes],
        ],
        compiler_params=pltpu.CompilerParams(vmem_limit_bytes=VMEM_BYTES),
        name="finish",
    )(tokens, shard, joined, down, sums)


def per_device_paired(
    tokens,
    doc_lengths,
    keep,
    w_query,
    b_query,
    w_key,
    w_value,
    b_value,
    w_out,
    b_out,
    gain_one,
    shift_one,
    w_up,
    w_down,
    b_down,
    gain_two,
    shift_two,
    cotangent,
):
    _, block_rows, model_width = tokens.shape
    length = 4 * block_rows
    half_rows = block_rows // 2
    local_heads = b_query.shape[0] // HEAD
    heads = local_heads // 2
    width = heads * HEAD
    cotangent = cotangent.reshape(2, 2, half_rows, model_width)
    half = lax.axis_index("ctx") % 2
    core = lax.axis_index("tp")
    slopes = head_slopes(core * local_heads + half * heads, heads)
    (
        sequence, full_joined, full_out, full_gate, up_lift, cot_far, cot_near, query_t, queries, keys, keys_t, values, values_t,
    ) = start(
        doc_lengths, slopes, tokens, keep, w_query, w_key, w_value, w_out, w_up, b_query, b_value,
        cotangent,
    )
    full_joined = full_joined.reshape(model_width, 3 * width)
    full_out = full_out.reshape(model_width, 2 * width)
    full_gate = full_gate.reshape(model_width, -1)
    lift_shards = [up_lift] + [
        lax.ppermute(up_lift, "fsdp", swap) for swap in (X_SWAP, Y_SWAP, D_SWAP)
    ]
    cotangents = (
        cotangent,
        lax.ppermute(cot_far, "ctx", [(3, 1), (0, 2), (1, 0), (2, 3)]),
        lax.ppermute(cot_near, "ctx", [(1, 2), (2, 1)]),
    )
    attended_all, attended_t, lse = attend(doc_lengths, slopes, query_t, keys, values_t)

    vectors = (b_out, gain_one, shift_one, b_down, gain_two, shift_two)
    out, grad_one, grad_heads, *early, late, down_sum, sums = middle(
        attended_all.reshape(8, half_rows, width),
        sequence.reshape(8, half_rows, model_width),
        cotangents,
        full_out,
        full_gate,
        w_down,
        lift_shards,
        vectors,
    )
    out = out.reshape(2, block_rows, model_width)
    grad_heads = grad_heads.reshape(length, width)
    moved = [
        lax.ppermute(early[other], "fsdp", swap)
        for other, swap in ((1, X_SWAP), (2, Y_SWAP), (3, D_SWAP))
    ]
    downs = (down_sum, lax.ppermute(down_sum, "ctx", [(0, 1), (3, 2)]))
    d_query, d_key, d_value = attend_back(
        doc_lengths, slopes, query_t, queries, keys, keys_t, values, grad_heads, attended_t, lse
    )
    d_tokens, shard, joined, down, sums = tail(
        d_query.reshape(8, half_rows, width),
        d_key.reshape(8, half_rows, width),
        d_value.reshape(8, half_rows, width),
        full_joined,
        sums,
        sequence.reshape(8, half_rows, model_width),
        grad_one,
        early[0],
        late,
        moved,
        downs,
    )
    (
        d_tokens, d_w_query, d_w_key, d_w_value, sum_out, sum_up, sum_down,
        total_gain_two, total_shift_two, total_b_down, total_gain_one, total_shift_one, total_b_out,
        total_b_query, total_b_value,
    ) = finish(
        d_tokens.reshape(2 * block_rows, model_width), shard, joined, down, sums
    )
    d_tokens = d_tokens.reshape(2, block_rows, model_width)
    return (
        out,
        d_tokens,
        d_w_query,
        total_b_query,
        d_w_key,
        d_w_value,
        total_b_value,
        sum_out,
        total_b_out,
        total_gain_one,
        total_shift_one,
        sum_up,
        sum_down,
        total_b_down,
        total_gain_two,
        total_shift_two,
    )


def paired(mesh, tokens, doc_lengths, b_query):
    sizes = dict(mesh.shape)
    return (
        sizes == {"fsdp": 4, "ctx": 4, "tp": 2}
        and tokens.shape[0] == 8
        and tokens.shape[1] % (8 * TILE) == 0
        and doc_lengths.shape[1] <= KEEP_ROW - DOC_ROW
        and b_query.shape[0] % (4 * HEAD) == 0
    )


def solution(mesh):
    in_specs = (
        P("fsdp", "ctx", None),
        P("fsdp", None),
        P("fsdp", "ctx"),
        P("fsdp", "tp"),
        P("tp"),
        P("fsdp", "tp"),
        P("fsdp", "tp"),
        P("tp"),
        P("fsdp", "tp"),
        P(),
        P(),
        P(),
        P("fsdp", None, "tp"),
        P("fsdp", "tp"),
        P(),
        P(),
        P(),
        P("fsdp", "ctx", None),
    )
    out_specs = (
        P("fsdp", "ctx", None),
        P("fsdp", "ctx", None),
        P("fsdp", "tp"),
        P("tp"),
        P("fsdp", "tp"),
        P("fsdp", "tp"),
        P("tp"),
        P("fsdp", "tp"),
        P(),
        P(),
        P(),
        P("fsdp", None, "tp"),
        P("fsdp", "tp"),
        P(),
        P(),
        P(),
    )

    def whole(*args):
        body = per_device_paired if paired(mesh, args[0], args[1], args[4]) else per_device_general
        return jax.shard_map(
            body, mesh=mesh, in_specs=in_specs, out_specs=out_specs, check_vma=False
        )(*args)

    return whole
```
